32 devices in a mesh: seq: 8 (over z, x), head: 4 (over y, core).
Axes of the slice: x: 2, y: 2, z: 4, core: 2. Of those that a mesh axis runs over, the one named last changes fastest.
Arguments:
- layer_in: bfloat16 [2, 4096, 2048], P(None, 'seq'), may hold values from -6 to 6
- seg_starts: int32 [2, 4096], P(None, 'seq'), may hold values from 0 to 1, as said below
- attn_gain: bfloat16 [2048], P('seq'), may hold values from 0.5 to 1.5
- query_weight: bfloat16 [2048, 1024], P('seq', 'head'), may hold values from -0.125 to 0.125
- key_weight: bfloat16 [2048, 1024], P('seq', 'head'), may hold values from -0.125 to 0.125
- value_weight: bfloat16 [2048, 2048], P('seq', 'head'), may hold values from -0.125 to 0.125
- gate_weight: bfloat16 [2048, 2048], P('seq', 'head'), may hold values from -0.125 to 0.125
- decay_down: bfloat16 [2048, 16], P('seq'), may hold values from -0.125 to 0.125
- decay_up: bfloat16 [16, 1024], P(None, ('head', 'seq')), may hold values from -1.5 to 1.5
- decay_bias: bfloat16 [1024], P(('head', 'seq')), may hold values from -1 to 9
- head_gain: bfloat16 [512], P('seq'), may hold values from 0.5 to 1.5
- out_weight: bfloat16 [2048, 2048], P('head', 'seq'), may hold values from -0.25 to 0.25
- ffn_gain: bfloat16 [2048], P('seq'), may hold values from 0.5 to 1.5
- ffn_gate: bfloat16 [2048, 5632], P('seq', 'head'), may hold values from -0.125 to 0.125
- ffn_up: bfloat16 [2048, 5632], P('seq', 'head'), may hold values from -0.125 to 0.125
- ffn_down: bfloat16 [5632, 2048], P('head', 'seq'), may hold values from -0.15625 to 0.15625
- out_grad: bfloat16 [2, 4096, 2048], P(None, 'seq'), may hold values from -6 to 6
Outputs:
- layer_out: bfloat16 [2, 4096, 2048], P(None, 'seq')
- input_grad: bfloat16 [2, 4096, 2048], P(None, 'seq')
- grad_attn_gain: float32 [2048], P('seq')
- grad_query: float32 [2048, 1024], P('seq', 'head')
- grad_key: float32 [2048, 1024], P('seq', 'head')
- grad_value: float32 [2048, 2048], P('seq', 'head')
- grad_gate: float32 [2048, 2048], P('seq', 'head')
- grad_decay_down: float32 [2048, 16], P('seq')
- grad_decay_up: float32 [16, 1024], P(None, ('head', 'seq'))
- grad_decay_bias: float32 [1024], P(('head', 'seq'))
- grad_head_gain: float32 [512], P('seq')
- grad_out_weight: float32 [2048, 2048], P('head', 'seq')
- grad_ffn_gain: float32 [2048], P('seq')
- grad_ffn_gate: float32 [2048, 5632], P('seq', 'head')
- grad_ffn_up: float32 [2048, 5632], P('seq', 'head')
- grad_ffn_down: float32 [5632, 2048], P('head', 'seq')
The draws below stay inside these ranges and needn't reach their ends.
Inputs may be any that keep to these rules, and one draw needn't show every extreme that they name: `seg_starts`: the first token of each sequence begins a segment; every segment holds 1024 tokens or more; in one micro-batch, drawn from the seed, the whole sequence is one segment.
All inputs are finite; a program needn't handle non-finite values.
Results may differ from the reference program's by a relative error of at most 0.039.
Values may be sent and summed in bfloat16 or wider, within the bound.
A program may use at most 256 MiB of HBM per device.

```python
import math
import jax
import jax.numpy as jnp
from jax import lax

D = 2048
HEADS = 4
DK = 256
DV = 512
RANK = 16
FF = 5632
GROUP = 64
MB = 2
SEG_MIN = 1024
SEQ_LEN = 4096
HK = 1024
HV = 2048


def draw_seg_starts(key, part):
    first_key, second_key = jax.random.split(jax.random.fold_in(key, 11))
    single = jax.random.randint(first_key, (), 0, MB)
    number = max(SEQ_LEN // (4 * SEG_MIN), 1)
    spare = SEQ_LEN - (number + 1) * SEG_MIN + 1
    offsets = jnp.sort(jax.random.randint(second_key, (MB, number), 0, spare), axis=1)
    cuts = offsets + SEG_MIN * jnp.arange(1, number + 1)
    places = jnp.arange(SEQ_LEN)
    marked = jnp.any(places[None, :, None] == cuts[:, None, :], axis=2)
    batch_ids = jnp.arange(MB)[:, None]
    marked = jnp.where(batch_ids == single, False, marked)
    marked = marked | (places[None, :] == 0)
    return marked.astype(jnp.int32)


def draw_decay_bias(key, part):
    coin_key, slow_key, fast_key = jax.random.split(jax.random.fold_in(key, 23), 3)
    share = 0.5
    slow = jnp.exp(jax.random.uniform(slow_key, (HK,), jnp.float32, math.log(0.2 / SEQ_LEN), math.log(1.0 / SEQ_LEN)))
    fast = jnp.exp(jax.random.uniform(fast_key, (HK,), jnp.float32, math.log(4.0 / SEQ_LEN), math.log(0.07)))
    chosen = jax.random.uniform(coin_key, (HK,), jnp.float32) < share
    rate = jnp.where(chosen, slow, fast)
    return (-jnp.log(jnp.expm1(16.0 * rate))).astype(jnp.bfloat16)


def level_of(key, dims, shards, low, high):
    loudness = 1.0
    for dim, blocks in shards:
        draws = jax.random.uniform(jax.random.fold_in(jax.random.fold_in(key, 6), dim), (blocks,), jnp.float32, low / len(shards), high / len(shards))
        loudness = loudness * jnp.repeat(jnp.exp(draws), dims[dim] // blocks).reshape((-1,) + (1,) * (len(dims) - 1 - dim))
    return loudness


def noise(key, shape, scale, bound, shards=(), kind=jnp.bfloat16):
    entries = scale * jax.random.normal(key, shape, jnp.float32)
    if shards:
        entries = entries * level_of(key, shape, shards, -0.22, 0.18)
    return jnp.clip(entries, -bound, bound).astype(kind)


def setup_inputs(seed: int = 0) -> dict:
    splits = jax.random.split(jax.random.key(seed), 18)
    layer_in = noise(splits[0], (MB, SEQ_LEN, D), 1.0, 6.0, ((1, 8),))
    seg_starts = draw_seg_starts(jax.random.fold_in(splits[17], 71), 0)
    attn_gain = jnp.clip(1.0 + 0.1 * jax.random.normal(splits[2], (D,), jnp.float32), 0.5, 1.5).astype(jnp.bfloat16)
    query_weight = noise(splits[3], (D, HK), D ** -0.5, 0.125, ((0, 8), (1, 4)))
    key_weight = noise(splits[4], (D, HK), D ** -0.5, 0.125, ((0, 8), (1, 4)))
    value_weight = noise(splits[5], (D, HV), D ** -0.5, 0.125, ((0, 8), (1, 4)))
    gate_weight = noise(splits[6], (D, HV), D ** -0.5, 0.125, ((0, 8), (1, 4)))
    decay_down = noise(splits[7], (D, RANK), D ** -0.5, 0.125, ((0, 8),))
    decay_up = noise(splits[8], (RANK, HK), RANK ** -0.5, 1.5, ((1, 32),))
    decay_bias = draw_decay_bias(jax.random.fold_in(splits[17], 71), 0)
    head_gain = jnp.clip(1.0 + 0.1 * jax.random.normal(splits[10], (DV,), jnp.float32), 0.5, 1.5).astype(jnp.bfloat16)
    out_weight = noise(splits[11], (HV, D), (HV // 4) ** -0.5, 0.25, ((0, 4), (1, 8)))
    ffn_gain = jnp.clip(1.0 + 0.1 * jax.random.normal(splits[12], (D,), jnp.float32), 0.5, 1.5).astype(jnp.bfloat16)
    ffn_gate = noise(splits[13], (D, FF), D ** -0.5, 0.125, ((0, 8), (1, 4)))
    ffn_up = noise(splits[14], (D, FF), D ** -0.5, 0.125, ((0, 8), (1, 4)))
    ffn_down = noise(splits[15], (FF, D), (FF // 4) ** -0.5, 0.15625, ((0, 4), (1, 8)))
    out_grad = noise(splits[16], (MB, SEQ_LEN, D), 1.0, 6.0, ((1, 8),))
    return dict(layer_in=layer_in, seg_starts=seg_starts, attn_gain=attn_gain, query_weight=query_weight, key_weight=key_weight, value_weight=value_weight, gate_weight=gate_weight, decay_down=decay_down, decay_up=decay_up, decay_bias=decay_bias, head_gain=head_gain, out_weight=out_weight, ffn_gain=ffn_gain, ffn_gate=ffn_gate, ffn_up=ffn_up, ffn_down=ffn_down, out_grad=out_grad)


EPS = 1e-06
HIGH = lax.Precision.HIGHEST

@jax.custom_vjp
def low(v):
    return lax.optimization_barrier(v.astype(jnp.bfloat16)).astype(jnp.float32)

@jax.custom_vjp
def low_back(v):
    return v

def low_keep(v):
    return (low(v), None)

def low_pass(kept, grad):
    return (grad,)

def back_keep(v):
    return (v, None)

def back_low(kept, grad):
    return (low(grad),)
low.defvjp(low_keep, low_pass)
low_back.defvjp(back_keep, back_low)

def product(left, right):
    return jnp.matmul(left, right, precision=HIGH)

def root_scale(field):
    return lax.rsqrt(lax.optimization_barrier(jnp.mean(field * field, axis=-1, keepdims=True)) + EPS)

def mixer_scan(queries, keys, values, decays, starts, state):
    batch, length, heads, key_size = queries.shape
    value_size = values.shape[-1]
    number = length // GROUP

    def blocks(field):
        return jnp.moveaxis(field.reshape((batch, number, GROUP) + field.shape[2:]), 1, 0)

    def advance(carry, piece):
        query_block, key_block, value_block, decay_block, start_block = piece
        cumulative = jnp.cumsum(decay_block, axis=1)
        segment = jnp.cumsum(start_block, axis=1, dtype=jnp.int32)
        untouched = (segment == 0).astype(jnp.float32)
        query_scaled = query_block * key_size ** (-0.5) * jnp.exp(cumulative)
        key_scaled = key_block * jnp.exp(-cumulative)
        scores = jnp.einsum('bthk,bshk->bhts', query_scaled, key_scaled, precision=HIGH)
        places = jnp.arange(GROUP)
        allowed = (segment[:, :, None] == segment[:, None, :]) & (places[:, None] >= places[None, :])[None]
        scores = jnp.where(allowed[:, None], scores, 0.0)
        within = jnp.einsum('bhts,bshv->bthv', scores, value_block, precision=HIGH)
        carried = jnp.einsum('bthk,bhkv->bthv', query_scaled * untouched[:, :, None, None], carry, precision=HIGH)
        final_decay = cumulative[:, -1]
        trailing = (segment == segment[:, -1:]).astype(jnp.float32)
        key_trailing = key_block * jnp.exp(final_decay[:, None] - cumulative) * trailing[:, :, None, None]
        kept_state = carry * (jnp.exp(final_decay) * untouched[:, -1, None, None])[..., None]
        carry = kept_state + jnp.einsum('bshk,bshv->bhkv', key_trailing, value_block, precision=HIGH)
        return (carry, within + carried)
    pieces = (blocks(queries), blocks(keys), blocks(values), blocks(decays), blocks(starts))
    final_state, outputs = lax.scan(jax.checkpoint(advance), state, pieces)
    return (jnp.moveaxis(outputs, 0, 1).reshape(batch, length, heads, value_size), final_state)

def forward(inputs, seg_starts, attn_gain, query_weight, key_weight, value_weight, gate_weight, decay_down, decay_up, decay_bias, head_gain, out_weight, ffn_gain, ffn_gate, ffn_up, ffn_down):
    batch, length = seg_starts.shape
    normed = low(inputs * root_scale(inputs) * attn_gain)
    queries = low(low_back(product(normed, query_weight)))
    keys = low(low_back(product(normed, key_weight)))
    values = low(low_back(product(normed, value_weight)))
    lowrank = low_back(product(normed, decay_down))
    raw = product(lowrank, decay_up) + decay_bias
    decays = jax.nn.log_sigmoid(raw) / 16.0
    gates = low_back(product(normed, gate_weight))
    zero_state = jnp.zeros((batch, HEADS, DK, DV), jnp.float32)
    mixed, final_state = mixer_scan(queries.reshape(batch, length, HEADS, DK), keys.reshape(batch, length, HEADS, DK), values.reshape(batch, length, HEADS, DV), decays.reshape(batch, length, HEADS, DK), seg_starts, zero_state)
    head_unit = mixed * root_scale(mixed)
    gate_act = jax.nn.silu(gates).reshape(batch, length, HEADS, DV)
    normed_heads = low((head_unit * head_gain * gate_act).reshape(batch, length, HEADS * DV))
    attn = low_back(product(normed_heads, out_weight))
    resid = inputs + attn
    normed_two = low(resid * root_scale(resid) * ffn_gain)
    pre_gate = low_back(product(normed_two, ffn_gate))
    pre_up = low_back(product(normed_two, ffn_up))
    act = low(jax.nn.silu(pre_gate) * pre_up)
    return resid + product(act, ffn_down)

def reference(layer_in, seg_starts, attn_gain, query_weight, key_weight, value_weight, gate_weight, decay_down, decay_up, decay_bias, head_gain, out_weight, ffn_gain, ffn_gate, ffn_up, ffn_down, out_grad):

    def wrapped(inputs, gain_one, query_w, key_w, value_w, gate_w, down_w, up_w, bias_w, gain_head, out_w, gain_two, fgate_w, fup_w, fdown_w):
        return forward(inputs, seg_starts, gain_one, query_w, key_w, value_w, gate_w, down_w, up_w, bias_w, gain_head, out_w, gain_two, fgate_w, fup_w, fdown_w)
    result, pullback = jax.vjp(wrapped, layer_in.astype(jnp.float32), attn_gain.astype(jnp.float32), query_weight.astype(jnp.float32), key_weight.astype(jnp.float32), value_weight.astype(jnp.float32), gate_weight.astype(jnp.float32), decay_down.astype(jnp.float32), decay_up.astype(jnp.float32), decay_bias.astype(jnp.float32), head_gain.astype(jnp.float32), out_weight.astype(jnp.float32), ffn_gain.astype(jnp.float32), ffn_gate.astype(jnp.float32), ffn_up.astype(jnp.float32), ffn_down.astype(jnp.float32))
    grads = pullback(out_grad.astype(jnp.float32))
    return (result.astype(jnp.bfloat16), grads[0].astype(jnp.bfloat16), grads[1], grads[2], grads[3], grads[4], grads[5], grads[6], grads[7], grads[8], grads[9], grads[10], grads[11], grads[12], grads[13], grads[14])
```

```python
import jax
import jax.numpy as jnp
from jax import lax
from jax.sharding import PartitionSpec as P

DK = 256
DV = 512
GROUP = 64


EPS = 1e-06
HIGH = lax.Precision.HIGHEST


def prefix_states(value, axis, join, neutral, later):
    count, mine = (lax.axis_size(axis), lax.axis_index(axis))
    pieces = (
        lax.all_gather(value[0], axis),
        lax.all_gather(value[1].astype(jnp.bfloat16), axis),
    )
    total = neutral
    for position in range(count - 1):
        source = count - 1 - position if later else position
        longer = join(total, (pieces[0][source], pieces[1][source].astype(jnp.float32)))
        use = source > mine if later else source < mine
        total = jax.tree.map(lambda new, old: jnp.where(use, new, old), longer, total)
    return total


def root_scale(field):
    return lax.rsqrt(jnp.mean(field * field, axis=-1, keepdims=True) + EPS)


def norm_back(upstream, unit, scale):
    return scale * (upstream - unit * jnp.mean(upstream * unit, axis=-1, keepdims=True))


def matmul(left, right):
    return jnp.dot(left, right, preferred_element_type=jnp.float32)


def matmul_nt(left, right):
    return lax.dot_general(
        left, right, (((1,), (1,)), ((), ())), preferred_element_type=jnp.float32
    )


def matmul_tn(left, right):
    return lax.dot_general(
        left, right, (((0,), (0,)), ((), ())), preferred_element_type=jnp.float32
    )


def running(field, axis=1):
    length = field.shape[axis]
    places = jnp.arange(length)
    lower = (places[:, None] >= places[None, :]).astype(jnp.float32)
    return jnp.einsum("ts,bs...->bt...", lower, field.astype(jnp.float32), precision=HIGH)


def ring_order(count):
    return list(range(0, count, 2)) + list(range(count - 1 - count % 2, 0, -2))


class Ring:
    def __init__(self, axis):
        self.axis = axis
        self.count = count = lax.axis_size(axis)
        order = ring_order(count)
        place = [order.index(i) for i in range(count)]
        self.right = [(order[i], order[(i + 1) % count]) for i in range(count)]
        self.left = [(order[i], order[(i - 1) % count]) for i in range(count)]
        owners = [[order[(place[i] + r) % count] for r in range(count)] for i in range(count)]
        slots = [[(place[i] - place[me]) % count for i in range(count)] for me in range(count)]
        mine = lax.axis_index(axis)
        self.owners = jnp.asarray(owners, jnp.int32)[mine]
        self.slots = jnp.asarray(slots, jnp.int32)[mine]

    def arrange(self, field, dim, table):
        width = field.shape[dim] // self.count
        return jnp.concatenate(
            [
                lax.dynamic_slice_in_dim(field, table[r] * width, width, dim)
                for r in range(self.count)
            ],
            axis=dim,
        )

    def near(self, field, dim):
        return self.arrange(field, dim, self.owners)

    def home(self, field, dim):
        return self.arrange(field, dim, self.slots)

    def gather(self, block, after=None):
        count, half = self.count, block.shape[0] // 2
        up, down = block[:half], block[half:]
        if after is not None:
            up, down, _ = lax.optimization_barrier((up, down, after))
        pieces = [None] * (2 * count)
        pieces[0], pieces[1] = up, down
        for step in range(1, count):
            up = lax.ppermute(up, self.axis, self.right)
            down = lax.ppermute(down, self.axis, self.left)
            pieces[2 * (count - step)] = up
            pieces[2 * step + 1] = down
            if step == count - 2:
                late = up[:8, :128]
        return jnp.concatenate(pieces, axis=0), late

    def scatter(self, total):
        count = self.count
        rows = total.shape[0] // count
        half = rows // 2

        def piece(slot, part):
            start = slot * rows + part * half
            return total[start : start + half]

        up, down = piece(count - 1, 0), piece(1, 1)
        for step in range(count - 1):
            up = lax.ppermute(up, self.axis, self.right)
            down = lax.ppermute(down, self.axis, self.left)
            up = up.astype(jnp.float32) + piece(count - 2 - step, 0).astype(jnp.float32)
            down = down.astype(jnp.float32) + piece((step + 2) % count, 1).astype(jnp.float32)
            if step < count - 2:
                up, down = up.astype(jnp.bfloat16), down.astype(jnp.bfloat16)
        return jnp.concatenate([up, down], axis=0)


def combine_states(earlier, later):
    return (earlier[0] * later[0], later[0][..., None] * earlier[1] + later[1])


def mixer_scan(queries, keys, values, decays, starts, state):
    batch, length, heads, key_size = queries.shape
    value_size = values.shape[-1]
    number = length // GROUP

    def blocks(field):
        return jnp.moveaxis(field.reshape((batch, number, GROUP) + field.shape[2:]), 1, 0)

    def advance(carry, piece):
        query_block, key_block, value_block, decay_block, start_block = piece
        cumulative = running(decay_block)
        segment = running(start_block)
        untouched = (segment == 0).astype(jnp.float32)
        query_scaled = query_block * key_size ** (-0.5) * jnp.exp(cumulative)
        key_scaled = key_block * jnp.exp(-cumulative)
        scores = jnp.einsum("bthk,bshk->bhts", query_scaled, key_scaled, precision=HIGH)
        places = jnp.arange(GROUP)
        allowed = (segment[:, :, None] == segment[:, None, :]) & (
            places[:, None] >= places[None, :]
        )[None]
        scores = jnp.where(allowed[:, None], scores, 0.0)
        within = jnp.einsum("bhts,bshv->bthv", scores, value_block, precision=HIGH)
        carried = jnp.einsum(
            "bthk,bhkv->bthv", query_scaled * untouched[:, :, None, None], carry, precision=HIGH
        )
        final_decay = cumulative[:, -1]
        trailing = (segment == segment[:, -1:]).astype(jnp.float32)
        key_trailing = (
            key_block * jnp.exp(final_decay[:, None] - cumulative) * trailing[:, :, None, None]
        )
        kept_state = carry * (jnp.exp(final_decay) * untouched[:, -1, None, None])[..., None]
        carry = kept_state + jnp.einsum(
            "bshk,bshv->bhkv", key_trailing, value_block, precision=HIGH
        )
        return (carry, within + carried)

    pieces = (blocks(queries), blocks(keys), blocks(values), blocks(decays), blocks(starts))
    final_state, outputs = lax.scan(jax.checkpoint(advance), state, pieces)
    return (jnp.moveaxis(outputs, 0, 1).reshape(batch, length, heads, value_size), final_state)


def shards(
    layer_in,
    seg_starts,
    attn_gain,
    query_weight,
    key_weight,
    value_weight,
    gate_weight,
    decay_down,
    decay_up,
    decay_bias,
    head_gain,
    out_weight,
    ffn_gain,
    ffn_gate,
    ffn_up,
    ffn_down,
    out_grad,
):
    ring = Ring("seq")
    batch, block, width = layer_in.shape
    key_cols, value_cols = key_weight.shape[1], value_weight.shape[1]
    rank = decay_down.shape[1]
    first, mark = ring.gather(jnp.concatenate([key_weight, value_weight, decay_down], axis=1))
    second, mark = ring.gather(jnp.concatenate([query_weight, gate_weight], axis=1), mark)
    out_t, mark = ring.gather(out_weight.T, mark)
    fgate_all, mark_gate = ring.gather(ffn_gate, mark)
    fup_all, mark_up = ring.gather(ffn_up, mark)
    fdown_t, mark = ring.gather(ffn_down.T, mark_up)
    small = jnp.concatenate([attn_gain, ffn_gain, head_gain, decay_bias, decay_up.reshape(-1)])
    small = lax.all_gather(small, "seq")
    cuts = [attn_gain.size, ffn_gain.size, head_gain.size, decay_bias.size]
    cuts = [sum(cuts[: i + 1]) for i in range(4)]
    gain_one_all = ring.near(small[:, : cuts[0]].reshape(-1), 0)
    gain_two_all = ring.near(small[:, cuts[0] : cuts[1]].reshape(-1), 0)
    head_gain_all = small[:, cuts[1] : cuts[2]].reshape(-1)
    bias_all = small[:, cuts[2] : cuts[3]].reshape(-1)
    up_all = jnp.moveaxis(small[:, cuts[3] :].reshape(ring.count, rank, -1), 0, 1)
    up_all = up_all.reshape(rank, -1)
    rows = batch * block
    inputs = ring.near(layer_in.reshape(rows, width), 1).astype(jnp.float32)
    scale_one = root_scale(inputs)
    unit_one = inputs * scale_one
    gain_one = gain_one_all.astype(jnp.float32)
    normed = (unit_one * gain_one).astype(jnp.bfloat16)
    firsts = matmul(normed, first)
    keys = firsts[:, :key_cols].astype(jnp.bfloat16)
    values = firsts[:, key_cols : key_cols + value_cols].astype(jnp.bfloat16)
    lowrank = firsts[:, key_cols + value_cols :]
    raw = jnp.dot(lowrank, up_all.astype(jnp.float32), precision=HIGH) + bias_all.astype(
        jnp.float32
    )
    decays = jax.nn.log_sigmoid(raw) / 16.0
    seconds = matmul(normed, second)
    queries = seconds[:, :key_cols].astype(jnp.bfloat16)
    gates = seconds[:, key_cols:]
    heads = values.shape[1] // DV
    query_heads = queries.astype(jnp.float32).reshape(batch, block, heads, DK)
    key_heads = keys.astype(jnp.float32).reshape(batch, block, heads, DK)
    value_heads = values.astype(jnp.float32).reshape(batch, block, heads, DV)
    decay_heads = decays.reshape(batch, block, heads, DK)
    zero_state = jnp.zeros((batch, heads, DK, DV), jnp.float32)
    local_out, local_state = mixer_scan(
        query_heads, key_heads, value_heads, decay_heads, seg_starts, zero_state
    )
    block_segment = running(seg_starts)
    untouched = (block_segment == 0).astype(jnp.float32)
    cumulative = running(decay_heads)
    carry_query = query_heads * DK ** (-0.5) * jnp.exp(cumulative) * untouched[:, :, None, None]
    block_decay = jnp.exp(cumulative[:, -1]) * untouched[:, -1, None, None]
    identity = (jnp.ones_like(block_decay), jnp.zeros_like(local_state))
    prefix = prefix_states((block_decay, local_state), "seq", combine_states, identity, False)
    state_in = prefix[1]
    mixed = local_out + jnp.einsum("bthk,bhkv->bthv", carry_query, state_in, precision=HIGH)
    head_scale = root_scale(mixed)
    head_unit = mixed * head_scale
    head_gain_f = head_gain_all.astype(jnp.float32)
    sigma_gate = jax.nn.sigmoid(gates)
    gate_act = (gates * sigma_gate).reshape(batch, block, heads, DV)
    normed_heads = (
        (head_unit * head_gain_f * gate_act).reshape(rows, heads * DV).astype(jnp.bfloat16)
    )
    attn_part = matmul_nt(normed_heads, out_t)
    gain_two = gain_two_all.astype(jnp.float32)
    attn = lax.psum(attn_part.astype(jnp.bfloat16), "head").astype(jnp.float32)
    resid = inputs + attn
    scale_two = root_scale(resid)
    unit_two = resid * scale_two
    normed_two = (unit_two * gain_two).astype(jnp.bfloat16)
    pre_gate = matmul(normed_two, fgate_all)
    pre_up = matmul(normed_two, fup_all)
    sigma_pre = jax.nn.sigmoid(pre_gate)
    silu_pre = pre_gate * sigma_pre
    act = (silu_pre * pre_up).astype(jnp.bfloat16)
    ffn_part = matmul_nt(act, fdown_t)
    ffn = lax.psum(ffn_part.astype(jnp.bfloat16), "head").astype(jnp.float32)
    layer_out = ring.home((resid + ffn).astype(jnp.bfloat16), 1).reshape(batch, block, width)
    grad_rows = ring.near(out_grad.reshape(rows, width), 1)
    grad_float = grad_rows.astype(jnp.float32)
    d_act = matmul(grad_rows, fdown_t)
    grad_fdown_t = matmul_tn(grad_rows, act).astype(jnp.bfloat16)
    d_pre_gate = (d_act * pre_up * sigma_pre * (1.0 + pre_gate * (1.0 - sigma_pre))).astype(
        jnp.bfloat16
    )
    d_pre_up = (d_act * silu_pre).astype(jnp.bfloat16)
    grad_fgate = matmul_tn(normed_two, d_pre_gate).astype(jnp.bfloat16)
    grad_fup = matmul_tn(normed_two, d_pre_up).astype(jnp.bfloat16)
    d_normed_two_part = matmul_nt(d_pre_gate, fgate_all) + matmul_nt(d_pre_up, fup_all)
    d_normed_two = lax.psum(d_normed_two_part.astype(jnp.bfloat16), "head").astype(jnp.float32)
    grad_gain_two = jnp.sum(d_normed_two * unit_two, axis=0)
    d_resid = grad_float + norm_back(d_normed_two * gain_two, unit_two, scale_two)
    d_attn = d_resid.astype(jnp.bfloat16)
    grad_out_t = matmul_tn(d_attn, normed_heads).astype(jnp.bfloat16)
    d_heads = matmul(d_attn, out_t).reshape(batch, block, heads, DV)
    d_gate_act = (d_heads * head_unit * head_gain_f).reshape(rows, heads * DV)
    d_gates = (d_gate_act * sigma_gate * (1.0 + gates * (1.0 - sigma_gate))).astype(jnp.bfloat16)
    grad_head_part = jnp.sum(d_heads * gate_act * head_unit, axis=(0, 1, 2))
    d_mixed = norm_back(d_heads * gate_act * head_gain_f, head_unit, head_scale)
    local_grad = jnp.einsum("bthk,bthv->bhkv", carry_query, d_mixed, precision=HIGH)
    suffix = prefix_states((block_decay, local_grad), "seq", combine_states, identity, True)

    def recurrence(query_in, key_in, value_in, decay_in):
        return mixer_scan(query_in, key_in, value_in, decay_in, seg_starts, state_in)

    unused, pullback = jax.vjp(recurrence, query_heads, key_heads, value_heads, decay_heads)
    d_query_heads, d_key_heads, d_value_heads, d_decay_heads = pullback((d_mixed, suffix[1]))
    d_raw = d_decay_heads.reshape(rows, heads * DK) / 16.0 * jax.nn.sigmoid(-raw)
    grad_up = jnp.dot(lowrank.T, d_raw, precision=HIGH)
    grad_bias = jnp.sum(d_raw, axis=0)
    d_lowrank = jnp.dot(d_raw, up_all.astype(jnp.float32).T, precision=HIGH).astype(jnp.bfloat16)
    d_queries = d_query_heads.reshape(rows, heads * DK).astype(jnp.bfloat16)
    d_keys = d_key_heads.reshape(rows, heads * DK).astype(jnp.bfloat16)
    d_values = d_value_heads.reshape(rows, heads * DV).astype(jnp.bfloat16)
    d_first = jnp.concatenate([d_keys, d_values, d_lowrank], axis=1)
    d_second = jnp.concatenate([d_queries, d_gates], axis=1)
    grad_first = matmul_tn(normed, d_first).astype(jnp.bfloat16)
    grad_second = matmul_tn(normed, d_second).astype(jnp.bfloat16)
    d_normed_part = matmul_nt(d_first, first) + matmul_nt(d_second, second)
    d_normed = lax.psum(d_normed_part.astype(jnp.bfloat16), "head").astype(jnp.float32)
    grad_gain_one = jnp.sum(d_normed * unit_one, axis=0)
    input_grad = (d_resid + norm_back(d_normed * gain_one, unit_one, scale_one)).astype(
        jnp.bfloat16
    )
    input_grad = ring.home(input_grad, 1).reshape(batch, block, width)
    grad_fdown = ring.scatter(grad_fdown_t).T
    grad_fgate = ring.scatter(grad_fgate)
    grad_fup = ring.scatter(grad_fup)
    grad_out = ring.scatter(grad_out_t).T
    grad_second = ring.scatter(grad_second)
    grad_first = ring.scatter(grad_first)
    share = lax.axis_index("seq")
    heads_sum = lax.psum((grad_first[:, key_cols + value_cols :], grad_head_part), "head")
    sums = (
        ring.home(grad_gain_one, 0),
        ring.home(grad_gain_two, 0),
        heads_sum[1],
        grad_bias,
        jnp.moveaxis(grad_up.reshape(rank, ring.count, -1), 1, 0).reshape(-1),
    )
    sizes = [part.size for part in sums]
    sums = lax.psum(jnp.concatenate(sums), "seq")
    ends = [sum(sizes[: i + 1]) for i in range(5)]
    mine = [
        lax.dynamic_slice_in_dim(
            sums[end - size : end], share * (size // ring.count), size // ring.count
        )
        for end, size in zip(ends, sizes)
    ]
    return (
        layer_out,
        input_grad,
        mine[0],
        grad_second[:, :key_cols],
        grad_first[:, :key_cols],
        grad_first[:, key_cols : key_cols + value_cols],
        grad_second[:, key_cols:],
        heads_sum[0],
        mine[4].reshape(rank, -1),
        mine[3],
        mine[2],
        grad_out,
        mine[1],
        grad_fgate,
        grad_fup,
        grad_fdown,
    )


def solution(mesh):
    return jax.shard_map(
        shards,
        mesh=mesh,
        in_specs=(
            P(None, "seq", None),
            P(None, "seq"),
            P("seq"),
            P("seq", "head"),
            P("seq", "head"),
            P("seq", "head"),
            P("seq", "head"),
            P("seq", None),
            P(None, ("head", "seq")),
            P(("head", "seq")),
            P("seq"),
            P("head", "seq"),
            P("seq"),
            P("seq", "head"),
            P("seq", "head"),
            P("head", "seq"),
            P(None, "seq", None),
        ),
        out_specs=(
            P(None, "seq", None),
            P(None, "seq", None),
            P("seq"),
            P("seq", "head"),
            P("seq", "head"),
            P("seq", "head"),
            P("seq", "head"),
            P("seq", None),
            P(None, ("head", "seq")),
            P(("head", "seq")),
            P("seq"),
            P("head", "seq"),
            P("seq"),
            P("seq", "head"),
            P("seq", "head"),
            P("head", "seq"),
        ),
        check_vma=False,
    )
```

```python
import functools

import jax
import jax.numpy as jnp
from jax import lax
from jax.experimental import pallas as pl
from jax.experimental.pallas import tpu as pltpu
from jax.sharding import PartitionSpec as P

DK = 256
DV = 512
CHUNK = 128
EPS = 1e-06
HIGH = lax.Precision.HIGHEST
NN = (((1,), (0,)), ((), ()))
NT = (((1,), (1,)), ((), ()))
TN = (((0,), (0,)), ((), ()))
VMEM_BYTES = 48 * 1024 * 1024


def product(left, right, dims, precision=None):
    return lax.dot_general(
        left, right, dims, precision=precision, preferred_element_type=jnp.float32
    )


def narrow(field):
    return field.astype(jnp.bfloat16)


def wide(field):
    return field.astype(jnp.float32)


def root_scale(field):
    return lax.rsqrt(jnp.mean(field * field, axis=-1, keepdims=True) + EPS)


def norm_back(upstream, unit, scale):
    return scale * (upstream - unit * jnp.mean(upstream * unit, axis=-1, keepdims=True))


def triangle(lower):
    rows = lax.broadcasted_iota(jnp.int32, (CHUNK, CHUNK), 0)
    columns = lax.broadcasted_iota(jnp.int32, (CHUNK, CHUNK), 1)
    return (rows >= columns if lower else rows <= columns).astype(jnp.float32)


def permitted(mark_column, mark_row):
    rows = lax.broadcasted_iota(jnp.int32, (CHUNK, CHUNK), 0)
    columns = lax.broadcasted_iota(jnp.int32, (CHUNK, CHUNK), 1)
    return (rows >= columns) & (mark_column == mark_row)


def state_kernel(
    value_ref, key_ref, low_ref, up_ref, bias_ref, mark_ref,
    run_ref, slope_ref, state_ref, total_ref, state, total,
):
    step = pl.program_id(0)

    @pl.when(step == 0)
    def _():
        state[...] = jnp.zeros_like(state)
        total[...] = jnp.ones_like(total)

    lower = triangle(True)
    for b in range(value_ref.shape[0]):
        raw = product(low_ref[b], up_ref[...], NN, HIGH) + bias_ref[...]
        soft = jnp.log1p(jnp.exp(-jnp.abs(raw)))
        decay = (jnp.minimum(raw, 0.0) - soft) / 16.0
        slope_ref[b] = jnp.exp(jnp.minimum(-raw, 0.0) - soft) / 16.0
        run = product(lower, decay, NN, HIGH)
        run_ref[b] = run
        mark = mark_ref[b]
        last = run[CHUNK - 1 :]
        trailing = mark == mark[CHUNK - 1 :]
        kept = jnp.where(trailing, jnp.exp(last - run), 0.0)
        keep = jnp.where(mark[CHUNK - 1 :] == 0.0, jnp.exp(last), 0.0)
        tail = narrow(wide(key_ref[b]) * kept)
        state[b] = state[b] * keep + product(value_ref[b], tail, TN)
        total[b] = total[b] * keep

    @pl.when(step == pl.num_programs(0) - 1)
    def _():
        state_ref[...] = narrow(state[...])
        total_ref[...] = total[...]


def mixer_kernel(
    query_ref, value_ref, key_ref, run_ref, mark_ref, row_ref, first_ref, gate_ref, gain_ref,
    heads_ref, mixed_ref, states_ref, state,
):
    step = pl.program_id(0)

    @pl.when(step == 0)
    def _():
        state[...] = wide(first_ref[...])

    for b in range(value_ref.shape[0]):
        run, mark = run_ref[b], mark_ref[b]
        middle, last = run[CHUNK // 2 - 1 : CHUNK // 2], run[CHUNK - 1 :]
        query = wide(query_ref[b]) * DK ** (-0.5)
        key = wide(key_ref[b])
        start = narrow(state[b])
        states_ref[0, b] = start
        scores = product(
            narrow(query * jnp.exp(run - middle)), narrow(key * jnp.exp(middle - run)), NT
        )
        scores = jnp.where(permitted(mark, row_ref[0, b]), scores, 0.0)
        opened = narrow(query * jnp.where(mark == 0.0, jnp.exp(run), 0.0))
        mixed = product(narrow(scores), value_ref[b], NN) + product(opened, start, NT)
        kept = jnp.where(mark == mark[CHUNK - 1 :], jnp.exp(last - run), 0.0)
        keep = jnp.where(mark[CHUNK - 1 :] == 0.0, jnp.exp(last), 0.0)
        state[b] = state[b] * keep + product(value_ref[b], narrow(key * kept), TN)
        states_ref[1, b] = narrow(state[b])
        mixed_ref[b] = mixed
        gate = gate_ref[b]
        active = gate * jax.nn.sigmoid(gate)
        heads_ref[b] = narrow(mixed * root_scale(mixed) * gain_ref[...] * active)


def head_back_kernel(
    grad_ref, gate_ref, mixed_ref, gain_ref, query_ref, run_ref, mark_ref,
    gate_grad_ref, mixed_grad_ref, gain_grad_ref, state_ref, state,
):
    step = pl.program_id(0)

    @pl.when(step == 0)
    def _():
        state[...] = jnp.zeros_like(state)
        gain_grad_ref[...] = jnp.zeros_like(gain_grad_ref)

    gain = gain_ref[...]
    for b in range(grad_ref.shape[0]):
        mixed, gate, grad = mixed_ref[b], gate_ref[b], wide(grad_ref[b])
        scale = root_scale(mixed)
        unit = mixed * scale
        sigma = jax.nn.sigmoid(gate)
        active = gate * sigma
        gate_grad_ref[b] = narrow(grad * unit * gain * sigma * (1.0 + gate * (1.0 - sigma)))
        weighted = grad * active
        gain_grad_ref[...] += jnp.sum(weighted * unit, axis=0, keepdims=True)
        mixed_grad = narrow(norm_back(weighted * gain, unit, scale))
        mixed_grad_ref[b] = mixed_grad
        run, mark = run_ref[b], mark_ref[b]
        last = run[CHUNK - 1 :]
        query = wide(query_ref[b]) * DK ** (-0.5)
        opened = narrow(query * jnp.where(mark == 0.0, jnp.exp(run), 0.0))
        keep = jnp.where(mark[CHUNK - 1 :] == 0.0, jnp.exp(last), 0.0)
        state[b] = state[b] * keep + product(mixed_grad, opened, TN)

    @pl.when(step == pl.num_programs(0) - 1)
    def _():
        state_ref[...] = narrow(state[...])


def mixer_back_kernel(
    query_ref, value_ref, key_ref, run_ref, slope_ref, mark_ref, row_ref, grad_ref,
    start_ref, end_ref, last_ref, low_ref, up_ref,
    query_grad_ref, value_grad_ref, key_grad_ref, low_grad_ref, up_grad_ref, bias_grad_ref, state,
):
    step = pl.program_id(0)

    @pl.when(step == 0)
    def _():
        state[...] = wide(last_ref[...])
        up_grad_ref[...] = jnp.zeros_like(up_grad_ref)
        bias_grad_ref[...] = jnp.zeros_like(bias_grad_ref)

    upper = triangle(False)
    for b in range(value_ref.shape[0]):
        run, mark = run_ref[b], mark_ref[b]
        middle, last = run[CHUNK // 2 - 1 : CHUNK // 2], run[CHUNK - 1 :]
        query = wide(query_ref[b]) * DK ** (-0.5)
        key, value, grad = wide(key_ref[b]), value_ref[b], grad_ref[b]
        start, later = start_ref[0, b], narrow(state[b])
        rise, fall = jnp.exp(run - middle), jnp.exp(middle - run)
        opens = jnp.where(mark == 0.0, jnp.exp(run), 0.0)
        kept = jnp.where(mark == mark[CHUNK - 1 :], jnp.exp(last - run), 0.0)
        keep = jnp.where(mark[CHUNK - 1 :] == 0.0, jnp.exp(last), 0.0)
        allowed = permitted(mark, row_ref[0, b])
        risen, fallen = narrow(query * rise), narrow(key * fall)
        scores = narrow(jnp.where(allowed, product(risen, fallen, NT), 0.0))
        scores_grad = narrow(jnp.where(allowed, product(grad, value, NT), 0.0))
        query_grad = rise * product(scores_grad, fallen, NN) + opens * product(grad, start, NN)
        key_grad = fall * product(scores_grad, risen, TN) + kept * product(value, later, NN)
        value_grad = product(scores, grad, TN) + product(narrow(key * kept), later, NT)
        ends = jnp.sum(state[b] * wide(end_ref[0, b]), axis=0, keepdims=True)
        state[b] = state[b] * keep + product(grad, narrow(query * opens), TN)
        turn = query * query_grad - key * key_grad
        raw_grad = (product(upper, turn, NN, HIGH) + ends) * slope_ref[b]
        query_grad_ref[b] = narrow(query_grad * DK ** (-0.5))
        key_grad_ref[b] = narrow(key_grad)
        value_grad_ref[b] = narrow(value_grad)
        low_grad_ref[b] = product(raw_grad, up_ref[...], NT, HIGH)
        up_grad_ref[...] += product(low_ref[b], raw_grad, TN, HIGH)
        bias_grad_ref[...] += jnp.sum(raw_grad, axis=0, keepdims=True)


def along(batch, width, last=0, reverse=0):
    if reverse:
        return pl.BlockSpec((batch, CHUNK, width), lambda i: (0, reverse - 1 - i, last))
    return pl.BlockSpec((batch, CHUNK, width), lambda i: (0, i, last))


def still(*shape):
    return pl.BlockSpec(shape, lambda i: (0,) * len(shape))


def shape_of(dtype, *shape):
    return jax.ShapeDtypeStruct(shape, dtype)


def call(kernel, steps, in_specs, out_specs, out_shape, scratch, operands, flops):
    moved = sum(a.size * a.dtype.itemsize for a in operands)
    moved += sum(s.size * s.dtype.itemsize for s in out_shape)
    return pl.pallas_call(
        kernel,
        grid=(steps,),
        in_specs=in_specs,
        out_specs=out_specs,
        out_shape=out_shape,
        scratch_shapes=scratch,
        cost_estimate=pl.CostEstimate(flops=flops, bytes_accessed=moved, transcendentals=0),
        compiler_params=pltpu.CompilerParams(
            dimension_semantics=("arbitrary",), vmem_limit_bytes=VMEM_BYTES
        ),
    )(*operands)


F32, BF16 = jnp.float32, jnp.bfloat16


def local_states(value_key, low, up, bias, mark):
    batch, block, rank = low.shape
    steps = block // CHUNK
    return call(
        state_kernel,
        steps,
        [along(batch, DV), along(batch, DK, DV // DK), along(batch, rank), still(rank, DK),
         still(1, DK), along(batch, 1)],
        [along(batch, DK), along(batch, DK), still(batch, DV, DK), still(batch, 1, DK)],
        [shape_of(F32, batch, block, DK), shape_of(F32, batch, block, DK),
         shape_of(BF16, batch, DV, DK), shape_of(F32, batch, 1, DK)],
        [pltpu.VMEM((batch, DV, DK), F32), pltpu.VMEM((batch, 1, DK), F32)],
        (value_key, value_key, low, up, bias, mark),
        2 * batch * block * DK * (DV + 6 * CHUNK),
    )


def mix(query, value_key, run, mark, row, first, gates, gain):
    batch, block, _ = run.shape
    steps = block // CHUNK
    heads, mixed, states = call(
        mixer_kernel,
        steps,
        [along(batch, DK), along(batch, DV), along(batch, DK, DV // DK), along(batch, DK),
         along(batch, 1), pl.BlockSpec((1, batch, 1, CHUNK), lambda i: (i, 0, 0, 0)),
         still(batch, DV, DK), along(batch, DV), still(1, DV)],
        [along(batch, DV), along(batch, DV),
         pl.BlockSpec((2, batch, DV, DK), lambda i: (i, 0, 0, 0))],
        [shape_of(BF16, batch, block, DV), shape_of(F32, batch, block, DV),
         shape_of(BF16, 2 * steps, batch, DV, DK)],
        [pltpu.VMEM((batch, DV, DK), F32)],
        (query, value_key, value_key, run, mark, row, first, gates, gain),
        2 * batch * block * DK * (2 * DV + 3 * CHUNK),
    )
    return heads, mixed, states


def head_back(grad, gates, mixed, gain, query, run, mark):
    batch, block, _ = run.shape
    steps = block // CHUNK
    return call(
        head_back_kernel,
        steps,
        [along(batch, DV, 0, steps), along(batch, DV, 0, steps), along(batch, DV, 0, steps),
         still(1, DV), along(batch, DK, 0, steps), along(batch, DK, 0, steps),
         along(batch, 1, 0, steps)],
        [along(batch, DV, 0, steps), along(batch, DV, 0, steps), still(1, DV),
         still(batch, DV, DK)],
        [shape_of(BF16, batch, block, DV), shape_of(BF16, batch, block, DV),
         shape_of(F32, 1, DV), shape_of(BF16, batch, DV, DK)],
        [pltpu.VMEM((batch, DV, DK), F32)],
        (grad, gates, mixed, gain, query, run, mark),
        2 * batch * block * DK * DV,
    )


def mix_back(query, value_key, run, slope, mark, row, grad, states, later, low, up):
    batch, block, rank = low.shape
    steps = block // CHUNK
    return call(
        mixer_back_kernel,
        steps,
        [along(batch, DK, 0, steps), along(batch, DV, 0, steps),
         along(batch, DK, DV // DK, steps), along(batch, DK, 0, steps),
         along(batch, DK, 0, steps), along(batch, 1, 0, steps),
         pl.BlockSpec((1, batch, 1, CHUNK), lambda i: (steps - 1 - i, 0, 0, 0)),
         along(batch, DV, 0, steps),
         pl.BlockSpec((1, batch, DV, DK), lambda i: (2 * (steps - 1 - i), 0, 0, 0)),
         pl.BlockSpec((1, batch, DV, DK), lambda i: (2 * (steps - 1 - i) + 1, 0, 0, 0)),
         still(batch, DV, DK), along(batch, rank, 0, steps), still(rank, DK)],
        [along(batch, DK, 0, steps), along(batch, DV, 0, steps), along(batch, DK, 0, steps),
         along(batch, rank, 0, steps), still(rank, DK), still(1, DK)],
        [shape_of(BF16, batch, block, DK), shape_of(BF16, batch, block, DV),
         shape_of(BF16, batch, block, DK), shape_of(F32, batch, block, rank),
         shape_of(F32, rank, DK), shape_of(F32, 1, DK)],
        [pltpu.VMEM((batch, DV, DK), F32)],
        (query, value_key, value_key, run, slope, mark, row, grad, states, states, later, low, up),
        2 * batch * block * DK * (5 * DV + 6 * CHUNK),
    )


def matmul(left, right):
    return product(left, right, NN)


def matmul_nt(left, right):
    return product(left, right, NT)


def matmul_tn(left, right):
    return product(left, right, TN)


def ring_order(count):
    return list(range(0, count, 2)) + list(range(count - 1 - count % 2, 0, -2))


class Ring:
    def __init__(self, axis):
        self.axis = axis
        self.count = count = lax.axis_size(axis)
        order = ring_order(count)
        place = [order.index(i) for i in range(count)]
        self.right = [(order[i], order[(i + 1) % count]) for i in range(count)]
        self.left = [(order[i], order[(i - 1) % count]) for i in range(count)]
        owners = [[order[(place[i] + r) % count] for r in range(count)] for i in range(count)]
        slots = [[(place[i] - place[me]) % count for i in range(count)] for me in range(count)]
        mine = lax.axis_index(axis)
        self.owners = jnp.asarray(owners, jnp.int32)[mine]
        self.slots = jnp.asarray(slots, jnp.int32)[mine]

    def arrange(self, field, dim, table):
        width = field.shape[dim] // self.count
        return jnp.concatenate(
            [
                lax.dynamic_slice_in_dim(field, table[r] * width, width, dim)
                for r in range(self.count)
            ],
            axis=dim,
        )

    def near(self, field, dim):
        return self.arrange(field, dim, self.owners)

    def home(self, field, dim):
        return self.arrange(field, dim, self.slots)

    def gather(self, block, after=None):
        count, half = self.count, block.shape[0] // 2
        up, down = block[:half], block[half:]
        if after is not None:
            up, down, _ = lax.optimization_barrier((up, down, after))
        pieces = [None] * (2 * count)
        pieces[0], pieces[1] = up, down
        for step in range(1, count):
            up = lax.ppermute(up, self.axis, self.right)
            down = lax.ppermute(down, self.axis, self.left)
            pieces[2 * (count - step)] = up
            pieces[2 * step + 1] = down
            if step == count - 2:
                late = up[:8, :128]
        return jnp.concatenate(pieces, axis=0), late

    def scatter(self, total):
        count = self.count
        rows = total.shape[0] // count
        half = rows // 2

        def piece(slot, part):
            start = slot * rows + part * half
            return total[start : start + half]

        up, down = piece(count - 1, 0), piece(1, 1)
        for step in range(count - 1):
            up = lax.ppermute(up, self.axis, self.right)
            down = lax.ppermute(down, self.axis, self.left)
            up = wide(up) + wide(piece(count - 2 - step, 0))
            down = wide(down) + wide(piece((step + 2) % count, 1))
            if step < count - 2:
                up, down = narrow(up), narrow(down)
        return jnp.concatenate([up, down], axis=0)


def swap(axis, distance):
    return [(i, i ^ distance) for i in range(lax.axis_size(axis))]


def head_scatter(part):
    count, mine = lax.axis_size("head"), lax.axis_index("head")
    rows = part.shape[0] // count
    held = part.reshape((count, rows) + part.shape[1:])
    distance = 1
    while distance < count:
        bit = (mine // distance) % 2
        split = held.reshape((held.shape[0] // 2, 2) + held.shape[1:])
        sent = lax.dynamic_index_in_dim(split, 1 - bit, 1, False)
        kept = lax.dynamic_index_in_dim(split, bit, 1, False)
        got = lax.ppermute(narrow(sent), "head", swap("head", distance))
        held = wide(kept) + wide(got)
        distance *= 2
    return held[0]


def head_gather(share):
    count, mine = lax.axis_size("head"), lax.axis_index("head")
    held = share[None]
    distance = count // 2
    while distance:
        bit = (mine // distance) % 2
        got = lax.ppermute(held, "head", swap("head", distance))
        lower = jnp.where(bit == 0, held, got)
        upper = jnp.where(bit == 0, got, held)
        held = jnp.stack([lower, upper], axis=1).reshape((-1,) + share.shape)
        distance //= 2
    return held.reshape((-1,) + share.shape[1:])


def with_decay(state, decay):
    high = narrow(decay)
    low = narrow(decay - wide(high))
    return jnp.concatenate([narrow(state), high, low], axis=1)


def split_decay(message):
    rows = message.shape[1] - 2
    decay = wide(message[:, rows : rows + 1]) + wide(message[:, rows + 1 :])
    return wide(message[:, :rows]), decay


def entering(state, decay, later):
    count, mine = lax.axis_size("seq"), lax.axis_index("seq")
    inner = mine % 2
    ahead = (inner == 0) != later
    half = state.shape[1] // 2
    kept = wide(lax.dynamic_slice_in_dim(state, inner * half, half, 1))
    sent = lax.dynamic_slice_in_dim(state, (1 - inner) * half, half, 1)
    pair = swap("seq", 1)
    other, other_decay = split_decay(lax.ppermute(with_decay(sent, decay), "seq", pair))
    earliest = jnp.where(ahead, kept, other)
    joined = jnp.where(ahead, other_decay, decay) * earliest + jnp.where(ahead, other, kept)
    message = with_decay(joined, decay * other_decay)
    if later:
        chain = [(i, i - 2) for i in range(2, count)]
    else:
        chain = [(i, i + 2) for i in range(count - 2)]
    before, reach = jnp.zeros_like(kept), jnp.ones_like(decay)
    for _ in range(count // 2 - 1):
        message = lax.ppermute(message, "seq", chain)
        far, far_decay = split_decay(message)
        before = before + reach * far
        reach = reach * far_decay
    second = jnp.where(ahead, decay, other_decay) * before + earliest
    got = lax.ppermute(narrow(jnp.where(ahead, second, before)), "seq", pair)
    own = narrow(jnp.where(ahead, before, second))
    return jnp.concatenate(
        [jnp.where(inner == 0, own, got), jnp.where(inner == 0, got, own)], axis=1
    )


def columns_of(vector, rows):
    width = -(-vector.shape[-1] // rows)
    pad = [(0, 0)] * (vector.ndim - 1) + [(0, width * rows - vector.shape[-1])]
    shaped = jnp.pad(vector, pad).reshape(vector.shape[:-1] + (width, rows))
    return jnp.swapaxes(shaped, -1, -2)


def shards(
    layer_in,
    seg_starts,
    attn_gain,
    query_weight,
    key_weight,
    value_weight,
    gate_weight,
    decay_down,
    decay_up,
    decay_bias,
    head_gain,
    out_weight,
    ffn_gain,
    ffn_gate,
    ffn_up,
    ffn_down,
    out_grad,
):
    ring = Ring("seq")
    count = ring.count
    batch, block, width = layer_in.shape
    rows = batch * block
    chunks = block // CHUNK
    rank, share = decay_down.shape[1], attn_gain.shape[0]
    hidden = ffn_gate.shape[1]
    mixed_cols, rank_end = DV + DK, DV + DK + rank

    sizes = [head_gain.size, decay_bias.size, decay_up.size]
    small = jnp.concatenate([head_gain, decay_bias, decay_up.reshape(-1)])
    extra = columns_of(small, share)
    block_one = jnp.concatenate(
        [value_weight, key_weight, decay_down, attn_gain[:, None], ffn_gain[:, None], extra], axis=1
    )
    block_two = jnp.concatenate([query_weight, gate_weight, out_weight.T], axis=1)
    first, mark = ring.gather(block_one)
    second, mark = ring.gather(block_two, mark)
    third, mark = ring.gather(jnp.concatenate([ffn_gate, ffn_up], axis=1), mark)
    fdown_t, mark = ring.gather(ffn_down.T, mark)
    vk_all, down_all = first[:, :mixed_cols], first[:, mixed_cols:rank_end]
    gain_one, gain_two = wide(first[:, rank_end]), wide(first[:, rank_end + 1])
    small = first[:, rank_end + 2 :].reshape(count, share, -1)
    small = ring.home(jnp.swapaxes(small, 1, 2).reshape(count, -1), 0)
    gain_head = wide(small[:, : sizes[0]]).reshape(1, DV)
    bias_all = wide(small[:, sizes[0] : sizes[0] + sizes[1]]).reshape(1, DK)
    up_all = small[:, sizes[0] + sizes[1] : sum(sizes)].reshape(count, rank, -1)
    up_all = wide(jnp.swapaxes(up_all, 0, 1).reshape(rank, DK))
    query_all, gate_all, out_t = second[:, :DK], second[:, DK:mixed_cols], second[:, mixed_cols:]

    starts = seg_starts.reshape(batch, chunks, CHUNK).astype(jnp.float32)
    places = jnp.arange(CHUNK)
    lower = (places[:, None] >= places[None, :]).astype(jnp.float32)
    marks = jnp.einsum("bcs,ts->bct", starts, lower, precision=HIGH)
    column, row = marks.reshape(batch, block, 1), jnp.swapaxes(marks, 0, 1)[:, :, None, :]

    inputs = ring.near(layer_in.reshape(rows, width), 1)
    grad_rows = ring.near(out_grad.reshape(rows, width), 1)
    head = lax.axis_index("head")
    quarter = rows // lax.axis_size("head")
    inputs_own = wide(lax.dynamic_slice_in_dim(inputs, head * quarter, quarter, 0))
    grad_own = wide(lax.dynamic_slice_in_dim(grad_rows, head * quarter, quarter, 0))
    scale_one = root_scale(wide(inputs))
    normed = narrow(wide(inputs) * scale_one * gain_one)

    def tokens(field):
        return field.reshape(batch, block, field.shape[-1])

    value_key = tokens(narrow(matmul(normed, vk_all)))
    low = tokens(matmul(normed, down_all))
    run, slope, state, total = local_states(value_key, low, up_all, bias_all, column)
    query = tokens(narrow(matmul(normed, query_all)))
    gates = tokens(matmul(normed, gate_all))
    state_in = entering(state, total, False)
    heads, mixed, states = mix(query, value_key, run, column, row, state_in, gates, gain_head)
    heads = heads.reshape(rows, DV)
    resid = inputs_own + head_scatter(narrow(matmul_nt(heads, out_t)))
    scale_two = root_scale(resid)
    unit_two = resid * scale_two
    normed_two = head_gather(narrow(unit_two * gain_two))
    pre_gate = matmul(normed_two, third[:, :hidden])
    pre_up = matmul(normed_two, third[:, hidden:])
    sigma = jax.nn.sigmoid(pre_gate)
    act = narrow(pre_gate * sigma * pre_up)
    layer_out = narrow(resid + head_scatter(narrow(matmul_nt(act, fdown_t))))
    layer_out = ring.home(head_gather(layer_out), 1)

    d_act = matmul(grad_rows, fdown_t)
    grad_fdown = ring.scatter(narrow(matmul_tn(grad_rows, act)))
    d_gate = narrow(d_act * pre_up * sigma * (1.0 + pre_gate * (1.0 - sigma)))
    d_up = narrow(d_act * pre_gate * sigma)
    d_third = jnp.concatenate([d_gate, d_up], axis=1)
    grad_third = ring.scatter(narrow(matmul_tn(normed_two, d_third)))
    d_normed_two = head_scatter(narrow(matmul_nt(d_third, third)))
    grad_gain_two = jnp.sum(d_normed_two * unit_two, axis=0)
    d_resid = grad_own + norm_back(d_normed_two * gain_two, unit_two, scale_two)
    d_attn = head_gather(narrow(d_resid))
    d_heads = tokens(matmul(d_attn, out_t))
    d_gates, d_mixed, grad_gain_head, state_grad = head_back(
        d_heads, gates, mixed, gain_head, query, run, column
    )
    state_back = entering(state_grad, total, True)
    d_query, d_value, d_key, d_low, grad_up, grad_bias = mix_back(
        query, value_key, run, slope, column, row, d_mixed, states, state_back, low, up_all
    )
    d_gates = d_gates.reshape(rows, DV)
    grad_out = matmul_tn(d_attn, heads)
    grad_gate = matmul_tn(normed, d_gates)
    grad_fourth = ring.scatter(narrow(jnp.concatenate([grad_gate, grad_out], axis=1)))
    d_first = jnp.concatenate(
        [d_value.reshape(rows, DV), d_key.reshape(rows, DK), narrow(d_low.reshape(rows, rank))],
        axis=1,
    )
    d_query = d_query.reshape(rows, DK)
    d_normed_part = (
        matmul_nt(d_first, first[:, :rank_end])
        + matmul_nt(d_query, query_all)
        + matmul_nt(d_gates, gate_all)
    )
    d_normed = head_scatter(narrow(d_normed_part))
    unit_own = inputs_own * root_scale(inputs_own)
    grad_gain_one = jnp.sum(d_normed * unit_own, axis=0)
    d_unit = norm_back(d_normed * gain_one, unit_own, root_scale(inputs_own))
    input_grad = ring.home(head_gather(narrow(d_resid + d_unit)), 1)

    small = jnp.concatenate(
        [
            grad_gain_head.reshape(count, -1),
            grad_bias.reshape(count, -1),
            jnp.swapaxes(grad_up.reshape(rank, count, -1), 0, 1).reshape(count, -1),
        ],
        axis=1,
    )
    small = columns_of(ring.near(small, 0), share).reshape(width, -1)
    grad_last = jnp.concatenate(
        [
            matmul_tn(normed, d_first),
            matmul_tn(normed, d_query),
            small,
            grad_gain_two[:, None],
        ],
        axis=1,
    )
    grad_last = ring.scatter(narrow(grad_last))
    gain_one_sum = lax.psum(ring.home(grad_gain_one, 0), ("seq", "head"))
    gain_one_sum = lax.dynamic_slice_in_dim(gain_one_sum, lax.axis_index("seq") * share, share)
    small = jnp.swapaxes(grad_last[:, rank_end + DK : -1], 0, 1).reshape(-1)
    shared = lax.psum(
        (
            grad_last[:, mixed_cols:rank_end],
            grad_last[:, -1],
            small[: sizes[0]],
        ),
        "head",
    )
    return (
        layer_out.reshape(batch, block, width),
        input_grad.reshape(batch, block, width),
        gain_one_sum,
        grad_last[:, rank_end : rank_end + DK],
        grad_last[:, DV:mixed_cols],
        grad_last[:, :DV],
        grad_fourth[:, :DV],
        shared[0],
        small[sizes[0] + sizes[1] : sum(sizes)].reshape(rank, -1),
        small[sizes[0] : sizes[0] + sizes[1]],
        shared[2],
        grad_fourth[:, DV:].T,
        shared[1],
        grad_third[:, :hidden],
        grad_third[:, hidden:],
        grad_fdown.T,
    )


def solution(mesh):
    return jax.shard_map(
        shards,
        mesh=mesh,
        in_specs=(
            P(None, "seq", None),
            P(None, "seq"),
            P("seq"),
            P("seq", "head"),
            P("seq", "head"),
            P("seq", "head"),
            P("seq", "head"),
            P("seq", None),
            P(None, ("head", "seq")),
            P(("head", "seq")),
            P("seq"),
            P("head", "seq"),
            P("seq"),
            P("seq", "head"),
            P("seq", "head"),
            P("head", "seq"),
            P(None, "seq", None),
        ),
        out_specs=(
            P(None, "seq", None),
            P(None, "seq", None),
            P("seq"),
            P("seq", "head"),
            P("seq", "head"),
            P("seq", "head"),
            P("seq", "head"),
            P("seq", None),
            P(None, ("head", "seq")),
            P(("head", "seq")),
            P("seq"),
            P("head", "seq"),
            P("seq"),
            P("seq", "head"),
            P("seq", "head"),
            P("head", "seq"),
        ),
        check_vma=False,
    )
```

```python
import functools

import jax
import jax.numpy as jnp
from jax import lax
from jax.experimental import pallas as pl
from jax.experimental.pallas import tpu as pltpu
from jax.sharding import PartitionSpec as P

DK = 256
DV = 512
CHUNK = 128
EPS = 1e-06
HIGH = lax.Precision.HIGHEST
NN = (((1,), (0,)), ((), ()))
NT = (((1,), (1,)), ((), ()))
TN = (((0,), (0,)), ((), ()))
VMEM_BYTES = 48 * 1024 * 1024
MESH = pl.DeviceIdType.MESH


def product(left, right, dims, precision=None):
    return lax.dot_general(
        left, right, dims, precision=precision, preferred_element_type=jnp.float32
    )


def narrow(field):
    return field.astype(jnp.bfloat16)


def wide(field):
    return field.astype(jnp.float32)


def root_scale(field):
    return lax.rsqrt(jnp.mean(field * field, axis=-1, keepdims=True) + EPS)


def norm_back(upstream, unit, scale):
    return scale * (upstream - unit * jnp.mean(upstream * unit, axis=-1, keepdims=True))


def triangle(lower):
    rows = lax.broadcasted_iota(jnp.int32, (CHUNK, CHUNK), 0)
    columns = lax.broadcasted_iota(jnp.int32, (CHUNK, CHUNK), 1)
    return (rows >= columns if lower else rows <= columns).astype(jnp.float32)


def permitted(mark_column, mark_row):
    rows = lax.broadcasted_iota(jnp.int32, (CHUNK, CHUNK), 0)
    columns = lax.broadcasted_iota(jnp.int32, (CHUNK, CHUNK), 1)
    return (rows >= columns) & (mark_column == mark_row)


def state_kernel(
    value_ref, key_ref, low_ref, up_ref, bias_ref, mark_ref,
    run_ref, slope_ref, state_ref, total_ref, state, total,
):
    step = pl.program_id(0)

    @pl.when(step == 0)
    def _():
        state[...] = jnp.zeros_like(state)
        total[...] = jnp.ones_like(total)

    lower = triangle(True)
    for b in range(value_ref.shape[0]):
        raw = product(low_ref[b], up_ref[...], NN, HIGH) + bias_ref[...]
        soft = jnp.log1p(jnp.exp(-jnp.abs(raw)))
        decay = (jnp.minimum(raw, 0.0) - soft) / 16.0
        slope_ref[b] = jnp.exp(jnp.minimum(-raw, 0.0) - soft) / 16.0
        run = product(lower, decay, NN, HIGH)
        run_ref[b] = run
        mark = mark_ref[b]
        last = run[CHUNK - 1 :]
        trailing = mark == mark[CHUNK - 1 :]
        kept = jnp.where(trailing, jnp.exp(last - run), 0.0)
        keep = jnp.where(mark[CHUNK - 1 :] == 0.0, jnp.exp(last), 0.0)
        tail = narrow(wide(key_ref[b]) * kept)
        state[b] = state[b] * keep + product(value_ref[b], tail, TN)
        total[b] = total[b] * keep

    @pl.when(step == pl.num_programs(0) - 1)
    def _():
        state_ref[...] = narrow(state[...])
        total_ref[...] = total[...]


def mixer_kernel(
    query_ref, value_ref, key_ref, run_ref, mark_ref, row_ref, first_ref, gate_ref, gain_ref,
    heads_ref, mixed_ref, states_ref, state,
):
    step = pl.program_id(0)

    @pl.when(step == 0)
    def _():
        state[...] = wide(first_ref[...])

    for b in range(value_ref.shape[0]):
        run, mark = run_ref[b], mark_ref[b]
        middle, last = run[CHUNK // 2 - 1 : CHUNK // 2], run[CHUNK - 1 :]
        query = wide(query_ref[b]) * DK ** (-0.5)
        key = wide(key_ref[b])
        start = narrow(state[b])
        states_ref[0, b] = start
        scores = product(
            narrow(query * jnp.exp(run - middle)), narrow(key * jnp.exp(middle - run)), NT
        )
        scores = jnp.where(permitted(mark, row_ref[0, b]), scores, 0.0)
        opened = narrow(query * jnp.where(mark == 0.0, jnp.exp(run), 0.0))
        mixed = product(narrow(scores), value_ref[b], NN) + product(opened, start, NT)
        kept = jnp.where(mark == mark[CHUNK - 1 :], jnp.exp(last - run), 0.0)
        keep = jnp.where(mark[CHUNK - 1 :] == 0.0, jnp.exp(last), 0.0)
        state[b] = state[b] * keep + product(value_ref[b], narrow(key * kept), TN)
        states_ref[1, b] = narrow(state[b])
        mixed_ref[b] = mixed
        gate = gate_ref[b]
        active = gate * jax.nn.sigmoid(gate)
        heads_ref[b] = narrow(mixed * root_scale(mixed) * gain_ref[...] * active)


def head_back_kernel(
    grad_ref, gate_ref, mixed_ref, gain_ref, query_ref, run_ref, mark_ref,
    gate_grad_ref, mixed_grad_ref, gain_grad_ref, state_ref, state,
):
    step = pl.program_id(0)

    @pl.when(step == 0)
    def _():
        state[...] = jnp.zeros_like(state)
        gain_grad_ref[...] = jnp.zeros_like(gain_grad_ref)

    gain = gain_ref[...]
    for b in range(grad_ref.shape[0]):
        mixed, gate, grad = mixed_ref[b], gate_ref[b], wide(grad_ref[b])
        scale = root_scale(mixed)
        unit = mixed * scale
        sigma = jax.nn.sigmoid(gate)
        active = gate * sigma
        gate_grad_ref[b] = narrow(grad * unit * gain * sigma * (1.0 + gate * (1.0 - sigma)))
        weighted = grad * active
        gain_grad_ref[...] += jnp.sum(weighted * unit, axis=0, keepdims=True)
        mixed_grad = narrow(norm_back(weighted * gain, unit, scale))
        mixed_grad_ref[b] = mixed_grad
        run, mark = run_ref[b], mark_ref[b]
        last = run[CHUNK - 1 :]
        query = wide(query_ref[b]) * DK ** (-0.5)
        opened = narrow(query * jnp.where(mark == 0.0, jnp.exp(run), 0.0))
        keep = jnp.where(mark[CHUNK - 1 :] == 0.0, jnp.exp(last), 0.0)
        state[b] = state[b] * keep + product(mixed_grad, opened, TN)

    @pl.when(step == pl.num_programs(0) - 1)
    def _():
        state_ref[...] = narrow(state[...])


def mixer_back_kernel(
    query_ref, value_ref, key_ref, run_ref, slope_ref, mark_ref, row_ref, grad_ref,
    start_ref, end_ref, last_ref, low_ref, up_ref,
    query_grad_ref, value_grad_ref, key_grad_ref, low_grad_ref, up_grad_ref, bias_grad_ref, state,
):
    step = pl.program_id(0)

    @pl.when(step == 0)
    def _():
        state[...] = wide(last_ref[...])
        up_grad_ref[...] = jnp.zeros_like(up_grad_ref)
        bias_grad_ref[...] = jnp.zeros_like(bias_grad_ref)

    upper = triangle(False)
    for b in range(value_ref.shape[0]):
        run, mark = run_ref[b], mark_ref[b]
        middle, last = run[CHUNK // 2 - 1 : CHUNK // 2], run[CHUNK - 1 :]
        query = wide(query_ref[b]) * DK ** (-0.5)
        key, value, grad = wide(key_ref[b]), value_ref[b], grad_ref[b]
        start, later = start_ref[0, b], narrow(state[b])
        rise, fall = jnp.exp(run - middle), jnp.exp(middle - run)
        opens = jnp.where(mark == 0.0, jnp.exp(run), 0.0)
        kept = jnp.where(mark == mark[CHUNK - 1 :], jnp.exp(last - run), 0.0)
        keep = jnp.where(mark[CHUNK - 1 :] == 0.0, jnp.exp(last), 0.0)
        allowed = permitted(mark, row_ref[0, b])
        risen, fallen = narrow(query * rise), narrow(key * fall)
        scores = narrow(jnp.where(allowed, product(risen, fallen, NT), 0.0))
        scores_grad = narrow(jnp.where(allowed, product(grad, value, NT), 0.0))
        query_grad = rise * product(scores_grad, fallen, NN) + opens * product(grad, start, NN)
        key_grad = fall * product(scores_grad, risen, TN) + kept * product(value, later, NN)
        value_grad = product(scores, grad, TN) + product(narrow(key * kept), later, NT)
        ends = jnp.sum(state[b] * wide(end_ref[0, b]), axis=0, keepdims=True)
        state[b] = state[b] * keep + product(grad, narrow(query * opens), TN)
        turn = query * query_grad - key * key_grad
        raw_grad = (product(upper, turn, NN, HIGH) + ends) * slope_ref[b]
        query_grad_ref[b] = narrow(query_grad * DK ** (-0.5))
        key_grad_ref[b] = narrow(key_grad)
        value_grad_ref[b] = narrow(value_grad)
        low_grad_ref[b] = product(raw_grad, up_ref[...], NT, HIGH)
        up_grad_ref[...] += product(low_ref[b], raw_grad, TN, HIGH)
        bias_grad_ref[...] += jnp.sum(raw_grad, axis=0, keepdims=True)


def along(batch, width, last=0, reverse=0):
    if reverse:
        return pl.BlockSpec((batch, CHUNK, width), lambda i: (0, reverse - 1 - i, last))
    return pl.BlockSpec((batch, CHUNK, width), lambda i: (0, i, last))


def still(*shape):
    return pl.BlockSpec(shape, lambda i: (0,) * len(shape))


def shape_of(dtype, *shape):
    return jax.ShapeDtypeStruct(shape, dtype)


def call(kernel, steps, in_specs, out_specs, out_shape, scratch, operands, flops):
    moved = sum(a.size * a.dtype.itemsize for a in operands)
    moved += sum(s.size * s.dtype.itemsize for s in out_shape)
    return pl.pallas_call(
        kernel,
        grid=(steps,),
        in_specs=in_specs,
        out_specs=out_specs,
        out_shape=out_shape,
        scratch_shapes=scratch,
        cost_estimate=pl.CostEstimate(flops=flops, bytes_accessed=moved, transcendentals=0),
        compiler_params=pltpu.CompilerParams(
            dimension_semantics=("arbitrary",), vmem_limit_bytes=VMEM_BYTES
        ),
    )(*operands)


F32, BF16 = jnp.float32, jnp.bfloat16


def local_states(value_key, low, up, bias, mark):
    batch, block, rank = low.shape
    steps = block // CHUNK
    return call(
        state_kernel,
        steps,
        [along(batch, DV), along(batch, DK, DV // DK), along(batch, rank), still(rank, DK),
         still(1, DK), along(batch, 1)],
        [along(batch, DK), along(batch, DK), still(batch, DV, DK), still(batch, 1, DK)],
        [shape_of(F32, batch, block, DK), shape_of(F32, batch, block, DK),
         shape_of(BF16, batch, DV, DK), shape_of(F32, batch, 1, DK)],
        [pltpu.VMEM((batch, DV, DK), F32), pltpu.VMEM((batch, 1, DK), F32)],
        (value_key, value_key, low, up, bias, mark),
        2 * batch * block * DK * (DV + 6 * CHUNK),
    )


def mix(query, value_key, run, mark, row, first, gates, gain):
    batch, block, _ = run.shape
    steps = block // CHUNK
    heads, mixed, states = call(
        mixer_kernel,
        steps,
        [along(batch, DK), along(batch, DV), along(batch, DK, DV // DK), along(batch, DK),
         along(batch, 1), pl.BlockSpec((1, batch, 1, CHUNK), lambda i: (i, 0, 0, 0)),
         still(batch, DV, DK), along(batch, DV), still(1, DV)],
        [along(batch, DV), along(batch, DV),
         pl.BlockSpec((2, batch, DV, DK), lambda i: (i, 0, 0, 0))],
        [shape_of(BF16, batch, block, DV), shape_of(F32, batch, block, DV),
         shape_of(BF16, 2 * steps, batch, DV, DK)],
        [pltpu.VMEM((batch, DV, DK), F32)],
        (query, value_key, value_key, run, mark, row, first, gates, gain),
        2 * batch * block * DK * (2 * DV + 3 * CHUNK),
    )
    return heads, mixed, states


def head_back(grad, gates, mixed, gain, query, run, mark):
    batch, block, _ = run.shape
    steps = block // CHUNK
    return call(
        head_back_kernel,
        steps,
        [along(batch, DV, 0, steps), along(batch, DV, 0, steps), along(batch, DV, 0, steps),
         still(1, DV), along(batch, DK, 0, steps), along(batch, DK, 0, steps),
         along(batch, 1, 0, steps)],
        [along(batch, DV, 0, steps), along(batch, DV, 0, steps), still(1, DV),
         still(batch, DV, DK)],
        [shape_of(BF16, batch, block, DV), shape_of(BF16, batch, block, DV),
         shape_of(F32, 1, DV), shape_of(BF16, batch, DV, DK)],
        [pltpu.VMEM((batch, DV, DK), F32)],
        (grad, gates, mixed, gain, query, run, mark),
        2 * batch * block * DK * DV,
    )


def mix_back(query, value_key, run, slope, mark, row, grad, states, later, low, up):
    batch, block, rank = low.shape
    steps = block // CHUNK
    return call(
        mixer_back_kernel,
        steps,
        [along(batch, DK, 0, steps), along(batch, DV, 0, steps),
         along(batch, DK, DV // DK, steps), along(batch, DK, 0, steps),
         along(batch, DK, 0, steps), along(batch, 1, 0, steps),
         pl.BlockSpec((1, batch, 1, CHUNK), lambda i: (steps - 1 - i, 0, 0, 0)),
         along(batch, DV, 0, steps),
         pl.BlockSpec((1, batch, DV, DK), lambda i: (2 * (steps - 1 - i), 0, 0, 0)),
         pl.BlockSpec((1, batch, DV, DK), lambda i: (2 * (steps - 1 - i) + 1, 0, 0, 0)),
         still(batch, DV, DK), along(batch, rank, 0, steps), still(rank, DK)],
        [along(batch, DK, 0, steps), along(batch, DV, 0, steps), along(batch, DK, 0, steps),
         along(batch, rank, 0, steps), still(rank, DK), still(1, DK)],
        [shape_of(BF16, batch, block, DK), shape_of(BF16, batch, block, DV),
         shape_of(BF16, batch, block, DK), shape_of(F32, batch, block, rank),
         shape_of(F32, rank, DK), shape_of(F32, 1, DK)],
        [pltpu.VMEM((batch, DV, DK), F32)],
        (query, value_key, value_key, run, slope, mark, row, grad, states, states, later, low, up),
        2 * batch * block * DK * (5 * DV + 6 * CHUNK),
    )


def place_of(table, index):
    found = jnp.int32(table[0])
    for i, entry in enumerate(table[1:], 1):
        found = jnp.where(index == i, jnp.int32(entry), found)
    return found


def block_at(order, distance):
    count = len(order)
    place = place_of([order.index(i) for i in range(count)], lax.axis_index("seq"))
    return place_of(order, lax.rem(place + distance + count, count))


def greet(axis, count):
    barrier, mine = pltpu.get_barrier_semaphore(), lax.axis_index(axis)
    for d in range(1, count):
        pl.semaphore_signal(
            barrier, inc=1, device_id={axis: lax.rem(mine + d, count)}, device_id_type=MESH
        )
    pl.semaphore_wait(barrier, count - 1)


def enter_kernel(
    order, input_ref, block_ref, small_ref,
    normed_ref, weight_ref, vk_ref, query_ref, gate_ref, low_ref, smalls_ref,
    total, low_total, send, receive, small_send, small_receive,
):
    count = len(order)
    share, half = block_ref.shape[0], block_ref.shape[0] // 2
    rows, tile = input_ref.shape[0], 256
    wide_cols = total.shape[1]
    low_start = block_ref.shape[1] - low_ref.shape[1]
    mine = lax.axis_index("seq")
    right, left = block_at(order, 1), block_at(order, -1)
    greet("seq", count)

    def hop(step, side):
        part = pl.ds(side * half, half)
        if step == 1:
            source = block_ref.at[part]
        else:
            source = weight_ref.at[(count - step + 1) if side == 0 else step - 1, part]
        return pltpu.make_async_remote_copy(
            src_ref=source,
            dst_ref=weight_ref.at[(count - step) if side == 0 else step, part],
            send_sem=send.at[step - 1, side],
            recv_sem=receive.at[step - 1, side],
            device_id={"seq": right if side == 0 else left},
            device_id_type=MESH,
        )

    def small_hop(d):
        return pltpu.make_async_remote_copy(
            src_ref=small_ref,
            dst_ref=smalls_ref.at[mine],
            send_sem=small_send.at[d - 1],
            recv_sem=small_receive.at[d - 1],
            device_id={"seq": lax.rem(mine + d, count)},
            device_id_type=MESH,
        )

    smalls = [small_hop(d) for d in range(1, count)]
    for copy in smalls:
        copy.start()
    hops = {(step, side): hop(step, side) for step in range(1, count) for side in range(2)}
    hops[1, 0].start()
    hops[1, 1].start()
    smalls_ref[mine] = small_ref[...]
    weight_ref[0] = block_ref[...]

    scales = []
    for t in range(rows // tile):
        field = wide(input_ref[t * tile : (t + 1) * tile])
        scales.append(root_scale(field))

    def gain_of(slot):
        owner = block_at(order, slot)
        return owner, wide(smalls_ref[owner])[:, :share]

    def multiply(first, second, begin):
        sides = []
        for slot, side in (first, second):
            owner, gain = gain_of(slot)
            sides.append((slot, side, owner, gain[:, side * half : (side + 1) * half]))
        for t in range(rows // tile):
            here = slice(t * tile, (t + 1) * tile)
            parts, blocks = [], []
            for slot, side, owner, gain in sides:
                start = pl.multiple_of(owner * share + side * half, half)
                field = wide(input_ref[here, pl.ds(start, half)])
                part = narrow(field * scales[t] * gain)
                column = slot * share + side * half
                normed_ref[here, column : column + half] = part
                parts.append(part)
                blocks.append(weight_ref[slot, side * half : (side + 1) * half, :])
            left_side = jnp.concatenate(parts, axis=1)
            right_side = jnp.concatenate(blocks, axis=0)
            added = product(left_side, right_side[:, :wide_cols], NN)
            low_added = product(left_side, right_side[:, low_start:], NN)
            if begin:
                total[here] = added
                low_total[here] = low_added
            else:
                total[here] += added
                low_total[here] += low_added

    for copy in smalls:
        copy.wait_recv()
    multiply((0, 0), (0, 1), True)
    for step in range(1, count):
        for side in range(2):
            hops[step, side].wait_recv()
            if step + 1 < count:
                hops[step + 1, side].start()
        multiply((count - step, 0), (step, 1), False)
    vk_cols, query_cols = vk_ref.shape[1], query_ref.shape[1]
    vk_ref[...] = narrow(total[:, :vk_cols])
    query_ref[...] = narrow(total[:, vk_cols : vk_cols + query_cols])
    gate_ref[...] = total[:, vk_cols + query_cols :]
    low_ref[...] = low_total[...]
    for copy in smalls + list(hops.values()):
        copy.wait_send()


def enter(inputs, block, small, rank):
    count = lax.axis_size("seq")
    rows, width = inputs.shape
    cols = DV + DK + DK + DV
    out_shape = [
        shape_of(BF16, rows, width),
        shape_of(BF16, count, *block.shape),
        shape_of(BF16, rows, DV + DK),
        shape_of(BF16, rows, DK),
        shape_of(F32, rows, DV),
        shape_of(F32, rows, rank),
        shape_of(BF16, count, *small.shape),
    ]
    steps = count - 1
    return pl.pallas_call(
        functools.partial(enter_kernel, ring_order(count)),
        in_specs=[pl.BlockSpec(memory_space=pltpu.VMEM)] * 3,
        out_specs=[pl.BlockSpec(memory_space=pltpu.VMEM)] * 7,
        out_shape=out_shape,
        scratch_shapes=[
            pltpu.VMEM((rows, cols), F32),
            pltpu.VMEM((rows, rank), F32),
            pltpu.SemaphoreType.DMA((steps, 2)),
            pltpu.SemaphoreType.DMA((steps, 2)),
            pltpu.SemaphoreType.DMA((steps,)),
            pltpu.SemaphoreType.DMA((steps,)),
        ],
        cost_estimate=pl.CostEstimate(
            flops=2 * rows * width * cols, bytes_accessed=400_000_000, transcendentals=0
        ),
        compiler_params=pltpu.CompilerParams(
            collective_id=0, has_side_effects=True, vmem_limit_bytes=VMEM_BYTES
        ),
    )(inputs, block, small)


def matmul(left, right):
    return product(left, right, NN)


def matmul_nt(left, right):
    return product(left, right, NT)


def matmul_tn(left, right):
    return product(left, right, TN)


def ring_order(count):
    return list(range(0, count, 2)) + list(range(count - 1 - count % 2, 0, -2))


class Ring:
    def __init__(self, axis):
        self.axis = axis
        self.count = count = lax.axis_size(axis)
        order = ring_order(count)
        place = [order.index(i) for i in range(count)]
        self.right = [(order[i], order[(i + 1) % count]) for i in range(count)]
        self.left = [(order[i], order[(i - 1) % count]) for i in range(count)]
        owners = [[order[(place[i] + r) % count] for r in range(count)] for i in range(count)]
        slots = [[(place[i] - place[me]) % count for i in range(count)] for me in range(count)]
        mine = lax.axis_index(axis)
        self.owners = jnp.asarray(owners, jnp.int32)[mine]
        self.slots = jnp.asarray(slots, jnp.int32)[mine]

    def arrange(self, field, dim, table):
        width = field.shape[dim] // self.count
        return jnp.concatenate(
            [
                lax.dynamic_slice_in_dim(field, table[r] * width, width, dim)
                for r in range(self.count)
            ],
            axis=dim,
        )

    def near(self, field, dim):
        return self.arrange(field, dim, self.owners)

    def home(self, field, dim):
        return self.arrange(field, dim, self.slots)

    def gather(self, block, after=None):
        count, half = self.count, block.shape[0] // 2
        up, down = block[:half], block[half:]
        if after is not None:
            up, down, _ = lax.optimization_barrier((up, down, after))
        pieces = [None] * (2 * count)
        pieces[0], pieces[1] = up, down
        for step in range(1, count):
            up = lax.ppermute(up, self.axis, self.right)
            down = lax.ppermute(down, self.axis, self.left)
            pieces[2 * (count - step)] = up
            pieces[2 * step + 1] = down
            if step == count - 2:
                late = up[:8, :128]
        return jnp.concatenate(pieces, axis=0), late

    def scatter(self, total):
        count = self.count
        rows = total.shape[0] // count
        half = rows // 2

        def piece(slot, part):
            start = slot * rows + part * half
            return total[start : start + half]

        up, down = piece(count - 1, 0), piece(1, 1)
        for step in range(count - 1):
            up = lax.ppermute(up, self.axis, self.right)
            down = lax.ppermute(down, self.axis, self.left)
            up = wide(up) + wide(piece(count - 2 - step, 0))
            down = wide(down) + wide(piece((step + 2) % count, 1))
            if step < count - 2:
                up, down = narrow(up), narrow(down)
        return jnp.concatenate([up, down], axis=0)


def swap(axis, distance):
    return [(i, i ^ distance) for i in range(lax.axis_size(axis))]


def head_scatter(part):
    count, mine = lax.axis_size("head"), lax.axis_index("head")
    rows = part.shape[0] // count
    held = part.reshape((count, rows) + part.shape[1:])
    distance = 1
    while distance < count:
        bit = (mine // distance) % 2
        split = held.reshape((held.shape[0] // 2, 2) + held.shape[1:])
        sent = lax.dynamic_index_in_dim(split, 1 - bit, 1, False)
        kept = lax.dynamic_index_in_dim(split, bit, 1, False)
        got = lax.ppermute(narrow(sent), "head", swap("head", distance))
        held = wide(kept) + wide(got)
        distance *= 2
    return held[0]


def head_gather(share):
    count, mine = lax.axis_size("head"), lax.axis_index("head")
    held = share[None]
    distance = count // 2
    while distance:
        bit = (mine // distance) % 2
        got = lax.ppermute(held, "head", swap("head", distance))
        lower = jnp.where(bit == 0, held, got)
        upper = jnp.where(bit == 0, got, held)
        held = jnp.stack([lower, upper], axis=1).reshape((-1,) + share.shape)
        distance //= 2
    return held.reshape((-1,) + share.shape[1:])


def with_decay(state, decay):
    high = narrow(decay)
    low = narrow(decay - wide(high))
    return jnp.concatenate([narrow(state), high, low], axis=1)


def split_decay(message):
    rows = message.shape[1] - 2
    decay = wide(message[:, rows : rows + 1]) + wide(message[:, rows + 1 :])
    return wide(message[:, :rows]), decay


def entering(state, decay, later):
    count, mine = lax.axis_size("seq"), lax.axis_index("seq")
    inner = mine % 2
    ahead = (inner == 0) != later
    half = state.shape[1] // 2
    kept = wide(lax.dynamic_slice_in_dim(state, inner * half, half, 1))
    sent = lax.dynamic_slice_in_dim(state, (1 - inner) * half, half, 1)
    pair = swap("seq", 1)
    other, other_decay = split_decay(lax.ppermute(with_decay(sent, decay), "seq", pair))
    earliest = jnp.where(ahead, kept, other)
    joined = jnp.where(ahead, other_decay, decay) * earliest + jnp.where(ahead, other, kept)
    message = with_decay(joined, decay * other_decay)
    if later:
        chain = [(i, i - 2) for i in range(2, count)]
    else:
        chain = [(i, i + 2) for i in range(count - 2)]
    before, reach = jnp.zeros_like(kept), jnp.ones_like(decay)
    for _ in range(count // 2 - 1):
        message = lax.ppermute(message, "seq", chain)
        far, far_decay = split_decay(message)
        before = before + reach * far
        reach = reach * far_decay
    second = jnp.where(ahead, decay, other_decay) * before + earliest
    got = lax.ppermute(narrow(jnp.where(ahead, second, before)), "seq", pair)
    own = narrow(jnp.where(ahead, before, second))
    return jnp.concatenate(
        [jnp.where(inner == 0, own, got), jnp.where(inner == 0, got, own)], axis=1
    )


def columns_of(vector, rows):
    width = -(-vector.shape[-1] // rows)
    pad = [(0, 0)] * (vector.ndim - 1) + [(0, width * rows - vector.shape[-1])]
    shaped = jnp.pad(vector, pad).reshape(vector.shape[:-1] + (width, rows))
    return jnp.swapaxes(shaped, -1, -2)


def shards(
    layer_in,
    seg_starts,
    attn_gain,
    query_weight,
    key_weight,
    value_weight,
    gate_weight,
    decay_down,
    decay_up,
    decay_bias,
    head_gain,
    out_weight,
    ffn_gain,
    ffn_gate,
    ffn_up,
    ffn_down,
    out_grad,
):
    ring = Ring("seq")
    count = ring.count
    batch, block, width = layer_in.shape
    rows = batch * block
    chunks = block // CHUNK
    rank, share = decay_down.shape[1], attn_gain.shape[0]
    hidden = ffn_gate.shape[1]

    smalls = [attn_gain, ffn_gain, head_gain, decay_bias, decay_up.reshape(-1)]
    ends = [sum(part.size for part in smalls[: i + 1]) for i in range(len(smalls))]
    small = jnp.pad(jnp.concatenate(smalls), (0, -ends[-1] % 128))[None]
    shard = jnp.concatenate(
        [value_weight, key_weight, query_weight, gate_weight, out_weight.T, decay_down], axis=1
    )
    inputs = layer_in.reshape(rows, width)
    if share % 256 == 0:
        normed, weights, value_key, query, gates, low, small = enter(inputs, shard, small, rank)
        weights = weights.reshape(width, -1)
        mark = low[:8]
    else:
        weights, mark = ring.gather(shard)
        small = lax.all_gather(small, "seq")
        gain = wide(small[:, 0, :share]).reshape(width)
        normed = ring.near(narrow(wide(inputs) * root_scale(wide(inputs)) * gain), 1)
        projected = matmul(normed, weights)
        value_key, query = narrow(projected[:, : DV + DK]), narrow(projected[:, DV + DK : DV + 2 * DK])
        gates, low = projected[:, DV + 2 * DK : 2 * DV + 2 * DK], projected[:, -rank:]
    third, mark = ring.gather(jnp.concatenate([ffn_gate, ffn_up], axis=1), mark)
    fdown_t, mark = ring.gather(ffn_down.T, mark)
    projections = weights[:, : 2 * DV + 2 * DK]
    out_t, down_all = weights[:, 2 * DV + 2 * DK : -rank], weights[:, -rank:]
    small = small[:, 0]
    gain_one = wide(ring.near(small[:, : ends[0]], 0)).reshape(width)
    gain_two = wide(ring.near(small[:, ends[0] : ends[1]], 0)).reshape(width)
    gain_head = wide(small[:, ends[1] : ends[2]]).reshape(1, DV)
    bias_all = wide(small[:, ends[2] : ends[3]]).reshape(1, DK)
    up_all = small[:, ends[3] : ends[4]].reshape(count, rank, -1)
    up_all = wide(jnp.swapaxes(up_all, 0, 1).reshape(rank, DK))

    starts = seg_starts.reshape(batch, chunks, CHUNK).astype(jnp.float32)
    places = jnp.arange(CHUNK)
    lower = (places[:, None] >= places[None, :]).astype(jnp.float32)
    marks = jnp.einsum("bcs,ts->bct", starts, lower, precision=HIGH)
    column, row = marks.reshape(batch, block, 1), jnp.swapaxes(marks, 0, 1)[:, :, None, :]

    grad_rows = ring.near(out_grad.reshape(rows, width), 1)
    head = lax.axis_index("head")
    quarter = rows // lax.axis_size("head")
    inputs_own = lax.dynamic_slice_in_dim(inputs, head * quarter, quarter, 0)
    inputs_own = wide(ring.near(inputs_own, 1))
    grad_own = wide(lax.dynamic_slice_in_dim(grad_rows, head * quarter, quarter, 0))

    def tokens(field):
        return field.reshape(batch, block, field.shape[-1])

    value_key, query, gates, low = map(tokens, (value_key, query, gates, low))
    run, slope, state, total = local_states(value_key, low, up_all, bias_all, column)
    state_in = entering(state, total, False)
    heads, mixed, states = mix(query, value_key, run, column, row, state_in, gates, gain_head)
    heads = heads.reshape(rows, DV)
    resid = inputs_own + head_scatter(narrow(matmul_nt(heads, out_t)))
    scale_two = root_scale(resid)
    unit_two = resid * scale_two
    normed_two = head_gather(narrow(unit_two * gain_two))
    pre_gate = matmul(normed_two, third[:, :hidden])
    pre_up = matmul(normed_two, third[:, hidden:])
    sigma = jax.nn.sigmoid(pre_gate)
    act = narrow(pre_gate * sigma * pre_up)
    layer_out = narrow(resid + head_scatter(narrow(matmul_nt(act, fdown_t))))
    layer_out = ring.home(head_gather(layer_out), 1)

    d_act = matmul(grad_rows, fdown_t)
    grad_fdown = ring.scatter(narrow(matmul_tn(grad_rows, act)))
    d_gate = narrow(d_act * pre_up * sigma * (1.0 + pre_gate * (1.0 - sigma)))
    d_up = narrow(d_act * pre_gate * sigma)
    d_third = jnp.concatenate([d_gate, d_up], axis=1)
    grad_third = ring.scatter(narrow(matmul_tn(normed_two, d_third)))
    d_normed_two = head_scatter(narrow(matmul_nt(d_third, third)))
    grad_gain_two = jnp.sum(d_normed_two * unit_two, axis=0)
    d_resid = grad_own + norm_back(d_normed_two * gain_two, unit_two, scale_two)
    d_attn = head_gather(narrow(d_resid))
    d_heads = tokens(matmul(d_attn, out_t))
    d_gates, d_mixed, grad_gain_head, state_grad = head_back(
        d_heads, gates, mixed, gain_head, query, run, column
    )
    state_back = entering(state_grad, total, True)
    d_query, d_value, d_key, d_low, grad_up, grad_bias = mix_back(
        query, value_key, run, slope, column, row, d_mixed, states, state_back, low, up_all
    )
    d_gates = d_gates.reshape(rows, DV)
    grad_out = matmul_tn(d_attn, heads)
    grad_gate = matmul_tn(normed, d_gates)
    grad_fourth = ring.scatter(narrow(jnp.concatenate([grad_gate, grad_out], axis=1)))
    d_low = narrow(d_low.reshape(rows, rank))
    d_last = jnp.concatenate(
        [d_value.reshape(rows, DV), d_key.reshape(rows, DK), d_query.reshape(rows, DK)], axis=1
    )
    d_normed_part = (
        matmul_nt(jnp.concatenate([d_last, d_gates], axis=1), projections)
        + matmul_nt(d_low, down_all)
    )
    d_normed = head_scatter(narrow(d_normed_part))
    scale_own = root_scale(inputs_own)
    unit_own = inputs_own * scale_own
    d_unit = norm_back(d_normed * gain_one, unit_own, scale_own)
    input_grad = ring.home(head_gather(narrow(d_resid + d_unit)), 1)
    unit_all = ring.near(wide(inputs) * root_scale(wide(inputs)), 1)
    grad_gain_one = jnp.sum(d_normed_part * unit_all, axis=0)

    small = jnp.concatenate(
        [
            grad_gain_head.reshape(count, -1),
            grad_bias.reshape(count, -1),
            jnp.swapaxes(grad_up.reshape(rank, count, -1), 0, 1).reshape(count, -1),
        ],
        axis=1,
    )
    small = columns_of(ring.near(small, 0), share).reshape(width, -1)
    small = jnp.concatenate([grad_gain_one[:, None], grad_gain_two[:, None], small], axis=1)
    used = d_last.shape[1] + rank
    spare = -(used + small.shape[1]) % 128
    d_last = jnp.concatenate(
        [d_last, d_low, jnp.zeros((rows, small.shape[1] + spare), BF16)], axis=1
    )
    grad_last = matmul_tn(normed, d_last) + jnp.pad(small, ((0, 0), (used, spare)))
    grad_last = ring.scatter(narrow(grad_last))
    shared = grad_last[:, used - rank :]
    distance = 1
    while distance < lax.axis_size("head"):
        shared = shared + lax.ppermute(shared, "head", swap("head", distance))
        distance *= 2

    def lone(field):
        return jnp.swapaxes(field[:, rank + 2 : rank + small.shape[1]], 0, 1).reshape(-1)

    own = lone(grad_last[:, used - rank :])
    bounds = [0, head_gain.size, head_gain.size + decay_bias.size]
    bounds.append(bounds[2] + decay_up.size)
    return (
        layer_out.reshape(batch, block, width),
        input_grad.reshape(batch, block, width),
        shared[:, rank],
        grad_last[:, DV + DK : DV + 2 * DK],
        grad_last[:, DV : DV + DK],
        grad_last[:, :DV],
        grad_fourth[:, :DV],
        shared[:, :rank],
        own[bounds[2] : bounds[3]].reshape(rank, -1),
        own[bounds[1] : bounds[2]],
        lone(shared)[: bounds[1]],
        grad_fourth[:, DV:].T,
        shared[:, rank + 1],
        grad_third[:, :hidden],
        grad_third[:, hidden:],
        grad_fdown.T,
    )


def solution(mesh):
    return jax.shard_map(
        shards,
        mesh=mesh,
        in_specs=(
            P(None, "seq", None),
            P(None, "seq"),
            P("seq"),
            P("seq", "head"),
            P("seq", "head"),
            P("seq", "head"),
            P("seq", "head"),
            P("seq", None),
            P(None, ("head", "seq")),
            P(("head", "seq")),
            P("seq"),
            P("head", "seq"),
            P("seq"),
            P("seq", "head"),
            P("seq", "head"),
            P("head", "seq"),
            P(None, "seq", None),
        ),
        out_specs=(
            P(None, "seq", None),
            P(None, "seq", None),
            P("seq"),
            P("seq", "head"),
            P("seq", "head"),
            P("seq", "head"),
            P("seq", "head"),
            P("seq", None),
            P(None, ("head", "seq")),
            P(("head", "seq")),
            P("seq"),
            P("head", "seq"),
            P("seq"),
            P("seq", "head"),
            P("seq", "head"),
            P("head", "seq"),
        ),
        check_vma=False,
    )
```

```python
import functools

import jax
import jax.numpy as jnp
from jax import lax
from jax.experimental import pallas as pl
from jax.experimental.pallas import tpu as pltpu
from jax.sharding import PartitionSpec as P

DK = 256
DV = 512
CHUNK = 128
EPS = 1e-06
HIGH = lax.Precision.HIGHEST
NN = (((1,), (0,)), ((), ()))
NT = (((1,), (1,)), ((), ()))
TN = (((0,), (0,)), ((), ()))
VMEM_BYTES = 56 * 1024 * 1024
MESH = pl.DeviceIdType.MESH


def product(left, right, dims, precision=None):
    return lax.dot_general(
        left, right, dims, precision=precision, preferred_element_type=jnp.float32
    )


def narrow(field):
    return field.astype(jnp.bfloat16)


def wide(field):
    return field.astype(jnp.float32)


def root_scale(field):
    return lax.rsqrt(jnp.mean(field * field, axis=-1, keepdims=True) + EPS)


def norm_back(upstream, unit, scale):
    return scale * (upstream - unit * jnp.mean(upstream * unit, axis=-1, keepdims=True))


def triangle(lower):
    rows = lax.broadcasted_iota(jnp.int32, (CHUNK, CHUNK), 0)
    columns = lax.broadcasted_iota(jnp.int32, (CHUNK, CHUNK), 1)
    return (rows >= columns if lower else rows <= columns).astype(jnp.float32)


def permitted(mark_column, mark_row):
    rows = lax.broadcasted_iota(jnp.int32, (CHUNK, CHUNK), 0)
    columns = lax.broadcasted_iota(jnp.int32, (CHUNK, CHUNK), 1)
    return (rows >= columns) & (mark_column == mark_row)


def state_chunk(
    value_ref, key_ref, low_ref, up_ref, bias_ref, mark_ref, run_ref, slope_ref, state, total
):
    lower = triangle(True)
    for b in range(value_ref.shape[0]):
        raw = product(low_ref[b], up_ref[...], NN, HIGH) + bias_ref[...]
        soft = jnp.log1p(jnp.exp(-jnp.abs(raw)))
        decay = (jnp.minimum(raw, 0.0) - soft) / 16.0
        slope_ref[b] = jnp.exp(jnp.minimum(-raw, 0.0) - soft) / 16.0
        run = product(lower, decay, NN, HIGH)
        run_ref[b] = run
        mark = mark_ref[b]
        last = run[CHUNK - 1 :]
        trailing = mark == mark[CHUNK - 1 :]
        kept = jnp.where(trailing, jnp.exp(last - run), 0.0)
        keep = jnp.where(mark[CHUNK - 1 :] == 0.0, jnp.exp(last), 0.0)
        tail = narrow(wide(key_ref[b]) * kept)
        state[b] = state[b] * keep + product(value_ref[b], tail, TN)
        total[b] = total[b] * keep


def state_kernel(
    value_ref, key_ref, low_ref, up_ref, bias_ref, mark_ref,
    run_ref, slope_ref, state_ref, total_ref, state, total,
):
    step = pl.program_id(0)

    @pl.when(step == 0)
    def _():
        state[...] = jnp.zeros_like(state)
        total[...] = jnp.ones_like(total)

    state_chunk(
        value_ref, key_ref, low_ref, up_ref, bias_ref, mark_ref, run_ref, slope_ref, state, total
    )

    @pl.when(step == pl.num_programs(0) - 1)
    def _():
        state_ref[...] = narrow(state[...])
        total_ref[...] = total[...]


def mixer_chunk(
    query_ref, value_ref, key_ref, run_ref, mark_ref, row_ref, gate_ref, gain_ref,
    heads_ref, mixed_ref, states_ref, state,
):
    for b in range(value_ref.shape[0]):
        run, mark = run_ref[b], mark_ref[b]
        middle, last = run[CHUNK // 2 - 1 : CHUNK // 2], run[CHUNK - 1 :]
        query = wide(query_ref[b]) * DK ** (-0.5)
        key = wide(key_ref[b])
        start = narrow(state[b])
        states_ref[0, b] = start
        scores = product(
            narrow(query * jnp.exp(run - middle)), narrow(key * jnp.exp(middle - run)), NT
        )
        scores = jnp.where(permitted(mark, row_ref[0, b]), scores, 0.0)
        opened = narrow(query * jnp.where(mark == 0.0, jnp.exp(run), 0.0))
        mixed = product(narrow(scores), value_ref[b], NN) + product(opened, start, NT)
        kept = jnp.where(mark == mark[CHUNK - 1 :], jnp.exp(last - run), 0.0)
        keep = jnp.where(mark[CHUNK - 1 :] == 0.0, jnp.exp(last), 0.0)
        state[b] = state[b] * keep + product(value_ref[b], narrow(key * kept), TN)
        states_ref[1, b] = narrow(state[b])
        mixed_ref[b] = mixed
        gate = gate_ref[b]
        active = gate * jax.nn.sigmoid(gate)
        heads_ref[b] = narrow(mixed * root_scale(mixed) * gain_ref[...] * active)


def mixer_kernel(
    query_ref, value_ref, key_ref, run_ref, mark_ref, row_ref, first_ref, gate_ref, gain_ref,
    heads_ref, mixed_ref, states_ref, state,
):
    @pl.when(pl.program_id(0) == 0)
    def _():
        state[...] = wide(first_ref[...])

    mixer_chunk(
        query_ref, value_ref, key_ref, run_ref, mark_ref, row_ref, gate_ref, gain_ref,
        heads_ref, mixed_ref, states_ref, state,
    )


def head_back_chunk(
    grad_ref, gate_ref, mixed_ref, gain_ref, query_ref, run_ref, mark_ref,
    gate_grad_ref, mixed_grad_ref, gain_grad_ref, state,
):
    gain = gain_ref[...]
    for b in range(grad_ref.shape[0]):
        mixed, gate, grad = mixed_ref[b], gate_ref[b], wide(grad_ref[b])
        scale = root_scale(mixed)
        unit = mixed * scale
        sigma = jax.nn.sigmoid(gate)
        active = gate * sigma
        gate_grad_ref[b] = narrow(grad * unit * gain * sigma * (1.0 + gate * (1.0 - sigma)))
        weighted = grad * active
        gain_grad_ref[...] += jnp.sum(weighted * unit, axis=0, keepdims=True)
        mixed_grad = narrow(norm_back(weighted * gain, unit, scale))
        mixed_grad_ref[b] = mixed_grad
        run, mark = run_ref[b], mark_ref[b]
        last = run[CHUNK - 1 :]
        query = wide(query_ref[b]) * DK ** (-0.5)
        opened = narrow(query * jnp.where(mark == 0.0, jnp.exp(run), 0.0))
        keep = jnp.where(mark[CHUNK - 1 :] == 0.0, jnp.exp(last), 0.0)
        state[b] = state[b] * keep + product(mixed_grad, opened, TN)


def head_back_kernel(
    grad_ref, gate_ref, mixed_ref, gain_ref, query_ref, run_ref, mark_ref,
    gate_grad_ref, mixed_grad_ref, gain_grad_ref, state_ref, state,
):
    step = pl.program_id(0)

    @pl.when(step == 0)
    def _():
        state[...] = jnp.zeros_like(state)
        gain_grad_ref[...] = jnp.zeros_like(gain_grad_ref)

    head_back_chunk(
        grad_ref, gate_ref, mixed_ref, gain_ref, query_ref, run_ref, mark_ref,
        gate_grad_ref, mixed_grad_ref, gain_grad_ref, state,
    )

    @pl.when(step == pl.num_programs(0) - 1)
    def _():
        state_ref[...] = narrow(state[...])


def mixer_back_chunk(
    query_ref, value_ref, key_ref, run_ref, slope_ref, mark_ref, row_ref, grad_ref,
    start_ref, end_ref, low_ref, up_ref,
    query_grad_ref, value_grad_ref, key_grad_ref, low_grad_ref, up_grad_ref, bias_grad_ref, state,
):
    upper = triangle(False)
    for b in range(value_ref.shape[0]):
        run, mark = run_ref[b], mark_ref[b]
        middle, last = run[CHUNK // 2 - 1 : CHUNK // 2], run[CHUNK - 1 :]
        query = wide(query_ref[b]) * DK ** (-0.5)
        key, value, grad = wide(key_ref[b]), value_ref[b], grad_ref[b]
        start, later = start_ref[0, b], narrow(state[b])
        rise, fall = jnp.exp(run - middle), jnp.exp(middle - run)
        opens = jnp.where(mark == 0.0, jnp.exp(run), 0.0)
        kept = jnp.where(mark == mark[CHUNK - 1 :], jnp.exp(last - run), 0.0)
        keep = jnp.where(mark[CHUNK - 1 :] == 0.0, jnp.exp(last), 0.0)
        allowed = permitted(mark, row_ref[0, b])
        risen, fallen = narrow(query * rise), narrow(key * fall)
        scores = narrow(jnp.where(allowed, product(risen, fallen, NT), 0.0))
        scores_grad = narrow(jnp.where(allowed, product(grad, value, NT), 0.0))
        query_grad = rise * product(scores_grad, fallen, NN) + opens * product(grad, start, NN)
        key_grad = fall * product(scores_grad, risen, TN) + kept * product(value, later, NN)
        value_grad = product(scores, grad, TN) + product(narrow(key * kept), later, NT)
        ends = jnp.sum(state[b] * wide(end_ref[0, b]), axis=0, keepdims=True)
        state[b] = state[b] * keep + product(grad, narrow(query * opens), TN)
        turn = query * query_grad - key * key_grad
        raw_grad = (product(upper, turn, NN, HIGH) + ends) * slope_ref[b]
        query_grad_ref[b] = narrow(query_grad * DK ** (-0.5))
        key_grad_ref[b] = narrow(key_grad)
        value_grad_ref[b] = narrow(value_grad)
        low_grad = narrow(product(raw_grad, up_ref[...], NT, HIGH))
        low_grad_ref[b, :, : low_grad.shape[1]] = low_grad
        up_grad_ref[...] += product(low_ref[b], raw_grad, TN, HIGH)
        bias_grad_ref[...] += jnp.sum(raw_grad, axis=0, keepdims=True)


def mixer_back_kernel(
    query_ref, value_ref, key_ref, run_ref, slope_ref, mark_ref, row_ref, grad_ref,
    start_ref, end_ref, last_ref, low_ref, up_ref,
    query_grad_ref, value_grad_ref, key_grad_ref, low_grad_ref, up_grad_ref, bias_grad_ref, state,
):
    @pl.when(pl.program_id(0) == 0)
    def _():
        state[...] = wide(last_ref[...])
        up_grad_ref[...] = jnp.zeros_like(up_grad_ref)
        bias_grad_ref[...] = jnp.zeros_like(bias_grad_ref)

    mixer_back_chunk(
        query_ref, value_ref, key_ref, run_ref, slope_ref, mark_ref, row_ref, grad_ref,
        start_ref, end_ref, low_ref, up_ref,
        query_grad_ref, value_grad_ref, key_grad_ref, low_grad_ref, up_grad_ref, bias_grad_ref,
        state,
    )


def along(batch, width, last=0, reverse=0):
    if reverse:
        return pl.BlockSpec((batch, CHUNK, width), lambda i: (0, reverse - 1 - i, last))
    return pl.BlockSpec((batch, CHUNK, width), lambda i: (0, i, last))


def still(*shape):
    return pl.BlockSpec(shape, lambda i: (0,) * len(shape))


def shape_of(dtype, *shape):
    return jax.ShapeDtypeStruct(shape, dtype)


def call(kernel, steps, in_specs, out_specs, out_shape, scratch, operands, flops):
    moved = sum(a.size * a.dtype.itemsize for a in operands)
    moved += sum(s.size * s.dtype.itemsize for s in out_shape)
    return pl.pallas_call(
        kernel,
        grid=(steps,),
        in_specs=in_specs,
        out_specs=out_specs,
        out_shape=out_shape,
        scratch_shapes=scratch,
        cost_estimate=pl.CostEstimate(flops=flops, bytes_accessed=moved, transcendentals=0),
        compiler_params=pltpu.CompilerParams(
            dimension_semantics=("arbitrary",), vmem_limit_bytes=VMEM_BYTES
        ),
    )(*operands)


F32, BF16 = jnp.float32, jnp.bfloat16


def local_states(value_key, low, up, bias, mark):
    batch, block, rank = low.shape
    steps = block // CHUNK
    return call(
        state_kernel,
        steps,
        [along(batch, DV), along(batch, DK, DV // DK), along(batch, rank), still(rank, DK),
         still(1, DK), along(batch, 1)],
        [along(batch, DK), along(batch, DK), still(batch, DV, DK), still(batch, 1, DK)],
        [shape_of(F32, batch, block, DK), shape_of(F32, batch, block, DK),
         shape_of(BF16, batch, DV, DK), shape_of(F32, batch, 1, DK)],
        [pltpu.VMEM((batch, DV, DK), F32), pltpu.VMEM((batch, 1, DK), F32)],
        (value_key, value_key, low, up, bias, mark),
        2 * batch * block * DK * (DV + 6 * CHUNK),
    )


def mix(query, value_key, run, mark, row, first, gates, gain):
    batch, block, _ = run.shape
    steps = block // CHUNK
    heads, mixed, states = call(
        mixer_kernel,
        steps,
        [along(batch, DK), along(batch, DV), along(batch, DK, DV // DK), along(batch, DK),
         along(batch, 1), pl.BlockSpec((1, batch, 1, CHUNK), lambda i: (i, 0, 0, 0)),
         still(batch, DV, DK), along(batch, DV), still(1, DV)],
        [along(batch, DV), along(batch, DV),
         pl.BlockSpec((2, batch, DV, DK), lambda i: (i, 0, 0, 0))],
        [shape_of(BF16, batch, block, DV), shape_of(F32, batch, block, DV),
         shape_of(BF16, 2 * steps, batch, DV, DK)],
        [pltpu.VMEM((batch, DV, DK), F32)],
        (query, value_key, value_key, run, mark, row, first, gates, gain),
        2 * batch * block * DK * (2 * DV + 3 * CHUNK),
    )
    return heads, mixed, states


def head_back(grad, gates, mixed, gain, query, run, mark):
    batch, block, _ = run.shape
    steps = block // CHUNK
    return call(
        head_back_kernel,
        steps,
        [along(batch, DV, 0, steps), along(batch, DV, 0, steps), along(batch, DV, 0, steps),
         still(1, DV), along(batch, DK, 0, steps), along(batch, DK, 0, steps),
         along(batch, 1, 0, steps)],
        [along(batch, DV, 0, steps), along(batch, DV, 0, steps), still(1, DV),
         still(batch, DV, DK)],
        [shape_of(BF16, batch, block, DV), shape_of(BF16, batch, block, DV),
         shape_of(F32, 1, DV), shape_of(BF16, batch, DV, DK)],
        [pltpu.VMEM((batch, DV, DK), F32)],
        (grad, gates, mixed, gain, query, run, mark),
        2 * batch * block * DK * DV,
    )


def mix_back(query, value_key, run, slope, mark, row, grad, states, later, low, up):
    batch, block, rank = low.shape
    steps = block // CHUNK
    return call(
        mixer_back_kernel,
        steps,
        [along(batch, DK, 0, steps), along(batch, DV, 0, steps),
         along(batch, DK, DV // DK, steps), along(batch, DK, 0, steps),
         along(batch, DK, 0, steps), along(batch, 1, 0, steps),
         pl.BlockSpec((1, batch, 1, CHUNK), lambda i: (steps - 1 - i, 0, 0, 0)),
         along(batch, DV, 0, steps),
         pl.BlockSpec((1, batch, DV, DK), lambda i: (2 * (steps - 1 - i), 0, 0, 0)),
         pl.BlockSpec((1, batch, DV, DK), lambda i: (2 * (steps - 1 - i) + 1, 0, 0, 0)),
         still(batch, DV, DK), along(batch, rank, 0, steps), still(rank, DK)],
        [along(batch, DK, 0, steps), along(batch, DV, 0, steps), along(batch, DK, 0, steps),
         along(batch, rank, 0, steps), still(rank, DK), still(1, DK)],
        [shape_of(BF16, batch, block, DK), shape_of(BF16, batch, block, DV),
         shape_of(BF16, batch, block, DK), shape_of(BF16, batch, block, rank),
         shape_of(F32, rank, DK), shape_of(F32, 1, DK)],
        [pltpu.VMEM((batch, DV, DK), F32)],
        (query, value_key, value_key, run, slope, mark, row, grad, states, states, later, low, up),
        2 * batch * block * DK * (5 * DV + 6 * CHUNK),
    )


def place_of(table, index):
    found = jnp.int32(table[0])
    for i, entry in enumerate(table[1:], 1):
        found = jnp.where(index == i, jnp.int32(entry), found)
    return found


def block_at(order, distance):
    count = len(order)
    place = place_of([order.index(i) for i in range(count)], lax.axis_index("seq"))
    return place_of(order, lax.rem(place + distance + count, count))


def greet(axis, count):
    barrier, mine = pltpu.get_barrier_semaphore(), lax.axis_index(axis)
    for d in range(1, count):
        pl.semaphore_signal(
            barrier, inc=1, device_id={axis: lax.rem(mine + d, count)}, device_id_type=MESH
        )
    pl.semaphore_wait(barrier, count - 1)


def enter_kernel(
    order, input_ref, block_ref, out_block_ref, small_ref, rise_ref,
    normed_ref, weight_ref, out_ref, vk_ref, query_ref, gate_ref, low_ref,
    gains_ref, head_gain_ref, bias_ref, up_ref,
    smalls_ref, rises_ref, total, small_send, small_receive, rise_send, rise_receive, *scratch,
):
    count = len(order)
    share, half = block_ref.shape[0], block_ref.shape[0] // 2
    rows, tile = input_ref.shape[0], 256
    mine = lax.axis_index("seq")
    ring = BlockRing(order, block_ref, weight_ref, *scratch[:3])
    out_ring = BlockRing(order, out_block_ref, out_ref, *scratch[3:])
    greet("seq", count)

    def spread(source, target, send, receive):
        return [
            pltpu.make_async_remote_copy(
                src_ref=source,
                dst_ref=target.at[mine],
                send_sem=send.at[d - 1],
                recv_sem=receive.at[d - 1],
                device_id={"seq": lax.rem(mine + d, count)},
                device_id_type=MESH,
            )
            for d in range(1, count)
        ]

    smalls = spread(small_ref, smalls_ref, small_send, small_receive)
    smalls += spread(rise_ref, rises_ref, rise_send, rise_receive)
    for copy in smalls:
        copy.start()
    ring.start()
    out_ring.start()
    smalls_ref[mine] = small_ref[...]
    rises_ref[mine] = rise_ref[...]

    scales = []
    for t in range(rows // tile):
        field = wide(input_ref[t * tile : (t + 1) * tile])
        scales.append(root_scale(field))

    def multiply(first, second, begin):
        sides = []
        for slot, side in (first, second):
            start = slot * share + side * half
            sides.append((slot, side, gains_ref[0:1, start : start + half]))
        for t in range(rows // tile):
            here = slice(t * tile, (t + 1) * tile)
            parts, blocks = [], []
            for slot, side, gain in sides:
                start = pl.multiple_of(block_at(order, slot) * share + side * half, half)
                field = wide(input_ref[here, pl.ds(start, half)])
                part = narrow(field * scales[t] * gain)
                column = slot * share + side * half
                normed_ref[here, column : column + half] = part
                parts.append(part)
                source = block_ref if slot == 0 else weight_ref.at[slot]
                blocks.append(source[side * half : (side + 1) * half])
            added = product(jnp.concatenate(parts, axis=1), jnp.concatenate(blocks, axis=0), NN)
            if begin:
                total[here] = added
            else:
                total[here] += added

    for copy in smalls:
        copy.wait_recv()
    head_share, bias_share = DV // count, DK // count
    for j in range(count):
        near = wide(smalls_ref[block_at(order, j)])
        gains_ref[0:1, j * share : (j + 1) * share] = near[:, :share]
        gains_ref[1:2, j * share : (j + 1) * share] = near[:, share : 2 * share]
        block = wide(smalls_ref[j])
        at = 2 * share
        head_gain_ref[:, j * head_share : (j + 1) * head_share] = block[:, at : at + head_share]
        at += head_share
        bias_ref[:, j * bias_share : (j + 1) * bias_share] = block[:, at : at + bias_share]
        up_ref[:, j * bias_share : (j + 1) * bias_share] = wide(rises_ref[j])
    multiply((0, 0), (0, 1), True)
    for step in range(1, count):
        ring.advance()
        out_ring.advance()
        multiply((count - step, 0), (step, 1), False)
    vk_cols, query_cols, gate_cols = vk_ref.shape[1], query_ref.shape[1], gate_ref.shape[1]
    vk_ref[...] = narrow(total[:, :vk_cols])
    query_ref[...] = narrow(total[:, vk_cols : vk_cols + query_cols])
    low_from = vk_cols + query_cols + gate_cols
    gate_ref[...] = total[:, vk_cols + query_cols : low_from]
    low_ref[...] = total[:, low_from : low_from + low_ref.shape[1]]
    for copy in smalls:
        copy.wait_send()
    ring.finish()
    out_ring.finish()


def enter(inputs, block, out_block, small, rise):
    count = lax.axis_size("seq")
    rows, width = inputs.shape
    rank, cols = rise.shape[0], block.shape[1]
    dma = [pltpu.SemaphoreType.DMA((count - 1,))] * 4
    return remote_call(
        functools.partial(enter_kernel, ring_order(count)),
        0,
        [NEAR] * 5,
        [NEAR] * 11,
        [
            shape_of(BF16, rows, width),
            shape_of(BF16, count, *block.shape),
            shape_of(BF16, count, *out_block.shape),
            shape_of(BF16, rows, DV + DK),
            shape_of(BF16, rows, DK),
            shape_of(F32, rows, DV),
            shape_of(F32, rows, rank),
            shape_of(F32, 2, width),
            shape_of(F32, 1, DV),
            shape_of(F32, 1, DK),
            shape_of(F32, rank, DK),
        ],
        [
            pltpu.VMEM((count, *small.shape), BF16),
            pltpu.VMEM((count, *rise.shape), BF16),
            pltpu.VMEM((rows, cols), F32),
        ]
        + dma
        + ring_semaphores(count)
        + ring_semaphores(count),
        (inputs, block, out_block, small, rise),
        2 * rows * width * cols,
    )


class BlockRing:
    def __init__(self, order, block_ref, whole_ref, send, receive, local):
        self.count = count = len(order)
        half = block_ref.shape[0] // 2
        aims = (block_at(order, 1), block_at(order, -1))
        self.local = pltpu.make_async_copy(block_ref, whole_ref.at[0], local)
        self.hops = {}
        for step in range(1, count):
            for side in range(2):
                part = pl.ds(side * half, half)
                held = (count - step + 1) if side == 0 else step - 1
                lands = (count - step) if side == 0 else step
                self.hops[step, side] = pltpu.make_async_remote_copy(
                    src_ref=(block_ref if step == 1 else whole_ref.at[held]).at[part],
                    dst_ref=whole_ref.at[lands, part],
                    send_sem=send.at[step - 1, side],
                    recv_sem=receive.at[step - 1, side],
                    device_id={"seq": aims[side]},
                    device_id_type=MESH,
                )
        self.step = 1

    def start(self):
        self.local.start()
        for side in range(2):
            self.hops[1, side].start()

    def advance(self):
        if self.step < self.count:
            for side in range(2):
                self.hops[self.step, side].wait_recv()
                if self.step + 1 < self.count:
                    self.hops[self.step + 1, side].start()
            self.step += 1

    def finish(self):
        while self.step < self.count:
            self.advance()
        for copy in self.hops.values():
            copy.wait_send()
        self.local.wait()


def ring_semaphores(count):
    return [
        pltpu.SemaphoreType.DMA((count - 1, 2)),
        pltpu.SemaphoreType.DMA((count - 1, 2)),
        pltpu.SemaphoreType.DMA,
    ]


class Handover:
    def __init__(self, count, later, state, decay, scratch):
        (self.decays, self.sent, self.got, self.chain, decay_send, decay_receive, send, receive) = scratch
        self.count, self.later, self.state, self.decay = count, later, state, decay
        self.mine = mine = lax.axis_index("seq")
        self.inner = lax.rem(mine, 2)
        self.pairs = count // 2
        self.pair = mine // 2
        self.place = self.pairs - 1 - self.pair if later else self.pair
        beside = mine + 1 - 2 * self.inner
        self.beside = beside
        self.ahead = (self.inner == 0) != later
        self.half = state.shape[1] // 2
        onward = mine - 2 if later else mine + 2
        self.decay_copies = [
            pltpu.make_async_remote_copy(
                src_ref=decay,
                dst_ref=self.decays.at[mine],
                send_sem=decay_send.at[d - 1],
                recv_sem=decay_receive.at[d - 1],
                device_id={"seq": lax.rem(mine + d, count)},
                device_id_type=MESH,
            )
            for d in range(1, count)
        ]
        self.swaps = [
            pltpu.make_async_remote_copy(
                src_ref=self.sent.at[i],
                dst_ref=self.got.at[i],
                send_sem=send.at[i],
                recv_sem=receive.at[i],
                device_id={"seq": beside},
                device_id_type=MESH,
            )
            for i in range(2)
        ]
        self.links = [
            pltpu.make_async_remote_copy(
                src_ref=self.chain.at[r],
                dst_ref=self.chain.at[r + 1],
                send_sem=send.at[2 + r],
                recv_sem=receive.at[2 + r],
                device_id={"seq": onward},
                device_id_type=MESH,
            )
            for r in range(self.pairs - 1)
        ]

    def clear(self):
        self.chain[...] = jnp.zeros_like(self.chain)

    def rows(self, own):
        part = self.inner if own else 1 - self.inner
        return pl.ds(pl.multiple_of(part * self.half, self.half), self.half)

    def begin(self):
        self.decays[self.mine] = self.decay[...]
        for copy in self.decay_copies:
            copy.start()
        for b in range(self.state.shape[0]):
            self.sent[0, b] = narrow(self.state[b, self.rows(False)])
        self.swaps[0].start()

    def firsts(self, b):
        kept, other = self.state[b, self.rows(True)], wide(self.got[0, b])
        decay, other_decay = self.decays[self.mine, b], self.decays[self.beside, b]
        return (
            jnp.where(self.ahead, kept, other),
            jnp.where(self.ahead, other, kept),
            jnp.where(self.ahead, decay, other_decay),
            jnp.where(self.ahead, other_decay, decay),
        )

    def send(self, r):
        @pl.when((self.place >= r) & (self.place + 1 < self.pairs))
        def _():
            self.links[r].start()

    def join(self):
        self.swaps[0].wait_recv()
        for copy in self.decay_copies:
            copy.wait_recv()
        for b in range(self.state.shape[0]):
            first, second, _, decay = self.firsts(b)
            self.chain[0, b] = narrow(decay * first + second)
        self.send(0)

    def hop(self, r):
        @pl.when(self.place >= r)
        def _():
            self.links[r - 1].wait_recv()

        if r < self.pairs - 1:
            self.send(r)

    def finish(self):
        own = []
        for b in range(self.state.shape[0]):
            before = wide(self.chain[1, b])
            reach = None
            for r in range(2, self.pairs):
                far = self.pair + r - 1 if self.later else self.pair - r + 1
                far = jnp.minimum(jnp.maximum(far, 0), self.pairs - 1)
                both = self.decays[2 * far, b] * self.decays[2 * far + 1, b]
                reach = both if reach is None else reach * both
                before = before + reach * wide(self.chain[r, b])
            first, _, decay, _ = self.firsts(b)
            after = decay * before + first
            self.sent[1, b] = narrow(jnp.where(self.ahead, after, before))
            own.append(jnp.where(self.ahead, before, after))
        self.swaps[1].start()
        for b in range(self.state.shape[0]):
            self.state[b, self.rows(True)] = own[b]
        self.swaps[1].wait_recv()
        for b in range(self.state.shape[0]):
            self.state[b, self.rows(False)] = wide(self.got[1, b])
        for copy in self.decay_copies + self.swaps:
            copy.wait_send()
        for r in range(self.pairs - 1):

            @pl.when((self.place >= r) & (self.place + 1 < self.pairs))
            def _(r=r):
                self.links[r].wait_send()


def handover_scratch(count, batch):
    half = (batch, DV // 2, DK)
    return [
        pltpu.VMEM((count, batch, 1, DK), F32),
        pltpu.VMEM((2, *half), BF16),
        pltpu.VMEM((2, *half), BF16),
        pltpu.VMEM((count // 2, *half), BF16),
        pltpu.SemaphoreType.DMA((count - 1,)),
        pltpu.SemaphoreType.DMA((count - 1,)),
        pltpu.SemaphoreType.DMA((count // 2 + 1,)),
        pltpu.SemaphoreType.DMA((count // 2 + 1,)),
    ]


PIECES = 4


class Rows:
    def __init__(self, part, out, scratch):
        self.got, self.across, self.far, send, receive = scratch
        self.part, self.out = part, out
        head = lax.axis_index("head")
        core, chip = lax.rem(head, 2), head // 2
        self.share = part.shape[0] // 4
        self.size = self.share // PIECES
        beside, facing = 2 * chip + 1 - core, 2 * (1 - chip) + core
        self.own, self.facing = head, facing
        corner = 2 * (1 - chip) + 1 - core

        def copy(kind, p, source, target, aim):
            return pltpu.make_async_remote_copy(
                src_ref=source,
                dst_ref=target,
                send_sem=send.at[kind, p],
                recv_sem=receive.at[kind, p],
                device_id={"head": aim},
                device_id_type=MESH,
            )

        self.copies = {}
        for p in range(PIECES):
            here = self.piece(p)
            mine = out.at[self.rows(head, p)]
            met = out.at[self.rows(facing, p)]
            self.copies[0, p] = copy(0, p, part.at[self.rows(corner, p)], self.got.at[0, here], beside)
            self.copies[1, p] = copy(1, p, part.at[self.rows(beside, p)], self.got.at[1, here], beside)
            self.copies[2, p] = copy(2, p, self.across.at[here], self.far.at[here], facing)
            self.copies[3, p] = copy(3, p, mine, mine, facing)
            self.copies[4, p] = copy(4, p, mine, mine, beside)
            self.copies[5, p] = copy(5, p, met, met, beside)

    def piece(self, p):
        return pl.ds(p * self.size, self.size)

    def rows(self, owner, p):
        return pl.ds(pl.multiple_of(owner * self.share + p * self.size, self.size), self.size)

    def start(self, p):
        self.copies[0, p].start()
        self.copies[1, p].start()

    def cross(self, p):
        self.copies[0, p].wait_recv()
        here = self.piece(p)
        self.across[here] = narrow(wide(self.part[self.rows(self.facing, p)]) + wide(self.got[0, here]))
        self.copies[2, p].start()

    def turn(self, p, middle):
        self.copies[1, p].wait_recv()
        self.copies[2, p].wait_recv()
        here = self.piece(p)
        total = wide(self.part[self.rows(self.own, p)]) + wide(self.got[1, here])
        self.out[self.rows(self.own, p)] = middle(here, total + wide(self.far[here]))
        self.copies[3, p].start()
        self.copies[4, p].start()

    def relay(self, p):
        self.copies[3, p].wait_recv()
        self.copies[5, p].start()

    def finish(self):
        for p in range(PIECES):
            self.copies[4, p].wait_recv()
            self.copies[5, p].wait_recv()
        for copy in self.copies.values():
            copy.wait_send()


def rows_scratch(share, width):
    return [
        pltpu.VMEM((2, share, width), BF16),
        pltpu.VMEM((share, width), BF16),
        pltpu.VMEM((share, width), BF16),
        pltpu.SemaphoreType.DMA((6, PIECES)),
        pltpu.SemaphoreType.DMA((6, PIECES)),
    ]


def greet_all(count, heads):
    barrier = pltpu.get_barrier_semaphore()
    for axis, size in (("seq", count), ("head", heads)):
        mine = lax.axis_index(axis)
        for d in range(1, size):
            pl.semaphore_signal(
                barrier, inc=1, device_id={axis: lax.rem(mine + d, size)}, device_id_type=MESH
            )
    pl.semaphore_wait(barrier, count + heads - 2)


def chunk_at(i):
    return pl.ds(pl.multiple_of(i * CHUNK, CHUNK), CHUNK)


def token_phase_kernel(
    order, vk_ref, query_ref, gate_ref, low_ref, up_ref, bias_ref, starts_ref, gain_ref,
    out_ref, block_ref,
    run_ref, slope_ref, total_ref, mixed_ref, heads_ref, states_ref, part_ref, whole_ref,
    state, ring_send, ring_receive, ring_local, mark_ref, row_ref, *scratch,
):
    count = len(order)
    ring = BlockRing(order, block_ref, whole_ref, ring_send, ring_receive, ring_local)
    hand = Handover(count, False, state, total_ref, scratch)
    hand.clear()
    greet("seq", count)
    ring.start()
    fill_marks(starts_ref, mark_ref, row_ref)
    state[...] = jnp.zeros_like(state)
    total_ref[...] = jnp.ones_like(total_ref)
    chunks = run_ref.shape[1] // CHUNK

    @pl.loop(0, chunks)
    def _(i):
        at = chunk_at(i)
        state_chunk(
            vk_ref.at[:, at, pl.ds(0, DV)], vk_ref.at[:, at, pl.ds(DV, DK)], low_ref.at[:, at],
            up_ref, bias_ref, mark_ref.at[:, at], run_ref.at[:, at], slope_ref.at[:, at],
            state, total_ref,
        )

    hand.begin()
    ring.advance()
    hand.join()
    ring.advance()
    for r in range(1, count // 2):
        hand.hop(r)
        if r % 2 == 0:
            ring.advance()
    hand.finish()
    ring.advance()

    @pl.loop(0, chunks)
    def _(i):
        at = chunk_at(i)
        mixer_chunk(
            query_ref.at[:, at], vk_ref.at[:, at, pl.ds(0, DV)], vk_ref.at[:, at, pl.ds(DV, DK)],
            run_ref.at[:, at], mark_ref.at[:, at], row_ref.at[pl.ds(i, 1)], gate_ref.at[:, at],
            gain_ref, heads_ref.at[:, at], mixed_ref.at[:, at], states_ref.at[pl.ds(2 * i, 2)],
            state,
        )

    ring.advance()
    batch, block, _ = heads_ref.shape
    tile = 256
    for b in range(batch):
        for t in range(block // tile):
            field = heads_ref[b, t * tile : (t + 1) * tile]
            start = b * block + t * tile
            part_ref[start : start + tile] = narrow(product(field, out_ref[...], NT))
        ring.advance()
    ring.finish()


def remote_call(kernel, number, in_specs, out_specs, out_shape, scratch, operands, flops):
    moved = sum(a.size * a.dtype.itemsize for a in operands)
    moved += sum(s.size * s.dtype.itemsize for s in out_shape)
    return pl.pallas_call(
        kernel,
        in_specs=in_specs,
        out_specs=out_specs,
        out_shape=out_shape,
        scratch_shapes=scratch,
        cost_estimate=pl.CostEstimate(flops=flops, bytes_accessed=moved, transcendentals=0),
        compiler_params=pltpu.CompilerParams(
            collective_id=number, has_side_effects=True, vmem_limit_bytes=VMEM_BYTES
        ),
    )(*operands)


NEAR = pl.BlockSpec(memory_space=pltpu.VMEM)
AWAY = pl.BlockSpec(memory_space=pl.ANY)


def token_phase(value_key, query, gates, low, up, bias, starts, gain, out_t, block):
    count = lax.axis_size("seq")
    batch, length, _ = low.shape
    chunks, width = length // CHUNK, out_t.shape[0]
    return remote_call(
        functools.partial(token_phase_kernel, ring_order(count)),
        1,
        [NEAR] * 9 + [AWAY],
        [NEAR] * 7 + [AWAY],
        [
            shape_of(F32, batch, length, DK),
            shape_of(F32, batch, length, DK),
            shape_of(F32, batch, 1, DK),
            shape_of(F32, batch, length, DV),
            shape_of(BF16, batch, length, DV),
            shape_of(BF16, 2 * chunks, batch, DV, DK),
            shape_of(BF16, batch * length, width),
            shape_of(BF16, count, *block.shape),
        ],
        [pltpu.VMEM((batch, DV, DK), F32)]
        + ring_semaphores(count)
        + marks_scratch(batch, length)
        + handover_scratch(count, batch),
        (value_key, query, gates, low, up, bias, starts, gain, out_t, block),
        2 * batch * length * DV * (2 * DK + width),
    )


def row_phase_kernel(
    order, heads, part_ref, input_ref, gain_ref, block_ref,
    resid_ref, normed_ref, whole_ref,
    own, own_sems, ring_send, ring_receive, ring_local, *scratch,
):
    ring = BlockRing(order, block_ref, whole_ref, ring_send, ring_receive, ring_local)
    rows = Rows(part_ref, normed_ref, scratch)
    first = pl.multiple_of(rows.own * rows.share, rows.share)
    copies = near_copies(order, input_ref, own, pl.ds(first, rows.share), own_sems)
    for copy in copies:
        copy.start()
    greet_all(len(order), heads)
    for p in range(PIECES):
        rows.start(p)
    ring.start()

    def middle(here, total):
        resid = wide(own[here]) + total
        resid_ref[here] = resid
        return narrow(resid * root_scale(resid) * gain_ref[1:2])

    for p in range(PIECES):
        rows.cross(p)
    for copy in copies:
        copy.wait()
    ring.advance()
    for p in range(PIECES):
        rows.turn(p, middle)
        if p % 2 == 0:
            ring.advance()
    ring.advance()
    for p in range(PIECES):
        rows.relay(p)
        if p % 2 == 0:
            ring.advance()
    rows.finish()
    ring.finish()


def row_phase(part, inputs, gains, block):
    count, heads = lax.axis_size("seq"), lax.axis_size("head")
    rows, width = part.shape
    return remote_call(
        functools.partial(row_phase_kernel, ring_order(count), heads),
        2,
        [NEAR, AWAY, NEAR, AWAY],
        [NEAR] * 2 + [AWAY],
        [
            shape_of(F32, rows // heads, width),
            shape_of(BF16, rows, width),
            shape_of(BF16, count, *block.shape),
        ],
        [pltpu.VMEM((rows // heads, width), BF16), pltpu.SemaphoreType.DMA((count,))]
        + ring_semaphores(count)
        + rows_scratch(rows // heads, width),
        (part, inputs, gains, block),
        16 * rows * width,
    )


def near_copies(order, source, target, rows, semaphores):
    share = source.shape[1] // len(order)
    return [
        pltpu.make_async_copy(
            source.at[rows, pl.ds(pl.multiple_of(block_at(order, r) * share, share), share)],
            target.at[:, pl.ds(r * share, share)],
            semaphores.at[r],
        )
        for r in range(len(order))
    ]


def home_copies(order, source, target, semaphores):
    share = source.shape[1] // len(order)
    return [
        pltpu.make_async_copy(
            source.at[:, pl.ds(r * share, share)],
            target.at[:, pl.ds(pl.multiple_of(block_at(order, r) * share, share), share)],
            semaphores.at[r],
        )
        for r in range(len(order))
    ]


def fill_marks(starts_ref, mark_ref, row_ref):
    batch, length, _ = mark_ref.shape
    chunks = length // CHUNK
    starts = starts_ref[...].astype(F32)
    across = product(starts, triangle(False), NN, HIGH)
    down = product(triangle(True), starts, NT, HIGH)
    for b in range(batch):
        for i in range(chunks):
            n = b * chunks + i
            mark_ref[b, i * CHUNK : (i + 1) * CHUNK] = down[:, n : n + 1]
            row_ref[i, b] = across[n : n + 1]


def marks_scratch(batch, length):
    return [
        pltpu.VMEM((batch, length, 1), F32),
        pltpu.VMEM((length // CHUNK, batch, 1, CHUNK), F32),
    ]


class SumRing:
    def __init__(self, order, items, out_ref, scratch):
        lefts = []
        for left, _, _ in items:
            if not any(left is other for other in lefts):
                lefts.append(left)
        buffers, rest = scratch[: len(lefts)], scratch[len(lefts) :]
        self.sent, self.got, load, send, receive = rest
        self.order, self.items, self.out = order, items, out_ref
        self.count = count = len(order)
        self.half = half = out_ref.shape[0] // 2
        self.buffers = {id(left): buffer for left, buffer in zip(lefts, buffers)}
        homes = {id(left): home for left, _, home in items}
        aims = (block_at(order, 1), block_at(order, -1))
        self.loads, self.hops = {}, {}
        for k in range(count):
            for side in range(2):
                slot = (count - 1 - k) if side == 0 else (k + 1) % count
                for n, (left, buffer) in enumerate(zip(lefts, buffers)):
                    block = block_at(order, slot) if homes[id(left)] else slot
                    column = pl.multiple_of(block * 2 * half + side * half, half)
                    self.loads[k, side, n] = pltpu.make_async_copy(
                        left.at[:, pl.ds(column, half)],
                        buffer.at[k % 2, side],
                        load.at[k % 2, side, n],
                    )
                if k < count - 1:
                    self.hops[k, side] = pltpu.make_async_remote_copy(
                        src_ref=self.sent.at[k % 2, side],
                        dst_ref=self.got.at[k, side],
                        send_sem=send.at[k, side],
                        recv_sem=receive.at[k, side],
                        device_id={"seq": aims[side]},
                        device_id_type=MESH,
                    )
        self.number = len(lefts)
        self.k = 0

    def load(self, k):
        if k < self.count:
            for side in range(2):
                for n in range(self.number):
                    self.loads[k, side, n].start()

    def prepare(self):
        self.load(0)
        self.load(1)

    def advance(self):
        k, last = self.k, self.count - 1
        if k > last:
            return
        for side in range(2):
            for n in range(self.number):
                self.loads[k, side, n].wait()
            products = [
                product(self.buffers[id(left)][k % 2, side], right[...], TN)
                for left, right, _ in self.items
            ]
            if k > 0:
                self.hops[k - 1, side].wait_recv()
            if 2 <= k < last:
                self.hops[k - 2, side].wait_send()
            column = 0
            for value in products:
                columns = slice(column, column + value.shape[1])
                column += value.shape[1]
                if k > 0:
                    value = value + wide(self.got[k - 1, side, :, columns])
                if k < last:
                    self.sent[k % 2, side, :, columns] = narrow(value)
                else:
                    self.out[side * self.half : (side + 1) * self.half, columns] = value
            if k < last:
                self.hops[k, side].start()
        self.load(k + 2)
        self.k += 1

    def finish(self):
        while self.k < self.count:
            self.advance()
        for k in (self.count - 3, self.count - 2):
            for side in range(2):
                self.hops[k, side].wait_send()


def sum_scratch(count, rows, lefts, half, columns):
    return [pltpu.VMEM((2, 2, rows, half), BF16)] * lefts + [
        pltpu.VMEM((2, 2, half, columns), BF16),
        pltpu.VMEM((count - 1, 2, half, columns), BF16),
        pltpu.SemaphoreType.DMA((2, 2, lefts)),
        pltpu.SemaphoreType.DMA((count - 1, 2)),
        pltpu.SemaphoreType.DMA((count - 1, 2)),
    ]


def unit_phase_kernel(
    order, normed_ref, gate_ref, up_ref, grad_ref, block_ref,
    act_ref, gate_grad_ref, up_grad_ref, whole_ref,
    pre_gate, pre_up, act_grad, tiles, tile_sems, ring_send, ring_receive, ring_local,
):
    count = len(order)
    ring = BlockRing(order, block_ref, whole_ref, ring_send, ring_receive, ring_local)
    greet("seq", count)
    ring.start()
    rows = normed_ref.shape[0]
    tile = 128
    share, half = block_ref.shape[0], block_ref.shape[0] // 2

    def written(kind, target, i):
        return pltpu.make_async_copy(
            tiles.at[kind], target.at[pl.ds(i * tile, tile)], tile_sems.at[kind]
        )

    def forward(begin, end):
        @pl.loop(begin, end)
        def _(i):
            here = pl.ds(pl.multiple_of(i * tile, tile), tile)
            field = normed_ref[here]
            gate = product(field, gate_ref[...], NN)
            up = product(field, up_ref[...], NN)
            pre_gate[here] = gate
            pre_up[here] = up

            @pl.when(i > 0)
            def _():
                written(0, act_ref, i - 1).wait()

            tiles[0] = narrow(gate * jax.nn.sigmoid(gate) * up)
            written(0, act_ref, i).start()

    def multiply(parts, begin):
        @pl.loop(0, rows // 256)
        def _(t):
            here = pl.ds(pl.multiple_of(t * 256, 256), 256)
            lefts, rights = [], []
            for slot, side in parts:
                start = pl.multiple_of(block_at(order, slot) * share + side * half, half)
                lefts.append(grad_ref[here, pl.ds(start, half)])
                source = block_ref if slot == 0 else whole_ref.at[slot]
                rights.append(source[side * half : (side + 1) * half])
            added = product(jnp.concatenate(lefts, axis=1), jnp.concatenate(rights, axis=0), NN)
            if begin:
                act_grad[here] = added
            else:
                act_grad[here] += added

    steps = rows // tile
    arrived = []
    done = 0
    for step in range(1, count):
        goal = min(steps, (step * steps + count - 3) // (count - 2))
        if goal > done:
            forward(done, goal)
            done = goal
        ring.advance()
        arrived += [(count - step, 0), (step, 1)]
        if step == 1:
            multiply([(0, 0), (0, 1)] + arrived, True)
            arrived = []
        elif len(arrived) == 4:
            multiply(arrived, False)
            arrived = []
    if arrived:
        multiply(arrived, False)
    written(0, act_ref, steps - 1).wait()

    @pl.loop(0, steps)
    def _(i):
        here = pl.ds(pl.multiple_of(i * tile, tile), tile)
        gate, up, grad = pre_gate[here], pre_up[here], act_grad[here]
        sigma = jax.nn.sigmoid(gate)

        @pl.when(i > 0)
        def _():
            written(0, gate_grad_ref, i - 1).wait()
            written(1, up_grad_ref, i - 1).wait()

        tiles[0] = narrow(grad * up * sigma * (1.0 + gate * (1.0 - sigma)))
        tiles[1] = narrow(grad * gate * sigma)
        written(0, gate_grad_ref, i).start()
        written(1, up_grad_ref, i).start()

    written(0, gate_grad_ref, steps - 1).wait()
    written(1, up_grad_ref, steps - 1).wait()
    ring.finish()


def unit_phase(normed_two, fgate, fup, grad_rows, block):
    count = lax.axis_size("seq")
    rows, width = normed_two.shape
    hidden = block.shape[1]
    flat = shape_of(BF16, rows, hidden)
    return remote_call(
        functools.partial(unit_phase_kernel, ring_order(count)),
        3,
        [NEAR] * 5,
        [AWAY] * 3 + [NEAR],
        [flat, flat, flat, shape_of(BF16, count, *block.shape)],
        [pltpu.VMEM((rows, hidden), F32)] * 3
        + [pltpu.VMEM((2, 128, hidden), BF16), pltpu.SemaphoreType.DMA((2,))]
        + ring_semaphores(count),
        (normed_two, fgate, fup, grad_rows, block),
        6 * rows * width * hidden,
    )


def resid_phase_kernel(
    order, heads, part_ref, resid_ref, grad_ref, gain_ref, out_ref, act_ref, normed_ref, up_grad_ref,
    resid_grad_ref, attn_grad_ref, heads_grad_ref, gain_grad_ref, sums_ref,
    own, own_sems, *scratch,
):
    count = len(order)
    rows = Rows(part_ref, attn_grad_ref, scratch[:5])
    ring = SumRing(
        order, [(grad_ref, act_ref, True), (normed_ref, up_grad_ref, False)], sums_ref, scratch[5:]
    )
    first = pl.multiple_of(rows.own * rows.share, rows.share)
    copies = near_copies(order, grad_ref, own, pl.ds(first, rows.share), own_sems)
    for copy in copies:
        copy.start()
    ring.prepare()
    greet_all(count, heads)
    for p in range(PIECES):
        rows.start(p)
    ring.advance()
    gain_grad_ref[...] = jnp.zeros_like(gain_grad_ref)

    def middle(here, total):
        resid = resid_ref[here]
        scale = root_scale(resid)
        unit = resid * scale
        gain_grad_ref[...] += jnp.sum(total * unit, axis=0, keepdims=True)
        grad = wide(own[here]) + norm_back(total * gain_ref[1:2], unit, scale)
        resid_grad_ref[here] = grad
        return narrow(grad)

    for p in range(PIECES):
        rows.cross(p)
    for copy in copies:
        copy.wait()
    rows.turn(0, middle)
    ring.advance()
    for p in range(1, PIECES):
        rows.turn(p, middle)
    ring.advance()
    for p in range(PIECES):
        rows.relay(p)
        if p == 2:
            ring.advance()
    rows.finish()
    for t in range(4):
        at = pl.ds(t * rows.share, rows.share)
        heads_grad_ref[at] = product(attn_grad_ref[at], out_ref[...], NN)
    ring.finish()


def resid_phase(part, resid, grad_rows, gains, out_t, act, normed_two, d_up):
    count, heads = lax.axis_size("seq"), lax.axis_size("head")
    rows, width = part.shape
    share, hidden = width // count, act.shape[1]
    quarter = rows // heads
    return remote_call(
        functools.partial(resid_phase_kernel, ring_order(count), heads),
        4,
        [NEAR, NEAR, AWAY, NEAR, NEAR, NEAR, AWAY, NEAR],
        [NEAR] * 5,
        [
            shape_of(F32, quarter, width),
            shape_of(BF16, rows, width),
            shape_of(F32, rows, DV),
            shape_of(F32, 1, width),
            shape_of(F32, share, 2 * hidden),
        ],
        [pltpu.VMEM((quarter, width), BF16), pltpu.SemaphoreType.DMA((count,))]
        + rows_scratch(quarter, width)
        + sum_scratch(count, rows, 2, share // 2, 2 * hidden),
        (part, resid, grad_rows, gains, out_t, act, normed_two, d_up),
        2 * rows * width * (2 * hidden + DV),
    )


def back_phase_kernel(
    order, heads, part_ref, resid_ref, heads_grad_ref, gate_ref, mixed_ref, gain_ref, query_ref,
    vk_ref, run_ref, slope_ref, states_ref, low_ref, up_ref, starts_ref, total_ref,
    normed_ref, act_grad_ref,
    packed_ref, up_grad_ref, bias_grad_ref, gain_grad_ref, layer_ref, sums_ref,
    state, mixed_grad, layer, layer_sems, mark_ref, row_ref, *scratch,
):
    count = len(order)
    rows = Rows(part_ref, layer, scratch[:5])
    hand = Handover(count, True, state, total_ref, scratch[5:13])
    ring = SumRing(order, [(normed_ref, act_grad_ref, False)], sums_ref, scratch[13:])
    hand.clear()
    ring.prepare()
    greet_all(count, heads)
    for p in range(PIECES):
        rows.start(p)
    ring.advance()
    batch, length, _ = run_ref.shape
    chunks = length // CHUNK
    gates_from, low_from = DV + 2 * DK, 2 * DV + 2 * DK
    fill_marks(starts_ref, mark_ref, row_ref)
    state[...] = jnp.zeros_like(state)
    for ref in (gain_grad_ref, up_grad_ref, bias_grad_ref):
        ref[...] = jnp.zeros_like(ref)
    packed_ref[:, :, low_from:] = jnp.zeros(packed_ref.shape[:2] + (packed_ref.shape[2] - low_from,), BF16)

    @pl.loop(0, chunks)
    def _(i):
        at = chunk_at(chunks - 1 - i)
        head_back_chunk(
            heads_grad_ref.at[:, at], gate_ref.at[:, at], mixed_ref.at[:, at], gain_ref,
            query_ref.at[:, at], run_ref.at[:, at], mark_ref.at[:, at],
            packed_ref.at[:, at, pl.ds(gates_from, DV)], mixed_grad.at[:, at], gain_grad_ref, state,
        )

    def middle(here, total):
        return narrow(resid_ref[here] + total)

    hand.begin()
    for p in range(PIECES):
        rows.cross(p)
    ring.advance()
    hand.join()
    rows.turn(0, middle)
    ring.advance()
    for r in range(1, count // 2):
        hand.hop(r)
        if r < PIECES:
            rows.turn(r, middle)
    ring.advance()
    hand.finish()
    for r in range(count // 2, PIECES):
        rows.turn(r, middle)
    rows.relay(0)
    rows.relay(1)
    ring.advance()

    def back(begin, end):
        @pl.loop(begin, end)
        def _(i):
            n = chunks - 1 - i
            at = chunk_at(n)
            mixer_back_chunk(
                query_ref.at[:, at], vk_ref.at[:, at, pl.ds(0, DV)],
                vk_ref.at[:, at, pl.ds(DV, DK)], run_ref.at[:, at], slope_ref.at[:, at],
                mark_ref.at[:, at], row_ref.at[pl.ds(n, 1)], mixed_grad.at[:, at],
                states_ref.at[pl.ds(2 * n, 1)], states_ref.at[pl.ds(2 * n + 1, 1)],
                low_ref.at[:, at], up_ref,
                packed_ref.at[:, at, pl.ds(DV + DK, DK)], packed_ref.at[:, at, pl.ds(0, DV)],
                packed_ref.at[:, at, pl.ds(DV, DK)], packed_ref.at[:, at, pl.ds(low_from, 128)],
                up_grad_ref, bias_grad_ref, state,
            )

    back(0, chunks // 2)
    rows.relay(2)
    ring.advance()
    back(chunks // 2, chunks)
    rows.relay(3)
    rows.finish()
    copies = home_copies(order, layer, layer_ref, layer_sems)
    for copy in copies:
        copy.start()
    ring.finish()
    for copy in copies:
        copy.wait()


def back_phase(
    part, resid, d_heads, gates, mixed, gain, query, vk, run, slope, states, low, up, starts, total,
    normed_two, d_gate, packed_cols,
):
    count, heads = lax.axis_size("seq"), lax.axis_size("head")
    rows, width = part.shape
    batch, length, rank = low.shape
    share, hidden, quarter = width // count, d_gate.shape[1], rows // heads
    return remote_call(
        functools.partial(back_phase_kernel, ring_order(count), heads),
        5,
        [NEAR] * 15 + [AWAY, NEAR],
        [NEAR] * 4 + [AWAY, NEAR],
        [
            shape_of(BF16, batch, length, packed_cols),
            shape_of(F32, rank, DK),
            shape_of(F32, 1, DK),
            shape_of(F32, 1, DV),
            shape_of(BF16, rows, width),
            shape_of(F32, share, hidden),
        ],
        [
            pltpu.VMEM((batch, DV, DK), F32),
            pltpu.VMEM((batch, length, DV), BF16),
            pltpu.VMEM((rows, width), BF16),
            pltpu.SemaphoreType.DMA((count,)),
        ]
        + marks_scratch(batch, length)
        + rows_scratch(quarter, width)
        + handover_scratch(count, batch)
        + sum_scratch(count, rows, 1, share // 2, hidden),
        (part, resid, d_heads, gates, mixed, gain, query, vk, run, slope, states, low, up, starts,
         total, normed_two, d_gate),
        2 * rows * width * hidden,
    )


SMALL = 24


def last_phase_kernel(
    order, heads, part_ref, input_ref, resid_grad_ref, gain_ref, normed_ref, packed_ref, attn_ref,
    heads_ref, ffn_gain_ref, head_gain_ref, bias_ref, up_ref,
    input_grad_ref, sums_ref, small_ref, tail_ref,
    own, own_sems, grads, grad_sems, gain_grad, stage, stage_got, shared, shared_got, tail_got,
    seq_send, seq_receive, head_send, head_receive, *scratch,
):
    count = len(order)
    rows = Rows(part_ref, grads, scratch[:5])
    ring = SumRing(
        order, [(normed_ref, packed_ref, False), (attn_ref, heads_ref, False)], sums_ref, scratch[5:]
    )
    first = pl.multiple_of(rows.own * rows.share, rows.share)
    copies = near_copies(order, input_ref, own, pl.ds(first, rows.share), own_sems)
    for copy in copies:
        copy.start()
    ring.prepare()
    greet_all(count, heads)
    for p in range(PIECES):
        rows.start(p)
    ring.advance()
    gain_grad[...] = jnp.zeros_like(gain_grad)

    def middle(here, total):
        field = wide(own[here])
        scale = root_scale(field)
        unit = field * scale
        gain_grad[...] += jnp.sum(total * unit, axis=0, keepdims=True)
        return narrow(resid_grad_ref[here] + norm_back(total * gain_ref[0:1], unit, scale))

    for p in range(PIECES):
        rows.cross(p)
    for copy in copies:
        copy.wait()
    ring.advance()
    for p in range(PIECES):
        rows.turn(p, middle)
        if p == 2:
            ring.advance()

    mine, head = lax.axis_index("seq"), lax.axis_index("head")
    share = sums_ref.shape[0]
    stage[...] = jnp.zeros_like(stage)
    pieces = [ref.shape[1] // count for ref in (head_gain_ref, bias_ref, up_ref)]
    for j in range(count):
        stage[j, 0:1, : pieces[0]] = head_gain_ref[:, j * pieces[0] : (j + 1) * pieces[0]]
        stage[j, 1:2, : pieces[1]] = bias_ref[:, j * pieces[1] : (j + 1) * pieces[1]]
        stage[j, 8:, : pieces[2]] = up_ref[:, j * pieces[2] : (j + 1) * pieces[2]]
        owner = block_at(order, j)
        for n, ref in ((2, gain_grad), (4, ffn_gain_ref)):
            for t in range(share // 128):
                start = j * share + t * 128
                stage[owner, n + t : n + t + 1, :] = ref[:, start : start + 128]
    stage_hops = []
    for d in range(1, count):
        aim = lax.rem(mine + d, count)
        stage_hops.append(
            pltpu.make_async_remote_copy(
                src_ref=stage.at[aim],
                dst_ref=stage_got.at[d - 1],
                send_sem=seq_send.at[d - 1],
                recv_sem=seq_receive.at[d - 1],
                device_id={"seq": aim},
                device_id_type=MESH,
            )
        )
    for hop in stage_hops:
        hop.start()

    def head_hops(kind, source, target):
        return [
            pltpu.make_async_remote_copy(
                src_ref=source,
                dst_ref=target.at[d - 1],
                send_sem=head_send.at[kind, d - 1],
                recv_sem=head_receive.at[kind, d - 1],
                device_id={"head": lax.rem(head + d, heads)},
                device_id_type=MESH,
            )
            for d in range(1, heads)
        ]

    rows.relay(0)
    rows.relay(1)
    ring.advance()
    rows.relay(2)
    rows.relay(3)
    for hop in stage_hops:
        hop.wait_recv()
    total = stage[mine]
    for d in range(count - 1):
        total = total + stage_got[d]
    small_ref[...] = total
    shared[...] = total[:8]
    shared_hops = head_hops(0, shared, shared_got)
    for hop in shared_hops:
        hop.start()
    ring.advance()
    rows.finish()
    backs = home_copies(order, grads, input_grad_ref, grad_sems)
    for copy in backs:
        copy.start()
    for hop in shared_hops:
        hop.wait_recv()
    small_ref[0:8] = shared[...] + (shared_got[0] + shared_got[1] + shared_got[2])
    small_ref[1:2] = shared[1:2]
    ring.finish()
    low_from = 2 * DV + 2 * DK
    tail_ref[...] = sums_ref[:, low_from : low_from + 128]
    tail_hops = head_hops(1, tail_ref, tail_got)
    for hop in tail_hops:
        hop.start()
    for hop in tail_hops:
        hop.wait_recv()
    for hop in stage_hops + shared_hops + tail_hops:
        hop.wait_send()
    tail_ref[...] = tail_ref[...] + (tail_got[0] + tail_got[1] + tail_got[2])
    for copy in backs:
        copy.wait()


def last_phase(
    part, inputs, d_resid, gains, normed, packed, d_attn, heads_out, ffn_gain, head_gain, bias, up
):
    count, heads = lax.axis_size("seq"), lax.axis_size("head")
    rows, width = part.shape
    share, quarter = width // count, rows // heads
    columns = packed.shape[1] + heads_out.shape[1]
    return remote_call(
        functools.partial(last_phase_kernel, ring_order(count), heads),
        6,
        [NEAR, AWAY, NEAR, NEAR, AWAY, NEAR, AWAY, NEAR, NEAR, NEAR, NEAR, NEAR],
        [AWAY, NEAR, NEAR, NEAR],
        [
            shape_of(BF16, rows, width),
            shape_of(F32, share, columns),
            shape_of(F32, SMALL, 128),
            shape_of(F32, share, 128),
        ],
        [
            pltpu.VMEM((quarter, width), BF16),
            pltpu.SemaphoreType.DMA((count,)),
            pltpu.VMEM((rows, width), BF16),
            pltpu.SemaphoreType.DMA((count,)),
            pltpu.VMEM((1, width), F32),
            pltpu.VMEM((count, SMALL, 128), F32),
            pltpu.VMEM((count - 1, SMALL, 128), F32),
            pltpu.VMEM((8, 128), F32),
            pltpu.VMEM((heads - 1, 8, 128), F32),
            pltpu.VMEM((heads - 1, share, 128), F32),
            pltpu.SemaphoreType.DMA((count - 1,)),
            pltpu.SemaphoreType.DMA((count - 1,)),
            pltpu.SemaphoreType.DMA((2, heads - 1)),
            pltpu.SemaphoreType.DMA((2, heads - 1)),
        ]
        + rows_scratch(quarter, width)
        + sum_scratch(count, rows, 2, share // 2, columns),
        (part, inputs, d_resid, gains, normed, packed, d_attn, heads_out, ffn_gain, head_gain, bias, up),
        2 * rows * width * columns,
    )


def matmul(left, right):
    return product(left, right, NN)


def matmul_nt(left, right):
    return product(left, right, NT)


def matmul_tn(left, right):
    return product(left, right, TN)


def ring_order(count):
    return list(range(0, count, 2)) + list(range(count - 1 - count % 2, 0, -2))


class Ring:
    def __init__(self, axis):
        self.axis = axis
        self.count = count = lax.axis_size(axis)
        order = ring_order(count)
        place = [order.index(i) for i in range(count)]
        self.right = [(order[i], order[(i + 1) % count]) for i in range(count)]
        self.left = [(order[i], order[(i - 1) % count]) for i in range(count)]
        owners = [[order[(place[i] + r) % count] for r in range(count)] for i in range(count)]
        slots = [[(place[i] - place[me]) % count for i in range(count)] for me in range(count)]
        mine = lax.axis_index(axis)
        self.owners = jnp.asarray(owners, jnp.int32)[mine]
        self.slots = jnp.asarray(slots, jnp.int32)[mine]

    def arrange(self, field, dim, table):
        width = field.shape[dim] // self.count
        return jnp.concatenate(
            [
                lax.dynamic_slice_in_dim(field, table[r] * width, width, dim)
                for r in range(self.count)
            ],
            axis=dim,
        )

    def near(self, field, dim):
        return self.arrange(field, dim, self.owners)

    def home(self, field, dim):
        return self.arrange(field, dim, self.slots)

    def gather(self, block, after=None):
        count, half = self.count, block.shape[0] // 2
        up, down = block[:half], block[half:]
        if after is not None:
            up, down, _ = lax.optimization_barrier((up, down, after))
        pieces = [None] * (2 * count)
        pieces[0], pieces[1] = up, down
        for step in range(1, count):
            up = lax.ppermute(up, self.axis, self.right)
            down = lax.ppermute(down, self.axis, self.left)
            pieces[2 * (count - step)] = up
            pieces[2 * step + 1] = down
            if step == count - 2:
                late = up[:8, :128]
        return jnp.concatenate(pieces, axis=0), late

    def scatter(self, total):
        count = self.count
        rows = total.shape[0] // count
        half = rows // 2

        def piece(slot, part):
            start = slot * rows + part * half
            return total[start : start + half]

        up, down = piece(count - 1, 0), piece(1, 1)
        for step in range(count - 1):
            up = lax.ppermute(up, self.axis, self.right)
            down = lax.ppermute(down, self.axis, self.left)
            up = wide(up) + wide(piece(count - 2 - step, 0))
            down = wide(down) + wide(piece((step + 2) % count, 1))
            if step < count - 2:
                up, down = narrow(up), narrow(down)
        return jnp.concatenate([up, down], axis=0)


def swap(axis, distance):
    return [(i, i ^ distance) for i in range(lax.axis_size(axis))]


def head_scatter(part):
    count, mine = lax.axis_size("head"), lax.axis_index("head")
    rows = part.shape[0] // count
    held = part.reshape((count, rows) + part.shape[1:])
    distance = 1
    while distance < count:
        bit = (mine // distance) % 2
        split = held.reshape((held.shape[0] // 2, 2) + held.shape[1:])
        sent = lax.dynamic_index_in_dim(split, 1 - bit, 1, False)
        kept = lax.dynamic_index_in_dim(split, bit, 1, False)
        got = lax.ppermute(narrow(sent), "head", swap("head", distance))
        held = wide(kept) + wide(got)
        distance *= 2
    return held[0]


def head_gather(share):
    count, mine = lax.axis_size("head"), lax.axis_index("head")
    held = share[None]
    distance = count // 2
    while distance:
        bit = (mine // distance) % 2
        got = lax.ppermute(held, "head", swap("head", distance))
        lower = jnp.where(bit == 0, held, got)
        upper = jnp.where(bit == 0, got, held)
        held = jnp.stack([lower, upper], axis=1).reshape((-1,) + share.shape)
        distance //= 2
    return held.reshape((-1,) + share.shape[1:])


def with_decay(state, decay):
    high = narrow(decay)
    low = narrow(decay - wide(high))
    return jnp.concatenate([narrow(state), high, low], axis=1)


def split_decay(message):
    rows = message.shape[1] - 2
    decay = wide(message[:, rows : rows + 1]) + wide(message[:, rows + 1 :])
    return wide(message[:, :rows]), decay


def entering(state, decay, later):
    count, mine = lax.axis_size("seq"), lax.axis_index("seq")
    inner = mine % 2
    ahead = (inner == 0) != later
    half = state.shape[1] // 2
    kept = wide(lax.dynamic_slice_in_dim(state, inner * half, half, 1))
    sent = lax.dynamic_slice_in_dim(state, (1 - inner) * half, half, 1)
    pair = swap("seq", 1)
    other, other_decay = split_decay(lax.ppermute(with_decay(sent, decay), "seq", pair))
    earliest = jnp.where(ahead, kept, other)
    joined = jnp.where(ahead, other_decay, decay) * earliest + jnp.where(ahead, other, kept)
    message = with_decay(joined, decay * other_decay)
    if later:
        chain = [(i, i - 2) for i in range(2, count)]
    else:
        chain = [(i, i + 2) for i in range(count - 2)]
    before, reach = jnp.zeros_like(kept), jnp.ones_like(decay)
    for _ in range(count // 2 - 1):
        message = lax.ppermute(message, "seq", chain)
        far, far_decay = split_decay(message)
        before = before + reach * far
        reach = reach * far_decay
    second = jnp.where(ahead, decay, other_decay) * before + earliest
    got = lax.ppermute(narrow(jnp.where(ahead, second, before)), "seq", pair)
    own = narrow(jnp.where(ahead, before, second))
    return jnp.concatenate(
        [jnp.where(inner == 0, own, got), jnp.where(inner == 0, got, own)], axis=1
    )


def columns_of(vector, rows):
    width = -(-vector.shape[-1] // rows)
    pad = [(0, 0)] * (vector.ndim - 1) + [(0, width * rows - vector.shape[-1])]
    shaped = jnp.pad(vector, pad).reshape(vector.shape[:-1] + (width, rows))
    return jnp.swapaxes(shaped, -1, -2)


def plain_layer(
    layer_in,
    seg_starts,
    attn_gain,
    query_weight,
    key_weight,
    value_weight,
    gate_weight,
    decay_down,
    decay_up,
    decay_bias,
    head_gain,
    out_weight,
    ffn_gain,
    ffn_gate,
    ffn_up,
    ffn_down,
    out_grad,
):
    ring = Ring("seq")
    count = ring.count
    batch, block, width = layer_in.shape
    rows = batch * block
    chunks = block // CHUNK
    rank, share = decay_down.shape[1], attn_gain.shape[0]
    hidden = ffn_gate.shape[1]

    smalls = [attn_gain, ffn_gain, head_gain, decay_bias, decay_up.reshape(-1)]
    ends = [sum(part.size for part in smalls[: i + 1]) for i in range(len(smalls))]
    small = jnp.pad(jnp.concatenate(smalls), (0, -ends[-1] % 128))[None]
    shard = jnp.concatenate(
        [value_weight, key_weight, query_weight, gate_weight, out_weight.T, decay_down], axis=1
    )
    inputs = layer_in.reshape(rows, width)
    weights, mark = ring.gather(shard)
    small = lax.all_gather(small, "seq")
    gain = wide(small[:, 0, :share]).reshape(width)
    normed = ring.near(narrow(wide(inputs) * root_scale(wide(inputs)) * gain), 1)
    projected = matmul(normed, weights)
    value_key, query = narrow(projected[:, : DV + DK]), narrow(projected[:, DV + DK : DV + 2 * DK])
    gates, low = projected[:, DV + 2 * DK : 2 * DV + 2 * DK], projected[:, -rank:]
    third, mark = ring.gather(jnp.concatenate([ffn_gate, ffn_up], axis=1), mark)
    fdown_t, mark = ring.gather(ffn_down.T, mark)
    projections = weights[:, : 2 * DV + 2 * DK]
    out_t, down_all = weights[:, 2 * DV + 2 * DK : -rank], weights[:, -rank:]
    small = small[:, 0]
    gain_one = wide(ring.near(small[:, : ends[0]], 0)).reshape(width)
    gain_two = wide(ring.near(small[:, ends[0] : ends[1]], 0)).reshape(width)
    gain_head = wide(small[:, ends[1] : ends[2]]).reshape(1, DV)
    bias_all = wide(small[:, ends[2] : ends[3]]).reshape(1, DK)
    up_all = small[:, ends[3] : ends[4]].reshape(count, rank, -1)
    up_all = wide(jnp.swapaxes(up_all, 0, 1).reshape(rank, DK))

    starts = seg_starts.reshape(batch, chunks, CHUNK).astype(jnp.float32)
    places = jnp.arange(CHUNK)
    lower = (places[:, None] >= places[None, :]).astype(jnp.float32)
    marks = jnp.einsum("bcs,ts->bct", starts, lower, precision=HIGH)
    column, row = marks.reshape(batch, block, 1), jnp.swapaxes(marks, 0, 1)[:, :, None, :]

    grad_rows = ring.near(out_grad.reshape(rows, width), 1)
    head = lax.axis_index("head")
    quarter = rows // lax.axis_size("head")
    inputs_own = lax.dynamic_slice_in_dim(inputs, head * quarter, quarter, 0)
    inputs_own = wide(ring.near(inputs_own, 1))
    grad_own = wide(lax.dynamic_slice_in_dim(grad_rows, head * quarter, quarter, 0))

    def tokens(field):
        return field.reshape(batch, block, field.shape[-1])

    value_key, query, gates, low = map(tokens, (value_key, query, gates, low))
    run, slope, state, total = local_states(value_key, low, up_all, bias_all, column)
    state_in = entering(state, total, False)
    heads, mixed, states = mix(query, value_key, run, column, row, state_in, gates, gain_head)
    heads = heads.reshape(rows, DV)
    resid = inputs_own + head_scatter(narrow(matmul_nt(heads, out_t)))
    scale_two = root_scale(resid)
    unit_two = resid * scale_two
    normed_two = head_gather(narrow(unit_two * gain_two))
    pre_gate = matmul(normed_two, third[:, :hidden])
    pre_up = matmul(normed_two, third[:, hidden:])
    sigma = jax.nn.sigmoid(pre_gate)
    act = narrow(pre_gate * sigma * pre_up)
    layer_out = narrow(resid + head_scatter(narrow(matmul_nt(act, fdown_t))))
    layer_out = ring.home(head_gather(layer_out), 1)

    d_act = matmul(grad_rows, fdown_t)
    grad_fdown = ring.scatter(narrow(matmul_tn(grad_rows, act)))
    d_gate = narrow(d_act * pre_up * sigma * (1.0 + pre_gate * (1.0 - sigma)))
    d_up = narrow(d_act * pre_gate * sigma)
    d_third = jnp.concatenate([d_gate, d_up], axis=1)
    grad_third = ring.scatter(narrow(matmul_tn(normed_two, d_third)))
    d_normed_two = head_scatter(narrow(matmul_nt(d_third, third)))
    grad_gain_two = jnp.sum(d_normed_two * unit_two, axis=0)
    d_resid = grad_own + norm_back(d_normed_two * gain_two, unit_two, scale_two)
    d_attn = head_gather(narrow(d_resid))
    d_heads = tokens(matmul(d_attn, out_t))
    d_gates, d_mixed, grad_gain_head, state_grad = head_back(
        d_heads, gates, mixed, gain_head, query, run, column
    )
    state_back = entering(state_grad, total, True)
    d_query, d_value, d_key, d_low, grad_up, grad_bias = mix_back(
        query, value_key, run, slope, column, row, d_mixed, states, state_back, low, up_all
    )
    d_gates = d_gates.reshape(rows, DV)
    grad_out = matmul_tn(d_attn, heads)
    grad_gate = matmul_tn(normed, d_gates)
    grad_fourth = ring.scatter(narrow(jnp.concatenate([grad_gate, grad_out], axis=1)))
    d_low = narrow(d_low.reshape(rows, rank))
    d_last = jnp.concatenate(
        [d_value.reshape(rows, DV), d_key.reshape(rows, DK), d_query.reshape(rows, DK)], axis=1
    )
    d_normed_part = (
        matmul_nt(jnp.concatenate([d_last, d_gates], axis=1), projections)
        + matmul_nt(d_low, down_all)
    )
    d_normed = head_scatter(narrow(d_normed_part))
    scale_own = root_scale(inputs_own)
    unit_own = inputs_own * scale_own
    d_unit = norm_back(d_normed * gain_one, unit_own, scale_own)
    input_grad = ring.home(head_gather(narrow(d_resid + d_unit)), 1)
    unit_all = ring.near(wide(inputs) * root_scale(wide(inputs)), 1)
    grad_gain_one = jnp.sum(d_normed_part * unit_all, axis=0)

    small = jnp.concatenate(
        [
            grad_gain_head.reshape(count, -1),
            grad_bias.reshape(count, -1),
            jnp.swapaxes(grad_up.reshape(rank, count, -1), 0, 1).reshape(count, -1),
        ],
        axis=1,
    )
    small = columns_of(ring.near(small, 0), share).reshape(width, -1)
    small = jnp.concatenate([grad_gain_one[:, None], grad_gain_two[:, None], small], axis=1)
    used = d_last.shape[1] + rank
    spare = -(used + small.shape[1]) % 128
    d_last = jnp.concatenate(
        [d_last, d_low, jnp.zeros((rows, small.shape[1] + spare), BF16)], axis=1
    )
    grad_last = matmul_tn(normed, d_last) + jnp.pad(small, ((0, 0), (used, spare)))
    grad_last = ring.scatter(narrow(grad_last))
    shared = grad_last[:, used - rank :]
    distance = 1
    while distance < lax.axis_size("head"):
        shared = shared + lax.ppermute(shared, "head", swap("head", distance))
        distance *= 2

    def lone(field):
        return jnp.swapaxes(field[:, rank + 2 : rank + small.shape[1]], 0, 1).reshape(-1)

    own = lone(grad_last[:, used - rank :])
    bounds = [0, head_gain.size, head_gain.size + decay_bias.size]
    bounds.append(bounds[2] + decay_up.size)
    return (
        layer_out.reshape(batch, block, width),
        input_grad.reshape(batch, block, width),
        shared[:, rank],
        grad_last[:, DV + DK : DV + 2 * DK],
        grad_last[:, DV : DV + DK],
        grad_last[:, :DV],
        grad_fourth[:, :DV],
        shared[:, :rank],
        own[bounds[2] : bounds[3]].reshape(rank, -1),
        own[bounds[1] : bounds[2]],
        lone(shared)[: bounds[1]],
        grad_fourth[:, DV:].T,
        shared[:, rank + 1],
        grad_third[:, :hidden],
        grad_third[:, hidden:],
        grad_fdown.T,
    )


def fused_layer(
    layer_in,
    seg_starts,
    attn_gain,
    query_weight,
    key_weight,
    value_weight,
    gate_weight,
    decay_down,
    decay_up,
    decay_bias,
    head_gain,
    out_weight,
    ffn_gain,
    ffn_gate,
    ffn_up,
    ffn_down,
    out_grad,
):
    count = lax.axis_size("seq")
    batch, block, width = layer_in.shape
    rows = batch * block
    rank, share = decay_down.shape[1], attn_gain.shape[0]
    hidden = ffn_gate.shape[1]
    used = 2 * DV + 2 * DK
    inputs, grad_rows = layer_in.reshape(rows, width), out_grad.reshape(rows, width)
    starts = seg_starts.reshape(-1, CHUNK)
    small = jnp.concatenate([attn_gain, ffn_gain, head_gain, decay_bias])
    small = jnp.pad(small, (0, -small.size % 128))[None]
    down = jnp.pad(decay_down, ((0, 0), (0, -rank % 128)))
    shard = jnp.concatenate([value_weight, key_weight, query_weight, gate_weight, down], axis=1)

    def tokens(field):
        return field.reshape(batch, block, field.shape[-1])

    normed, weights, out_t, value_key, query, gates, low, gains, gain_head, bias, up = enter(
        inputs, shard, out_weight.T, small, decay_up
    )
    value_key, query, gates, low = map(tokens, (value_key, query, gates, low))
    weights, out_t = weights.reshape(width, -1), out_t.reshape(width, DV)
    run, slope, total, mixed, heads, states, part, fgate = token_phase(
        value_key, query, gates, low, up, bias, starts, gain_head, out_t, ffn_gate
    )
    resid, normed_two, fup = row_phase(part, inputs, gains, ffn_up)
    fgate, fup = fgate.reshape(width, hidden), fup.reshape(width, hidden)
    act, d_gate, d_up, fdown_t = unit_phase(normed_two, fgate, fup, grad_rows, ffn_down.T)
    fdown_t = fdown_t.reshape(width, hidden)
    ffn_part = narrow(matmul_nt(act, fdown_t))
    part = narrow(matmul_nt(d_gate, fgate) + matmul_nt(d_up, fup))
    d_resid, d_attn, d_heads, grad_gain_two, grad_first = resid_phase(
        part, resid, grad_rows, gains, out_t, act, normed_two, d_up
    )
    packed, grad_up, grad_bias, grad_gain_head, layer_out, grad_fgate = back_phase(
        ffn_part, resid, tokens(d_heads), gates, mixed, gain_head, query, value_key, run, slope,
        states, low, up, starts, total, normed_two, d_gate, shard.shape[1],
    )
    packed = packed.reshape(rows, -1)
    part = narrow(matmul_nt(packed, weights))
    input_grad, grad_last, small, tail = last_phase(
        part, inputs, d_resid, gains, normed, packed, d_attn, heads.reshape(rows, DV),
        grad_gain_two, grad_gain_head, grad_bias, grad_up,
    )
    lines = share // 128
    return (
        layer_out.reshape(batch, block, width),
        input_grad.reshape(batch, block, width),
        small[2 : 2 + lines].reshape(share),
        grad_last[:, DV + DK : DV + 2 * DK],
        grad_last[:, DV : DV + DK],
        grad_last[:, :DV],
        grad_last[:, DV + 2 * DK : used],
        tail[:, :rank],
        small[8:, : decay_up.shape[1]],
        small[1, : decay_bias.size],
        small[0, : head_gain.size],
        grad_last[:, shard.shape[1] :].T,
        small[4 : 4 + lines].reshape(share),
        grad_fgate,
        grad_first[:, hidden:],
        grad_first[:, :hidden].T,
    )


def shards(layer_in, seg_starts, attn_gain, *rest):
    fits = attn_gain.shape[0] == 256 and lax.axis_size("head") == 4
    layer = fused_layer if fits and rest[4].shape[1] == 16 else plain_layer
    return layer(layer_in, seg_starts, attn_gain, *rest)


def solution(mesh):
    return jax.shard_map(
        shards,
        mesh=mesh,
        in_specs=(
            P(None, "seq", None),
            P(None, "seq"),
            P("seq"),
            P("seq", "head"),
            P("seq", "head"),
            P("seq", "head"),
            P("seq", "head"),
            P("seq", None),
            P(None, ("head", "seq")),
            P(("head", "seq")),
            P("seq"),
            P("head", "seq"),
            P("seq"),
            P("seq", "head"),
            P("seq", "head"),
            P("head", "seq"),
            P(None, "seq", None),
        ),
        out_specs=(
            P(None, "seq", None),
            P(None, "seq", None),
            P("seq"),
            P("seq", "head"),
            P("seq", "head"),
            P("seq", "head"),
            P("seq", "head"),
            P("seq", None),
            P(None, ("head", "seq")),
            P(("head", "seq")),
            P("seq"),
            P("head", "seq"),
            P("seq"),
            P("seq", "head"),
            P("seq", "head"),
            P("head", "seq"),
        ),
        check_vma=False,
    )
```

```python
import functools

import jax
import jax.numpy as jnp
from jax import lax
from jax.experimental import pallas as pl
from jax.experimental.pallas import tpu as pltpu
from jax.sharding import PartitionSpec as P

DK = 256
DV = 512
CHUNK = 128
EPS = 1e-06
HIGH = lax.Precision.HIGHEST
NN = (((1,), (0,)), ((), ()))
NT = (((1,), (1,)), ((), ()))
TN = (((0,), (0,)), ((), ()))
VMEM_BYTES = 60 * 1024 * 1024
MESH = pl.DeviceIdType.MESH


def product(left, right, dims, precision=None):
    return lax.dot_general(
        left, right, dims, precision=precision, preferred_element_type=jnp.float32
    )


def narrow(field):
    return field.astype(jnp.bfloat16)


def wide(field):
    return field.astype(jnp.float32)


def root_scale(field):
    return lax.rsqrt(jnp.mean(field * field, axis=-1, keepdims=True) + EPS)


def norm_back(upstream, unit, scale):
    return scale * (upstream - unit * jnp.mean(upstream * unit, axis=-1, keepdims=True))


def triangle(lower):
    rows = lax.broadcasted_iota(jnp.int32, (CHUNK, CHUNK), 0)
    columns = lax.broadcasted_iota(jnp.int32, (CHUNK, CHUNK), 1)
    return (rows >= columns if lower else rows <= columns).astype(jnp.float32)


def permitted(mark_column, mark_row):
    rows = lax.broadcasted_iota(jnp.int32, (CHUNK, CHUNK), 0)
    columns = lax.broadcasted_iota(jnp.int32, (CHUNK, CHUNK), 1)
    return (rows >= columns) & (mark_column == mark_row)


def state_chunk(
    value_ref, key_ref, low_ref, up_ref, bias_ref, mark_ref, run_ref, slope_ref, state, total
):
    lower = triangle(True)
    for b in range(value_ref.shape[0]):
        raw = product(low_ref[b], up_ref[...], NN, HIGH) + bias_ref[...]
        soft = jnp.log1p(jnp.exp(-jnp.abs(raw)))
        decay = (jnp.minimum(raw, 0.0) - soft) / 16.0
        slope_ref[b] = jnp.exp(jnp.minimum(-raw, 0.0) - soft) / 16.0
        run = product(lower, decay, NN, HIGH)
        run_ref[b] = run
        mark = mark_ref[b]
        last = run[CHUNK - 1 :]
        trailing = mark == mark[CHUNK - 1 :]
        kept = jnp.where(trailing, jnp.exp(last - run), 0.0)
        keep = jnp.where(mark[CHUNK - 1 :] == 0.0, jnp.exp(last), 0.0)
        tail = narrow(wide(key_ref[b]) * kept)
        state[b] = state[b] * keep + product(value_ref[b], tail, TN)
        total[b] = total[b] * keep


def state_kernel(
    value_ref, key_ref, low_ref, up_ref, bias_ref, mark_ref,
    run_ref, slope_ref, state_ref, total_ref, state, total,
):
    step = pl.program_id(0)

    @pl.when(step == 0)
    def _():
        state[...] = jnp.zeros_like(state)
        total[...] = jnp.ones_like(total)

    state_chunk(
        value_ref, key_ref, low_ref, up_ref, bias_ref, mark_ref, run_ref, slope_ref, state, total
    )

    @pl.when(step == pl.num_programs(0) - 1)
    def _():
        state_ref[...] = narrow(state[...])
        total_ref[...] = total[...]


def mixer_chunk(
    query_ref, value_ref, key_ref, run_ref, mark_ref, row_ref, gate_ref, gain_ref,
    heads_ref, mixed_ref, states_ref, state,
):
    for b in range(value_ref.shape[0]):
        run, mark = run_ref[b], mark_ref[b]
        middle, last = run[CHUNK // 2 - 1 : CHUNK // 2], run[CHUNK - 1 :]
        query = wide(query_ref[b]) * DK ** (-0.5)
        key = wide(key_ref[b])
        start = narrow(state[b])
        states_ref[0, b] = start
        scores = product(
            narrow(query * jnp.exp(run - middle)), narrow(key * jnp.exp(middle - run)), NT
        )
        scores = jnp.where(permitted(mark, row_ref[0, b]), scores, 0.0)
        opened = narrow(query * jnp.where(mark == 0.0, jnp.exp(run), 0.0))
        mixed = product(narrow(scores), value_ref[b], NN) + product(opened, start, NT)
        kept = jnp.where(mark == mark[CHUNK - 1 :], jnp.exp(last - run), 0.0)
        keep = jnp.where(mark[CHUNK - 1 :] == 0.0, jnp.exp(last), 0.0)
        state[b] = state[b] * keep + product(value_ref[b], narrow(key * kept), TN)
        states_ref[1, b] = narrow(state[b])
        mixed_ref[b] = mixed
        gate = gate_ref[b]
        active = gate * jax.nn.sigmoid(gate)
        heads_ref[b] = narrow(mixed * root_scale(mixed) * gain_ref[...] * active)


def mixer_kernel(
    query_ref, value_ref, key_ref, run_ref, mark_ref, row_ref, first_ref, gate_ref, gain_ref,
    heads_ref, mixed_ref, states_ref, state,
):
    @pl.when(pl.program_id(0) == 0)
    def _():
        state[...] = wide(first_ref[...])

    mixer_chunk(
        query_ref, value_ref, key_ref, run_ref, mark_ref, row_ref, gate_ref, gain_ref,
        heads_ref, mixed_ref, states_ref, state,
    )


def head_back_chunk(
    grad_ref, gate_ref, mixed_ref, gain_ref, query_ref, run_ref, mark_ref,
    gate_grad_ref, mixed_grad_ref, gain_grad_ref, state,
):
    gain = gain_ref[...]
    for b in range(grad_ref.shape[0]):
        mixed, gate, grad = mixed_ref[b], gate_ref[b], wide(grad_ref[b])
        scale = root_scale(mixed)
        unit = mixed * scale
        sigma = jax.nn.sigmoid(gate)
        active = gate * sigma
        gate_grad_ref[b] = narrow(grad * unit * gain * sigma * (1.0 + gate * (1.0 - sigma)))
        weighted = grad * active
        gain_grad_ref[...] += jnp.sum(weighted * unit, axis=0, keepdims=True)
        mixed_grad = narrow(norm_back(weighted * gain, unit, scale))
        mixed_grad_ref[b] = mixed_grad
        run, mark = run_ref[b], mark_ref[b]
        last = run[CHUNK - 1 :]
        query = wide(query_ref[b]) * DK ** (-0.5)
        opened = narrow(query * jnp.where(mark == 0.0, jnp.exp(run), 0.0))
        keep = jnp.where(mark[CHUNK - 1 :] == 0.0, jnp.exp(last), 0.0)
        state[b] = state[b] * keep + product(mixed_grad, opened, TN)


def head_back_kernel(
    grad_ref, gate_ref, mixed_ref, gain_ref, query_ref, run_ref, mark_ref,
    gate_grad_ref, mixed_grad_ref, gain_grad_ref, state_ref, state,
):
    step = pl.program_id(0)

    @pl.when(step == 0)
    def _():
        state[...] = jnp.zeros_like(state)
        gain_grad_ref[...] = jnp.zeros_like(gain_grad_ref)

    head_back_chunk(
        grad_ref, gate_ref, mixed_ref, gain_ref, query_ref, run_ref, mark_ref,
        gate_grad_ref, mixed_grad_ref, gain_grad_ref, state,
    )

    @pl.when(step == pl.num_programs(0) - 1)
    def _():
        state_ref[...] = narrow(state[...])


def mixer_back_chunk(
    query_ref, value_ref, key_ref, run_ref, slope_ref, mark_ref, row_ref, grad_ref,
    start_ref, end_ref, low_ref, up_ref,
    query_grad_ref, value_grad_ref, key_grad_ref, low_grad_ref, up_grad_ref, bias_grad_ref, state,
):
    upper = triangle(False)
    for b in range(value_ref.shape[0]):
        run, mark = run_ref[b], mark_ref[b]
        middle, last = run[CHUNK // 2 - 1 : CHUNK // 2], run[CHUNK - 1 :]
        query = wide(query_ref[b]) * DK ** (-0.5)
        key, value, grad = wide(key_ref[b]), value_ref[b], grad_ref[b]
        start, later = start_ref[0, b], narrow(state[b])
        rise, fall = jnp.exp(run - middle), jnp.exp(middle - run)
        opens = jnp.where(mark == 0.0, jnp.exp(run), 0.0)
        kept = jnp.where(mark == mark[CHUNK - 1 :], jnp.exp(last - run), 0.0)
        keep = jnp.where(mark[CHUNK - 1 :] == 0.0, jnp.exp(last), 0.0)
        allowed = permitted(mark, row_ref[0, b])
        risen, fallen = narrow(query * rise), narrow(key * fall)
        scores = narrow(jnp.where(allowed, product(risen, fallen, NT), 0.0))
        scores_grad = narrow(jnp.where(allowed, product(grad, value, NT), 0.0))
        query_grad = rise * product(scores_grad, fallen, NN) + opens * product(grad, start, NN)
        key_grad = fall * product(scores_grad, risen, TN) + kept * product(value, later, NN)
        value_grad = product(scores, grad, TN) + product(narrow(key * kept), later, NT)
        ends = jnp.sum(state[b] * wide(end_ref[0, b]), axis=0, keepdims=True)
        state[b] = state[b] * keep + product(grad, narrow(query * opens), TN)
        turn = query * query_grad - key * key_grad
        raw_grad = (product(upper, turn, NN, HIGH) + ends) * slope_ref[b]
        query_grad_ref[b] = narrow(query_grad * DK ** (-0.5))
        key_grad_ref[b] = narrow(key_grad)
        value_grad_ref[b] = narrow(value_grad)
        low_grad = narrow(product(raw_grad, up_ref[...], NT, HIGH))
        low_grad_ref[b, :, : low_grad.shape[1]] = low_grad
        up_grad_ref[...] += product(low_ref[b], raw_grad, TN, HIGH)
        bias_grad_ref[...] += jnp.sum(raw_grad, axis=0, keepdims=True)


def mixer_back_kernel(
    query_ref, value_ref, key_ref, run_ref, slope_ref, mark_ref, row_ref, grad_ref,
    start_ref, end_ref, last_ref, low_ref, up_ref,
    query_grad_ref, value_grad_ref, key_grad_ref, low_grad_ref, up_grad_ref, bias_grad_ref, state,
):
    @pl.when(pl.program_id(0) == 0)
    def _():
        state[...] = wide(last_ref[...])
        up_grad_ref[...] = jnp.zeros_like(up_grad_ref)
        bias_grad_ref[...] = jnp.zeros_like(bias_grad_ref)

    mixer_back_chunk(
        query_ref, value_ref, key_ref, run_ref, slope_ref, mark_ref, row_ref, grad_ref,
        start_ref, end_ref, low_ref, up_ref,
        query_grad_ref, value_grad_ref, key_grad_ref, low_grad_ref, up_grad_ref, bias_grad_ref,
        state,
    )


def along(batch, width, last=0, reverse=0):
    if reverse:
        return pl.BlockSpec((batch, CHUNK, width), lambda i: (0, reverse - 1 - i, last))
    return pl.BlockSpec((batch, CHUNK, width), lambda i: (0, i, last))


def still(*shape):
    return pl.BlockSpec(shape, lambda i: (0,) * len(shape))


def shape_of(dtype, *shape):
    return jax.ShapeDtypeStruct(shape, dtype)


def call(kernel, steps, in_specs, out_specs, out_shape, scratch, operands, flops):
    moved = sum(a.size * a.dtype.itemsize for a in operands)
    moved += sum(s.size * s.dtype.itemsize for s in out_shape)
    return pl.pallas_call(
        kernel,
        grid=(steps,),
        in_specs=in_specs,
        out_specs=out_specs,
        out_shape=out_shape,
        scratch_shapes=scratch,
        cost_estimate=pl.CostEstimate(flops=flops, bytes_accessed=moved, transcendentals=0),
        compiler_params=pltpu.CompilerParams(
            dimension_semantics=("arbitrary",), vmem_limit_bytes=VMEM_BYTES
        ),
    )(*operands)


F32, BF16 = jnp.float32, jnp.bfloat16


def local_states(value_key, low, up, bias, mark):
    batch, block, rank = low.shape
    steps = block // CHUNK
    return call(
        state_kernel,
        steps,
        [along(batch, DV), along(batch, DK, DV // DK), along(batch, rank), still(rank, DK),
         still(1, DK), along(batch, 1)],
        [along(batch, DK), along(batch, DK), still(batch, DV, DK), still(batch, 1, DK)],
        [shape_of(F32, batch, block, DK), shape_of(F32, batch, block, DK),
         shape_of(BF16, batch, DV, DK), shape_of(F32, batch, 1, DK)],
        [pltpu.VMEM((batch, DV, DK), F32), pltpu.VMEM((batch, 1, DK), F32)],
        (value_key, value_key, low, up, bias, mark),
        2 * batch * block * DK * (DV + 6 * CHUNK),
    )


def mix(query, value_key, run, mark, row, first, gates, gain):
    batch, block, _ = run.shape
    steps = block // CHUNK
    heads, mixed, states = call(
        mixer_kernel,
        steps,
        [along(batch, DK), along(batch, DV), along(batch, DK, DV // DK), along(batch, DK),
         along(batch, 1), pl.BlockSpec((1, batch, 1, CHUNK), lambda i: (i, 0, 0, 0)),
         still(batch, DV, DK), along(batch, DV), still(1, DV)],
        [along(batch, DV), along(batch, DV),
         pl.BlockSpec((2, batch, DV, DK), lambda i: (i, 0, 0, 0))],
        [shape_of(BF16, batch, block, DV), shape_of(F32, batch, block, DV),
         shape_of(BF16, 2 * steps, batch, DV, DK)],
        [pltpu.VMEM((batch, DV, DK), F32)],
        (query, value_key, value_key, run, mark, row, first, gates, gain),
        2 * batch * block * DK * (2 * DV + 3 * CHUNK),
    )
    return heads, mixed, states


def head_back(grad, gates, mixed, gain, query, run, mark):
    batch, block, _ = run.shape
    steps = block // CHUNK
    return call(
        head_back_kernel,
        steps,
        [along(batch, DV, 0, steps), along(batch, DV, 0, steps), along(batch, DV, 0, steps),
         still(1, DV), along(batch, DK, 0, steps), along(batch, DK, 0, steps),
         along(batch, 1, 0, steps)],
        [along(batch, DV, 0, steps), along(batch, DV, 0, steps), still(1, DV),
         still(batch, DV, DK)],
        [shape_of(BF16, batch, block, DV), shape_of(BF16, batch, block, DV),
         shape_of(F32, 1, DV), shape_of(BF16, batch, DV, DK)],
        [pltpu.VMEM((batch, DV, DK), F32)],
        (grad, gates, mixed, gain, query, run, mark),
        2 * batch * block * DK * DV,
    )


def mix_back(query, value_key, run, slope, mark, row, grad, states, later, low, up):
    batch, block, rank = low.shape
    steps = block // CHUNK
    return call(
        mixer_back_kernel,
        steps,
        [along(batch, DK, 0, steps), along(batch, DV, 0, steps),
         along(batch, DK, DV // DK, steps), along(batch, DK, 0, steps),
         along(batch, DK, 0, steps), along(batch, 1, 0, steps),
         pl.BlockSpec((1, batch, 1, CHUNK), lambda i: (steps - 1 - i, 0, 0, 0)),
         along(batch, DV, 0, steps),
         pl.BlockSpec((1, batch, DV, DK), lambda i: (2 * (steps - 1 - i), 0, 0, 0)),
         pl.BlockSpec((1, batch, DV, DK), lambda i: (2 * (steps - 1 - i) + 1, 0, 0, 0)),
         still(batch, DV, DK), along(batch, rank, 0, steps), still(rank, DK)],
        [along(batch, DK, 0, steps), along(batch, DV, 0, steps), along(batch, DK, 0, steps),
         along(batch, rank, 0, steps), still(rank, DK), still(1, DK)],
        [shape_of(BF16, batch, block, DK), shape_of(BF16, batch, block, DV),
         shape_of(BF16, batch, block, DK), shape_of(BF16, batch, block, rank),
         shape_of(F32, rank, DK), shape_of(F32, 1, DK)],
        [pltpu.VMEM((batch, DV, DK), F32)],
        (query, value_key, value_key, run, slope, mark, row, grad, states, states, later, low, up),
        2 * batch * block * DK * (5 * DV + 6 * CHUNK),
    )


def place_of(table, index):
    found = jnp.int32(table[0])
    for i, entry in enumerate(table[1:], 1):
        found = jnp.where(index == i, jnp.int32(entry), found)
    return found


def block_at(order, distance):
    count = len(order)
    place = place_of([order.index(i) for i in range(count)], lax.axis_index("seq"))
    return place_of(order, lax.rem(place + distance + count, count))


def greet(axis, count):
    barrier, mine = pltpu.get_barrier_semaphore(), lax.axis_index(axis)
    for d in range(1, count):
        pl.semaphore_signal(
            barrier, inc=1, device_id={axis: lax.rem(mine + d, count)}, device_id_type=MESH
        )
    pl.semaphore_wait(barrier, count - 1)


def enter_kernel(
    order, ready, input_ref, block_ref, out_block_ref, small_ref, rise_ref,
    normed_ref, weight_ref, out_ref, vk_ref, query_ref, gate_ref, low_ref,
    gains_ref, head_gain_ref, bias_ref, up_ref,
    smalls_ref, rises_ref, total, small_send, small_receive, rise_send, rise_receive, *scratch,
):
    count = len(order)
    share, half = block_ref.shape[0], block_ref.shape[0] // 2
    rows, tile = input_ref.shape[0], 256
    mine = lax.axis_index("seq")
    ring = BlockRing(order, block_ref, weight_ref, *scratch[:3])
    out_ring = BlockRing(order, out_block_ref, out_ref, *scratch[3:])
    greet("seq", count)

    def spread(source, target, send, receive):
        return [
            pltpu.make_async_remote_copy(
                src_ref=source,
                dst_ref=target.at[mine],
                send_sem=send.at[d - 1],
                recv_sem=receive.at[d - 1],
                device_id={"seq": lax.rem(mine + d, count)},
                device_id_type=MESH,
            )
            for d in range(1, count)
        ]

    smalls = spread(small_ref, smalls_ref, small_send, small_receive)
    smalls += spread(rise_ref, rises_ref, rise_send, rise_receive)
    for copy in smalls:
        copy.start()
    ring.start()
    out_ring.start()
    smalls_ref[mine] = small_ref[...]
    rises_ref[mine] = rise_ref[...]
    ready()

    scales = []
    for t in range(rows // tile):
        field = wide(input_ref[t * tile : (t + 1) * tile])
        scales.append(root_scale(field))

    def multiply(first, second, begin):
        sides = []
        for slot, side in (first, second):
            start = slot * share + side * half
            sides.append((slot, side, gains_ref[0:1, start : start + half]))
        for t in range(rows // tile):
            here = slice(t * tile, (t + 1) * tile)
            parts, blocks = [], []
            for slot, side, gain in sides:
                start = pl.multiple_of(block_at(order, slot) * share + side * half, half)
                field = wide(input_ref[here, pl.ds(start, half)])
                part = narrow(field * scales[t] * gain)
                column = slot * share + side * half
                normed_ref[here, column : column + half] = part
                parts.append(part)
                source = block_ref if slot == 0 else weight_ref.at[slot]
                blocks.append(source[side * half : (side + 1) * half])
            added = product(jnp.concatenate(parts, axis=1), jnp.concatenate(blocks, axis=0), NN)
            if begin:
                total[here] = added
            else:
                total[here] += added

    for copy in smalls:
        copy.wait_recv()
    head_share, bias_share = DV // count, DK // count
    for j in range(count):
        near = wide(smalls_ref[block_at(order, j)])
        gains_ref[0:1, j * share : (j + 1) * share] = near[:, :share]
        gains_ref[1:2, j * share : (j + 1) * share] = near[:, share : 2 * share]
        block = wide(smalls_ref[j])
        at = 2 * share
        head_gain_ref[:, j * head_share : (j + 1) * head_share] = block[:, at : at + head_share]
        at += head_share
        bias_ref[:, j * bias_share : (j + 1) * bias_share] = block[:, at : at + bias_share]
        up_ref[:, j * bias_share : (j + 1) * bias_share] = wide(rises_ref[j])
    multiply((0, 0), (0, 1), True)
    for step in range(1, count):
        ring.advance()
        out_ring.advance()
        multiply((count - step, 0), (step, 1), False)
    vk_cols, query_cols, gate_cols = vk_ref.shape[1], query_ref.shape[1], gate_ref.shape[1]
    vk_ref[...] = narrow(total[:, :vk_cols])
    query_ref[...] = narrow(total[:, vk_cols : vk_cols + query_cols])
    low_from = vk_cols + query_cols + gate_cols
    gate_ref[...] = total[:, vk_cols + query_cols : low_from]
    low_ref[...] = total[:, low_from : low_from + low_ref.shape[1]]
    for copy in smalls:
        copy.wait_send()
    ring.finish()
    out_ring.finish()


def enter(inputs, block, out_block, small, rise):
    count = lax.axis_size("seq")
    rows, width = inputs.shape
    rank, cols = rise.shape[0], block.shape[1]
    dma = [pltpu.SemaphoreType.DMA((count - 1,))] * 4
    return remote_call(
        functools.partial(enter_kernel, ring_order(count)),
        0,
        [LOAD, NEAR, NEAR, NEAR, NEAR],
        [NEAR] * 11,
        [
            shape_of(BF16, rows, width),
            shape_of(BF16, count, *block.shape),
            shape_of(BF16, count, *out_block.shape),
            shape_of(BF16, rows, DV + DK),
            shape_of(BF16, rows, DK),
            shape_of(F32, rows, DV),
            shape_of(F32, rows, rank),
            shape_of(F32, 2, width),
            shape_of(F32, 1, DV),
            shape_of(F32, 1, DK),
            shape_of(F32, rank, DK),
        ],
        [
            pltpu.VMEM((count, *small.shape), BF16),
            pltpu.VMEM((count, *rise.shape), BF16),
            pltpu.VMEM((rows, cols), F32),
        ]
        + dma
        + ring_semaphores(count)
        + ring_semaphores(count),
        (inputs, block, out_block, small, rise),
        2 * rows * width * cols,
    )


PARTS = 2


class BlockRing:
    def __init__(self, order, block_ref, whole_ref, send, receive, local):
        self.count = count = len(order)
        half = block_ref.shape[0] // 2
        size = half // PARTS
        aims = (block_at(order, 1), block_at(order, -1))
        self.local = pltpu.make_async_copy(block_ref, whole_ref.at[0], local)
        self.hops = {}
        for step in range(1, count):
            for side in range(2):
                held = (count - step + 1) if side == 0 else step - 1
                lands = (count - step) if side == 0 else step
                for n in range(PARTS):
                    part = pl.ds(side * half + n * size, size)
                    self.hops[step, n, side] = pltpu.make_async_remote_copy(
                        src_ref=(block_ref if step == 1 else whole_ref.at[held]).at[part],
                        dst_ref=whole_ref.at[lands, part],
                        send_sem=send.at[step - 1, side, n],
                        recv_sem=receive.at[step - 1, side, n],
                        device_id={"seq": aims[side]},
                        device_id_type=MESH,
                    )
        self.step = 1

    def start(self):
        for n in range(PARTS):
            for side in range(2):
                self.hops[1, n, side].start()
        self.local.start()

    def advance(self):
        if self.step < self.count:
            for n in range(PARTS):
                for side in range(2):
                    self.hops[self.step, n, side].wait_recv()
                    if self.step + 1 < self.count:
                        self.hops[self.step + 1, n, side].start()
            self.step += 1

    def finish(self):
        while self.step < self.count:
            self.advance()
        for copy in self.hops.values():
            copy.wait_send()
        self.local.wait()


def ring_semaphores(count):
    return [
        pltpu.SemaphoreType.DMA((count - 1, 2, PARTS)),
        pltpu.SemaphoreType.DMA((count - 1, 2, PARTS)),
        pltpu.SemaphoreType.DMA,
    ]


class Handover:
    def __init__(self, count, later, state, decay, scratch):
        (self.decays, self.sent, self.got, self.chain, decay_send, decay_receive, send, receive) = scratch
        self.count, self.later, self.state, self.decay = count, later, state, decay
        self.mine = mine = lax.axis_index("seq")
        self.inner = lax.rem(mine, 2)
        self.pairs = count // 2
        self.pair = mine // 2
        self.place = self.pairs - 1 - self.pair if later else self.pair
        beside = mine + 1 - 2 * self.inner
        self.beside = beside
        self.ahead = (self.inner == 0) != later
        self.half = state.shape[1] // 2
        onward = mine - 2 if later else mine + 2
        self.decay_copies = [
            pltpu.make_async_remote_copy(
                src_ref=decay,
                dst_ref=self.decays.at[mine],
                send_sem=decay_send.at[d - 1],
                recv_sem=decay_receive.at[d - 1],
                device_id={"seq": lax.rem(mine + d, count)},
                device_id_type=MESH,
            )
            for d in range(1, count)
        ]
        self.batch = state.shape[0]
        self.swaps = [
            [
                pltpu.make_async_remote_copy(
                    src_ref=self.sent.at[i, b],
                    dst_ref=self.got.at[i, b],
                    send_sem=send.at[i, b],
                    recv_sem=receive.at[i, b],
                    device_id={"seq": beside},
                    device_id_type=MESH,
                )
                for b in range(self.batch)
            ]
            for i in range(2)
        ]
        self.links = [
            [
                pltpu.make_async_remote_copy(
                    src_ref=self.chain.at[r, b],
                    dst_ref=self.chain.at[r + 1, b],
                    send_sem=send.at[2 + r, b],
                    recv_sem=receive.at[2 + r, b],
                    device_id={"seq": onward},
                    device_id_type=MESH,
                )
                for b in range(self.batch)
            ]
            for r in range(self.pairs - 1)
        ]

    def clear(self):
        self.chain[...] = jnp.zeros_like(self.chain)

    def rows(self, own):
        part = self.inner if own else 1 - self.inner
        return pl.ds(pl.multiple_of(part * self.half, self.half), self.half)

    def begin(self):
        self.decays[self.mine] = self.decay[...]
        for copy in self.decay_copies:
            copy.start()
        for b in range(self.batch):
            self.sent[0, b] = narrow(self.state[b, self.rows(False)])
            self.swaps[0][b].start()

    def firsts(self, b):
        kept, other = self.state[b, self.rows(True)], wide(self.got[0, b])
        decay, other_decay = self.decays[self.mine, b], self.decays[self.beside, b]
        return (
            jnp.where(self.ahead, kept, other),
            jnp.where(self.ahead, other, kept),
            jnp.where(self.ahead, decay, other_decay),
            jnp.where(self.ahead, other_decay, decay),
        )

    def sends(self, r):
        return (self.place >= r) & (self.place + 1 < self.pairs)

    def join(self):
        for copy in self.decay_copies:
            copy.wait_recv()
        for b in range(self.batch):
            self.swaps[0][b].wait_recv()
            first, second, _, decay = self.firsts(b)
            self.chain[0, b] = narrow(decay * first + second)

            @pl.when(self.sends(0))
            def _(b=b):
                self.links[0][b].start()

    def hop(self, r):
        for b in range(self.batch):

            @pl.when(self.place >= r)
            def _(b=b):
                self.links[r - 1][b].wait_recv()

            if r < self.pairs - 1:

                @pl.when(self.sends(r))
                def _(b=b):
                    self.links[r][b].start()

    def close(self):
        for b in range(self.batch):
            before = wide(self.chain[1, b])
            reach = None
            for r in range(2, self.pairs):
                far = self.pair + r - 1 if self.later else self.pair - r + 1
                far = jnp.minimum(jnp.maximum(far, 0), self.pairs - 1)
                both = self.decays[2 * far, b] * self.decays[2 * far + 1, b]
                reach = both if reach is None else reach * both
                before = before + reach * wide(self.chain[r, b])
            first, _, decay, _ = self.firsts(b)
            after = decay * before + first
            self.sent[1, b] = narrow(jnp.where(self.ahead, after, before))
            self.swaps[1][b].start()
            self.state[b, self.rows(True)] = jnp.where(self.ahead, before, after)

    def finish(self):
        for b in range(self.batch):
            self.swaps[1][b].wait_recv()
            self.state[b, self.rows(False)] = wide(self.got[1, b])
        for copy in self.decay_copies + self.swaps[0] + self.swaps[1]:
            copy.wait_send()
        for r in range(self.pairs - 1):

            @pl.when(self.sends(r))
            def _(r=r):
                for b in range(self.batch):
                    self.links[r][b].wait_send()


def handover_scratch(count, batch):
    half = (batch, DV // 2, DK)
    return [
        pltpu.VMEM((count, batch, 1, DK), F32),
        pltpu.VMEM((2, *half), BF16),
        pltpu.VMEM((2, *half), BF16),
        pltpu.VMEM((count // 2, *half), BF16),
        pltpu.SemaphoreType.DMA((count - 1,)),
        pltpu.SemaphoreType.DMA((count - 1,)),
        pltpu.SemaphoreType.DMA((count // 2 + 1, batch)),
        pltpu.SemaphoreType.DMA((count // 2 + 1, batch)),
    ]


PIECES = 4


class Rows:
    def __init__(self, part, out, scratch):
        self.got, self.across, self.far, send, receive = scratch
        self.part, self.out = part, out
        head = lax.axis_index("head")
        core, chip = lax.rem(head, 2), head // 2
        self.share = part.shape[0] // 4
        self.size = self.share // PIECES
        beside, facing = 2 * chip + 1 - core, 2 * (1 - chip) + core
        self.own, self.facing = head, facing
        corner = 2 * (1 - chip) + 1 - core

        def copy(kind, p, source, target, aim):
            return pltpu.make_async_remote_copy(
                src_ref=source,
                dst_ref=target,
                send_sem=send.at[kind, p],
                recv_sem=receive.at[kind, p],
                device_id={"head": aim},
                device_id_type=MESH,
            )

        self.copies = {}
        for p in range(PIECES):
            here = self.piece(p)
            mine = out.at[self.rows(head, p)]
            met = out.at[self.rows(facing, p)]
            self.copies[0, p] = copy(0, p, part.at[self.rows(corner, p)], self.got.at[0, here], beside)
            self.copies[1, p] = copy(1, p, part.at[self.rows(beside, p)], self.got.at[1, here], beside)
            self.copies[2, p] = copy(2, p, self.across.at[here], self.far.at[here], facing)
            self.copies[3, p] = copy(3, p, mine, mine, facing)
            self.copies[4, p] = copy(4, p, mine, mine, beside)
            self.copies[5, p] = copy(5, p, met, met, beside)

    def piece(self, p):
        return pl.ds(p * self.size, self.size)

    def rows(self, owner, p):
        return pl.ds(pl.multiple_of(owner * self.share + p * self.size, self.size), self.size)

    def start(self, p):
        self.copies[0, p].start()
        self.copies[1, p].start()

    def cross(self, p):
        self.copies[0, p].wait_recv()
        here = self.piece(p)
        self.across[here] = narrow(wide(self.part[self.rows(self.facing, p)]) + wide(self.got[0, here]))
        self.copies[2, p].start()

    def turn(self, p, middle):
        self.copies[1, p].wait_recv()
        self.copies[2, p].wait_recv()
        here = self.piece(p)
        total = wide(self.part[self.rows(self.own, p)]) + wide(self.got[1, here])
        self.out[self.rows(self.own, p)] = middle(here, total + wide(self.far[here]))
        self.copies[3, p].start()
        self.copies[4, p].start()

    def relay(self, p):
        self.copies[3, p].wait_recv()
        self.copies[5, p].start()

    def finish(self):
        for p in range(PIECES):
            self.copies[4, p].wait_recv()
            self.copies[5, p].wait_recv()
        for copy in self.copies.values():
            copy.wait_send()


def rows_scratch(share, width):
    return [
        pltpu.VMEM((2, share, width), BF16),
        pltpu.VMEM((share, width), BF16),
        pltpu.VMEM((share, width), BF16),
        pltpu.SemaphoreType.DMA((6, PIECES)),
        pltpu.SemaphoreType.DMA((6, PIECES)),
    ]


def greet_all(count, heads):
    barrier = pltpu.get_barrier_semaphore()
    for axis, size in (("seq", count), ("head", heads)):
        mine = lax.axis_index(axis)
        for d in range(1, size):
            pl.semaphore_signal(
                barrier, inc=1, device_id={axis: lax.rem(mine + d, size)}, device_id_type=MESH
            )
    pl.semaphore_wait(barrier, count + heads - 2)


def chunk_at(i):
    return pl.ds(pl.multiple_of(i * CHUNK, CHUNK), CHUNK)


def token_phase_kernel(
    order, early, ready, vk_ref, query_ref, gate_ref, low_ref, up_ref, bias_ref, starts_ref, gain_ref,
    out_ref, block_ref, down_ref,
    run_ref, slope_ref, total_ref, mixed_ref, heads_ref, states_ref, part_ref, whole_ref, down_whole,
    state, ring_send, ring_receive, ring_local, down_send, down_receive, down_local,
    mark_ref, row_ref, *scratch,
):
    count = len(order)
    ring = BlockRing(order, block_ref, whole_ref, ring_send, ring_receive, ring_local)
    hand = Handover(count, False, state, total_ref, scratch)
    down_ring = BlockRing(
        order, down_ref.at[:, pl.ds(0, early)], down_whole, down_send, down_receive, down_local
    )
    hand.clear()
    greet("seq", count)
    ready(9)
    ring.start()
    fill_marks(starts_ref, mark_ref, row_ref)
    state[...] = jnp.zeros_like(state)
    total_ref[...] = jnp.ones_like(total_ref)
    chunks = run_ref.shape[1] // CHUNK
    ready(0, 3)

    @pl.loop(0, chunks)
    def _(i):
        at = chunk_at(i)
        state_chunk(
            vk_ref.at[:, at, pl.ds(0, DV)], vk_ref.at[:, at, pl.ds(DV, DK)], low_ref.at[:, at],
            up_ref, bias_ref, mark_ref.at[:, at], run_ref.at[:, at], slope_ref.at[:, at],
            state, total_ref,
        )

    hand.begin()
    ring.advance()
    hand.join()
    ring.advance()
    for r in range(1, count // 2):
        hand.hop(r)
        ring.advance()
    hand.close()
    ready()
    ring.advance()
    down_ring.start()
    hand.finish()
    ring.finish()
    down_ring.advance()

    def mixer(begin, end):
        @pl.loop(begin, end)
        def _(i):
            at = chunk_at(i)
            mixer_chunk(
                query_ref.at[:, at], vk_ref.at[:, at, pl.ds(0, DV)],
                vk_ref.at[:, at, pl.ds(DV, DK)], run_ref.at[:, at], mark_ref.at[:, at],
                row_ref.at[pl.ds(i, 1)], gate_ref.at[:, at], gain_ref, heads_ref.at[:, at],
                mixed_ref.at[:, at], states_ref.at[pl.ds(2 * i, 2)], state,
            )

    mixer(0, chunks // 2)
    down_ring.advance()
    mixer(chunks // 2, chunks)
    down_ring.advance()
    batch, block, _ = heads_ref.shape
    tile = 256
    for b in range(batch):
        for t in range(block // tile):
            field = heads_ref[b, t * tile : (t + 1) * tile]
            start = b * block + t * tile
            part_ref[start : start + tile] = narrow(product(field, out_ref[...], NT))
        down_ring.advance()
    down_ring.finish()


def remote_call(kernel, number, in_specs, out_specs, out_shape, scratch, operands, flops):
    moved = sum(a.size * a.dtype.itemsize for a in operands)
    moved += sum(s.size * s.dtype.itemsize for s in out_shape)
    loads = [i for i, spec in enumerate(in_specs) if spec is LOAD]
    scratch = list(scratch)
    scratch += [pltpu.VMEM(operands[i].shape, operands[i].dtype) for i in loads]
    scratch += [pltpu.SemaphoreType.DMA((max(len(loads), 1),))]

    def body(*refs):
        refs = list(refs)
        refs, buffers, arrivals = refs[: -1 - len(loads)], refs[-1 - len(loads) : -1], refs[-1]
        waits = {}
        for n, (i, buffer) in enumerate(zip(loads, buffers)):
            waits[i] = pltpu.make_async_copy(refs[i], buffer, arrivals.at[n])
            waits[i].start()
            refs[i] = buffer

        def ready(*positions):
            for i in positions or list(waits):
                waits.pop(i).wait()

        kernel(ready, *refs)

    return pl.pallas_call(
        body,
        in_specs=[AWAY if spec is LOAD else spec for spec in in_specs],
        out_specs=out_specs,
        out_shape=out_shape,
        scratch_shapes=scratch,
        cost_estimate=pl.CostEstimate(flops=flops, bytes_accessed=moved, transcendentals=0),
        compiler_params=pltpu.CompilerParams(
            collective_id=number, has_side_effects=True, vmem_limit_bytes=VMEM_BYTES
        ),
    )(*operands)


LOAD = None
NEAR = pl.BlockSpec(memory_space=pltpu.VMEM)
AWAY = pl.BlockSpec(memory_space=pl.ANY)


def token_phase(value_key, query, gates, low, up, bias, starts, gain, out_t, block, down, early):
    count = lax.axis_size("seq")
    batch, length, _ = low.shape
    chunks, width = length // CHUNK, out_t.shape[0]
    return remote_call(
        functools.partial(token_phase_kernel, ring_order(count), early),
        1,
        [LOAD, LOAD, LOAD, LOAD, NEAR, NEAR, NEAR, NEAR, LOAD, LOAD, LOAD],
        [NEAR] * 7 + [AWAY] * 2,
        [
            shape_of(F32, batch, length, DK),
            shape_of(F32, batch, length, DK),
            shape_of(F32, batch, 1, DK),
            shape_of(F32, batch, length, DV),
            shape_of(BF16, batch, length, DV),
            shape_of(BF16, 2 * chunks, batch, DV, DK),
            shape_of(BF16, batch * length, width),
            shape_of(BF16, count, *block.shape),
            shape_of(BF16, count, down.shape[0], early),
        ],
        [pltpu.VMEM((batch, DV, DK), F32)]
        + ring_semaphores(count)
        + ring_semaphores(count)
        + marks_scratch(batch, length)
        + handover_scratch(count, batch),
        (value_key, query, gates, low, up, bias, starts, gain, out_t, block, down),
        2 * batch * length * DV * (2 * DK + width),
    )


def row_phase_kernel(
    order, heads, ready, part_ref, input_ref, gain_ref, block_ref,
    resid_ref, normed_ref, whole_ref,
    own, own_sems, ring_send, ring_receive, ring_local, *scratch,
):
    ring = BlockRing(order, block_ref, whole_ref, ring_send, ring_receive, ring_local)
    rows = Rows(part_ref, normed_ref, scratch)
    first = pl.multiple_of(rows.own * rows.share, rows.share)
    copies = near_copies(order, input_ref, own, pl.ds(first, rows.share), own_sems)
    for copy in copies:
        copy.start()
    greet_all(len(order), heads)
    ready(3)
    ring.start()
    ready()
    for p in range(PIECES):
        rows.start(p)

    def middle(here, total):
        resid = wide(own[here]) + total
        resid_ref[here] = resid
        return narrow(resid * root_scale(resid) * gain_ref[1:2])

    for p in range(PIECES):
        rows.cross(p)
    for copy in copies:
        copy.wait()
    ring.advance()
    for p in range(PIECES):
        rows.turn(p, middle)
        if p % 2 == 0:
            ring.advance()
    ring.advance()
    for p in range(PIECES):
        rows.relay(p)
        if p % 2 == 0:
            ring.advance()
    rows.finish()
    ring.finish()


def row_phase(part, inputs, gains, block):
    count, heads = lax.axis_size("seq"), lax.axis_size("head")
    rows, width = part.shape
    return remote_call(
        functools.partial(row_phase_kernel, ring_order(count), heads),
        2,
        [LOAD, AWAY, NEAR, LOAD],
        [NEAR] * 2 + [AWAY],
        [
            shape_of(F32, rows // heads, width),
            shape_of(BF16, rows, width),
            shape_of(BF16, count, *block.shape),
        ],
        [pltpu.VMEM((rows // heads, width), BF16), pltpu.SemaphoreType.DMA((count,))]
        + ring_semaphores(count)
        + rows_scratch(rows // heads, width),
        (part, inputs, gains, block),
        16 * rows * width,
    )


def near_copies(order, source, target, rows, semaphores):
    share = source.shape[1] // len(order)
    return [
        pltpu.make_async_copy(
            source.at[rows, pl.ds(pl.multiple_of(block_at(order, r) * share, share), share)],
            target.at[:, pl.ds(r * share, share)],
            semaphores.at[r],
        )
        for r in range(len(order))
    ]


def home_copies(order, source, target, semaphores):
    share = source.shape[1] // len(order)
    return [
        pltpu.make_async_copy(
            source.at[:, pl.ds(r * share, share)],
            target.at[:, pl.ds(pl.multiple_of(block_at(order, r) * share, share), share)],
            semaphores.at[r],
        )
        for r in range(len(order))
    ]


def fill_marks(starts_ref, mark_ref, row_ref):
    batch, length, _ = mark_ref.shape
    chunks = length // CHUNK
    starts = starts_ref[...].astype(F32)
    across = product(starts, triangle(False), NN, HIGH)
    down = product(triangle(True), starts, NT, HIGH)
    for b in range(batch):
        for i in range(chunks):
            n = b * chunks + i
            mark_ref[b, i * CHUNK : (i + 1) * CHUNK] = down[:, n : n + 1]
            row_ref[i, b] = across[n : n + 1]


def marks_scratch(batch, length):
    return [
        pltpu.VMEM((batch, length, 1), F32),
        pltpu.VMEM((length // CHUNK, batch, 1, CHUNK), F32),
    ]


def split_columns(widths):
    pieces, begin = [], 0
    for item, columns in enumerate(widths):
        number = -(-columns // 1024)
        size = -(-columns // (128 * number)) * 128
        for start in range(0, columns, size):
            pieces.append((item, start, min(size, columns - start), begin + start))
        begin += columns
    return pieces


class SumRing:
    def __init__(self, order, items, out_ref, scratch):
        lefts = []
        for left, _, _ in items:
            if not any(left is other for other in lefts):
                lefts.append(left)
        buffers, rest = scratch[: len(lefts)], scratch[len(lefts) :]
        self.sent, self.got, load, send, receive = rest
        self.order, self.items, self.out = order, items, out_ref
        self.count = count = len(order)
        self.half = half = out_ref.shape[0] // 2
        self.buffers = {id(left): buffer for left, buffer in zip(lefts, buffers)}
        self.pieces = split_columns([right.shape[1] for _, right, _ in items])
        homes = {id(left): home for left, _, home in items}
        aims = (block_at(order, 1), block_at(order, -1))
        self.loads, self.hops = {}, {}
        for k in range(count):
            for side in range(2):
                slot = (count - 1 - k) if side == 0 else (k + 1) % count
                for n, (left, buffer) in enumerate(zip(lefts, buffers)):
                    block = block_at(order, slot) if homes[id(left)] else slot
                    column = pl.multiple_of(block * 2 * half + side * half, half)
                    self.loads[k, side, n] = pltpu.make_async_copy(
                        left.at[:, pl.ds(column, half)],
                        buffer.at[k % 2, side],
                        load.at[k % 2, side, n],
                    )
                if k == count - 1:
                    continue
                for n, (_, _, size, begin) in enumerate(self.pieces):
                    self.hops[k, side, n] = pltpu.make_async_remote_copy(
                        src_ref=self.sent.at[k % 2, side, :, pl.ds(begin, size)],
                        dst_ref=self.got.at[k, side, :, pl.ds(begin, size)],
                        send_sem=send.at[k, side, n],
                        recv_sem=receive.at[k, side, n],
                        device_id={"seq": aims[side]},
                        device_id_type=MESH,
                    )
        self.number = len(lefts)
        self.k = 0

    def load(self, k):
        if k < self.count:
            for side in range(2):
                for n in range(self.number):
                    self.loads[k, side, n].start()

    def prepare(self):
        self.load(0)
        self.load(1)

    def advance(self):
        k, last = self.k, self.count - 1
        if k > last:
            return
        for side in range(2):
            for n in range(self.number):
                self.loads[k, side, n].wait()
        for n, (item, start, size, begin) in enumerate(self.pieces):
            left, right, _ = self.items[item]
            columns = slice(begin, begin + size)
            for side in range(2):
                buffer = self.buffers[id(left)]
                value = product(buffer[k % 2, side], right[:, start : start + size], TN)
                if k > 0:
                    self.hops[k - 1, side, n].wait_recv()
                    value = value + wide(self.got[k - 1, side, :, columns])
                if k < last:
                    if k >= 2:
                        self.hops[k - 2, side, n].wait_send()
                    self.sent[k % 2, side, :, columns] = narrow(value)
                    self.hops[k, side, n].start()
                else:
                    self.out[side * self.half : (side + 1) * self.half, columns] = value
        self.load(k + 2)
        self.k += 1

    def finish(self):
        while self.k < self.count:
            self.advance()
        for k in (self.count - 3, self.count - 2):
            for n in range(len(self.pieces)):
                for side in range(2):
                    self.hops[k, side, n].wait_send()


def sum_scratch(count, rows, lefts, half, widths):
    columns, pieces = sum(widths), len(split_columns(widths))
    return [pltpu.VMEM((2, 2, rows, half), BF16)] * lefts + [
        pltpu.VMEM((2, 2, half, columns), BF16),
        pltpu.VMEM((count - 1, 2, half, columns), BF16),
        pltpu.SemaphoreType.DMA((2, 2, lefts)),
        pltpu.SemaphoreType.DMA((count - 1, 2, pieces)),
        pltpu.SemaphoreType.DMA((count - 1, 2, pieces)),
    ]


def unit_phase_kernel(
    order, ready, normed_ref, gate_ref, up_ref, grad_ref, block_ref, early_ref,
    act_ref, gate_grad_ref, up_grad_ref, whole_ref,
    pre_gate, pre_up, act_grad, tiles, tile_sems, early_sem, ring_send, ring_receive, ring_local,
):
    count = len(order)
    early = early_ref.shape[2]
    late = block_ref.shape[1] - early
    ring = BlockRing(
        order, block_ref.at[:, pl.ds(early, late)], whole_ref.at[:, :, pl.ds(early, late)],
        ring_send, ring_receive, ring_local,
    )
    placed = pltpu.make_async_copy(early_ref, whole_ref.at[:, :, pl.ds(0, early)], early_sem)
    greet("seq", count)
    ring.start()
    rows, width = normed_ref.shape
    tile = 256
    share = block_ref.shape[0]

    def written(kind, target, i):
        return pltpu.make_async_copy(
            tiles.at[kind], target.at[pl.ds(i * tile, tile)], tile_sems.at[kind]
        )

    ready(0, 1, 2)
    placed.start()
    steps = rows // tile
    for i in range(steps):
        here = pl.ds(i * tile, tile)
        field = normed_ref[here]
        gate = product(field, gate_ref[...], NN)
        pre_gate[here] = gate
        up = product(field, up_ref[...], NN)
        pre_up[here] = up
        if i > 0:
            written(0, act_ref, i - 1).wait()
        tiles[0] = narrow(gate * jax.nn.sigmoid(gate) * up)
        written(0, act_ref, i).start()
        ring.advance()
    ready()
    placed.wait()

    def against(here, columns):
        parts = [
            grad_ref[here, pl.ds(pl.multiple_of(block_at(order, r) * share, share), share)]
            for r in range(count)
        ]
        right = whole_ref[:, :, columns].reshape(width, -1)
        return product(jnp.concatenate(parts, axis=1), right, NN)

    for i in range(steps):
        act_grad[i * tile : (i + 1) * tile] = against(pl.ds(i * tile, tile), slice(0, early))
        if i % 2:
            ring.advance()
    written(0, act_ref, steps - 1).wait()
    ring.finish()
    for i in range(steps):
        here = pl.ds(i * tile, tile)
        ends = against(here, slice(early, early + late))
        for kind, target in ((0, gate_grad_ref), (1, up_grad_ref)):
            if i > 0:
                written(kind, target, i - 1).wait()
        for columns, grad in ((slice(0, early), act_grad[here]), (slice(early, early + late), ends)):
            gate, up = pre_gate[here, columns], pre_up[here, columns]
            sigma = jax.nn.sigmoid(gate)
            tiles[0, :, columns] = narrow(grad * up * sigma * (1.0 + gate * (1.0 - sigma)))
            tiles[1, :, columns] = narrow(grad * gate * sigma)
        for kind, target in ((0, gate_grad_ref), (1, up_grad_ref)):
            written(kind, target, i).start()
    for kind, target in ((0, gate_grad_ref), (1, up_grad_ref)):
        written(kind, target, steps - 1).wait()


def unit_phase(normed_two, fgate, fup, grad_rows, block, early):
    count = lax.axis_size("seq")
    rows, width = normed_two.shape
    hidden = block.shape[1]
    flat = shape_of(BF16, rows, hidden)
    return remote_call(
        functools.partial(unit_phase_kernel, ring_order(count)),
        3,
        [LOAD] * 4 + [AWAY, AWAY],
        [AWAY] * 3 + [NEAR],
        [flat, flat, flat, shape_of(BF16, count, *block.shape)],
        [
            pltpu.VMEM((rows, hidden), F32),
            pltpu.VMEM((rows, hidden), F32),
            pltpu.VMEM((rows, early.shape[2]), F32),
            pltpu.VMEM((2, 256, hidden), BF16),
            pltpu.SemaphoreType.DMA((2,)),
            pltpu.SemaphoreType.DMA,
        ]
        + ring_semaphores(count),
        (normed_two, fgate, fup, grad_rows, block, early),
        6 * rows * width * hidden,
    )


def resid_phase_kernel(
    order, heads, ready, part_ref, resid_ref, grad_ref, gain_ref, out_ref, act_ref, normed_ref,
    up_grad_ref, gate_ref, mixed_ref, head_gain_ref, query_ref, run_ref, starts_ref, total_ref, ffn_ref,
    resid_grad_ref, attn_grad_ref, gates_grad_ref, mixed_grad_ref, state_ref, gain_grad_ref,
    head_gain_grad_ref, layer_ref, sums_ref,
    own, own_sems, wholes, whole_sems, ffn_sem, pair, pair_sems, heads_grad, state, mark_ref, row_ref,
    *scratch,
):
    count = len(order)
    rows = Rows(part_ref, wholes, scratch[:5])
    hand = Handover(count, True, state, total_ref, scratch[5:13])
    ring = SumRing(
        order, [(grad_ref, act_ref, True), (normed_ref, up_grad_ref, False)], sums_ref, scratch[13:]
    )
    first = pl.multiple_of(rows.own * rows.share, rows.share)
    copies = near_copies(order, grad_ref, own, pl.ds(first, rows.share), own_sems)
    ring.prepare()
    for copy in copies:
        copy.start()
    batch, length, _ = run_ref.shape
    chunks = length // CHUNK
    pairs = [
        [
            pltpu.make_async_copy(
                field.at[:, pl.ds((chunks - 1 - i) * CHUNK, CHUNK)],
                pair.at[i % 2, kind],
                pair_sems.at[i % 2, kind],
            )
            for kind, field in enumerate((gate_ref, mixed_ref))
        ]
        for i in range(chunks)
    ]
    hand.clear()
    greet_all(count, heads)
    ready(0)
    for p in range(PIECES):
        rows.start(p)
    ready(5, 7)
    ring.advance()
    for copy in pairs[0] + pairs[1]:
        copy.start()
    gain_grad_ref[...] = jnp.zeros_like(gain_grad_ref)
    head_gain_grad_ref[...] = jnp.zeros_like(head_gain_grad_ref)
    state[...] = jnp.zeros_like(state)
    fill_marks(starts_ref, mark_ref, row_ref)

    def middle(here, total):
        resid = resid_ref[here]
        scale = root_scale(resid)
        unit = resid * scale
        gain_grad_ref[...] += jnp.sum(total * unit, axis=0, keepdims=True)
        grad = wide(own[here]) + norm_back(total * gain_ref[1:2], unit, scale)
        resid_grad_ref[here] = grad
        return narrow(grad)

    def layer(here, total):
        return narrow(resid_ref[here] + total)

    for p in range(PIECES):
        rows.cross(p)
    for copy in copies:
        copy.wait()
    ready()
    rows.turn(0, middle)
    ring.advance()
    for p in range(1, PIECES):
        rows.turn(p, middle)
    ring.advance()
    for p in range(PIECES):
        rows.relay(p)
        if p == 2:
            ring.advance()
    rows.finish()
    kept = pltpu.make_async_copy(wholes, attn_grad_ref, whole_sems.at[0])
    kept.start()
    following = pltpu.make_async_copy(ffn_ref, part_ref, ffn_sem)
    following.start()

    for i in range(chunks):
        at = pl.ds((chunks - 1 - i) * CHUNK, CHUNK)
        for copy in pairs[i]:
            copy.wait()
        for b in range(batch):
            here = pl.ds(b * length + (chunks - 1 - i) * CHUNK, CHUNK)
            heads_grad[b] = product(wholes[here], out_ref[...], NN)
        head_back_chunk(
            heads_grad, pair.at[i % 2, 0], pair.at[i % 2, 1], head_gain_ref,
            query_ref.at[:, at], run_ref.at[:, at], mark_ref.at[:, at],
            gates_grad_ref.at[:, at], mixed_grad_ref.at[:, at], head_gain_grad_ref, state,
        )
        if i + 2 < chunks:
            for copy in pairs[i + 2]:
                copy.start()

    hand.begin()
    kept.wait()
    following.wait()
    for p in range(PIECES):
        rows.start(p)
    ring.advance()
    hand.join()
    for p in range(PIECES):
        rows.cross(p)
    for r in range(1, count // 2):
        hand.hop(r)
        if r < PIECES:
            rows.turn(r - 1, layer)
        if r == 2:
            ring.advance()
    for r in range(count // 2 - 1, PIECES):
        rows.turn(r, layer)
    hand.close()
    ring.advance()
    hand.finish()
    state_ref[...] = narrow(state[...])
    for p in range(PIECES):
        rows.relay(p)
        if p == 2:
            ring.advance()
    rows.finish()
    backs = home_copies(order, wholes, layer_ref, whole_sems)
    for copy in backs:
        copy.start()
    ring.finish()
    for copy in backs:
        copy.wait()


def resid_phase(
    part, resid, grad_rows, gains, out_t, act, normed_two, d_up, gates, mixed, head_gain, query, run,
    starts, total, ffn_part,
):
    count, heads = lax.axis_size("seq"), lax.axis_size("head")
    rows, width = part.shape
    batch, length, _ = run.shape
    share, hidden = width // count, act.shape[1]
    quarter = rows // heads
    return remote_call(
        functools.partial(resid_phase_kernel, ring_order(count), heads),
        4,
        [LOAD, LOAD, AWAY, NEAR, LOAD, LOAD, AWAY, LOAD, AWAY, AWAY, NEAR, LOAD, LOAD, NEAR, NEAR, AWAY],
        [NEAR, AWAY, NEAR, NEAR, NEAR, NEAR, NEAR, AWAY, NEAR],
        [
            shape_of(F32, quarter, width),
            shape_of(BF16, rows, width),
            shape_of(BF16, batch, length, DV),
            shape_of(BF16, batch, length, DV),
            shape_of(BF16, batch, DV, DK),
            shape_of(F32, 1, width),
            shape_of(F32, 1, DV),
            shape_of(BF16, rows, width),
            shape_of(F32, share, 2 * hidden),
        ],
        [
            pltpu.VMEM((quarter, width), BF16),
            pltpu.SemaphoreType.DMA((count,)),
            pltpu.VMEM((rows, width), BF16),
            pltpu.SemaphoreType.DMA((count,)),
            pltpu.SemaphoreType.DMA,
            pltpu.VMEM((2, 2, batch, CHUNK, DV), F32),
            pltpu.SemaphoreType.DMA((2, 2)),
            pltpu.VMEM((batch, CHUNK, DV), F32),
            pltpu.VMEM((batch, DV, DK), F32),
        ]
        + marks_scratch(batch, length)
        + rows_scratch(quarter, width)
        + handover_scratch(count, batch)
        + sum_scratch(count, rows, 2, share // 2, [hidden, hidden]),
        (part, resid, grad_rows, gains, out_t, act, normed_two, d_up, gates, mixed, head_gain, query,
         run, starts, total, ffn_part),
        2 * rows * width * (2 * hidden + DV),
    )


def back_phase_kernel(
    order, ready, query_ref, vk_ref, run_ref, slope_ref, states_ref, low_ref, up_ref, starts_ref,
    mixed_grad_ref, later_ref, gates_grad_ref, normed_ref, act_grad_ref, weight_ref,
    packed_ref, up_grad_ref, bias_grad_ref, part_ref, sums_ref,
    state, mark_ref, row_ref, *scratch,
):
    count = len(order)
    ring = SumRing(order, [(normed_ref, act_grad_ref, False)], sums_ref, scratch)
    ring.prepare()
    greet("seq", count)
    ready(12)
    ring.advance()
    batch, length, _ = run_ref.shape
    chunks = length // CHUNK
    gates_from, low_from = DV + 2 * DK, 2 * DV + 2 * DK
    fill_marks(starts_ref, mark_ref, row_ref)
    for ref in (up_grad_ref, bias_grad_ref):
        ref[...] = jnp.zeros_like(ref)
    spare = packed_ref.shape[2] - low_from
    packed_ref[:, :, low_from:] = jnp.zeros((batch, length, spare), BF16)
    ready(0, 1, 2, 3, 4, 5, 8, 9, 10)
    state[...] = wide(later_ref[...])
    packed_ref[:, :, gates_from:low_from] = gates_grad_ref[...]

    def back(begin, end):
        @pl.loop(begin, end)
        def _(i):
            n = chunks - 1 - i
            at = chunk_at(n)
            mixer_back_chunk(
                query_ref.at[:, at], vk_ref.at[:, at, pl.ds(0, DV)],
                vk_ref.at[:, at, pl.ds(DV, DK)], run_ref.at[:, at], slope_ref.at[:, at],
                mark_ref.at[:, at], row_ref.at[pl.ds(n, 1)], mixed_grad_ref.at[:, at],
                states_ref.at[pl.ds(2 * n, 1)], states_ref.at[pl.ds(2 * n + 1, 1)],
                low_ref.at[:, at], up_ref,
                packed_ref.at[:, at, pl.ds(DV + DK, DK)], packed_ref.at[:, at, pl.ds(0, DV)],
                packed_ref.at[:, at, pl.ds(DV, DK)], packed_ref.at[:, at, pl.ds(low_from, 128)],
                up_grad_ref, bias_grad_ref, state,
            )

    back(0, chunks // 2)
    ring.advance()
    back(chunks // 2, chunks)
    ring.advance()
    ready()
    tile = 256
    for b in range(batch):
        for t in range(length // tile):
            field = packed_ref[b, t * tile : (t + 1) * tile]
            start = b * length + t * tile
            part_ref[start : start + tile] = narrow(product(field, weight_ref[...], NT))
        ring.advance()
    ring.finish()


def back_phase(
    query, vk, run, slope, states, low, up, starts, d_mixed, later, d_gates, normed_two, d_gate, weights
):
    count = lax.axis_size("seq")
    batch, length, rank = low.shape
    width, packed_cols = weights.shape
    share, hidden, rows = width // count, d_gate.shape[1], d_gate.shape[0]
    return remote_call(
        functools.partial(back_phase_kernel, ring_order(count)),
        5,
        [LOAD] * 6 + [NEAR, NEAR, LOAD, LOAD, LOAD, AWAY, LOAD, LOAD],
        [NEAR] * 5,
        [
            shape_of(BF16, batch, length, packed_cols),
            shape_of(F32, rank, DK),
            shape_of(F32, 1, DK),
            shape_of(BF16, rows, width),
            shape_of(F32, share, hidden),
        ],
        [pltpu.VMEM((batch, DV, DK), F32)]
        + marks_scratch(batch, length)
        + sum_scratch(count, rows, 1, share // 2, [hidden]),
        (query, vk, run, slope, states, low, up, starts, d_mixed, later, d_gates, normed_two, d_gate,
         weights),
        2 * rows * width * hidden,
    )


SMALL = 24


def last_phase_kernel(
    order, heads, ready, part_ref, input_ref, resid_grad_ref, gain_ref, normed_ref, packed_ref, attn_ref,
    heads_ref, ffn_gain_ref, head_gain_ref, bias_ref, up_ref,
    input_grad_ref, sums_ref, small_ref, tail_ref,
    own, own_sems, grads, grad_sems, gain_grad, stage, stage_got, shared, shared_got, tail_got,
    seq_send, seq_receive, head_send, head_receive, *scratch,
):
    count = len(order)
    rows = Rows(part_ref, grads, scratch[:5])
    ring = SumRing(
        order, [(normed_ref, packed_ref, False), (attn_ref, heads_ref, False)], sums_ref, scratch[5:]
    )
    first = pl.multiple_of(rows.own * rows.share, rows.share)
    copies = near_copies(order, input_ref, own, pl.ds(first, rows.share), own_sems)
    for copy in copies:
        copy.start()
    ring.prepare()
    greet_all(count, heads)
    ready(0)
    for p in range(PIECES):
        rows.start(p)
    ready(5, 7)
    ring.advance()
    ready()
    gain_grad[...] = jnp.zeros_like(gain_grad)

    def middle(here, total):
        field = wide(own[here])
        scale = root_scale(field)
        unit = field * scale
        gain_grad[...] += jnp.sum(total * unit, axis=0, keepdims=True)
        return narrow(resid_grad_ref[here] + norm_back(total * gain_ref[0:1], unit, scale))

    for p in range(PIECES):
        rows.cross(p)
    for copy in copies:
        copy.wait()
    ring.advance()
    for p in range(PIECES):
        rows.turn(p, middle)
        if p == 2:
            ring.advance()

    mine, head = lax.axis_index("seq"), lax.axis_index("head")
    share = sums_ref.shape[0]
    stage[...] = jnp.zeros_like(stage)
    pieces = [ref.shape[1] // count for ref in (head_gain_ref, bias_ref, up_ref)]
    for j in range(count):
        stage[j, 0:1, : pieces[0]] = head_gain_ref[:, j * pieces[0] : (j + 1) * pieces[0]]
        stage[j, 1:2, : pieces[1]] = bias_ref[:, j * pieces[1] : (j + 1) * pieces[1]]
        stage[j, 8:, : pieces[2]] = up_ref[:, j * pieces[2] : (j + 1) * pieces[2]]
        owner = block_at(order, j)
        for n, ref in ((2, gain_grad), (4, ffn_gain_ref)):
            for t in range(share // 128):
                start = j * share + t * 128
                stage[owner, n + t : n + t + 1, :] = ref[:, start : start + 128]
    stage_hops = []
    for d in range(1, count):
        aim = lax.rem(mine + d, count)
        stage_hops.append(
            pltpu.make_async_remote_copy(
                src_ref=stage.at[aim],
                dst_ref=stage_got.at[d - 1],
                send_sem=seq_send.at[d - 1],
                recv_sem=seq_receive.at[d - 1],
                device_id={"seq": aim},
                device_id_type=MESH,
            )
        )
    for hop in stage_hops:
        hop.start()

    def head_hops(kind, source, target):
        return [
            pltpu.make_async_remote_copy(
                src_ref=source,
                dst_ref=target.at[d - 1],
                send_sem=head_send.at[kind, d - 1],
                recv_sem=head_receive.at[kind, d - 1],
                device_id={"head": lax.rem(head + d, heads)},
                device_id_type=MESH,
            )
            for d in range(1, heads)
        ]

    rows.relay(0)
    rows.relay(1)
    ring.advance()
    rows.relay(2)
    rows.relay(3)
    for hop in stage_hops:
        hop.wait_recv()
    total = stage[mine]
    for d in range(count - 1):
        total = total + stage_got[d]
    small_ref[...] = total
    shared[...] = total[:8]
    shared_hops = head_hops(0, shared, shared_got)
    for hop in shared_hops:
        hop.start()
    ring.advance()
    rows.finish()
    backs = home_copies(order, grads, input_grad_ref, grad_sems)
    for copy in backs:
        copy.start()
    for hop in shared_hops:
        hop.wait_recv()
    small_ref[0:8] = shared[...] + (shared_got[0] + shared_got[1] + shared_got[2])
    small_ref[1:2] = shared[1:2]
    ring.finish()
    low_from = 2 * DV + 2 * DK
    tail_ref[...] = sums_ref[:, low_from : low_from + 128]
    tail_hops = head_hops(1, tail_ref, tail_got)
    for hop in tail_hops:
        hop.start()
    for hop in tail_hops:
        hop.wait_recv()
    for hop in stage_hops + shared_hops + tail_hops:
        hop.wait_send()
    tail_ref[...] = tail_ref[...] + (tail_got[0] + tail_got[1] + tail_got[2])
    for copy in backs:
        copy.wait()


def last_phase(
    part, inputs, d_resid, gains, normed, packed, d_attn, heads_out, ffn_gain, head_gain, bias, up
):
    count, heads = lax.axis_size("seq"), lax.axis_size("head")
    rows, width = part.shape
    share, quarter = width // count, rows // heads
    columns = packed.shape[1] + heads_out.shape[1]
    return remote_call(
        functools.partial(last_phase_kernel, ring_order(count), heads),
        6,
        [LOAD, AWAY, LOAD, NEAR, AWAY, LOAD, AWAY, LOAD, NEAR, NEAR, NEAR, NEAR],
        [AWAY, NEAR, NEAR, NEAR],
        [
            shape_of(BF16, rows, width),
            shape_of(F32, share, columns),
            shape_of(F32, SMALL, 128),
            shape_of(F32, share, 128),
        ],
        [
            pltpu.VMEM((quarter, width), BF16),
            pltpu.SemaphoreType.DMA((count,)),
            pltpu.VMEM((rows, width), BF16),
            pltpu.SemaphoreType.DMA((count,)),
            pltpu.VMEM((1, width), F32),
            pltpu.VMEM((count, SMALL, 128), F32),
            pltpu.VMEM((count - 1, SMALL, 128), F32),
            pltpu.VMEM((8, 128), F32),
            pltpu.VMEM((heads - 1, 8, 128), F32),
            pltpu.VMEM((heads - 1, share, 128), F32),
            pltpu.SemaphoreType.DMA((count - 1,)),
            pltpu.SemaphoreType.DMA((count - 1,)),
            pltpu.SemaphoreType.DMA((2, heads - 1)),
            pltpu.SemaphoreType.DMA((2, heads - 1)),
        ]
        + rows_scratch(quarter, width)
        + sum_scratch(count, rows, 2, share // 2, [packed.shape[1], DV]),
        (part, inputs, d_resid, gains, normed, packed, d_attn, heads_out, ffn_gain, head_gain, bias, up),
        2 * rows * width * columns,
    )


def leave_kernel(
    layer_ref, input_ref, first_ref, gate_ref, last_ref,
    layer_out, input_out, query_out, key_out, value_out, gates_out, attn_out, ffn_gate_out,
    ffn_up_out, ffn_down_out,
):
    hidden = gate_ref.shape[1]
    used = last_ref.shape[1] - DV
    layer_out[...] = layer_ref[...]
    input_out[...] = input_ref[...]
    ffn_gate_out[...] = gate_ref[...]
    ffn_up_out[...] = first_ref[:, hidden:]
    ffn_down_out[...] = first_ref[:, :hidden].T
    value_out[...] = last_ref[:, :DV]
    key_out[...] = last_ref[:, DV : DV + DK]
    query_out[...] = last_ref[:, DV + DK : DV + 2 * DK]
    gates_out[...] = last_ref[:, DV + 2 * DK : 2 * DV + 2 * DK]
    attn_out[...] = last_ref[:, used:].T


def leave(layer, input_grad, first, gate, last):
    share, hidden = gate.shape
    steps = share // 128

    def by_rows(field):
        return pl.BlockSpec((field.shape[0] // steps, field.shape[1]), lambda i: (i, 0))

    out_shape = [
        shape_of(BF16, *layer.shape),
        shape_of(BF16, *layer.shape),
        shape_of(F32, share, DK),
        shape_of(F32, share, DK),
        shape_of(F32, share, DV),
        shape_of(F32, share, DV),
        shape_of(F32, DV, share),
        shape_of(F32, share, hidden),
        shape_of(F32, share, hidden),
        shape_of(F32, hidden, share),
    ]
    specs = [by_rows(shape) for shape in out_shape]
    for n in (6, 9):
        specs[n] = pl.BlockSpec((out_shape[n].shape[0], 128), lambda i: (0, i))
    operands = (layer, input_grad, first, gate, last)
    return pl.pallas_call(
        leave_kernel,
        grid=(steps,),
        in_specs=[by_rows(field) for field in operands],
        out_specs=specs,
        out_shape=out_shape,
        compiler_params=pltpu.CompilerParams(
            dimension_semantics=("arbitrary",), vmem_limit_bytes=VMEM_BYTES
        ),
    )(*operands)


EARLY = 384


def matmul(left, right):
    return product(left, right, NN)


def matmul_nt(left, right):
    return product(left, right, NT)


def matmul_tn(left, right):
    return product(left, right, TN)


def ring_order(count):
    return list(range(0, count, 2)) + list(range(count - 1 - count % 2, 0, -2))


class Ring:
    def __init__(self, axis):
        self.axis = axis
        self.count = count = lax.axis_size(axis)
        order = ring_order(count)
        place = [order.index(i) for i in range(count)]
        self.right = [(order[i], order[(i + 1) % count]) for i in range(count)]
        self.left = [(order[i], order[(i - 1) % count]) for i in range(count)]
        owners = [[order[(place[i] + r) % count] for r in range(count)] for i in range(count)]
        slots = [[(place[i] - place[me]) % count for i in range(count)] for me in range(count)]
        mine = lax.axis_index(axis)
        self.owners = jnp.asarray(owners, jnp.int32)[mine]
        self.slots = jnp.asarray(slots, jnp.int32)[mine]

    def arrange(self, field, dim, table):
        width = field.shape[dim] // self.count
        return jnp.concatenate(
            [
                lax.dynamic_slice_in_dim(field, table[r] * width, width, dim)
                for r in range(self.count)
            ],
            axis=dim,
        )

    def near(self, field, dim):
        return self.arrange(field, dim, self.owners)

    def home(self, field, dim):
        return self.arrange(field, dim, self.slots)

    def gather(self, block, after=None):
        count, half = self.count, block.shape[0] // 2
        up, down = block[:half], block[half:]
        if after is not None:
            up, down, _ = lax.optimization_barrier((up, down, after))
        pieces = [None] * (2 * count)
        pieces[0], pieces[1] = up, down
        for step in range(1, count):
            up = lax.ppermute(up, self.axis, self.right)
            down = lax.ppermute(down, self.axis, self.left)
            pieces[2 * (count - step)] = up
            pieces[2 * step + 1] = down
            if step == count - 2:
                late = up[:8, :128]
        return jnp.concatenate(pieces, axis=0), late

    def scatter(self, total):
        count = self.count
        rows = total.shape[0] // count
        half = rows // 2

        def piece(slot, part):
            start = slot * rows + part * half
            return total[start : start + half]

        up, down = piece(count - 1, 0), piece(1, 1)
        for step in range(count - 1):
            up = lax.ppermute(up, self.axis, self.right)
            down = lax.ppermute(down, self.axis, self.left)
            up = wide(up) + wide(piece(count - 2 - step, 0))
            down = wide(down) + wide(piece((step + 2) % count, 1))
            if step < count - 2:
                up, down = narrow(up), narrow(down)
        return jnp.concatenate([up, down], axis=0)


def swap(axis, distance):
    return [(i, i ^ distance) for i in range(lax.axis_size(axis))]


def head_scatter(part):
    count, mine = lax.axis_size("head"), lax.axis_index("head")
    rows = part.shape[0] // count
    held = part.reshape((count, rows) + part.shape[1:])
    distance = 1
    while distance < count:
        bit = (mine // distance) % 2
        split = held.reshape((held.shape[0] // 2, 2) + held.shape[1:])
        sent = lax.dynamic_index_in_dim(split, 1 - bit, 1, False)
        kept = lax.dynamic_index_in_dim(split, bit, 1, False)
        got = lax.ppermute(narrow(sent), "head", swap("head", distance))
        held = wide(kept) + wide(got)
        distance *= 2
    return held[0]


def head_gather(share):
    count, mine = lax.axis_size("head"), lax.axis_index("head")
    held = share[None]
    distance = count // 2
    while distance:
        bit = (mine // distance) % 2
        got = lax.ppermute(held, "head", swap("head", distance))
        lower = jnp.where(bit == 0, held, got)
        upper = jnp.where(bit == 0, got, held)
        held = jnp.stack([lower, upper], axis=1).reshape((-1,) + share.shape)
        distance //= 2
    return held.reshape((-1,) + share.shape[1:])


def with_decay(state, decay):
    high = narrow(decay)
    low = narrow(decay - wide(high))
    return jnp.concatenate([narrow(state), high, low], axis=1)


def split_decay(message):
    rows = message.shape[1] - 2
    decay = wide(message[:, rows : rows + 1]) + wide(message[:, rows + 1 :])
    return wide(message[:, :rows]), decay


def entering(state, decay, later):
    count, mine = lax.axis_size("seq"), lax.axis_index("seq")
    inner = mine % 2
    ahead = (inner == 0) != later
    half = state.shape[1] // 2
    kept = wide(lax.dynamic_slice_in_dim(state, inner * half, half, 1))
    sent = lax.dynamic_slice_in_dim(state, (1 - inner) * half, half, 1)
    pair = swap("seq", 1)
    other, other_decay = split_decay(lax.ppermute(with_decay(sent, decay), "seq", pair))
    earliest = jnp.where(ahead, kept, other)
    joined = jnp.where(ahead, other_decay, decay) * earliest + jnp.where(ahead, other, kept)
    message = with_decay(joined, decay * other_decay)
    if later:
        chain = [(i, i - 2) for i in range(2, count)]
    else:
        chain = [(i, i + 2) for i in range(count - 2)]
    before, reach = jnp.zeros_like(kept), jnp.ones_like(decay)
    for _ in range(count // 2 - 1):
        message = lax.ppermute(message, "seq", chain)
        far, far_decay = split_decay(message)
        before = before + reach * far
        reach = reach * far_decay
    second = jnp.where(ahead, decay, other_decay) * before + earliest
    got = lax.ppermute(narrow(jnp.where(ahead, second, before)), "seq", pair)
    own = narrow(jnp.where(ahead, before, second))
    return jnp.concatenate(
        [jnp.where(inner == 0, own, got), jnp.where(inner == 0, got, own)], axis=1
    )


def columns_of(vector, rows):
    width = -(-vector.shape[-1] // rows)
    pad = [(0, 0)] * (vector.ndim - 1) + [(0, width * rows - vector.shape[-1])]
    shaped = jnp.pad(vector, pad).reshape(vector.shape[:-1] + (width, rows))
    return jnp.swapaxes(shaped, -1, -2)


def plain_layer(
    layer_in,
    seg_starts,
    attn_gain,
    query_weight,
    key_weight,
    value_weight,
    gate_weight,
    decay_down,
    decay_up,
    decay_bias,
    head_gain,
    out_weight,
    ffn_gain,
    ffn_gate,
    ffn_up,
    ffn_down,
    out_grad,
):
    ring = Ring("seq")
    count = ring.count
    batch, block, width = layer_in.shape
    rows = batch * block
    chunks = block // CHUNK
    rank, share = decay_down.shape[1], attn_gain.shape[0]
    hidden = ffn_gate.shape[1]

    smalls = [attn_gain, ffn_gain, head_gain, decay_bias, decay_up.reshape(-1)]
    ends = [sum(part.size for part in smalls[: i + 1]) for i in range(len(smalls))]
    small = jnp.pad(jnp.concatenate(smalls), (0, -ends[-1] % 128))[None]
    shard = jnp.concatenate(
        [value_weight, key_weight, query_weight, gate_weight, out_weight.T, decay_down], axis=1
    )
    inputs = layer_in.reshape(rows, width)
    weights, mark = ring.gather(shard)
    small = lax.all_gather(small, "seq")
    gain = wide(small[:, 0, :share]).reshape(width)
    normed = ring.near(narrow(wide(inputs) * root_scale(wide(inputs)) * gain), 1)
    projected = matmul(normed, weights)
    value_key, query = narrow(projected[:, : DV + DK]), narrow(projected[:, DV + DK : DV + 2 * DK])
    gates, low = projected[:, DV + 2 * DK : 2 * DV + 2 * DK], projected[:, -rank:]
    third, mark = ring.gather(jnp.concatenate([ffn_gate, ffn_up], axis=1), mark)
    fdown_t, mark = ring.gather(ffn_down.T, mark)
    projections = weights[:, : 2 * DV + 2 * DK]
    out_t, down_all = weights[:, 2 * DV + 2 * DK : -rank], weights[:, -rank:]
    small = small[:, 0]
    gain_one = wide(ring.near(small[:, : ends[0]], 0)).reshape(width)
    gain_two = wide(ring.near(small[:, ends[0] : ends[1]], 0)).reshape(width)
    gain_head = wide(small[:, ends[1] : ends[2]]).reshape(1, DV)
    bias_all = wide(small[:, ends[2] : ends[3]]).reshape(1, DK)
    up_all = small[:, ends[3] : ends[4]].reshape(count, rank, -1)
    up_all = wide(jnp.swapaxes(up_all, 0, 1).reshape(rank, DK))

    starts = seg_starts.reshape(batch, chunks, CHUNK).astype(jnp.float32)
    places = jnp.arange(CHUNK)
    lower = (places[:, None] >= places[None, :]).astype(jnp.float32)
    marks = jnp.einsum("bcs,ts->bct", starts, lower, precision=HIGH)
    column, row = marks.reshape(batch, block, 1), jnp.swapaxes(marks, 0, 1)[:, :, None, :]

    grad_rows = ring.near(out_grad.reshape(rows, width), 1)
    head = lax.axis_index("head")
    quarter = rows // lax.axis_size("head")
    inputs_own = lax.dynamic_slice_in_dim(inputs, head * quarter, quarter, 0)
    inputs_own = wide(ring.near(inputs_own, 1))
    grad_own = wide(lax.dynamic_slice_in_dim(grad_rows, head * quarter, quarter, 0))

    def tokens(field):
        return field.reshape(batch, block, field.shape[-1])

    value_key, query, gates, low = map(tokens, (value_key, query, gates, low))
    run, slope, state, total = local_states(value_key, low, up_all, bias_all, column)
    state_in = entering(state, total, False)
    heads, mixed, states = mix(query, value_key, run, column, row, state_in, gates, gain_head)
    heads = heads.reshape(rows, DV)
    resid = inputs_own + head_scatter(narrow(matmul_nt(heads, out_t)))
    scale_two = root_scale(resid)
    unit_two = resid * scale_two
    normed_two = head_gather(narrow(unit_two * gain_two))
    pre_gate = matmul(normed_two, third[:, :hidden])
    pre_up = matmul(normed_two, third[:, hidden:])
    sigma = jax.nn.sigmoid(pre_gate)
    act = narrow(pre_gate * sigma * pre_up)
    layer_out = narrow(resid + head_scatter(narrow(matmul_nt(act, fdown_t))))
    layer_out = ring.home(head_gather(layer_out), 1)

    d_act = matmul(grad_rows, fdown_t)
    grad_fdown = ring.scatter(narrow(matmul_tn(grad_rows, act)))
    d_gate = narrow(d_act * pre_up * sigma * (1.0 + pre_gate * (1.0 - sigma)))
    d_up = narrow(d_act * pre_gate * sigma)
    d_third = jnp.concatenate([d_gate, d_up], axis=1)
    grad_third = ring.scatter(narrow(matmul_tn(normed_two, d_third)))
    d_normed_two = head_scatter(narrow(matmul_nt(d_third, third)))
    grad_gain_two = jnp.sum(d_normed_two * unit_two, axis=0)
    d_resid = grad_own + norm_back(d_normed_two * gain_two, unit_two, scale_two)
    d_attn = head_gather(narrow(d_resid))
    d_heads = tokens(matmul(d_attn, out_t))
    d_gates, d_mixed, grad_gain_head, state_grad = head_back(
        d_heads, gates, mixed, gain_head, query, run, column
    )
    state_back = entering(state_grad, total, True)
    d_query, d_value, d_key, d_low, grad_up, grad_bias = mix_back(
        query, value_key, run, slope, column, row, d_mixed, states, state_back, low, up_all
    )
    d_gates = d_gates.reshape(rows, DV)
    grad_out = matmul_tn(d_attn, heads)
    grad_gate = matmul_tn(normed, d_gates)
    grad_fourth = ring.scatter(narrow(jnp.concatenate([grad_gate, grad_out], axis=1)))
    d_low = narrow(d_low.reshape(rows, rank))
    d_last = jnp.concatenate(
        [d_value.reshape(rows, DV), d_key.reshape(rows, DK), d_query.reshape(rows, DK)], axis=1
    )
    d_normed_part = (
        matmul_nt(jnp.concatenate([d_last, d_gates], axis=1), projections)
        + matmul_nt(d_low, down_all)
    )
    d_normed = head_scatter(narrow(d_normed_part))
    scale_own = root_scale(inputs_own)
    unit_own = inputs_own * scale_own
    d_unit = norm_back(d_normed * gain_one, unit_own, scale_own)
    input_grad = ring.home(head_gather(narrow(d_resid + d_unit)), 1)
    unit_all = ring.near(wide(inputs) * root_scale(wide(inputs)), 1)
    grad_gain_one = jnp.sum(d_normed_part * unit_all, axis=0)

    small = jnp.concatenate(
        [
            grad_gain_head.reshape(count, -1),
            grad_bias.reshape(count, -1),
            jnp.swapaxes(grad_up.reshape(rank, count, -1), 0, 1).reshape(count, -1),
        ],
        axis=1,
    )
    small = columns_of(ring.near(small, 0), share).reshape(width, -1)
    small = jnp.concatenate([grad_gain_one[:, None], grad_gain_two[:, None], small], axis=1)
    used = d_last.shape[1] + rank
    spare = -(used + small.shape[1]) % 128
    d_last = jnp.concatenate(
        [d_last, d_low, jnp.zeros((rows, small.shape[1] + spare), BF16)], axis=1
    )
    grad_last = matmul_tn(normed, d_last) + jnp.pad(small, ((0, 0), (used, spare)))
    grad_last = ring.scatter(narrow(grad_last))
    shared = grad_last[:, used - rank :]
    distance = 1
    while distance < lax.axis_size("head"):
        shared = shared + lax.ppermute(shared, "head", swap("head", distance))
        distance *= 2

    def lone(field):
        return jnp.swapaxes(field[:, rank + 2 : rank + small.shape[1]], 0, 1).reshape(-1)

    own = lone(grad_last[:, used - rank :])
    bounds = [0, head_gain.size, head_gain.size + decay_bias.size]
    bounds.append(bounds[2] + decay_up.size)
    return (
        layer_out.reshape(batch, block, width),
        input_grad.reshape(batch, block, width),
        shared[:, rank],
        grad_last[:, DV + DK : DV + 2 * DK],
        grad_last[:, DV : DV + DK],
        grad_last[:, :DV],
        grad_fourth[:, :DV],
        shared[:, :rank],
        own[bounds[2] : bounds[3]].reshape(rank, -1),
        own[bounds[1] : bounds[2]],
        lone(shared)[: bounds[1]],
        grad_fourth[:, DV:].T,
        shared[:, rank + 1],
        grad_third[:, :hidden],
        grad_third[:, hidden:],
        grad_fdown.T,
    )


def fused_layer(
    layer_in,
    seg_starts,
    attn_gain,
    query_weight,
    key_weight,
    value_weight,
    gate_weight,
    decay_down,
    decay_up,
    decay_bias,
    head_gain,
    out_weight,
    ffn_gain,
    ffn_gate,
    ffn_up,
    ffn_down,
    out_grad,
):
    count = lax.axis_size("seq")
    batch, block, width = layer_in.shape
    rows = batch * block
    rank, share = decay_down.shape[1], attn_gain.shape[0]
    hidden = ffn_gate.shape[1]
    used = 2 * DV + 2 * DK
    inputs, grad_rows = layer_in.reshape(rows, width), out_grad.reshape(rows, width)
    starts = seg_starts.reshape(-1, CHUNK)
    small = jnp.concatenate([attn_gain, ffn_gain, head_gain, decay_bias])
    small = jnp.pad(small, (0, -small.size % 128))[None]
    down = jnp.pad(decay_down, ((0, 0), (0, -rank % 128)))
    shard = jnp.concatenate([value_weight, key_weight, query_weight, gate_weight, down], axis=1)

    def tokens(field):
        return field.reshape(batch, block, field.shape[-1])

    normed, weights, out_t, value_key, query, gates, low, gains, gain_head, bias, up = enter(
        inputs, shard, out_weight.T, small, decay_up
    )
    value_key, query, gates, low = map(tokens, (value_key, query, gates, low))
    weights, out_t = weights.reshape(width, -1), out_t.reshape(width, DV)
    down_block = ffn_down.T
    run, slope, total, mixed, heads, states, part, fgate, fdown = token_phase(
        value_key, query, gates, low, up, bias, starts, gain_head, out_t, ffn_gate, down_block, EARLY
    )
    resid, normed_two, fup = row_phase(part, inputs, gains, ffn_up)
    fgate, fup = fgate.reshape(width, hidden), fup.reshape(width, hidden)
    act, d_gate, d_up, fdown_t = unit_phase(normed_two, fgate, fup, grad_rows, down_block, fdown)
    fdown_t = fdown_t.reshape(width, hidden)
    ffn_part = narrow(matmul_nt(act, fdown_t))
    part = narrow(matmul_nt(d_gate, fgate) + matmul_nt(d_up, fup))
    (
        d_resid, d_attn, d_gates, d_mixed, state_back, grad_gain_two, grad_gain_head, layer_out, grad_first
    ) = resid_phase(
        part, resid, grad_rows, gains, out_t, act, normed_two, d_up, gates, mixed, gain_head, query,
        run, starts, total, ffn_part,
    )
    packed, grad_up, grad_bias, part, grad_fgate = back_phase(
        query, value_key, run, slope, states, low, up, starts, d_mixed, state_back, d_gates,
        normed_two, d_gate, weights,
    )
    packed = packed.reshape(rows, -1)
    input_grad, grad_last, small, tail = last_phase(
        part, inputs, d_resid, gains, normed, packed, d_attn, heads.reshape(rows, DV),
        grad_gain_two, grad_gain_head, grad_bias, grad_up,
    )
    lines = share // 128
    results = leave(layer_out, input_grad, grad_first, grad_fgate, grad_last)
    layer_out, input_grad, grad_query, grad_key, grad_value, grad_gate, grad_out = results[:7]
    return (
        layer_out.reshape(batch, block, width),
        input_grad.reshape(batch, block, width),
        small[2 : 2 + lines].reshape(share),
        grad_query,
        grad_key,
        grad_value,
        grad_gate,
        tail[:, :rank],
        small[8:, : decay_up.shape[1]],
        small[1, : decay_bias.size],
        small[0, : head_gain.size],
        grad_out,
        small[4 : 4 + lines].reshape(share),
        *results[7:],
    )


def shards(layer_in, seg_starts, attn_gain, *rest):
    fits = attn_gain.shape[0] == 256 and lax.axis_size("head") == 4
    layer = fused_layer if fits and rest[4].shape[1] == 16 else plain_layer
    return layer(layer_in, seg_starts, attn_gain, *rest)


def solution(mesh):
    return jax.shard_map(
        shards,
        mesh=mesh,
        in_specs=(
            P(None, "seq", None),
            P(None, "seq"),
            P("seq"),
            P("seq", "head"),
            P("seq", "head"),
            P("seq", "head"),
            P("seq", "head"),
            P("seq", None),
            P(None, ("head", "seq")),
            P(("head", "seq")),
            P("seq"),
            P("head", "seq"),
            P("seq"),
            P("seq", "head"),
            P("seq", "head"),
            P("head", "seq"),
            P(None, "seq", None),
        ),
        out_specs=(
            P(None, "seq", None),
            P(None, "seq", None),
            P("seq"),
            P("seq", "head"),
            P("seq", "head"),
            P("seq", "head"),
            P("seq", "head"),
            P("seq", None),
            P(None, ("head", "seq")),
            P(("head", "seq")),
            P("seq"),
            P("head", "seq"),
            P("seq"),
            P("seq", "head"),
            P("seq", "head"),
            P("head", "seq"),
        ),
        check_vma=False,
    )
```

```python
import functools

import jax
import jax.numpy as jnp
from jax import lax
from jax.experimental import pallas as pl
from jax.experimental.pallas import tpu as pltpu
from jax.sharding import PartitionSpec as P

DK = 256
DV = 512
CHUNK = 128
EPS = 1e-06
HIGH = lax.Precision.HIGHEST
NN = (((1,), (0,)), ((), ()))
NT = (((1,), (1,)), ((), ()))
TN = (((0,), (0,)), ((), ()))
VMEM_BYTES = 60 * 1024 * 1024
MESH = pl.DeviceIdType.MESH


def product(left, right, dims, precision=None):
    return lax.dot_general(
        left, right, dims, precision=precision, preferred_element_type=jnp.float32
    )


def narrow(field):
    return field.astype(jnp.bfloat16)


def wide(field):
    return field.astype(jnp.float32)


def root_scale(field):
    return lax.rsqrt(jnp.mean(field * field, axis=-1, keepdims=True) + EPS)


def norm_back(upstream, unit, scale):
    return scale * (upstream - unit * jnp.mean(upstream * unit, axis=-1, keepdims=True))


def triangle(lower):
    rows = lax.broadcasted_iota(jnp.int32, (CHUNK, CHUNK), 0)
    columns = lax.broadcasted_iota(jnp.int32, (CHUNK, CHUNK), 1)
    return (rows >= columns if lower else rows <= columns).astype(jnp.float32)


def permitted(mark_column, mark_row):
    rows = lax.broadcasted_iota(jnp.int32, (CHUNK, CHUNK), 0)
    columns = lax.broadcasted_iota(jnp.int32, (CHUNK, CHUNK), 1)
    return (rows >= columns) & (mark_column == mark_row)


def state_chunk(
    value_ref, key_ref, low_ref, up_ref, bias_ref, mark_ref, run_ref, slope_ref, state, total
):
    lower = triangle(True)
    for b in range(value_ref.shape[0]):
        raw = product(low_ref[b], up_ref[...], NN, HIGH) + bias_ref[...]
        soft = jnp.log1p(jnp.exp(-jnp.abs(raw)))
        decay = (jnp.minimum(raw, 0.0) - soft) / 16.0
        slope_ref[b] = jnp.exp(jnp.minimum(-raw, 0.0) - soft) / 16.0
        run = product(lower, decay, NN, HIGH)
        run_ref[b] = run
        mark = mark_ref[b]
        last = run[CHUNK - 1 :]
        trailing = mark == mark[CHUNK - 1 :]
        kept = jnp.where(trailing, jnp.exp(last - run), 0.0)
        keep = jnp.where(mark[CHUNK - 1 :] == 0.0, jnp.exp(last), 0.0)
        tail = narrow(wide(key_ref[b]) * kept)
        state[b] = state[b] * keep + product(value_ref[b], tail, TN)
        total[b] = total[b] * keep


def state_kernel(
    value_ref, key_ref, low_ref, up_ref, bias_ref, mark_ref,
    run_ref, slope_ref, state_ref, total_ref, state, total,
):
    step = pl.program_id(0)

    @pl.when(step == 0)
    def _():
        state[...] = jnp.zeros_like(state)
        total[...] = jnp.ones_like(total)

    state_chunk(
        value_ref, key_ref, low_ref, up_ref, bias_ref, mark_ref, run_ref, slope_ref, state, total
    )

    @pl.when(step == pl.num_programs(0) - 1)
    def _():
        state_ref[...] = narrow(state[...])
        total_ref[...] = total[...]


def mixer_chunk(
    query_ref, value_ref, key_ref, run_ref, mark_ref, row_ref, gate_ref, gain_ref,
    heads_ref, mixed_ref, states_ref, state,
):
    for b in range(value_ref.shape[0]):
        run, mark = run_ref[b], mark_ref[b]
        middle, last = run[CHUNK // 2 - 1 : CHUNK // 2], run[CHUNK - 1 :]
        query = wide(query_ref[b]) * DK ** (-0.5)
        key = wide(key_ref[b])
        start = narrow(state[b])
        states_ref[0, b] = start
        scores = product(
            narrow(query * jnp.exp(run - middle)), narrow(key * jnp.exp(middle - run)), NT
        )
        scores = jnp.where(permitted(mark, row_ref[0, b]), scores, 0.0)
        opened = narrow(query * jnp.where(mark == 0.0, jnp.exp(run), 0.0))
        mixed = product(narrow(scores), value_ref[b], NN) + product(opened, start, NT)
        kept = jnp.where(mark == mark[CHUNK - 1 :], jnp.exp(last - run), 0.0)
        keep = jnp.where(mark[CHUNK - 1 :] == 0.0, jnp.exp(last), 0.0)
        state[b] = state[b] * keep + product(value_ref[b], narrow(key * kept), TN)
        states_ref[1, b] = narrow(state[b])
        mixed_ref[b] = mixed
        gate = gate_ref[b]
        active = gate * jax.nn.sigmoid(gate)
        heads_ref[b] = narrow(mixed * root_scale(mixed) * gain_ref[...] * active)


def mixer_kernel(
    query_ref, value_ref, key_ref, run_ref, mark_ref, row_ref, first_ref, gate_ref, gain_ref,
    heads_ref, mixed_ref, states_ref, state,
):
    @pl.when(pl.program_id(0) == 0)
    def _():
        state[...] = wide(first_ref[...])

    mixer_chunk(
        query_ref, value_ref, key_ref, run_ref, mark_ref, row_ref, gate_ref, gain_ref,
        heads_ref, mixed_ref, states_ref, state,
    )


def head_back_chunk(
    grad_ref, gate_ref, mixed_ref, gain_ref, query_ref, run_ref, mark_ref,
    gate_grad_ref, mixed_grad_ref, gain_grad_ref, state,
):
    gain = gain_ref[...]
    for b in range(grad_ref.shape[0]):
        mixed, gate, grad = mixed_ref[b], gate_ref[b], wide(grad_ref[b])
        scale = root_scale(mixed)
        unit = mixed * scale
        sigma = jax.nn.sigmoid(gate)
        active = gate * sigma
        gate_grad_ref[b] = narrow(grad * unit * gain * sigma * (1.0 + gate * (1.0 - sigma)))
        weighted = grad * active
        gain_grad_ref[...] += jnp.sum(weighted * unit, axis=0, keepdims=True)
        mixed_grad = narrow(norm_back(weighted * gain, unit, scale))
        mixed_grad_ref[b] = mixed_grad
        run, mark = run_ref[b], mark_ref[b]
        last = run[CHUNK - 1 :]
        query = wide(query_ref[b]) * DK ** (-0.5)
        opened = narrow(query * jnp.where(mark == 0.0, jnp.exp(run), 0.0))
        keep = jnp.where(mark[CHUNK - 1 :] == 0.0, jnp.exp(last), 0.0)
        state[b] = state[b] * keep + product(mixed_grad, opened, TN)


def head_back_kernel(
    grad_ref, gate_ref, mixed_ref, gain_ref, query_ref, run_ref, mark_ref,
    gate_grad_ref, mixed_grad_ref, gain_grad_ref, state_ref, state,
):
    step = pl.program_id(0)

    @pl.when(step == 0)
    def _():
        state[...] = jnp.zeros_like(state)
        gain_grad_ref[...] = jnp.zeros_like(gain_grad_ref)

    head_back_chunk(
        grad_ref, gate_ref, mixed_ref, gain_ref, query_ref, run_ref, mark_ref,
        gate_grad_ref, mixed_grad_ref, gain_grad_ref, state,
    )

    @pl.when(step == pl.num_programs(0) - 1)
    def _():
        state_ref[...] = narrow(state[...])


def mixer_back_chunk(
    query_ref, value_ref, key_ref, run_ref, slope_ref, mark_ref, row_ref, grad_ref,
    start_ref, end_ref, low_ref, up_ref,
    query_grad_ref, value_grad_ref, key_grad_ref, low_grad_ref, up_grad_ref, bias_grad_ref, state,
):
    upper = triangle(False)
    for b in range(value_ref.shape[0]):
        run, mark = run_ref[b], mark_ref[b]
        middle, last = run[CHUNK // 2 - 1 : CHUNK // 2], run[CHUNK - 1 :]
        query = wide(query_ref[b]) * DK ** (-0.5)
        key, value, grad = wide(key_ref[b]), value_ref[b], grad_ref[b]
        start, later = start_ref[0, b], narrow(state[b])
        rise, fall = jnp.exp(run - middle), jnp.exp(middle - run)
        opens = jnp.where(mark == 0.0, jnp.exp(run), 0.0)
        kept = jnp.where(mark == mark[CHUNK - 1 :], jnp.exp(last - run), 0.0)
        keep = jnp.where(mark[CHUNK - 1 :] == 0.0, jnp.exp(last), 0.0)
        allowed = permitted(mark, row_ref[0, b])
        risen, fallen = narrow(query * rise), narrow(key * fall)
        scores = narrow(jnp.where(allowed, product(risen, fallen, NT), 0.0))
        scores_grad = narrow(jnp.where(allowed, product(grad, value, NT), 0.0))
        query_grad = rise * product(scores_grad, fallen, NN) + opens * product(grad, start, NN)
        key_grad = fall * product(scores_grad, risen, TN) + kept * product(value, later, NN)
        value_grad = product(scores, grad, TN) + product(narrow(key * kept), later, NT)
        ends = jnp.sum(state[b] * wide(end_ref[0, b]), axis=0, keepdims=True)
        state[b] = state[b] * keep + product(grad, narrow(query * opens), TN)
        turn = query * query_grad - key * key_grad
        raw_grad = (product(upper, turn, NN, HIGH) + ends) * slope_ref[b]
        query_grad_ref[b] = narrow(query_grad * DK ** (-0.5))
        key_grad_ref[b] = narrow(key_grad)
        value_grad_ref[b] = narrow(value_grad)
        low_grad = narrow(product(raw_grad, up_ref[...], NT, HIGH))
        low_grad_ref[b, :, : low_grad.shape[1]] = low_grad
        up_grad_ref[...] += product(low_ref[b], raw_grad, TN, HIGH)
        bias_grad_ref[...] += jnp.sum(raw_grad, axis=0, keepdims=True)


def mixer_back_kernel(
    query_ref, value_ref, key_ref, run_ref, slope_ref, mark_ref, row_ref, grad_ref,
    start_ref, end_ref, last_ref, low_ref, up_ref,
    query_grad_ref, value_grad_ref, key_grad_ref, low_grad_ref, up_grad_ref, bias_grad_ref, state,
):
    @pl.when(pl.program_id(0) == 0)
    def _():
        state[...] = wide(last_ref[...])
        up_grad_ref[...] = jnp.zeros_like(up_grad_ref)
        bias_grad_ref[...] = jnp.zeros_like(bias_grad_ref)

    mixer_back_chunk(
        query_ref, value_ref, key_ref, run_ref, slope_ref, mark_ref, row_ref, grad_ref,
        start_ref, end_ref, low_ref, up_ref,
        query_grad_ref, value_grad_ref, key_grad_ref, low_grad_ref, up_grad_ref, bias_grad_ref,
        state,
    )


def along(batch, width, last=0, reverse=0):
    if reverse:
        return pl.BlockSpec((batch, CHUNK, width), lambda i: (0, reverse - 1 - i, last))
    return pl.BlockSpec((batch, CHUNK, width), lambda i: (0, i, last))


def still(*shape):
    return pl.BlockSpec(shape, lambda i: (0,) * len(shape))


def shape_of(dtype, *shape):
    return jax.ShapeDtypeStruct(shape, dtype)


def call(kernel, steps, in_specs, out_specs, out_shape, scratch, operands, flops):
    moved = sum(a.size * a.dtype.itemsize for a in operands)
    moved += sum(s.size * s.dtype.itemsize for s in out_shape)
    return pl.pallas_call(
        kernel,
        grid=(steps,),
        in_specs=in_specs,
        out_specs=out_specs,
        out_shape=out_shape,
        scratch_shapes=scratch,
        cost_estimate=pl.CostEstimate(flops=flops, bytes_accessed=moved, transcendentals=0),
        compiler_params=pltpu.CompilerParams(
            dimension_semantics=("arbitrary",), vmem_limit_bytes=VMEM_BYTES
        ),
    )(*operands)


F32, BF16 = jnp.float32, jnp.bfloat16


def local_states(value_key, low, up, bias, mark):
    batch, block, rank = low.shape
    steps = block // CHUNK
    return call(
        state_kernel,
        steps,
        [along(batch, DV), along(batch, DK, DV // DK), along(batch, rank), still(rank, DK),
         still(1, DK), along(batch, 1)],
        [along(batch, DK), along(batch, DK), still(batch, DV, DK), still(batch, 1, DK)],
        [shape_of(F32, batch, block, DK), shape_of(F32, batch, block, DK),
         shape_of(BF16, batch, DV, DK), shape_of(F32, batch, 1, DK)],
        [pltpu.VMEM((batch, DV, DK), F32), pltpu.VMEM((batch, 1, DK), F32)],
        (value_key, value_key, low, up, bias, mark),
        2 * batch * block * DK * (DV + 6 * CHUNK),
    )


def mix(query, value_key, run, mark, row, first, gates, gain):
    batch, block, _ = run.shape
    steps = block // CHUNK
    heads, mixed, states = call(
        mixer_kernel,
        steps,
        [along(batch, DK), along(batch, DV), along(batch, DK, DV // DK), along(batch, DK),
         along(batch, 1), pl.BlockSpec((1, batch, 1, CHUNK), lambda i: (i, 0, 0, 0)),
         still(batch, DV, DK), along(batch, DV), still(1, DV)],
        [along(batch, DV), along(batch, DV),
         pl.BlockSpec((2, batch, DV, DK), lambda i: (i, 0, 0, 0))],
        [shape_of(BF16, batch, block, DV), shape_of(F32, batch, block, DV),
         shape_of(BF16, 2 * steps, batch, DV, DK)],
        [pltpu.VMEM((batch, DV, DK), F32)],
        (query, value_key, value_key, run, mark, row, first, gates, gain),
        2 * batch * block * DK * (2 * DV + 3 * CHUNK),
    )
    return heads, mixed, states


def head_back(grad, gates, mixed, gain, query, run, mark):
    batch, block, _ = run.shape
    steps = block // CHUNK
    return call(
        head_back_kernel,
        steps,
        [along(batch, DV, 0, steps), along(batch, DV, 0, steps), along(batch, DV, 0, steps),
         still(1, DV), along(batch, DK, 0, steps), along(batch, DK, 0, steps),
         along(batch, 1, 0, steps)],
        [along(batch, DV, 0, steps), along(batch, DV, 0, steps), still(1, DV),
         still(batch, DV, DK)],
        [shape_of(BF16, batch, block, DV), shape_of(BF16, batch, block, DV),
         shape_of(F32, 1, DV), shape_of(BF16, batch, DV, DK)],
        [pltpu.VMEM((batch, DV, DK), F32)],
        (grad, gates, mixed, gain, query, run, mark),
        2 * batch * block * DK * DV,
    )


def mix_back(query, value_key, run, slope, mark, row, grad, states, later, low, up):
    batch, block, rank = low.shape
    steps = block // CHUNK
    return call(
        mixer_back_kernel,
        steps,
        [along(batch, DK, 0, steps), along(batch, DV, 0, steps),
         along(batch, DK, DV // DK, steps), along(batch, DK, 0, steps),
         along(batch, DK, 0, steps), along(batch, 1, 0, steps),
         pl.BlockSpec((1, batch, 1, CHUNK), lambda i: (steps - 1 - i, 0, 0, 0)),
         along(batch, DV, 0, steps),
         pl.BlockSpec((1, batch, DV, DK), lambda i: (2 * (steps - 1 - i), 0, 0, 0)),
         pl.BlockSpec((1, batch, DV, DK), lambda i: (2 * (steps - 1 - i) + 1, 0, 0, 0)),
         still(batch, DV, DK), along(batch, rank, 0, steps), still(rank, DK)],
        [along(batch, DK, 0, steps), along(batch, DV, 0, steps), along(batch, DK, 0, steps),
         along(batch, rank, 0, steps), still(rank, DK), still(1, DK)],
        [shape_of(BF16, batch, block, DK), shape_of(BF16, batch, block, DV),
         shape_of(BF16, batch, block, DK), shape_of(BF16, batch, block, rank),
         shape_of(F32, rank, DK), shape_of(F32, 1, DK)],
        [pltpu.VMEM((batch, DV, DK), F32)],
        (query, value_key, value_key, run, slope, mark, row, grad, states, states, later, low, up),
        2 * batch * block * DK * (5 * DV + 6 * CHUNK),
    )


def place_of(table, index):
    found = jnp.int32(table[0])
    for i, entry in enumerate(table[1:], 1):
        found = jnp.where(index == i, jnp.int32(entry), found)
    return found


def block_at(order, distance):
    count = len(order)
    place = place_of([order.index(i) for i in range(count)], lax.axis_index("seq"))
    return place_of(order, lax.rem(place + distance + count, count))


def greet(axis, count):
    barrier, mine = pltpu.get_barrier_semaphore(), lax.axis_index(axis)
    for d in range(1, count):
        pl.semaphore_signal(
            barrier, inc=1, device_id={axis: lax.rem(mine + d, count)}, device_id_type=MESH
        )
    pl.semaphore_wait(barrier, count - 1)


def enter_kernel(
    order, ready, input_ref, value_ref, key_ref, query_weight_ref, gate_weight_ref, down_ref,
    out_block_ref, ffn_down_ref, small_ref, rise_ref,
    normed_out, weight_out, out_out, turned_ref, downs_ref, vk_ref, query_ref, gate_ref, low_ref,
    gains_ref, head_gain_ref, bias_ref, up_ref,
    normed_ref, weight_ref, out_ref, down_t, smalls_ref, rises_ref, total, low_total,
    places, keeps, small_send, small_receive, rise_send, rise_receive, down_send, down_receive,
    ring_send, ring_receive, out_send, out_receive,
):
    count = len(order)
    share, half = down_ref.shape[0], down_ref.shape[0] // 2
    rows, tile = input_ref.shape[0], 256
    mine = lax.axis_index("seq")
    placed, column = [], 0
    for n, ref in enumerate((value_ref, key_ref, query_weight_ref, gate_weight_ref)):
        target = weight_ref.at[0, :, pl.ds(column, ref.shape[1])]
        placed.append(pltpu.make_async_copy(ref, target, places.at[n]))
        placed[-1].start()
        column += ref.shape[1]
    ring = BlockRing(order, weight_ref.at[0], weight_ref, ring_send, ring_receive, None)
    out_ring = BlockRing(order, out_ref.at[0], out_ref, out_send, out_receive, None)
    down_t[...] = down_ref[...].T
    out_ref[0] = out_block_ref[...].T
    greet("seq", count)
    for copy in placed:
        copy.wait()
    ring.start()
    out_ring.start()

    def spread(source, target, send, receive):
        return [
            pltpu.make_async_remote_copy(
                src_ref=source,
                dst_ref=target.at[mine],
                send_sem=send.at[d - 1],
                recv_sem=receive.at[d - 1],
                device_id={"seq": lax.rem(mine + d, count)},
                device_id_type=MESH,
            )
            for d in range(1, count)
        ]

    smalls = spread(small_ref, smalls_ref, small_send, small_receive)
    smalls += spread(rise_ref, rises_ref, rise_send, rise_receive)
    smalls += spread(down_t, downs_ref, down_send, down_receive)
    for copy in smalls:
        copy.start()
    smalls_ref[mine] = small_ref[...]
    rises_ref[mine] = rise_ref[...]
    downs_ref[mine] = down_t[...]
    turned_ref[...] = ffn_down_ref[...].T
    ready()
    kept = []

    def keep(slot, side):
        part = pl.ds(side * half, half)
        column = pl.ds(slot * share + side * half, half)
        pairs = (
            (weight_ref.at[slot, part], weight_out.at[slot, part]),
            (out_ref.at[slot, part], out_out.at[slot, part]),
            (normed_ref.at[:, column], normed_out.at[:, column]),
        )
        for n, (source, target) in enumerate(pairs):
            kept.append(pltpu.make_async_copy(source, target, keeps.at[slot, side, n]))
            kept[-1].start()

    scales = []
    for t in range(rows // tile):
        field = wide(input_ref[t * tile : (t + 1) * tile])
        scales.append(root_scale(field))

    def multiply(first, second, begin):
        sides = []
        for slot, side in (first, second):
            start = slot * share + side * half
            sides.append((slot, side, gains_ref[0:1, start : start + half]))
        for t in range(rows // tile):
            here = slice(t * tile, (t + 1) * tile)
            parts, blocks, downs = [], [], []
            for slot, side, gain in sides:
                owner = block_at(order, slot)
                start = pl.multiple_of(owner * share + side * half, half)
                field = wide(input_ref[here, pl.ds(start, half)])
                part = narrow(field * scales[t] * gain)
                column = slot * share + side * half
                normed_ref[here, column : column + half] = part
                parts.append(part)
                blocks.append(weight_ref[slot, side * half : (side + 1) * half])
                downs.append(downs_ref[owner][:, side * half : (side + 1) * half])
            left = jnp.concatenate(parts, axis=1)
            added = product(left, jnp.concatenate(blocks, axis=0), NN)
            low_added = product(left, jnp.concatenate(downs, axis=1), NT)
            if begin:
                total[here] = added
                low_total[here] = low_added
            else:
                total[here] += added
                low_total[here] += low_added
        for slot, side in (first, second):
            keep(slot, side)

    for copy in smalls:
        copy.wait_recv()
    head_share, bias_share = DV // count, DK // count
    for j in range(count):
        near = wide(smalls_ref[block_at(order, j)])
        gains_ref[0:1, j * share : (j + 1) * share] = near[:, :share]
        gains_ref[1:2, j * share : (j + 1) * share] = near[:, share : 2 * share]
        block = wide(smalls_ref[j])
        at = 2 * share
        head_gain_ref[:, j * head_share : (j + 1) * head_share] = block[:, at : at + head_share]
        at += head_share
        bias_ref[:, j * bias_share : (j + 1) * bias_share] = block[:, at : at + bias_share]
        up_ref[:, j * bias_share : (j + 1) * bias_share] = wide(rises_ref[j])
    multiply((0, 0), (0, 1), True)
    for step in range(1, count):
        ring.advance()
        out_ring.advance()
        multiply((count - step, 0), (step, 1), False)
    vk_cols, query_cols = vk_ref.shape[1], query_ref.shape[1]
    vk_ref[...] = narrow(total[:, :vk_cols])
    query_ref[...] = narrow(total[:, vk_cols : vk_cols + query_cols])
    gate_ref[...] = total[:, vk_cols + query_cols :]
    low_ref[...] = low_total[...]
    for copy in smalls:
        copy.wait_send()
    ring.finish()
    out_ring.finish()
    for copy in kept:
        copy.wait()


def enter(inputs, value, key, query, gate, down, out_block, ffn_down, small, rise):
    count = lax.axis_size("seq")
    rows, width = inputs.shape
    share, rank = down.shape
    cols = 2 * DV + 2 * DK
    dma = [pltpu.SemaphoreType.DMA((count - 1,))] * 6
    whole, outs = (count, share, cols), (count, share, DV)
    return remote_call(
        functools.partial(enter_kernel, ring_order(count)),
        0,
        [LOAD] + [AWAY] * 4 + [NEAR] * 5,
        [AWAY] * 3 + [NEAR] * 10,
        [
            shape_of(BF16, rows, width),
            shape_of(BF16, *whole),
            shape_of(BF16, *outs),
            shape_of(BF16, share, ffn_down.shape[0]),
            shape_of(BF16, count, rank, share),
            shape_of(BF16, rows, DV + DK),
            shape_of(BF16, rows, DK),
            shape_of(F32, rows, DV),
            shape_of(F32, rows, rank),
            shape_of(F32, 2, width),
            shape_of(F32, 1, DV),
            shape_of(F32, 1, DK),
            shape_of(F32, rank, DK),
        ],
        [
            pltpu.VMEM((rows, width), BF16),
            pltpu.VMEM(whole, BF16),
            pltpu.VMEM(outs, BF16),
            pltpu.VMEM((rank, share), BF16),
            pltpu.VMEM((count, *small.shape), BF16),
            pltpu.VMEM((count, *rise.shape), BF16),
            pltpu.VMEM((rows, cols), F32),
            pltpu.VMEM((rows, rank), F32),
            pltpu.SemaphoreType.DMA((4,)),
            pltpu.SemaphoreType.DMA((count, 2, 3)),
        ]
        + dma
        + ring_semaphores(count)[:2]
        + ring_semaphores(count)[:2],
        (inputs, value, key, query, gate, down, out_block, ffn_down, small, rise),
        2 * rows * width * cols,
    )


PARTS = 2


class BlockRing:
    def __init__(self, order, block_ref, whole_ref, send, receive, local):
        self.count = count = len(order)
        half = block_ref.shape[0] // 2
        size = half // PARTS
        aims = (block_at(order, 1), block_at(order, -1))
        self.local = None
        if local is not None:
            self.local = pltpu.make_async_copy(block_ref, whole_ref.at[0], local)
        self.hops = {}
        for step in range(1, count):
            for side in range(2):
                held = (count - step + 1) if side == 0 else step - 1
                lands = (count - step) if side == 0 else step
                for n in range(PARTS):
                    part = pl.ds(side * half + n * size, size)
                    self.hops[step, n, side] = pltpu.make_async_remote_copy(
                        src_ref=(block_ref if step == 1 else whole_ref.at[held]).at[part],
                        dst_ref=whole_ref.at[lands, part],
                        send_sem=send.at[step - 1, side, n],
                        recv_sem=receive.at[step - 1, side, n],
                        device_id={"seq": aims[side]},
                        device_id_type=MESH,
                    )
        self.step = 1

    def start(self):
        for n in range(PARTS):
            for side in range(2):
                self.hops[1, n, side].start()
        if self.local is not None:
            self.local.start()

    def advance(self):
        if self.step < self.count:
            for n in range(PARTS):
                for side in range(2):
                    self.hops[self.step, n, side].wait_recv()
                    if self.step + 1 < self.count:
                        self.hops[self.step + 1, n, side].start()
            self.step += 1

    def finish(self):
        while self.step < self.count:
            self.advance()
        for copy in self.hops.values():
            copy.wait_send()
        if self.local is not None:
            self.local.wait()


def ring_semaphores(count):
    return [
        pltpu.SemaphoreType.DMA((count - 1, 2, PARTS)),
        pltpu.SemaphoreType.DMA((count - 1, 2, PARTS)),
        pltpu.SemaphoreType.DMA,
    ]


class Handover:
    def __init__(self, count, later, state, decay, scratch):
        (self.decays, self.sent, self.got, self.chain, decay_send, decay_receive, send, receive) = scratch
        self.count, self.later, self.state, self.decay = count, later, state, decay
        self.mine = mine = lax.axis_index("seq")
        self.inner = lax.rem(mine, 2)
        self.pairs = count // 2
        self.pair = mine // 2
        self.place = self.pairs - 1 - self.pair if later else self.pair
        beside = mine + 1 - 2 * self.inner
        self.beside = beside
        self.ahead = (self.inner == 0) != later
        self.half = state.shape[1] // 2
        onward = mine - 2 if later else mine + 2
        self.decay_copies = [
            pltpu.make_async_remote_copy(
                src_ref=decay,
                dst_ref=self.decays.at[mine],
                send_sem=decay_send.at[d - 1],
                recv_sem=decay_receive.at[d - 1],
                device_id={"seq": lax.rem(mine + d, count)},
                device_id_type=MESH,
            )
            for d in range(1, count)
        ]
        self.batch = state.shape[0]
        self.swaps = [
            [
                pltpu.make_async_remote_copy(
                    src_ref=self.sent.at[i, b],
                    dst_ref=self.got.at[i, b],
                    send_sem=send.at[i, b],
                    recv_sem=receive.at[i, b],
                    device_id={"seq": beside},
                    device_id_type=MESH,
                )
                for b in range(self.batch)
            ]
            for i in range(2)
        ]
        self.links = [
            [
                pltpu.make_async_remote_copy(
                    src_ref=self.chain.at[r, b],
                    dst_ref=self.chain.at[r + 1, b],
                    send_sem=send.at[2 + r, b],
                    recv_sem=receive.at[2 + r, b],
                    device_id={"seq": onward},
                    device_id_type=MESH,
                )
                for b in range(self.batch)
            ]
            for r in range(self.pairs - 1)
        ]

    def clear(self):
        self.chain[...] = jnp.zeros_like(self.chain)

    def rows(self, own):
        part = self.inner if own else 1 - self.inner
        return pl.ds(pl.multiple_of(part * self.half, self.half), self.half)

    def begin(self):
        self.decays[self.mine] = self.decay[...]
        for copy in self.decay_copies:
            copy.start()
        for b in range(self.batch):
            self.sent[0, b] = narrow(self.state[b, self.rows(False)])
            self.swaps[0][b].start()

    def firsts(self, b):
        kept, other = self.state[b, self.rows(True)], wide(self.got[0, b])
        decay, other_decay = self.decays[self.mine, b], self.decays[self.beside, b]
        return (
            jnp.where(self.ahead, kept, other),
            jnp.where(self.ahead, other, kept),
            jnp.where(self.ahead, decay, other_decay),
            jnp.where(self.ahead, other_decay, decay),
        )

    def sends(self, r):
        return (self.place >= r) & (self.place + 1 < self.pairs)

    def join(self):
        for copy in self.decay_copies:
            copy.wait_recv()
        for b in range(self.batch):
            self.swaps[0][b].wait_recv()
            first, second, _, decay = self.firsts(b)
            self.chain[0, b] = narrow(decay * first + second)

            @pl.when(self.sends(0))
            def _(b=b):
                self.links[0][b].start()

    def hop(self, r):
        for b in range(self.batch):

            @pl.when(self.place >= r)
            def _(b=b):
                self.links[r - 1][b].wait_recv()

            if r < self.pairs - 1:

                @pl.when(self.sends(r))
                def _(b=b):
                    self.links[r][b].start()

    def close(self):
        for b in range(self.batch):
            before = wide(self.chain[1, b])
            reach = None
            for r in range(2, self.pairs):
                far = self.pair + r - 1 if self.later else self.pair - r + 1
                far = jnp.minimum(jnp.maximum(far, 0), self.pairs - 1)
                both = self.decays[2 * far, b] * self.decays[2 * far + 1, b]
                reach = both if reach is None else reach * both
                before = before + reach * wide(self.chain[r, b])
            first, _, decay, _ = self.firsts(b)
            after = decay * before + first
            self.sent[1, b] = narrow(jnp.where(self.ahead, after, before))
            self.swaps[1][b].start()
            self.state[b, self.rows(True)] = jnp.where(self.ahead, before, after)

    def finish(self):
        for b in range(self.batch):
            self.swaps[1][b].wait_recv()
            self.state[b, self.rows(False)] = wide(self.got[1, b])
        for copy in self.decay_copies + self.swaps[0] + self.swaps[1]:
            copy.wait_send()
        for r in range(self.pairs - 1):

            @pl.when(self.sends(r))
            def _(r=r):
                for b in range(self.batch):
                    self.links[r][b].wait_send()


def handover_scratch(count, batch):
    half = (batch, DV // 2, DK)
    return [
        pltpu.VMEM((count, batch, 1, DK), F32),
        pltpu.VMEM((2, *half), BF16),
        pltpu.VMEM((2, *half), BF16),
        pltpu.VMEM((count // 2, *half), BF16),
        pltpu.SemaphoreType.DMA((count - 1,)),
        pltpu.SemaphoreType.DMA((count - 1,)),
        pltpu.SemaphoreType.DMA((count // 2 + 1, batch)),
        pltpu.SemaphoreType.DMA((count // 2 + 1, batch)),
    ]


PIECES = 4


class Rows:
    def __init__(self, part, out, scratch):
        self.got, self.across, self.far, send, receive = scratch
        self.part, self.out = part, out
        head = lax.axis_index("head")
        core, chip = lax.rem(head, 2), head // 2
        self.share = part.shape[0] // 4
        self.size = self.share // PIECES
        beside, facing = 2 * chip + 1 - core, 2 * (1 - chip) + core
        self.own, self.facing = head, facing
        corner = 2 * (1 - chip) + 1 - core

        def copy(kind, p, source, target, aim):
            return pltpu.make_async_remote_copy(
                src_ref=source,
                dst_ref=target,
                send_sem=send.at[kind, p],
                recv_sem=receive.at[kind, p],
                device_id={"head": aim},
                device_id_type=MESH,
            )

        self.copies = {}
        for p in range(PIECES):
            here = self.piece(p)
            mine = out.at[self.rows(head, p)]
            met = out.at[self.rows(facing, p)]
            self.copies[0, p] = copy(0, p, part.at[self.rows(corner, p)], self.got.at[0, here], beside)
            self.copies[1, p] = copy(1, p, part.at[self.rows(beside, p)], self.got.at[1, here], beside)
            self.copies[2, p] = copy(2, p, self.across.at[here], self.far.at[here], facing)
            self.copies[3, p] = copy(3, p, mine, mine, facing)
            self.copies[4, p] = copy(4, p, mine, mine, beside)
            self.copies[5, p] = copy(5, p, met, met, beside)

    def piece(self, p):
        return pl.ds(p * self.size, self.size)

    def rows(self, owner, p):
        return pl.ds(pl.multiple_of(owner * self.share + p * self.size, self.size), self.size)

    def start(self, p):
        self.copies[0, p].start()
        self.copies[1, p].start()

    def cross(self, p):
        self.copies[0, p].wait_recv()
        here = self.piece(p)
        self.across[here] = narrow(wide(self.part[self.rows(self.facing, p)]) + wide(self.got[0, here]))
        self.copies[2, p].start()

    def turn(self, p, middle):
        self.copies[1, p].wait_recv()
        self.copies[2, p].wait_recv()
        here = self.piece(p)
        total = wide(self.part[self.rows(self.own, p)]) + wide(self.got[1, here])
        self.out[self.rows(self.own, p)] = middle(here, total + wide(self.far[here]))
        self.copies[3, p].start()
        self.copies[4, p].start()

    def relay(self, p):
        self.copies[3, p].wait_recv()
        self.copies[5, p].start()

    def finish(self):
        for p in range(PIECES):
            self.copies[4, p].wait_recv()
            self.copies[5, p].wait_recv()
        for copy in self.copies.values():
            copy.wait_send()


def rows_scratch(share, width):
    return [
        pltpu.VMEM((2, share, width), BF16),
        pltpu.VMEM((share, width), BF16),
        pltpu.VMEM((share, width), BF16),
        pltpu.SemaphoreType.DMA((6, PIECES)),
        pltpu.SemaphoreType.DMA((6, PIECES)),
    ]


def greet_all(count, heads):
    barrier = pltpu.get_barrier_semaphore()
    for axis, size in (("seq", count), ("head", heads)):
        mine = lax.axis_index(axis)
        for d in range(1, size):
            pl.semaphore_signal(
                barrier, inc=1, device_id={axis: lax.rem(mine + d, size)}, device_id_type=MESH
            )
    pl.semaphore_wait(barrier, count + heads - 2)


def chunk_at(i):
    return pl.ds(pl.multiple_of(i * CHUNK, CHUNK), CHUNK)


def token_phase_kernel(
    order, early, ready, vk_ref, query_ref, gate_ref, low_ref, up_ref, bias_ref, starts_ref, gain_ref,
    out_ref, block_ref, down_ref,
    run_ref, slope_ref, total_ref, mixed_ref, heads_ref, states_ref, part_ref, whole_ref, down_whole,
    state, ring_send, ring_receive, ring_local, down_send, down_receive, down_local,
    mark_ref, row_ref, *scratch,
):
    count = len(order)
    ring = BlockRing(order, block_ref, whole_ref, ring_send, ring_receive, ring_local)
    hand = Handover(count, False, state, total_ref, scratch)
    down_ring = BlockRing(
        order, down_ref.at[:, pl.ds(0, early)], down_whole, down_send, down_receive, down_local
    )
    hand.clear()
    greet("seq", count)
    ready(9)
    ring.start()
    fill_marks(starts_ref, mark_ref, row_ref)
    state[...] = jnp.zeros_like(state)
    total_ref[...] = jnp.ones_like(total_ref)
    chunks = run_ref.shape[1] // CHUNK
    ready(0, 3)

    @pl.loop(0, chunks)
    def _(i):
        at = chunk_at(i)
        state_chunk(
            vk_ref.at[:, at, pl.ds(0, DV)], vk_ref.at[:, at, pl.ds(DV, DK)], low_ref.at[:, at],
            up_ref, bias_ref, mark_ref.at[:, at], run_ref.at[:, at], slope_ref.at[:, at],
            state, total_ref,
        )

    hand.begin()
    ready.save(0, 1)
    ring.advance()
    hand.join()
    ring.advance()
    for r in range(1, count // 2):
        hand.hop(r)
        ring.advance()
    hand.close()
    ready()
    ring.advance()
    down_ring.start()
    hand.finish()
    ring.finish()
    down_ring.advance()

    def mixer(begin, end):
        @pl.loop(begin, end)
        def _(i):
            at = chunk_at(i)
            mixer_chunk(
                query_ref.at[:, at], vk_ref.at[:, at, pl.ds(0, DV)],
                vk_ref.at[:, at, pl.ds(DV, DK)], run_ref.at[:, at], mark_ref.at[:, at],
                row_ref.at[pl.ds(i, 1)], gate_ref.at[:, at], gain_ref, heads_ref.at[:, at],
                mixed_ref.at[:, at], states_ref.at[pl.ds(2 * i, 2)], state,
            )

    mixer(0, chunks // 2)
    down_ring.advance()
    mixer(chunks // 2, chunks)
    ready.save(3, 4, 5)
    down_ring.advance()
    batch, block, _ = heads_ref.shape
    tile = 256
    for b in range(batch):
        for t in range(block // tile):
            field = heads_ref[b, t * tile : (t + 1) * tile]
            start = b * block + t * tile
            part_ref[start : start + tile] = narrow(product(field, out_ref[...], NT))
        down_ring.advance()
    down_ring.finish()


def remote_call(kernel, number, in_specs, out_specs, out_shape, scratch, operands, flops):
    moved = sum(a.size * a.dtype.itemsize for a in operands)
    moved += sum(s.size * s.dtype.itemsize for s in out_shape)
    loads = [i for i, spec in enumerate(in_specs) if spec is LOAD]
    saves = [i for i, spec in enumerate(out_specs) if spec is SAVE]
    scratch = list(scratch)
    scratch += [pltpu.VMEM(out_shape[i].shape, out_shape[i].dtype) for i in saves]
    scratch += [pltpu.VMEM(operands[i].shape, operands[i].dtype) for i in loads]
    scratch += [pltpu.SemaphoreType.DMA((max(len(loads), 1),))]
    scratch += [pltpu.SemaphoreType.DMA((max(len(saves), 1),))]

    def body(*refs):
        refs = list(refs)
        arrivals, departures = refs[-2:]
        refs = refs[:-2]
        refs, buffers = refs[: len(refs) - len(loads)], refs[len(refs) - len(loads) :]
        refs, results = refs[: len(refs) - len(saves)], refs[len(refs) - len(saves) :]
        pending, started = {}, []
        for n, (i, buffer) in enumerate(zip(saves, results)):
            pending[i] = pltpu.make_async_copy(buffer, refs[len(in_specs) + i], departures.at[n])
            refs[len(in_specs) + i] = buffer
        waits = {}
        for n, (i, buffer) in enumerate(zip(loads, buffers)):
            waits[i] = pltpu.make_async_copy(refs[i], buffer, arrivals.at[n])
            waits[i].start()
            refs[i] = buffer

        def ready(*positions):
            for i in positions or list(waits):
                waits.pop(i).wait()

        def save(*positions):
            for i in positions:
                started.append(pending.pop(i))
                started[-1].start()

        ready.save = save
        kernel(ready, *refs)
        save(*list(pending))
        for copy in started:
            copy.wait()

    return pl.pallas_call(
        body,
        in_specs=[AWAY if spec is LOAD else spec for spec in in_specs],
        out_specs=[AWAY if spec is SAVE else spec for spec in out_specs],
        out_shape=out_shape,
        scratch_shapes=scratch,
        cost_estimate=pl.CostEstimate(flops=flops, bytes_accessed=moved, transcendentals=0),
        compiler_params=pltpu.CompilerParams(
            collective_id=number, has_side_effects=True, vmem_limit_bytes=VMEM_BYTES
        ),
    )(*operands)


LOAD, SAVE = "load", "save"
NEAR = pl.BlockSpec(memory_space=pltpu.VMEM)
AWAY = pl.BlockSpec(memory_space=pl.ANY)


def token_phase(value_key, query, gates, low, up, bias, starts, gain, out_t, block, down, early):
    count = lax.axis_size("seq")
    batch, length, _ = low.shape
    chunks, width = length // CHUNK, out_t.shape[0]
    return remote_call(
        functools.partial(token_phase_kernel, ring_order(count), early),
        1,
        [LOAD, LOAD, LOAD, LOAD, NEAR, NEAR, NEAR, NEAR, LOAD, LOAD, LOAD],
        [SAVE, SAVE, NEAR, SAVE, SAVE, SAVE, NEAR] + [AWAY] * 2,
        [
            shape_of(F32, batch, length, DK),
            shape_of(F32, batch, length, DK),
            shape_of(F32, batch, 1, DK),
            shape_of(F32, batch, length, DV),
            shape_of(BF16, batch, length, DV),
            shape_of(BF16, 2 * chunks, batch, DV, DK),
            shape_of(BF16, batch * length, width),
            shape_of(BF16, count, *block.shape),
            shape_of(BF16, count, down.shape[0], early),
        ],
        [pltpu.VMEM((batch, DV, DK), F32)]
        + ring_semaphores(count)
        + ring_semaphores(count)
        + marks_scratch(batch, length)
        + handover_scratch(count, batch),
        (value_key, query, gates, low, up, bias, starts, gain, out_t, block, down),
        2 * batch * length * DV * (2 * DK + width),
    )


def row_phase_kernel(
    order, heads, ready, part_ref, input_ref, gain_ref, block_ref,
    resid_ref, normed_ref, whole_ref,
    own, own_sems, ring_send, ring_receive, ring_local, *scratch,
):
    ring = BlockRing(order, block_ref, whole_ref, ring_send, ring_receive, ring_local)
    rows = Rows(part_ref, normed_ref, scratch)
    first = pl.multiple_of(rows.own * rows.share, rows.share)
    copies = near_copies(order, input_ref, own, pl.ds(first, rows.share), own_sems)
    for copy in copies:
        copy.start()
    greet_all(len(order), heads)
    ready(3)
    ring.start()
    ready()
    for p in range(PIECES):
        rows.start(p)

    def middle(here, total):
        resid = wide(own[here]) + total
        resid_ref[here] = resid
        return narrow(resid * root_scale(resid) * gain_ref[1:2])

    for p in range(PIECES):
        rows.cross(p)
    for copy in copies:
        copy.wait()
    ring.advance()
    for p in range(PIECES):
        rows.turn(p, middle)
        if p % 2 == 0:
            ring.advance()
    ring.advance()
    for p in range(PIECES):
        rows.relay(p)
        if p % 2 == 0:
            ring.advance()
    rows.finish()
    ring.finish()


def row_phase(part, inputs, gains, block):
    count, heads = lax.axis_size("seq"), lax.axis_size("head")
    rows, width = part.shape
    return remote_call(
        functools.partial(row_phase_kernel, ring_order(count), heads),
        2,
        [LOAD, AWAY, NEAR, LOAD],
        [NEAR] * 2 + [AWAY],
        [
            shape_of(F32, rows // heads, width),
            shape_of(BF16, rows, width),
            shape_of(BF16, count, *block.shape),
        ],
        [pltpu.VMEM((rows // heads, width), BF16), pltpu.SemaphoreType.DMA((count,))]
        + ring_semaphores(count)
        + rows_scratch(rows // heads, width),
        (part, inputs, gains, block),
        16 * rows * width,
    )


def near_copies(order, source, target, rows, semaphores):
    share = source.shape[1] // len(order)
    return [
        pltpu.make_async_copy(
            source.at[rows, pl.ds(pl.multiple_of(block_at(order, r) * share, share), share)],
            target.at[:, pl.ds(r * share, share)],
            semaphores.at[r],
        )
        for r in range(len(order))
    ]


def home_copies(order, source, target, semaphores):
    share = source.shape[1] // len(order)
    return [
        pltpu.make_async_copy(
            source.at[:, pl.ds(r * share, share)],
            target.at[:, pl.ds(pl.multiple_of(block_at(order, r) * share, share), share)],
            semaphores.at[r],
        )
        for r in range(len(order))
    ]


def fill_marks(starts_ref, mark_ref, row_ref):
    batch, length, _ = mark_ref.shape
    chunks = length // CHUNK
    starts = starts_ref[...].astype(F32)
    across = product(starts, triangle(False), NN, HIGH)
    down = product(triangle(True), starts, NT, HIGH)
    for b in range(batch):
        for i in range(chunks):
            n = b * chunks + i
            mark_ref[b, i * CHUNK : (i + 1) * CHUNK] = down[:, n : n + 1]
            row_ref[i, b] = across[n : n + 1]


def marks_scratch(batch, length):
    return [
        pltpu.VMEM((batch, length, 1), F32),
        pltpu.VMEM((length // CHUNK, batch, 1, CHUNK), F32),
    ]


def split_columns(widths):
    pieces, begin = [], 0
    for item, columns in enumerate(widths):
        number = -(-columns // 1024)
        size = -(-columns // (128 * number)) * 128
        for start in range(0, columns, size):
            pieces.append((item, start, min(size, columns - start), begin + start))
        begin += columns
    return pieces


class SumRing:
    def __init__(self, order, items, out_ref, scratch):
        lefts = []
        for left, _, _ in items:
            if not any(left is other for other in lefts):
                lefts.append(left)
        buffers, rest = scratch[: len(lefts)], scratch[len(lefts) :]
        self.sent, self.got, load, send, receive = rest
        self.order, self.items, self.out = order, items, out_ref
        self.count = count = len(order)
        self.half = half = out_ref.shape[0] // 2
        self.buffers = {id(left): buffer for left, buffer in zip(lefts, buffers)}
        self.pieces = split_columns([right.shape[1] for _, right, _ in items])
        homes = {id(left): home for left, _, home in items}
        aims = (block_at(order, 1), block_at(order, -1))
        self.loads, self.hops = {}, {}
        for k in range(count):
            for side in range(2):
                slot = (count - 1 - k) if side == 0 else (k + 1) % count
                for n, (left, buffer) in enumerate(zip(lefts, buffers)):
                    block = block_at(order, slot) if homes[id(left)] else slot
                    column = pl.multiple_of(block * 2 * half + side * half, half)
                    self.loads[k, side, n] = pltpu.make_async_copy(
                        left.at[:, pl.ds(column, half)],
                        buffer.at[k % 2, side],
                        load.at[k % 2, side, n],
                    )
                if k == count - 1:
                    continue
                for n, (_, _, size, begin) in enumerate(self.pieces):
                    self.hops[k, side, n] = pltpu.make_async_remote_copy(
                        src_ref=self.sent.at[k % 2, side, :, pl.ds(begin, size)],
                        dst_ref=self.got.at[k, side, :, pl.ds(begin, size)],
                        send_sem=send.at[k, side, n],
                        recv_sem=receive.at[k, side, n],
                        device_id={"seq": aims[side]},
                        device_id_type=MESH,
                    )
        self.number = len(lefts)
        self.k = 0

    def load(self, k):
        if k < self.count:
            for side in range(2):
                for n in range(self.number):
                    self.loads[k, side, n].start()

    def prepare(self):
        self.load(0)
        self.load(1)

    def advance(self):
        k, last = self.k, self.count - 1
        if k > last:
            return
        for side in range(2):
            for n in range(self.number):
                self.loads[k, side, n].wait()
        for n, (item, start, size, begin) in enumerate(self.pieces):
            left, right, _ = self.items[item]
            columns = slice(begin, begin + size)
            for side in range(2):
                buffer = self.buffers[id(left)]
                value = product(buffer[k % 2, side], right[:, start : start + size], TN)
                if k > 0:
                    self.hops[k - 1, side, n].wait_recv()
                    value = value + wide(self.got[k - 1, side, :, columns])
                if k < last:
                    if k >= 2:
                        self.hops[k - 2, side, n].wait_send()
                    self.sent[k % 2, side, :, columns] = narrow(value)
                    self.hops[k, side, n].start()
                else:
                    self.out[side * self.half : (side + 1) * self.half, columns] = value
        self.load(k + 2)
        self.k += 1

    def finish(self):
        while self.k < self.count:
            self.advance()
        for k in (self.count - 3, self.count - 2):
            for n in range(len(self.pieces)):
                for side in range(2):
                    self.hops[k, side, n].wait_send()


def sum_scratch(count, rows, lefts, half, widths):
    columns, pieces = sum(widths), len(split_columns(widths))
    return [pltpu.VMEM((2, 2, rows, half), BF16)] * lefts + [
        pltpu.VMEM((2, 2, half, columns), BF16),
        pltpu.VMEM((count - 1, 2, half, columns), BF16),
        pltpu.SemaphoreType.DMA((2, 2, lefts)),
        pltpu.SemaphoreType.DMA((count - 1, 2, pieces)),
        pltpu.SemaphoreType.DMA((count - 1, 2, pieces)),
    ]


def unit_phase_kernel(
    order, ready, normed_ref, gate_ref, up_ref, grad_ref, block_ref, early_ref,
    act_ref, gate_grad_ref, up_grad_ref, ffn_ref, part_ref,
    whole_ref, pre_gate, pre_up, act_grad, tiles, tile_sems, early_sem, ring_send, ring_receive, ring_local,
):
    count = len(order)
    early = early_ref.shape[2]
    late = block_ref.shape[1] - early
    ring = BlockRing(
        order, block_ref.at[:, pl.ds(early, late)], whole_ref.at[:, :, pl.ds(early, late)],
        ring_send, ring_receive, ring_local,
    )
    placed = pltpu.make_async_copy(early_ref, whole_ref.at[:, :, pl.ds(0, early)], early_sem)
    greet("seq", count)
    ring.start()
    rows, width = normed_ref.shape
    tile = 256
    share = block_ref.shape[0]

    def written(kind, target, i):
        return pltpu.make_async_copy(
            tiles.at[kind], target.at[pl.ds(i * tile, tile)], tile_sems.at[kind]
        )

    ready(0, 1, 2)
    placed.start()
    steps = rows // tile
    for i in range(steps):
        here = pl.ds(i * tile, tile)
        field = normed_ref[here]
        gate = product(field, gate_ref[...], NN)
        pre_gate[here] = gate
        up = product(field, up_ref[...], NN)
        pre_up[here] = up
        act_ref[here] = narrow(gate * jax.nn.sigmoid(gate) * up)
        ring.advance()
    ready.save(0)
    ready()
    placed.wait()

    def against(here, columns):
        parts = [
            grad_ref[here, pl.ds(pl.multiple_of(block_at(order, r) * share, share), share)]
            for r in range(count)
        ]
        right = whole_ref[:, :, columns].reshape(width, -1)
        return product(jnp.concatenate(parts, axis=1), right, NN)

    for i in range(steps):
        act_grad[i * tile : (i + 1) * tile] = against(pl.ds(i * tile, tile), slice(0, early))
        if i % 2:
            ring.advance()
    ring.finish()
    for i in range(steps):
        here = pl.ds(i * tile, tile)
        ends = against(here, slice(early, early + late))
        for kind, target in ((0, gate_grad_ref), (1, up_grad_ref)):
            if i > 0:
                written(kind, target, i - 1).wait()
        for columns, grad in ((slice(0, early), act_grad[here]), (slice(early, early + late), ends)):
            gate, up = pre_gate[here, columns], pre_up[here, columns]
            sigma = jax.nn.sigmoid(gate)
            tiles[0, :, columns] = narrow(grad * up * sigma * (1.0 + gate * (1.0 - sigma)))
            tiles[1, :, columns] = narrow(grad * gate * sigma)
        for kind, target in ((0, gate_grad_ref), (1, up_grad_ref)):
            written(kind, target, i).start()
        part = product(tiles[0], gate_ref[...], NT) + product(tiles[1], up_ref[...], NT)
        part_ref[here] = narrow(part)
        ffn_ref[here] = narrow(product(act_ref[here], whole_ref[...].reshape(width, -1), NT))
    for kind, target in ((0, gate_grad_ref), (1, up_grad_ref)):
        written(kind, target, steps - 1).wait()


def unit_phase(normed_two, fgate, fup, grad_rows, block, early):
    count = lax.axis_size("seq")
    rows, width = normed_two.shape
    hidden = block.shape[1]
    flat = shape_of(BF16, rows, hidden)
    return remote_call(
        functools.partial(unit_phase_kernel, ring_order(count)),
        3,
        [LOAD] * 4 + [AWAY, AWAY],
        [SAVE, AWAY, AWAY, SAVE, SAVE],
        [flat, flat, flat, shape_of(BF16, rows, width), shape_of(BF16, rows, width)],
        [
            pltpu.VMEM((count, *block.shape), BF16),
            pltpu.VMEM((rows, hidden), F32),
            pltpu.VMEM((rows, hidden), F32),
            pltpu.VMEM((rows, early.shape[2]), F32),
            pltpu.VMEM((2, 256, hidden), BF16),
            pltpu.SemaphoreType.DMA((2,)),
            pltpu.SemaphoreType.DMA,
        ]
        + ring_semaphores(count),
        (normed_two, fgate, fup, grad_rows, block, early),
        6 * rows * width * hidden,
    )


def resid_phase_kernel(
    order, heads, ready, part_ref, resid_ref, grad_ref, gain_ref, out_ref, act_ref, normed_ref,
    up_grad_ref, gate_ref, mixed_ref, head_gain_ref, query_ref, run_ref, starts_ref, total_ref, ffn_ref,
    resid_grad_ref, attn_grad_ref, gates_grad_ref, mixed_grad_ref, state_ref, gain_grad_ref,
    head_gain_grad_ref, layer_ref, sums_ref,
    own, own_sems, wholes, whole_sems, ffn_sem, pair, pair_sems, heads_grad, state, mark_ref, row_ref,
    *scratch,
):
    count = len(order)
    rows = Rows(part_ref, wholes, scratch[:5])
    hand = Handover(count, True, state, total_ref, scratch[5:13])
    ring = SumRing(
        order, [(grad_ref, act_ref, True), (normed_ref, up_grad_ref, False)], sums_ref, scratch[13:]
    )
    first = pl.multiple_of(rows.own * rows.share, rows.share)
    copies = near_copies(order, grad_ref, own, pl.ds(first, rows.share), own_sems)
    ring.prepare()
    for copy in copies:
        copy.start()
    batch, length, _ = run_ref.shape
    chunks = length // CHUNK
    pairs = [
        [
            pltpu.make_async_copy(
                field.at[:, pl.ds((chunks - 1 - i) * CHUNK, CHUNK)],
                pair.at[i % 2, kind],
                pair_sems.at[i % 2, kind],
            )
            for kind, field in enumerate((gate_ref, mixed_ref))
        ]
        for i in range(chunks)
    ]
    hand.clear()
    greet_all(count, heads)
    ready(0)
    for p in range(PIECES):
        rows.start(p)
    ready(5, 7)
    ring.advance()
    for copy in pairs[0] + pairs[1]:
        copy.start()
    gain_grad_ref[...] = jnp.zeros_like(gain_grad_ref)
    head_gain_grad_ref[...] = jnp.zeros_like(head_gain_grad_ref)
    state[...] = jnp.zeros_like(state)
    fill_marks(starts_ref, mark_ref, row_ref)

    def middle(here, total):
        resid = resid_ref[here]
        scale = root_scale(resid)
        unit = resid * scale
        gain_grad_ref[...] += jnp.sum(total * unit, axis=0, keepdims=True)
        grad = wide(own[here]) + norm_back(total * gain_ref[1:2], unit, scale)
        resid_grad_ref[here] = grad
        return narrow(grad)

    def layer(here, total):
        return narrow(resid_ref[here] + total)

    for p in range(PIECES):
        rows.cross(p)
    for copy in copies:
        copy.wait()
    ready()
    rows.turn(0, middle)
    ring.advance()
    for p in range(1, PIECES):
        rows.turn(p, middle)
    ring.advance()
    for p in range(PIECES):
        rows.relay(p)
        if p == 2:
            ring.advance()
    rows.finish()
    ready.save(0)
    kept = pltpu.make_async_copy(wholes, attn_grad_ref, whole_sems.at[0])
    kept.start()
    following = pltpu.make_async_copy(ffn_ref, part_ref, ffn_sem)
    following.start()

    for i in range(chunks):
        at = pl.ds((chunks - 1 - i) * CHUNK, CHUNK)
        for copy in pairs[i]:
            copy.wait()
        for b in range(batch):
            here = pl.ds(b * length + (chunks - 1 - i) * CHUNK, CHUNK)
            heads_grad[b] = product(wholes[here], out_ref[...], NN)
        head_back_chunk(
            heads_grad, pair.at[i % 2, 0], pair.at[i % 2, 1], head_gain_ref,
            query_ref.at[:, at], run_ref.at[:, at], mark_ref.at[:, at],
            gates_grad_ref.at[:, at], mixed_grad_ref.at[:, at], head_gain_grad_ref, state,
        )
        if i + 2 < chunks:
            for copy in pairs[i + 2]:
                copy.start()

    hand.begin()
    ready.save(2, 3)
    kept.wait()
    following.wait()
    for p in range(PIECES):
        rows.start(p)
    ring.advance()
    hand.join()
    for p in range(PIECES):
        rows.cross(p)
    for r in range(1, count // 2):
        hand.hop(r)
        if r < PIECES:
            rows.turn(r - 1, layer)
        if r == 2:
            ring.advance()
    for r in range(count // 2 - 1, PIECES):
        rows.turn(r, layer)
    hand.close()
    ring.advance()
    hand.finish()
    state_ref[...] = narrow(state[...])
    for p in range(PIECES):
        rows.relay(p)
        if p == 2:
            ring.advance()
    rows.finish()
    backs = home_copies(order, wholes, layer_ref, whole_sems)
    for copy in backs:
        copy.start()
    ring.finish()
    for copy in backs:
        copy.wait()


def resid_phase(
    part, resid, grad_rows, gains, out_t, act, normed_two, d_up, gates, mixed, head_gain, query, run,
    starts, total, ffn_part,
):
    count, heads = lax.axis_size("seq"), lax.axis_size("head")
    rows, width = part.shape
    batch, length, _ = run.shape
    share, hidden = width // count, act.shape[1]
    quarter = rows // heads
    return remote_call(
        functools.partial(resid_phase_kernel, ring_order(count), heads),
        4,
        [LOAD, LOAD, AWAY, NEAR, LOAD, LOAD, AWAY, LOAD, AWAY, AWAY, NEAR, LOAD, LOAD, NEAR, NEAR, AWAY],
        [SAVE, AWAY, SAVE, SAVE, NEAR, NEAR, NEAR, AWAY, NEAR],
        [
            shape_of(F32, quarter, width),
            shape_of(BF16, rows, width),
            shape_of(BF16, batch, length, DV),
            shape_of(BF16, batch, length, DV),
            shape_of(BF16, batch, DV, DK),
            shape_of(F32, 1, width),
            shape_of(F32, 1, DV),
            shape_of(BF16, rows, width),
            shape_of(F32, share, 2 * hidden),
        ],
        [
            pltpu.VMEM((quarter, width), BF16),
            pltpu.SemaphoreType.DMA((count,)),
            pltpu.VMEM((rows, width), BF16),
            pltpu.SemaphoreType.DMA((count,)),
            pltpu.SemaphoreType.DMA,
            pltpu.VMEM((2, 2, batch, CHUNK, DV), F32),
            pltpu.SemaphoreType.DMA((2, 2)),
            pltpu.VMEM((batch, CHUNK, DV), F32),
            pltpu.VMEM((batch, DV, DK), F32),
        ]
        + marks_scratch(batch, length)
        + rows_scratch(quarter, width)
        + handover_scratch(count, batch)
        + sum_scratch(count, rows, 2, share // 2, [hidden, hidden]),
        (part, resid, grad_rows, gains, out_t, act, normed_two, d_up, gates, mixed, head_gain, query,
         run, starts, total, ffn_part),
        2 * rows * width * (2 * hidden + DV),
    )


def back_phase_kernel(
    order, ready, query_ref, vk_ref, run_ref, slope_ref, states_ref, low_ref, up_ref, starts_ref,
    mixed_grad_ref, later_ref, gates_grad_ref, normed_ref, act_grad_ref, weight_ref, down_ref,
    packed_ref, up_grad_ref, bias_grad_ref, part_ref, sums_ref,
    state, mark_ref, row_ref, *scratch,
):
    count = len(order)
    ring = SumRing(order, [(normed_ref, act_grad_ref, False)], sums_ref, scratch)
    ring.prepare()
    greet("seq", count)
    ready(12)
    ring.advance()
    batch, length, _ = run_ref.shape
    chunks = length // CHUNK
    gates_from, low_from = DV + 2 * DK, 2 * DV + 2 * DK
    fill_marks(starts_ref, mark_ref, row_ref)
    for ref in (up_grad_ref, bias_grad_ref):
        ref[...] = jnp.zeros_like(ref)
    spare = packed_ref.shape[2] - low_from
    packed_ref[:, :, low_from:] = jnp.zeros((batch, length, spare), BF16)
    ready(0, 1, 2, 3, 4, 5, 8, 9, 10)
    state[...] = wide(later_ref[...])
    packed_ref[:, :, gates_from:low_from] = gates_grad_ref[...]

    def back(begin, end):
        @pl.loop(begin, end)
        def _(i):
            n = chunks - 1 - i
            at = chunk_at(n)
            mixer_back_chunk(
                query_ref.at[:, at], vk_ref.at[:, at, pl.ds(0, DV)],
                vk_ref.at[:, at, pl.ds(DV, DK)], run_ref.at[:, at], slope_ref.at[:, at],
                mark_ref.at[:, at], row_ref.at[pl.ds(n, 1)], mixed_grad_ref.at[:, at],
                states_ref.at[pl.ds(2 * n, 1)], states_ref.at[pl.ds(2 * n + 1, 1)],
                low_ref.at[:, at], up_ref,
                packed_ref.at[:, at, pl.ds(DV + DK, DK)], packed_ref.at[:, at, pl.ds(0, DV)],
                packed_ref.at[:, at, pl.ds(DV, DK)], packed_ref.at[:, at, pl.ds(low_from, 128)],
                up_grad_ref, bias_grad_ref, state,
            )

    back(0, chunks // 2)
    ring.advance()
    back(chunks // 2, chunks)
    ready.save(0)
    ring.advance()
    ready()
    tile, rank = 256, low_ref.shape[2]
    down = [down_ref[block_at(order, r)] for r in range(count)]
    down = jnp.concatenate(down, axis=1)
    for b in range(batch):
        for t in range(length // tile):
            field = packed_ref[b, t * tile : (t + 1) * tile, :low_from]
            low = packed_ref[b, t * tile : (t + 1) * tile, low_from : low_from + rank]
            start = b * length + t * tile
            total = product(field, weight_ref[...], NT) + product(low, down, NN)
            part_ref[start : start + tile] = narrow(total)
        ring.advance()
    ring.finish()


def back_phase(
    query, vk, run, slope, states, low, up, starts, d_mixed, later, d_gates, normed_two, d_gate, weights,
    down,
):
    count = lax.axis_size("seq")
    batch, length, rank = low.shape
    width, packed_cols = weights.shape[0], weights.shape[1] + 128
    share, hidden, rows = width // count, d_gate.shape[1], d_gate.shape[0]
    return remote_call(
        functools.partial(back_phase_kernel, ring_order(count)),
        5,
        [LOAD] * 6 + [NEAR, NEAR, LOAD, LOAD, LOAD, AWAY, LOAD, LOAD, NEAR],
        [SAVE] + [NEAR] * 4,
        [
            shape_of(BF16, batch, length, packed_cols),
            shape_of(F32, rank, DK),
            shape_of(F32, 1, DK),
            shape_of(BF16, rows, width),
            shape_of(F32, share, hidden),
        ],
        [pltpu.VMEM((batch, DV, DK), F32)]
        + marks_scratch(batch, length)
        + sum_scratch(count, rows, 1, share // 2, [hidden]),
        (query, vk, run, slope, states, low, up, starts, d_mixed, later, d_gates, normed_two, d_gate,
         weights, down),
        2 * rows * width * hidden,
    )


SMALL = 24


def last_phase_kernel(
    order, heads, ready, part_ref, input_ref, resid_grad_ref, gain_ref, normed_ref, packed_ref, attn_ref,
    heads_ref, ffn_gain_ref, head_gain_ref, bias_ref, up_ref,
    input_grad_ref, sums_ref, small_ref, tail_ref,
    own, own_sems, grads, grad_sems, gain_grad, stage, stage_got, shared, shared_got, tail_got,
    seq_send, seq_receive, head_send, head_receive, *scratch,
):
    count = len(order)
    rows = Rows(part_ref, grads, scratch[:5])
    ring = SumRing(
        order, [(normed_ref, packed_ref, False), (attn_ref, heads_ref, False)], sums_ref, scratch[5:]
    )
    first = pl.multiple_of(rows.own * rows.share, rows.share)
    copies = near_copies(order, input_ref, own, pl.ds(first, rows.share), own_sems)
    for copy in copies:
        copy.start()
    ring.prepare()
    greet_all(count, heads)
    ready(0)
    for p in range(PIECES):
        rows.start(p)
    ready(5, 7)
    ring.advance()
    ready()
    gain_grad[...] = jnp.zeros_like(gain_grad)

    def middle(here, total):
        field = wide(own[here])
        scale = root_scale(field)
        unit = field * scale
        gain_grad[...] += jnp.sum(total * unit, axis=0, keepdims=True)
        return narrow(resid_grad_ref[here] + norm_back(total * gain_ref[0:1], unit, scale))

    for p in range(PIECES):
        rows.cross(p)
    for copy in copies:
        copy.wait()
    ring.advance()
    for p in range(PIECES):
        rows.turn(p, middle)
        if p == 2:
            ring.advance()

    mine, head = lax.axis_index("seq"), lax.axis_index("head")
    share = sums_ref.shape[0]
    stage[...] = jnp.zeros_like(stage)
    pieces = [ref.shape[1] // count for ref in (head_gain_ref, bias_ref, up_ref)]
    for j in range(count):
        stage[j, 0:1, : pieces[0]] = head_gain_ref[:, j * pieces[0] : (j + 1) * pieces[0]]
        stage[j, 1:2, : pieces[1]] = bias_ref[:, j * pieces[1] : (j + 1) * pieces[1]]
        stage[j, 8:, : pieces[2]] = up_ref[:, j * pieces[2] : (j + 1) * pieces[2]]
        owner = block_at(order, j)
        for n, ref in ((2, gain_grad), (4, ffn_gain_ref)):
            for t in range(share // 128):
                start = j * share + t * 128
                stage[owner, n + t : n + t + 1, :] = ref[:, start : start + 128]
    stage_hops = []
    for d in range(1, count):
        aim = lax.rem(mine + d, count)
        stage_hops.append(
            pltpu.make_async_remote_copy(
                src_ref=stage.at[aim],
                dst_ref=stage_got.at[d - 1],
                send_sem=seq_send.at[d - 1],
                recv_sem=seq_receive.at[d - 1],
                device_id={"seq": aim},
                device_id_type=MESH,
            )
        )
    for hop in stage_hops:
        hop.start()

    def head_hops(kind, source, target):
        return [
            pltpu.make_async_remote_copy(
                src_ref=source,
                dst_ref=target.at[d - 1],
                send_sem=head_send.at[kind, d - 1],
                recv_sem=head_receive.at[kind, d - 1],
                device_id={"head": lax.rem(head + d, heads)},
                device_id_type=MESH,
            )
            for d in range(1, heads)
        ]

    rows.relay(0)
    rows.relay(1)
    ring.advance()
    rows.relay(2)
    rows.relay(3)
    for hop in stage_hops:
        hop.wait_recv()
    total = stage[mine]
    for d in range(count - 1):
        total = total + stage_got[d]
    small_ref[...] = total
    shared[...] = total[:8]
    shared_hops = head_hops(0, shared, shared_got)
    for hop in shared_hops:
        hop.start()
    ring.advance()
    rows.finish()
    backs = home_copies(order, grads, input_grad_ref, grad_sems)
    for copy in backs:
        copy.start()
    for hop in shared_hops:
        hop.wait_recv()
    small_ref[0:8] = shared[...] + (shared_got[0] + shared_got[1] + shared_got[2])
    small_ref[1:2] = shared[1:2]
    ring.finish()
    low_from = 2 * DV + 2 * DK
    tail_ref[...] = sums_ref[:, low_from : low_from + 128]
    tail_hops = head_hops(1, tail_ref, tail_got)
    for hop in tail_hops:
        hop.start()
    for hop in tail_hops:
        hop.wait_recv()
    for hop in stage_hops + shared_hops + tail_hops:
        hop.wait_send()
    tail_ref[...] = tail_ref[...] + (tail_got[0] + tail_got[1] + tail_got[2])
    for copy in backs:
        copy.wait()


def last_phase(
    part, inputs, d_resid, gains, normed, packed, d_attn, heads_out, ffn_gain, head_gain, bias, up
):
    count, heads = lax.axis_size("seq"), lax.axis_size("head")
    rows, width = part.shape
    share, quarter = width // count, rows // heads
    columns = packed.shape[1] + heads_out.shape[1]
    return remote_call(
        functools.partial(last_phase_kernel, ring_order(count), heads),
        6,
        [LOAD, AWAY, LOAD, NEAR, AWAY, LOAD, AWAY, LOAD, NEAR, NEAR, NEAR, NEAR],
        [AWAY, NEAR, NEAR, NEAR],
        [
            shape_of(BF16, rows, width),
            shape_of(F32, share, columns),
            shape_of(F32, SMALL, 128),
            shape_of(F32, share, 128),
        ],
        [
            pltpu.VMEM((quarter, width), BF16),
            pltpu.SemaphoreType.DMA((count,)),
            pltpu.VMEM((rows, width), BF16),
            pltpu.SemaphoreType.DMA((count,)),
            pltpu.VMEM((1, width), F32),
            pltpu.VMEM((count, SMALL, 128), F32),
            pltpu.VMEM((count - 1, SMALL, 128), F32),
            pltpu.VMEM((8, 128), F32),
            pltpu.VMEM((heads - 1, 8, 128), F32),
            pltpu.VMEM((heads - 1, share, 128), F32),
            pltpu.SemaphoreType.DMA((count - 1,)),
            pltpu.SemaphoreType.DMA((count - 1,)),
            pltpu.SemaphoreType.DMA((2, heads - 1)),
            pltpu.SemaphoreType.DMA((2, heads - 1)),
        ]
        + rows_scratch(quarter, width)
        + sum_scratch(count, rows, 2, share // 2, [packed.shape[1], DV]),
        (part, inputs, d_resid, gains, normed, packed, d_attn, heads_out, ffn_gain, head_gain, bias, up),
        2 * rows * width * columns,
    )


def leave_kernel(
    layer_ref, input_ref, first_ref, gate_ref, last_ref,
    layer_out, input_out, query_out, key_out, value_out, gates_out, attn_out, ffn_gate_out,
    ffn_up_out, ffn_down_out,
):
    hidden = gate_ref.shape[1]
    used = last_ref.shape[1] - DV
    layer_out[...] = layer_ref[...]
    input_out[...] = input_ref[...]
    ffn_gate_out[...] = gate_ref[...]
    ffn_up_out[...] = first_ref[:, hidden:]
    ffn_down_out[...] = first_ref[:, :hidden].T
    value_out[...] = last_ref[:, :DV]
    key_out[...] = last_ref[:, DV : DV + DK]
    query_out[...] = last_ref[:, DV + DK : DV + 2 * DK]
    gates_out[...] = last_ref[:, DV + 2 * DK : 2 * DV + 2 * DK]
    attn_out[...] = last_ref[:, used:].T


def leave(layer, input_grad, first, gate, last):
    share, hidden = gate.shape
    steps = share // 128

    def by_rows(field):
        return pl.BlockSpec((field.shape[0] // steps, field.shape[1]), lambda i: (i, 0))

    out_shape = [
        shape_of(BF16, *layer.shape),
        shape_of(BF16, *layer.shape),
        shape_of(F32, share, DK),
        shape_of(F32, share, DK),
        shape_of(F32, share, DV),
        shape_of(F32, share, DV),
        shape_of(F32, DV, share),
        shape_of(F32, share, hidden),
        shape_of(F32, share, hidden),
        shape_of(F32, hidden, share),
    ]
    specs = [by_rows(shape) for shape in out_shape]
    for n in (6, 9):
        specs[n] = pl.BlockSpec((out_shape[n].shape[0], 128), lambda i: (0, i))
    operands = (layer, input_grad, first, gate, last)
    return pl.pallas_call(
        leave_kernel,
        grid=(steps,),
        in_specs=[by_rows(field) for field in operands],
        out_specs=specs,
        out_shape=out_shape,
        compiler_params=pltpu.CompilerParams(
            dimension_semantics=("arbitrary",), vmem_limit_bytes=VMEM_BYTES
        ),
    )(*operands)


EARLY = 384


def matmul(left, right):
    return product(left, right, NN)


def matmul_nt(left, right):
    return product(left, right, NT)


def matmul_tn(left, right):
    return product(left, right, TN)


def ring_order(count):
    return list(range(0, count, 2)) + list(range(count - 1 - count % 2, 0, -2))


class Ring:
    def __init__(self, axis):
        self.axis = axis
        self.count = count = lax.axis_size(axis)
        order = ring_order(count)
        place = [order.index(i) for i in range(count)]
        self.right = [(order[i], order[(i + 1) % count]) for i in range(count)]
        self.left = [(order[i], order[(i - 1) % count]) for i in range(count)]
        owners = [[order[(place[i] + r) % count] for r in range(count)] for i in range(count)]
        slots = [[(place[i] - place[me]) % count for i in range(count)] for me in range(count)]
        mine = lax.axis_index(axis)
        self.owners = jnp.asarray(owners, jnp.int32)[mine]
        self.slots = jnp.asarray(slots, jnp.int32)[mine]

    def arrange(self, field, dim, table):
        width = field.shape[dim] // self.count
        return jnp.concatenate(
            [
                lax.dynamic_slice_in_dim(field, table[r] * width, width, dim)
                for r in range(self.count)
            ],
            axis=dim,
        )

    def near(self, field, dim):
        return self.arrange(field, dim, self.owners)

    def home(self, field, dim):
        return self.arrange(field, dim, self.slots)

    def gather(self, block, after=None):
        count, half = self.count, block.shape[0] // 2
        up, down = block[:half], block[half:]
        if after is not None:
            up, down, _ = lax.optimization_barrier((up, down, after))
        pieces = [None] * (2 * count)
        pieces[0], pieces[1] = up, down
        for step in range(1, count):
            up = lax.ppermute(up, self.axis, self.right)
            down = lax.ppermute(down, self.axis, self.left)
            pieces[2 * (count - step)] = up
            pieces[2 * step + 1] = down
            if step == count - 2:
                late = up[:8, :128]
        return jnp.concatenate(pieces, axis=0), late

    def scatter(self, total):
        count = self.count
        rows = total.shape[0] // count
        half = rows // 2

        def piece(slot, part):
            start = slot * rows + part * half
            return total[start : start + half]

        up, down = piece(count - 1, 0), piece(1, 1)
        for step in range(count - 1):
            up = lax.ppermute(up, self.axis, self.right)
            down = lax.ppermute(down, self.axis, self.left)
            up = wide(up) + wide(piece(count - 2 - step, 0))
            down = wide(down) + wide(piece((step + 2) % count, 1))
            if step < count - 2:
                up, down = narrow(up), narrow(down)
        return jnp.concatenate([up, down], axis=0)


def swap(axis, distance):
    return [(i, i ^ distance) for i in range(lax.axis_size(axis))]


def head_scatter(part):
    count, mine = lax.axis_size("head"), lax.axis_index("head")
    rows = part.shape[0] // count
    held = part.reshape((count, rows) + part.shape[1:])
    distance = 1
    while distance < count:
        bit = (mine // distance) % 2
        split = held.reshape((held.shape[0] // 2, 2) + held.shape[1:])
        sent = lax.dynamic_index_in_dim(split, 1 - bit, 1, False)
        kept = lax.dynamic_index_in_dim(split, bit, 1, False)
        got = lax.ppermute(narrow(sent), "head", swap("head", distance))
        held = wide(kept) + wide(got)
        distance *= 2
    return held[0]


def head_gather(share):
    count, mine = lax.axis_size("head"), lax.axis_index("head")
    held = share[None]
    distance = count // 2
    while distance:
        bit = (mine // distance) % 2
        got = lax.ppermute(held, "head", swap("head", distance))
        lower = jnp.where(bit == 0, held, got)
        upper = jnp.where(bit == 0, got, held)
        held = jnp.stack([lower, upper], axis=1).reshape((-1,) + share.shape)
        distance //= 2
    return held.reshape((-1,) + share.shape[1:])


def with_decay(state, decay):
    high = narrow(decay)
    low = narrow(decay - wide(high))
    return jnp.concatenate([narrow(state), high, low], axis=1)


def split_decay(message):
    rows = message.shape[1] - 2
    decay = wide(message[:, rows : rows + 1]) + wide(message[:, rows + 1 :])
    return wide(message[:, :rows]), decay


def entering(state, decay, later):
    count, mine = lax.axis_size("seq"), lax.axis_index("seq")
    inner = mine % 2
    ahead = (inner == 0) != later
    half = state.shape[1] // 2
    kept = wide(lax.dynamic_slice_in_dim(state, inner * half, half, 1))
    sent = lax.dynamic_slice_in_dim(state, (1 - inner) * half, half, 1)
    pair = swap("seq", 1)
    other, other_decay = split_decay(lax.ppermute(with_decay(sent, decay), "seq", pair))
    earliest = jnp.where(ahead, kept, other)
    joined = jnp.where(ahead, other_decay, decay) * earliest + jnp.where(ahead, other, kept)
    message = with_decay(joined, decay * other_decay)
    if later:
        chain = [(i, i - 2) for i in range(2, count)]
    else:
        chain = [(i, i + 2) for i in range(count - 2)]
    before, reach = jnp.zeros_like(kept), jnp.ones_like(decay)
    for _ in range(count // 2 - 1):
        message = lax.ppermute(message, "seq", chain)
        far, far_decay = split_decay(message)
        before = before + reach * far
        reach = reach * far_decay
    second = jnp.where(ahead, decay, other_decay) * before + earliest
    got = lax.ppermute(narrow(jnp.where(ahead, second, before)), "seq", pair)
    own = narrow(jnp.where(ahead, before, second))
    return jnp.concatenate(
        [jnp.where(inner == 0, own, got), jnp.where(inner == 0, got, own)], axis=1
    )


def columns_of(vector, rows):
    width = -(-vector.shape[-1] // rows)
    pad = [(0, 0)] * (vector.ndim - 1) + [(0, width * rows - vector.shape[-1])]
    shaped = jnp.pad(vector, pad).reshape(vector.shape[:-1] + (width, rows))
    return jnp.swapaxes(shaped, -1, -2)


def plain_layer(
    layer_in,
    seg_starts,
    attn_gain,
    query_weight,
    key_weight,
    value_weight,
    gate_weight,
    decay_down,
    decay_up,
    decay_bias,
    head_gain,
    out_weight,
    ffn_gain,
    ffn_gate,
    ffn_up,
    ffn_down,
    out_grad,
):
    ring = Ring("seq")
    count = ring.count
    batch, block, width = layer_in.shape
    rows = batch * block
    chunks = block // CHUNK
    rank, share = decay_down.shape[1], attn_gain.shape[0]
    hidden = ffn_gate.shape[1]

    smalls = [attn_gain, ffn_gain, head_gain, decay_bias, decay_up.reshape(-1)]
    ends = [sum(part.size for part in smalls[: i + 1]) for i in range(len(smalls))]
    small = jnp.pad(jnp.concatenate(smalls), (0, -ends[-1] % 128))[None]
    shard = jnp.concatenate(
        [value_weight, key_weight, query_weight, gate_weight, out_weight.T, decay_down], axis=1
    )
    inputs = layer_in.reshape(rows, width)
    weights, mark = ring.gather(shard)
    small = lax.all_gather(small, "seq")
    gain = wide(small[:, 0, :share]).reshape(width)
    normed = ring.near(narrow(wide(inputs) * root_scale(wide(inputs)) * gain), 1)
    projected = matmul(normed, weights)
    value_key, query = narrow(projected[:, : DV + DK]), narrow(projected[:, DV + DK : DV + 2 * DK])
    gates, low = projected[:, DV + 2 * DK : 2 * DV + 2 * DK], projected[:, -rank:]
    third, mark = ring.gather(jnp.concatenate([ffn_gate, ffn_up], axis=1), mark)
    fdown_t, mark = ring.gather(ffn_down.T, mark)
    projections = weights[:, : 2 * DV + 2 * DK]
    out_t, down_all = weights[:, 2 * DV + 2 * DK : -rank], weights[:, -rank:]
    small = small[:, 0]
    gain_one = wide(ring.near(small[:, : ends[0]], 0)).reshape(width)
    gain_two = wide(ring.near(small[:, ends[0] : ends[1]], 0)).reshape(width)
    gain_head = wide(small[:, ends[1] : ends[2]]).reshape(1, DV)
    bias_all = wide(small[:, ends[2] : ends[3]]).reshape(1, DK)
    up_all = small[:, ends[3] : ends[4]].reshape(count, rank, -1)
    up_all = wide(jnp.swapaxes(up_all, 0, 1).reshape(rank, DK))

    starts = seg_starts.reshape(batch, chunks, CHUNK).astype(jnp.float32)
    places = jnp.arange(CHUNK)
    lower = (places[:, None] >= places[None, :]).astype(jnp.float32)
    marks = jnp.einsum("bcs,ts->bct", starts, lower, precision=HIGH)
    column, row = marks.reshape(batch, block, 1), jnp.swapaxes(marks, 0, 1)[:, :, None, :]

    grad_rows = ring.near(out_grad.reshape(rows, width), 1)
    head = lax.axis_index("head")
    quarter = rows // lax.axis_size("head")
    inputs_own = lax.dynamic_slice_in_dim(inputs, head * quarter, quarter, 0)
    inputs_own = wide(ring.near(inputs_own, 1))
    grad_own = wide(lax.dynamic_slice_in_dim(grad_rows, head * quarter, quarter, 0))

    def tokens(field):
        return field.reshape(batch, block, field.shape[-1])

    value_key, query, gates, low = map(tokens, (value_key, query, gates, low))
    run, slope, state, total = local_states(value_key, low, up_all, bias_all, column)
    state_in = entering(state, total, False)
    heads, mixed, states = mix(query, value_key, run, column, row, state_in, gates, gain_head)
    heads = heads.reshape(rows, DV)
    resid = inputs_own + head_scatter(narrow(matmul_nt(heads, out_t)))
    scale_two = root_scale(resid)
    unit_two = resid * scale_two
    normed_two = head_gather(narrow(unit_two * gain_two))
    pre_gate = matmul(normed_two, third[:, :hidden])
    pre_up = matmul(normed_two, third[:, hidden:])
    sigma = jax.nn.sigmoid(pre_gate)
    act = narrow(pre_gate * sigma * pre_up)
    layer_out = narrow(resid + head_scatter(narrow(matmul_nt(act, fdown_t))))
    layer_out = ring.home(head_gather(layer_out), 1)

    d_act = matmul(grad_rows, fdown_t)
    grad_fdown = ring.scatter(narrow(matmul_tn(grad_rows, act)))
    d_gate = narrow(d_act * pre_up * sigma * (1.0 + pre_gate * (1.0 - sigma)))
    d_up = narrow(d_act * pre_gate * sigma)
    d_third = jnp.concatenate([d_gate, d_up], axis=1)
    grad_third = ring.scatter(narrow(matmul_tn(normed_two, d_third)))
    d_normed_two = head_scatter(narrow(matmul_nt(d_third, third)))
    grad_gain_two = jnp.sum(d_normed_two * unit_two, axis=0)
    d_resid = grad_own + norm_back(d_normed_two * gain_two, unit_two, scale_two)
    d_attn = head_gather(narrow(d_resid))
    d_heads = tokens(matmul(d_attn, out_t))
    d_gates, d_mixed, grad_gain_head, state_grad = head_back(
        d_heads, gates, mixed, gain_head, query, run, column
    )
    state_back = entering(state_grad, total, True)
    d_query, d_value, d_key, d_low, grad_up, grad_bias = mix_back(
        query, value_key, run, slope, column, row, d_mixed, states, state_back, low, up_all
    )
    d_gates = d_gates.reshape(rows, DV)
    grad_out = matmul_tn(d_attn, heads)
    grad_gate = matmul_tn(normed, d_gates)
    grad_fourth = ring.scatter(narrow(jnp.concatenate([grad_gate, grad_out], axis=1)))
    d_low = narrow(d_low.reshape(rows, rank))
    d_last = jnp.concatenate(
        [d_value.reshape(rows, DV), d_key.reshape(rows, DK), d_query.reshape(rows, DK)], axis=1
    )
    d_normed_part = (
        matmul_nt(jnp.concatenate([d_last, d_gates], axis=1), projections)
        + matmul_nt(d_low, down_all)
    )
    d_normed = head_scatter(narrow(d_normed_part))
    scale_own = root_scale(inputs_own)
    unit_own = inputs_own * scale_own
    d_unit = norm_back(d_normed * gain_one, unit_own, scale_own)
    input_grad = ring.home(head_gather(narrow(d_resid + d_unit)), 1)
    unit_all = ring.near(wide(inputs) * root_scale(wide(inputs)), 1)
    grad_gain_one = jnp.sum(d_normed_part * unit_all, axis=0)

    small = jnp.concatenate(
        [
            grad_gain_head.reshape(count, -1),
            grad_bias.reshape(count, -1),
            jnp.swapaxes(grad_up.reshape(rank, count, -1), 0, 1).reshape(count, -1),
        ],
        axis=1,
    )
    small = columns_of(ring.near(small, 0), share).reshape(width, -1)
    small = jnp.concatenate([grad_gain_one[:, None], grad_gain_two[:, None], small], axis=1)
    used = d_last.shape[1] + rank
    spare = -(used + small.shape[1]) % 128
    d_last = jnp.concatenate(
        [d_last, d_low, jnp.zeros((rows, small.shape[1] + spare), BF16)], axis=1
    )
    grad_last = matmul_tn(normed, d_last) + jnp.pad(small, ((0, 0), (used, spare)))
    grad_last = ring.scatter(narrow(grad_last))
    shared = grad_last[:, used - rank :]
    distance = 1
    while distance < lax.axis_size("head"):
        shared = shared + lax.ppermute(shared, "head", swap("head", distance))
        distance *= 2

    def lone(field):
        return jnp.swapaxes(field[:, rank + 2 : rank + small.shape[1]], 0, 1).reshape(-1)

    own = lone(grad_last[:, used - rank :])
    bounds = [0, head_gain.size, head_gain.size + decay_bias.size]
    bounds.append(bounds[2] + decay_up.size)
    return (
        layer_out.reshape(batch, block, width),
        input_grad.reshape(batch, block, width),
        shared[:, rank],
        grad_last[:, DV + DK : DV + 2 * DK],
        grad_last[:, DV : DV + DK],
        grad_last[:, :DV],
        grad_fourth[:, :DV],
        shared[:, :rank],
        own[bounds[2] : bounds[3]].reshape(rank, -1),
        own[bounds[1] : bounds[2]],
        lone(shared)[: bounds[1]],
        grad_fourth[:, DV:].T,
        shared[:, rank + 1],
        grad_third[:, :hidden],
        grad_third[:, hidden:],
        grad_fdown.T,
    )


def fused_layer(
    layer_in,
    seg_starts,
    attn_gain,
    query_weight,
    key_weight,
    value_weight,
    gate_weight,
    decay_down,
    decay_up,
    decay_bias,
    head_gain,
    out_weight,
    ffn_gain,
    ffn_gate,
    ffn_up,
    ffn_down,
    out_grad,
):
    count = lax.axis_size("seq")
    batch, block, width = layer_in.shape
    rows = batch * block
    rank, share = decay_down.shape[1], attn_gain.shape[0]
    hidden = ffn_gate.shape[1]
    used = 2 * DV + 2 * DK
    inputs, grad_rows = layer_in.reshape(rows, width), out_grad.reshape(rows, width)
    starts = seg_starts.reshape(-1, CHUNK)
    small = jnp.concatenate([attn_gain, ffn_gain, head_gain, decay_bias])
    small = jnp.pad(small, (0, -small.size % 128))[None]

    def tokens(field):
        return field.reshape(batch, block, field.shape[-1])

    (
        normed, weights, out_t, down_block, down, value_key, query, gates, low, gains, gain_head, bias, up
    ) = enter(
        inputs, value_weight, key_weight, query_weight, gate_weight, decay_down, out_weight, ffn_down,
        small, decay_up,
    )
    value_key, query, gates, low = map(tokens, (value_key, query, gates, low))
    weights, out_t = weights.reshape(width, -1), out_t.reshape(width, DV)
    run, slope, total, mixed, heads, states, part, fgate, fdown = token_phase(
        value_key, query, gates, low, up, bias, starts, gain_head, out_t, ffn_gate, down_block, EARLY
    )
    resid, normed_two, fup = row_phase(part, inputs, gains, ffn_up)
    fgate, fup = fgate.reshape(width, hidden), fup.reshape(width, hidden)
    act, d_gate, d_up, ffn_part, part = unit_phase(normed_two, fgate, fup, grad_rows, down_block, fdown)
    (
        d_resid, d_attn, d_gates, d_mixed, state_back, grad_gain_two, grad_gain_head, layer_out, grad_first
    ) = resid_phase(
        part, resid, grad_rows, gains, out_t, act, normed_two, d_up, gates, mixed, gain_head, query,
        run, starts, total, ffn_part,
    )
    packed, grad_up, grad_bias, part, grad_fgate = back_phase(
        query, value_key, run, slope, states, low, up, starts, d_mixed, state_back, d_gates,
        normed_two, d_gate, weights, down,
    )
    packed = packed.reshape(rows, -1)
    input_grad, grad_last, small, tail = last_phase(
        part, inputs, d_resid, gains, normed, packed, d_attn, heads.reshape(rows, DV),
        grad_gain_two, grad_gain_head, grad_bias, grad_up,
    )
    lines = share // 128
    results = leave(layer_out, input_grad, grad_first, grad_fgate, grad_last)
    layer_out, input_grad, grad_query, grad_key, grad_value, grad_gate, grad_out = results[:7]
    return (
        layer_out.reshape(batch, block, width),
        input_grad.reshape(batch, block, width),
        small[2 : 2 + lines].reshape(share),
        grad_query,
        grad_key,
        grad_value,
        grad_gate,
        tail[:, :rank],
        small[8:, : decay_up.shape[1]],
        small[1, : decay_bias.size],
        small[0, : head_gain.size],
        grad_out,
        small[4 : 4 + lines].reshape(share),
        *results[7:],
    )


def shards(layer_in, seg_starts, attn_gain, *rest):
    fits = attn_gain.shape[0] == 256 and lax.axis_size("head") == 4
    layer = fused_layer if fits and rest[4].shape[1] == 16 else plain_layer
    return layer(layer_in, seg_starts, attn_gain, *rest)


def solution(mesh):
    return jax.shard_map(
        shards,
        mesh=mesh,
        in_specs=(
            P(None, "seq", None),
            P(None, "seq"),
            P("seq"),
            P("seq", "head"),
            P("seq", "head"),
            P("seq", "head"),
            P("seq", "head"),
            P("seq", None),
            P(None, ("head", "seq")),
            P(("head", "seq")),
            P("seq"),
            P("head", "seq"),
            P("seq"),
            P("seq", "head"),
            P("seq", "head"),
            P("head", "seq"),
            P(None, "seq", None),
        ),
        out_specs=(
            P(None, "seq", None),
            P(None, "seq", None),
            P("seq"),
            P("seq", "head"),
            P("seq", "head"),
            P("seq", "head"),
            P("seq", "head"),
            P("seq", None),
            P(None, ("head", "seq")),
            P(("head", "seq")),
            P("seq"),
            P("head", "seq"),
            P("seq"),
            P("seq", "head"),
            P("seq", "head"),
            P("head", "seq"),
        ),
        check_vma=False,
    )
```

```python
import functools

import jax
import jax.numpy as jnp
from jax import lax
from jax.experimental import pallas as pl
from jax.experimental.pallas import tpu as pltpu
from jax.sharding import PartitionSpec as P

DK = 256
DV = 512
CHUNK = 128
EPS = 1e-06
HIGH = lax.Precision.HIGHEST
NN = (((1,), (0,)), ((), ()))
NT = (((1,), (1,)), ((), ()))
TN = (((0,), (0,)), ((), ()))
VMEM_BYTES = 60 * 1024 * 1024
MESH = pl.DeviceIdType.MESH


def product(left, right, dims, precision=None):
    return lax.dot_general(
        left, right, dims, precision=precision, preferred_element_type=jnp.float32
    )


def narrow(field):
    return field.astype(jnp.bfloat16)


def wide(field):
    return field.astype(jnp.float32)


def root_scale(field):
    return lax.rsqrt(jnp.mean(field * field, axis=-1, keepdims=True) + EPS)


def norm_back(upstream, unit, scale):
    return scale * (upstream - unit * jnp.mean(upstream * unit, axis=-1, keepdims=True))


def triangle(lower):
    rows = lax.broadcasted_iota(jnp.int32, (CHUNK, CHUNK), 0)
    columns = lax.broadcasted_iota(jnp.int32, (CHUNK, CHUNK), 1)
    return (rows >= columns if lower else rows <= columns).astype(jnp.float32)


def permitted(mark_column, mark_row):
    rows = lax.broadcasted_iota(jnp.int32, (CHUNK, CHUNK), 0)
    columns = lax.broadcasted_iota(jnp.int32, (CHUNK, CHUNK), 1)
    return (rows >= columns) & (mark_column == mark_row)


def state_chunk(
    value_ref, key_ref, low_ref, up_ref, bias_ref, mark_ref, run_ref, slope_ref, state, total
):
    lower = triangle(True)
    for b in range(value_ref.shape[0]):
        raw = product(low_ref[b], up_ref[...], NN, HIGH) + bias_ref[...]
        soft = jnp.log1p(jnp.exp(-jnp.abs(raw)))
        decay = (jnp.minimum(raw, 0.0) - soft) / 16.0
        slope_ref[b] = jnp.exp(jnp.minimum(-raw, 0.0) - soft) / 16.0
        run = product(lower, decay, NN, HIGH)
        run_ref[b] = run
        mark = mark_ref[b]
        last = run[CHUNK - 1 :]
        trailing = mark == mark[CHUNK - 1 :]
        kept = jnp.where(trailing, jnp.exp(last - run), 0.0)
        keep = jnp.where(mark[CHUNK - 1 :] == 0.0, jnp.exp(last), 0.0)
        tail = narrow(wide(key_ref[b]) * kept)
        state[b] = state[b] * keep + product(value_ref[b], tail, TN)
        total[b] = total[b] * keep


def state_kernel(
    value_ref, key_ref, low_ref, up_ref, bias_ref, mark_ref,
    run_ref, slope_ref, state_ref, total_ref, state, total,
):
    step = pl.program_id(0)

    @pl.when(step == 0)
    def _():
        state[...] = jnp.zeros_like(state)
        total[...] = jnp.ones_like(total)

    state_chunk(
        value_ref, key_ref, low_ref, up_ref, bias_ref, mark_ref, run_ref, slope_ref, state, total
    )

    @pl.when(step == pl.num_programs(0) - 1)
    def _():
        state_ref[...] = narrow(state[...])
        total_ref[...] = total[...]


def mixer_chunk(
    query_ref, value_ref, key_ref, run_ref, mark_ref, row_ref, gate_ref, gain_ref,
    heads_ref, mixed_ref, states_ref, state,
):
    for b in range(value_ref.shape[0]):
        run, mark = run_ref[b], mark_ref[b]
        middle, last = run[CHUNK // 2 - 1 : CHUNK // 2], run[CHUNK - 1 :]
        query = wide(query_ref[b]) * DK ** (-0.5)
        key = wide(key_ref[b])
        start = narrow(state[b])
        states_ref[0, b] = start
        scores = product(
            narrow(query * jnp.exp(run - middle)), narrow(key * jnp.exp(middle - run)), NT
        )
        scores = jnp.where(permitted(mark, row_ref[0, b]), scores, 0.0)
        opened = narrow(query * jnp.where(mark == 0.0, jnp.exp(run), 0.0))
        mixed = product(narrow(scores), value_ref[b], NN) + product(opened, start, NT)
        kept = jnp.where(mark == mark[CHUNK - 1 :], jnp.exp(last - run), 0.0)
        keep = jnp.where(mark[CHUNK - 1 :] == 0.0, jnp.exp(last), 0.0)
        state[b] = state[b] * keep + product(value_ref[b], narrow(key * kept), TN)
        states_ref[1, b] = narrow(state[b])
        mixed_ref[b] = mixed
        gate = gate_ref[b]
        active = gate * jax.nn.sigmoid(gate)
        heads_ref[b] = narrow(mixed * root_scale(mixed) * gain_ref[...] * active)


def mixer_kernel(
    query_ref, value_ref, key_ref, run_ref, mark_ref, row_ref, first_ref, gate_ref, gain_ref,
    heads_ref, mixed_ref, states_ref, state,
):
    @pl.when(pl.program_id(0) == 0)
    def _():
        state[...] = wide(first_ref[...])

    mixer_chunk(
        query_ref, value_ref, key_ref, run_ref, mark_ref, row_ref, gate_ref, gain_ref,
        heads_ref, mixed_ref, states_ref, state,
    )


def head_back_chunk(
    grad_ref, gate_ref, mixed_ref, gain_ref, query_ref, run_ref, mark_ref,
    gate_grad_ref, mixed_grad_ref, gain_grad_ref, state,
):
    gain = gain_ref[...]
    for b in range(grad_ref.shape[0]):
        mixed, gate, grad = mixed_ref[b], gate_ref[b], wide(grad_ref[b])
        scale = root_scale(mixed)
        unit = mixed * scale
        sigma = jax.nn.sigmoid(gate)
        active = gate * sigma
        gate_grad_ref[b] = narrow(grad * unit * gain * sigma * (1.0 + gate * (1.0 - sigma)))
        weighted = grad * active
        gain_grad_ref[...] += jnp.sum(weighted * unit, axis=0, keepdims=True)
        mixed_grad = narrow(norm_back(weighted * gain, unit, scale))
        mixed_grad_ref[b] = mixed_grad
        run, mark = run_ref[b], mark_ref[b]
        last = run[CHUNK - 1 :]
        query = wide(query_ref[b]) * DK ** (-0.5)
        opened = narrow(query * jnp.where(mark == 0.0, jnp.exp(run), 0.0))
        keep = jnp.where(mark[CHUNK - 1 :] == 0.0, jnp.exp(last), 0.0)
        state[b] = state[b] * keep + product(mixed_grad, opened, TN)


def head_back_kernel(
    grad_ref, gate_ref, mixed_ref, gain_ref, query_ref, run_ref, mark_ref,
    gate_grad_ref, mixed_grad_ref, gain_grad_ref, state_ref, state,
):
    step = pl.program_id(0)

    @pl.when(step == 0)
    def _():
        state[...] = jnp.zeros_like(state)
        gain_grad_ref[...] = jnp.zeros_like(gain_grad_ref)

    head_back_chunk(
        grad_ref, gate_ref, mixed_ref, gain_ref, query_ref, run_ref, mark_ref,
        gate_grad_ref, mixed_grad_ref, gain_grad_ref, state,
    )

    @pl.when(step == pl.num_programs(0) - 1)
    def _():
        state_ref[...] = narrow(state[...])


def mixer_back_chunk(
    query_ref, value_ref, key_ref, run_ref, slope_ref, mark_ref, row_ref, grad_ref,
    start_ref, end_ref, low_ref, up_ref,
    query_grad_ref, value_grad_ref, key_grad_ref, low_grad_ref, up_grad_ref, bias_grad_ref, state,
):
    upper = triangle(False)
    for b in range(value_ref.shape[0]):
        run, mark = run_ref[b], mark_ref[b]
        middle, last = run[CHUNK // 2 - 1 : CHUNK // 2], run[CHUNK - 1 :]
        query = wide(query_ref[b]) * DK ** (-0.5)
        key, value, grad = wide(key_ref[b]), value_ref[b], grad_ref[b]
        start, later = start_ref[0, b], narrow(state[b])
        rise, fall = jnp.exp(run - middle), jnp.exp(middle - run)
        opens = jnp.where(mark == 0.0, jnp.exp(run), 0.0)
        kept = jnp.where(mark == mark[CHUNK - 1 :], jnp.exp(last - run), 0.0)
        keep = jnp.where(mark[CHUNK - 1 :] == 0.0, jnp.exp(last), 0.0)
        allowed = permitted(mark, row_ref[0, b])
        risen, fallen = narrow(query * rise), narrow(key * fall)
        scores = narrow(jnp.where(allowed, product(risen, fallen, NT), 0.0))
        scores_grad = narrow(jnp.where(allowed, product(grad, value, NT), 0.0))
        query_grad = rise * product(scores_grad, fallen, NN) + opens * product(grad, start, NN)
        key_grad = fall * product(scores_grad, risen, TN) + kept * product(value, later, NN)
        value_grad = product(scores, grad, TN) + product(narrow(key * kept), later, NT)
        ends = jnp.sum(state[b] * wide(end_ref[0, b]), axis=0, keepdims=True)
        state[b] = state[b] * keep + product(grad, narrow(query * opens), TN)
        turn = query * query_grad - key * key_grad
        raw_grad = (product(upper, turn, NN, HIGH) + ends) * slope_ref[b]
        query_grad_ref[b] = narrow(query_grad * DK ** (-0.5))
        key_grad_ref[b] = narrow(key_grad)
        value_grad_ref[b] = narrow(value_grad)
        low_grad = narrow(product(raw_grad, up_ref[...], NT, HIGH))
        low_grad_ref[b, :, : low_grad.shape[1]] = low_grad
        up_grad_ref[...] += product(low_ref[b], raw_grad, TN, HIGH)
        bias_grad_ref[...] += jnp.sum(raw_grad, axis=0, keepdims=True)


def mixer_back_kernel(
    query_ref, value_ref, key_ref, run_ref, slope_ref, mark_ref, row_ref, grad_ref,
    start_ref, end_ref, last_ref, low_ref, up_ref,
    query_grad_ref, value_grad_ref, key_grad_ref, low_grad_ref, up_grad_ref, bias_grad_ref, state,
):
    @pl.when(pl.program_id(0) == 0)
    def _():
        state[...] = wide(last_ref[...])
        up_grad_ref[...] = jnp.zeros_like(up_grad_ref)
        bias_grad_ref[...] = jnp.zeros_like(bias_grad_ref)

    mixer_back_chunk(
        query_ref, value_ref, key_ref, run_ref, slope_ref, mark_ref, row_ref, grad_ref,
        start_ref, end_ref, low_ref, up_ref,
        query_grad_ref, value_grad_ref, key_grad_ref, low_grad_ref, up_grad_ref, bias_grad_ref,
        state,
    )


def along(batch, width, last=0, reverse=0):
    if reverse:
        return pl.BlockSpec((batch, CHUNK, width), lambda i: (0, reverse - 1 - i, last))
    return pl.BlockSpec((batch, CHUNK, width), lambda i: (0, i, last))


def still(*shape):
    return pl.BlockSpec(shape, lambda i: (0,) * len(shape))


def shape_of(dtype, *shape):
    return jax.ShapeDtypeStruct(shape, dtype)


def call(kernel, steps, in_specs, out_specs, out_shape, scratch, operands, flops):
    moved = sum(a.size * a.dtype.itemsize for a in operands)
    moved += sum(s.size * s.dtype.itemsize for s in out_shape)
    return pl.pallas_call(
        kernel,
        grid=(steps,),
        in_specs=in_specs,
        out_specs=out_specs,
        out_shape=out_shape,
        scratch_shapes=scratch,
        cost_estimate=pl.CostEstimate(flops=flops, bytes_accessed=moved, transcendentals=0),
        compiler_params=pltpu.CompilerParams(
            dimension_semantics=("arbitrary",), vmem_limit_bytes=VMEM_BYTES
        ),
    )(*operands)


F32, BF16 = jnp.float32, jnp.bfloat16


def local_states(value_key, low, up, bias, mark):
    batch, block, rank = low.shape
    steps = block // CHUNK
    return call(
        state_kernel,
        steps,
        [along(batch, DV), along(batch, DK, DV // DK), along(batch, rank), still(rank, DK),
         still(1, DK), along(batch, 1)],
        [along(batch, DK), along(batch, DK), still(batch, DV, DK), still(batch, 1, DK)],
        [shape_of(F32, batch, block, DK), shape_of(F32, batch, block, DK),
         shape_of(BF16, batch, DV, DK), shape_of(F32, batch, 1, DK)],
        [pltpu.VMEM((batch, DV, DK), F32), pltpu.VMEM((batch, 1, DK), F32)],
        (value_key, value_key, low, up, bias, mark),
        2 * batch * block * DK * (DV + 6 * CHUNK),
    )


def mix(query, value_key, run, mark, row, first, gates, gain):
    batch, block, _ = run.shape
    steps = block // CHUNK
    heads, mixed, states = call(
        mixer_kernel,
        steps,
        [along(batch, DK), along(batch, DV), along(batch, DK, DV // DK), along(batch, DK),
         along(batch, 1), pl.BlockSpec((1, batch, 1, CHUNK), lambda i: (i, 0, 0, 0)),
         still(batch, DV, DK), along(batch, DV), still(1, DV)],
        [along(batch, DV), along(batch, DV),
         pl.BlockSpec((2, batch, DV, DK), lambda i: (i, 0, 0, 0))],
        [shape_of(BF16, batch, block, DV), shape_of(F32, batch, block, DV),
         shape_of(BF16, 2 * steps, batch, DV, DK)],
        [pltpu.VMEM((batch, DV, DK), F32)],
        (query, value_key, value_key, run, mark, row, first, gates, gain),
        2 * batch * block * DK * (2 * DV + 3 * CHUNK),
    )
    return heads, mixed, states


def head_back(grad, gates, mixed, gain, query, run, mark):
    batch, block, _ = run.shape
    steps = block // CHUNK
    return call(
        head_back_kernel,
        steps,
        [along(batch, DV, 0, steps), along(batch, DV, 0, steps), along(batch, DV, 0, steps),
         still(1, DV), along(batch, DK, 0, steps), along(batch, DK, 0, steps),
         along(batch, 1, 0, steps)],
        [along(batch, DV, 0, steps), along(batch, DV, 0, steps), still(1, DV),
         still(batch, DV, DK)],
        [shape_of(BF16, batch, block, DV), shape_of(BF16, batch, block, DV),
         shape_of(F32, 1, DV), shape_of(BF16, batch, DV, DK)],
        [pltpu.VMEM((batch, DV, DK), F32)],
        (grad, gates, mixed, gain, query, run, mark),
        2 * batch * block * DK * DV,
    )


def mix_back(query, value_key, run, slope, mark, row, grad, states, later, low, up):
    batch, block, rank = low.shape
    steps = block // CHUNK
    return call(
        mixer_back_kernel,
        steps,
        [along(batch, DK, 0, steps), along(batch, DV, 0, steps),
         along(batch, DK, DV // DK, steps), along(batch, DK, 0, steps),
         along(batch, DK, 0, steps), along(batch, 1, 0, steps),
         pl.BlockSpec((1, batch, 1, CHUNK), lambda i: (steps - 1 - i, 0, 0, 0)),
         along(batch, DV, 0, steps),
         pl.BlockSpec((1, batch, DV, DK), lambda i: (2 * (steps - 1 - i), 0, 0, 0)),
         pl.BlockSpec((1, batch, DV, DK), lambda i: (2 * (steps - 1 - i) + 1, 0, 0, 0)),
         still(batch, DV, DK), along(batch, rank, 0, steps), still(rank, DK)],
        [along(batch, DK, 0, steps), along(batch, DV, 0, steps), along(batch, DK, 0, steps),
         along(batch, rank, 0, steps), still(rank, DK), still(1, DK)],
        [shape_of(BF16, batch, block, DK), shape_of(BF16, batch, block, DV),
         shape_of(BF16, batch, block, DK), shape_of(BF16, batch, block, rank),
         shape_of(F32, rank, DK), shape_of(F32, 1, DK)],
        [pltpu.VMEM((batch, DV, DK), F32)],
        (query, value_key, value_key, run, slope, mark, row, grad, states, states, later, low, up),
        2 * batch * block * DK * (5 * DV + 6 * CHUNK),
    )


def place_of(table, index):
    found = jnp.int32(table[0])
    for i, entry in enumerate(table[1:], 1):
        found = jnp.where(index == i, jnp.int32(entry), found)
    return found


def block_at(order, distance):
    count = len(order)
    place = place_of([order.index(i) for i in range(count)], lax.axis_index("seq"))
    return place_of(order, lax.rem(place + distance + count, count))


def greet(axis, count):
    barrier, mine = pltpu.get_barrier_semaphore(), lax.axis_index(axis)
    for d in range(1, count):
        pl.semaphore_signal(
            barrier, inc=1, device_id={axis: lax.rem(mine + d, count)}, device_id_type=MESH
        )
    pl.semaphore_wait(barrier, count - 1)


def enter_kernel(
    order, ready, input_ref, value_ref, key_ref, query_weight_ref, gate_weight_ref, down_ref,
    out_block_ref, ffn_down_ref, small_ref, rise_ref,
    normed_out, weight_out, out_out, turned_ref, downs_ref, vk_ref, query_ref, gate_ref, low_ref,
    gains_ref, head_gain_ref, bias_ref, up_ref,
    normed_ref, weight_ref, out_ref, down_t, smalls_ref, rises_ref, total, low_total,
    places, keeps, small_send, small_receive, rise_send, rise_receive, down_send, down_receive,
    ring_send, ring_receive, out_send, out_receive,
):
    count = len(order)
    share, half = down_ref.shape[0], down_ref.shape[0] // 2
    rows, tile = input_ref.shape[0], 256
    mine = lax.axis_index("seq")
    placed, column = [], 0
    for n, ref in enumerate((value_ref, key_ref, query_weight_ref, gate_weight_ref)):
        target = weight_ref.at[0, :, pl.ds(column, ref.shape[1])]
        placed.append(pltpu.make_async_copy(ref, target, places.at[n]))
        placed[-1].start()
        column += ref.shape[1]
    ring = BlockRing(order, weight_ref.at[0], weight_ref, ring_send, ring_receive, None)
    out_ring = BlockRing(order, out_ref.at[0], out_ref, out_send, out_receive, None)
    down_t[...] = down_ref[...].T
    out_ref[0] = out_block_ref[...].T
    greet("seq", count)
    for copy in placed:
        copy.wait()
    ring.start()
    out_ring.start()

    def spread(source, target, send, receive):
        return [
            pltpu.make_async_remote_copy(
                src_ref=source,
                dst_ref=target.at[mine],
                send_sem=send.at[d - 1],
                recv_sem=receive.at[d - 1],
                device_id={"seq": lax.rem(mine + d, count)},
                device_id_type=MESH,
            )
            for d in range(1, count)
        ]

    smalls = spread(small_ref, smalls_ref, small_send, small_receive)
    smalls += spread(rise_ref, rises_ref, rise_send, rise_receive)
    smalls += spread(down_t, downs_ref, down_send, down_receive)
    for copy in smalls:
        copy.start()
    smalls_ref[mine] = small_ref[...]
    rises_ref[mine] = rise_ref[...]
    downs_ref[mine] = down_t[...]
    turned_ref[...] = ffn_down_ref[...].T
    ready()
    kept = []

    def keep(slot, side):
        part = pl.ds(side * half, half)
        column = pl.ds(slot * share + side * half, half)
        pairs = (
            (weight_ref.at[slot, part], weight_out.at[slot, part]),
            (out_ref.at[slot, part], out_out.at[slot, part]),
            (normed_ref.at[:, column], normed_out.at[:, column]),
        )
        for n, (source, target) in enumerate(pairs):
            kept.append(pltpu.make_async_copy(source, target, keeps.at[slot, side, n]))
            kept[-1].start()

    scales = []
    for t in range(rows // tile):
        field = wide(input_ref[t * tile : (t + 1) * tile])
        scales.append(root_scale(field))

    def multiply(first, second, begin):
        sides = []
        for slot, side in (first, second):
            start = slot * share + side * half
            sides.append((slot, side, gains_ref[0:1, start : start + half]))
        for t in range(rows // tile):
            here = slice(t * tile, (t + 1) * tile)
            parts, blocks, downs = [], [], []
            for slot, side, gain in sides:
                owner = block_at(order, slot)
                start = pl.multiple_of(owner * share + side * half, half)
                field = wide(input_ref[here, pl.ds(start, half)])
                part = narrow(field * scales[t] * gain)
                column = slot * share + side * half
                normed_ref[here, column : column + half] = part
                parts.append(part)
                blocks.append(weight_ref[slot, side * half : (side + 1) * half])
                downs.append(downs_ref[owner][:, side * half : (side + 1) * half])
            left = jnp.concatenate(parts, axis=1)
            added = product(left, jnp.concatenate(blocks, axis=0), NN)
            low_added = product(left, jnp.concatenate(downs, axis=1), NT)
            if begin:
                total[here] = added
                low_total[here] = low_added
            else:
                total[here] += added
                low_total[here] += low_added
        for slot, side in (first, second):
            keep(slot, side)

    for copy in smalls:
        copy.wait_recv()
    head_share, bias_share = DV // count, DK // count
    for j in range(count):
        near = wide(smalls_ref[block_at(order, j)])
        gains_ref[0:1, j * share : (j + 1) * share] = near[:, :share]
        gains_ref[1:2, j * share : (j + 1) * share] = near[:, share : 2 * share]
        block = wide(smalls_ref[j])
        at = 2 * share
        head_gain_ref[:, j * head_share : (j + 1) * head_share] = block[:, at : at + head_share]
        at += head_share
        bias_ref[:, j * bias_share : (j + 1) * bias_share] = block[:, at : at + bias_share]
        up_ref[:, j * bias_share : (j + 1) * bias_share] = wide(rises_ref[j])
    multiply((0, 0), (0, 1), True)
    for step in range(1, count):
        ring.advance()
        out_ring.advance()
        multiply((count - step, 0), (step, 1), False)
    vk_cols, query_cols = vk_ref.shape[1], query_ref.shape[1]
    vk_ref[...] = narrow(total[:, :vk_cols])
    query_ref[...] = narrow(total[:, vk_cols : vk_cols + query_cols])
    gate_ref[...] = total[:, vk_cols + query_cols :]
    low_ref[...] = low_total[...]
    for copy in smalls:
        copy.wait_send()
    ring.finish()
    out_ring.finish()
    for copy in kept:
        copy.wait()


def enter(inputs, value, key, query, gate, down, out_block, ffn_down, small, rise):
    count = lax.axis_size("seq")
    rows, width = inputs.shape
    share, rank = down.shape
    cols = 2 * DV + 2 * DK
    dma = [pltpu.SemaphoreType.DMA((count - 1,))] * 6
    whole, outs = (count, share, cols), (count, share, DV)
    return remote_call(
        functools.partial(enter_kernel, ring_order(count)),
        0,
        [LOAD] + [AWAY] * 4 + [NEAR] * 5,
        [AWAY] * 3 + [NEAR] * 10,
        [
            shape_of(BF16, rows, width),
            shape_of(BF16, *whole),
            shape_of(BF16, *outs),
            shape_of(BF16, share, ffn_down.shape[0]),
            shape_of(BF16, count, rank, share),
            shape_of(BF16, rows, DV + DK),
            shape_of(BF16, rows, DK),
            shape_of(F32, rows, DV),
            shape_of(F32, rows, rank),
            shape_of(F32, 2, width),
            shape_of(F32, 1, DV),
            shape_of(F32, 1, DK),
            shape_of(F32, rank, DK),
        ],
        [
            pltpu.VMEM((rows, width), BF16),
            pltpu.VMEM(whole, BF16),
            pltpu.VMEM(outs, BF16),
            pltpu.VMEM((rank, share), BF16),
            pltpu.VMEM((count, *small.shape), BF16),
            pltpu.VMEM((count, *rise.shape), BF16),
            pltpu.VMEM((rows, cols), F32),
            pltpu.VMEM((rows, rank), F32),
            pltpu.SemaphoreType.DMA((4,)),
            pltpu.SemaphoreType.DMA((count, 2, 3)),
        ]
        + dma
        + ring_semaphores(count)[:2]
        + ring_semaphores(count)[:2],
        (inputs, value, key, query, gate, down, out_block, ffn_down, small, rise),
        2 * rows * width * cols,
    )


PARTS = 2


class BlockRing:
    def __init__(self, order, block_ref, whole_ref, send, receive, local):
        self.count = count = len(order)
        half = block_ref.shape[0] // 2
        size = half // PARTS
        aims = (block_at(order, 1), block_at(order, -1))
        self.local = None
        if local is not None:
            self.local = pltpu.make_async_copy(block_ref, whole_ref.at[0], local)
        self.hops = {}
        for step in range(1, count):
            for side in range(2):
                held = (count - step + 1) if side == 0 else step - 1
                lands = (count - step) if side == 0 else step
                for n in range(PARTS):
                    part = pl.ds(side * half + n * size, size)
                    self.hops[step, n, side] = pltpu.make_async_remote_copy(
                        src_ref=(block_ref if step == 1 else whole_ref.at[held]).at[part],
                        dst_ref=whole_ref.at[lands, part],
                        send_sem=send.at[step - 1, side, n],
                        recv_sem=receive.at[step - 1, side, n],
                        device_id={"seq": aims[side]},
                        device_id_type=MESH,
                    )
        self.step = 1

    def start(self):
        for n in range(PARTS):
            for side in range(2):
                self.hops[1, n, side].start()
        if self.local is not None:
            self.local.start()

    def advance(self):
        if self.step < self.count:
            for n in range(PARTS):
                for side in range(2):
                    self.hops[self.step, n, side].wait_recv()
                    if self.step + 1 < self.count:
                        self.hops[self.step + 1, n, side].start()
            self.step += 1

    def finish(self):
        while self.step < self.count:
            self.advance()
        for copy in self.hops.values():
            copy.wait_send()
        if self.local is not None:
            self.local.wait()


def ring_semaphores(count):
    return [
        pltpu.SemaphoreType.DMA((count - 1, 2, PARTS)),
        pltpu.SemaphoreType.DMA((count - 1, 2, PARTS)),
        pltpu.SemaphoreType.DMA,
    ]


class Handover:
    def __init__(self, count, later, state, decay, scratch):
        (self.decays, self.sent, self.got, self.chain, decay_send, decay_receive, send, receive) = scratch
        self.count, self.later, self.state, self.decay = count, later, state, decay
        self.mine = mine = lax.axis_index("seq")
        self.inner = lax.rem(mine, 2)
        self.pairs = count // 2
        self.pair = mine // 2
        self.place = self.pairs - 1 - self.pair if later else self.pair
        beside = mine + 1 - 2 * self.inner
        self.beside = beside
        self.ahead = (self.inner == 0) != later
        self.half = state.shape[1] // 2
        onward = mine - 2 if later else mine + 2
        self.decay_copies = [
            pltpu.make_async_remote_copy(
                src_ref=decay,
                dst_ref=self.decays.at[mine],
                send_sem=decay_send.at[d - 1],
                recv_sem=decay_receive.at[d - 1],
                device_id={"seq": lax.rem(mine + d, count)},
                device_id_type=MESH,
            )
            for d in range(1, count)
        ]
        self.batch = state.shape[0]
        self.swaps = [
            [
                pltpu.make_async_remote_copy(
                    src_ref=self.sent.at[i, b],
                    dst_ref=self.got.at[i, b],
                    send_sem=send.at[i, b],
                    recv_sem=receive.at[i, b],
                    device_id={"seq": beside},
                    device_id_type=MESH,
                )
                for b in range(self.batch)
            ]
            for i in range(2)
        ]
        self.links = [
            [
                pltpu.make_async_remote_copy(
                    src_ref=self.chain.at[r, b],
                    dst_ref=self.chain.at[r + 1, b],
                    send_sem=send.at[2 + r, b],
                    recv_sem=receive.at[2 + r, b],
                    device_id={"seq": onward},
                    device_id_type=MESH,
                )
                for b in range(self.batch)
            ]
            for r in range(self.pairs - 1)
        ]

    def clear(self):
        self.chain[...] = jnp.zeros_like(self.chain)

    def rows(self, own):
        part = self.inner if own else 1 - self.inner
        return pl.ds(pl.multiple_of(part * self.half, self.half), self.half)

    def begin(self):
        self.decays[self.mine] = self.decay[...]
        for copy in self.decay_copies:
            copy.start()
        for b in range(self.batch):
            self.sent[0, b] = narrow(self.state[b, self.rows(False)])
            self.swaps[0][b].start()

    def firsts(self, b):
        kept, other = self.state[b, self.rows(True)], wide(self.got[0, b])
        decay, other_decay = self.decays[self.mine, b], self.decays[self.beside, b]
        return (
            jnp.where(self.ahead, kept, other),
            jnp.where(self.ahead, other, kept),
            jnp.where(self.ahead, decay, other_decay),
            jnp.where(self.ahead, other_decay, decay),
        )

    def sends(self, r):
        return (self.place >= r) & (self.place + 1 < self.pairs)

    def join(self):
        for copy in self.decay_copies:
            copy.wait_recv()
        for b in range(self.batch):
            self.swaps[0][b].wait_recv()
            first, second, _, decay = self.firsts(b)
            self.chain[0, b] = narrow(decay * first + second)

            @pl.when(self.sends(0))
            def _(b=b):
                self.links[0][b].start()

    def hop(self, r):
        for b in range(self.batch):

            @pl.when(self.place >= r)
            def _(b=b):
                self.links[r - 1][b].wait_recv()

            if r < self.pairs - 1:

                @pl.when(self.sends(r))
                def _(b=b):
                    self.links[r][b].start()

    def close(self):
        for b in range(self.batch):
            before = wide(self.chain[1, b])
            reach = None
            for r in range(2, self.pairs):
                far = self.pair + r - 1 if self.later else self.pair - r + 1
                far = jnp.minimum(jnp.maximum(far, 0), self.pairs - 1)
                both = self.decays[2 * far, b] * self.decays[2 * far + 1, b]
                reach = both if reach is None else reach * both
                before = before + reach * wide(self.chain[r, b])
            first, _, decay, _ = self.firsts(b)
            after = decay * before + first
            self.sent[1, b] = narrow(jnp.where(self.ahead, after, before))
            self.swaps[1][b].start()
            self.state[b, self.rows(True)] = jnp.where(self.ahead, before, after)

    def finish(self):
        for b in range(self.batch):
            self.swaps[1][b].wait_recv()
            self.state[b, self.rows(False)] = wide(self.got[1, b])
        for copy in self.decay_copies + self.swaps[0] + self.swaps[1]:
            copy.wait_send()
        for r in range(self.pairs - 1):

            @pl.when(self.sends(r))
            def _(r=r):
                for b in range(self.batch):
                    self.links[r][b].wait_send()


def handover_scratch(count, batch):
    half = (batch, DV // 2, DK)
    return [
        pltpu.VMEM((count, batch, 1, DK), F32),
        pltpu.VMEM((2, *half), BF16),
        pltpu.VMEM((2, *half), BF16),
        pltpu.VMEM((count // 2, *half), BF16),
        pltpu.SemaphoreType.DMA((count - 1,)),
        pltpu.SemaphoreType.DMA((count - 1,)),
        pltpu.SemaphoreType.DMA((count // 2 + 1, batch)),
        pltpu.SemaphoreType.DMA((count // 2 + 1, batch)),
    ]


PIECES = 4


class Rows:
    def __init__(self, part, out, scratch):
        self.got, self.across, self.far, send, receive = scratch
        self.part, self.out = part, out
        head = lax.axis_index("head")
        core, chip = lax.rem(head, 2), head // 2
        self.share = part.shape[0] // 4
        self.size = self.share // PIECES
        beside, facing = 2 * chip + 1 - core, 2 * (1 - chip) + core
        self.own, self.facing = head, facing
        corner = 2 * (1 - chip) + 1 - core

        def copy(kind, p, source, target, aim):
            return pltpu.make_async_remote_copy(
                src_ref=source,
                dst_ref=target,
                send_sem=send.at[kind, p],
                recv_sem=receive.at[kind, p],
                device_id={"head": aim},
                device_id_type=MESH,
            )

        self.copies = {}
        for p in range(PIECES):
            here = self.piece(p)
            mine = out.at[self.rows(head, p)]
            met = out.at[self.rows(facing, p)]
            self.copies[0, p] = copy(0, p, part.at[self.rows(corner, p)], self.got.at[0, here], beside)
            self.copies[1, p] = copy(1, p, part.at[self.rows(beside, p)], self.got.at[1, here], beside)
            self.copies[2, p] = copy(2, p, self.across.at[here], self.far.at[here], facing)
            self.copies[3, p] = copy(3, p, mine, mine, facing)
            self.copies[4, p] = copy(4, p, mine, mine, beside)
            self.copies[5, p] = copy(5, p, met, met, beside)

    def piece(self, p):
        return pl.ds(p * self.size, self.size)

    def rows(self, owner, p):
        return pl.ds(pl.multiple_of(owner * self.share + p * self.size, self.size), self.size)

    def start(self, p):
        self.copies[0, p].start()
        self.copies[1, p].start()

    def cross(self, p):
        self.copies[0, p].wait_recv()
        here = self.piece(p)
        self.across[here] = narrow(wide(self.part[self.rows(self.facing, p)]) + wide(self.got[0, here]))
        self.copies[2, p].start()

    def turn(self, p, middle):
        self.copies[1, p].wait_recv()
        self.copies[2, p].wait_recv()
        here = self.piece(p)
        total = wide(self.part[self.rows(self.own, p)]) + wide(self.got[1, here])
        self.out[self.rows(self.own, p)] = middle(here, total + wide(self.far[here]))
        self.copies[3, p].start()
        self.copies[4, p].start()

    def relay(self, p):
        self.copies[3, p].wait_recv()
        self.copies[5, p].start()

    def finish(self):
        for p in range(PIECES):
            self.copies[4, p].wait_recv()
            self.copies[5, p].wait_recv()
        for copy in self.copies.values():
            copy.wait_send()


def rows_scratch(share, width):
    return [
        pltpu.VMEM((2, share, width), BF16),
        pltpu.VMEM((share, width), BF16),
        pltpu.VMEM((share, width), BF16),
        pltpu.SemaphoreType.DMA((6, PIECES)),
        pltpu.SemaphoreType.DMA((6, PIECES)),
    ]


def greet_all(count, heads):
    barrier = pltpu.get_barrier_semaphore()
    for axis, size in (("seq", count), ("head", heads)):
        mine = lax.axis_index(axis)
        for d in range(1, size):
            pl.semaphore_signal(
                barrier, inc=1, device_id={axis: lax.rem(mine + d, size)}, device_id_type=MESH
            )
    pl.semaphore_wait(barrier, count + heads - 2)


def chunk_at(i):
    return pl.ds(pl.multiple_of(i * CHUNK, CHUNK), CHUNK)


def token_phase_kernel(
    order, early, ready, vk_ref, query_ref, gate_ref, low_ref, up_ref, bias_ref, starts_ref, gain_ref,
    out_ref, block_ref, down_ref,
    run_ref, slope_ref, total_ref, mixed_ref, heads_ref, states_ref, part_ref, whole_ref, down_whole,
    state, ring_send, ring_receive, ring_local, down_send, down_receive, down_local,
    mark_ref, row_ref, *scratch,
):
    count = len(order)
    ring = BlockRing(order, block_ref, whole_ref, ring_send, ring_receive, ring_local)
    hand = Handover(count, False, state, total_ref, scratch)
    down_ring = BlockRing(
        order, down_ref.at[:, pl.ds(0, early)], down_whole, down_send, down_receive, down_local
    )
    hand.clear()
    greet("seq", count)
    ready(9)
    ring.start()
    fill_marks(starts_ref, mark_ref, row_ref)
    state[...] = jnp.zeros_like(state)
    total_ref[...] = jnp.ones_like(total_ref)
    chunks = run_ref.shape[1] // CHUNK
    ready(0, 3)

    @pl.loop(0, chunks)
    def _(i):
        at = chunk_at(i)
        state_chunk(
            vk_ref.at[:, at, pl.ds(0, DV)], vk_ref.at[:, at, pl.ds(DV, DK)], low_ref.at[:, at],
            up_ref, bias_ref, mark_ref.at[:, at], run_ref.at[:, at], slope_ref.at[:, at],
            state, total_ref,
        )

    hand.begin()
    ready.save(0, 1)
    ring.advance()
    hand.join()
    ring.advance()
    ready(10)
    down_ring.start()
    for r in range(1, count // 2):
        hand.hop(r)
        ring.advance()
        if r > 1:
            down_ring.advance()
    hand.close()
    ready()
    ring.advance()
    down_ring.advance()
    hand.finish()
    ring.finish()
    down_ring.advance()

    def mixer(begin, end):
        @pl.loop(begin, end)
        def _(i):
            at = chunk_at(i)
            mixer_chunk(
                query_ref.at[:, at], vk_ref.at[:, at, pl.ds(0, DV)],
                vk_ref.at[:, at, pl.ds(DV, DK)], run_ref.at[:, at], mark_ref.at[:, at],
                row_ref.at[pl.ds(i, 1)], gate_ref.at[:, at], gain_ref, heads_ref.at[:, at],
                mixed_ref.at[:, at], states_ref.at[pl.ds(2 * i, 2)], state,
            )

    mixer(0, chunks // 2)
    down_ring.advance()
    mixer(chunks // 2, chunks)
    ready.save(3, 4, 5)
    down_ring.advance()
    batch, block, _ = heads_ref.shape
    tile = 256
    for b in range(batch):
        for t in range(block // tile):
            field = heads_ref[b, t * tile : (t + 1) * tile]
            start = b * block + t * tile
            part_ref[start : start + tile] = narrow(product(field, out_ref[...], NT))
        down_ring.advance()
    down_ring.finish()


def remote_call(kernel, number, in_specs, out_specs, out_shape, scratch, operands, flops):
    moved = sum(a.size * a.dtype.itemsize for a in operands)
    moved += sum(s.size * s.dtype.itemsize for s in out_shape)
    loads = [i for i, spec in enumerate(in_specs) if spec is LOAD]
    saves = [i for i, spec in enumerate(out_specs) if spec is SAVE]
    scratch = list(scratch)
    scratch += [pltpu.VMEM(out_shape[i].shape, out_shape[i].dtype) for i in saves]
    scratch += [pltpu.VMEM(operands[i].shape, operands[i].dtype) for i in loads]
    scratch += [pltpu.SemaphoreType.DMA((max(len(loads), 1),))]
    scratch += [pltpu.SemaphoreType.DMA((max(len(saves), 1),))]

    def body(*refs):
        refs = list(refs)
        arrivals, departures = refs[-2:]
        refs = refs[:-2]
        refs, buffers = refs[: len(refs) - len(loads)], refs[len(refs) - len(loads) :]
        refs, results = refs[: len(refs) - len(saves)], refs[len(refs) - len(saves) :]
        pending, started = {}, []
        for n, (i, buffer) in enumerate(zip(saves, results)):
            pending[i] = pltpu.make_async_copy(buffer, refs[len(in_specs) + i], departures.at[n])
            refs[len(in_specs) + i] = buffer
        waits = {}
        for n, (i, buffer) in enumerate(zip(loads, buffers)):
            waits[i] = pltpu.make_async_copy(refs[i], buffer, arrivals.at[n])
            waits[i].start()
            refs[i] = buffer

        def ready(*positions):
            for i in positions or list(waits):
                waits.pop(i).wait()

        def save(*positions):
            for i in positions:
                started.append(pending.pop(i))
                started[-1].start()

        ready.save = save
        kernel(ready, *refs)
        save(*list(pending))
        for copy in started:
            copy.wait()

    return pl.pallas_call(
        body,
        in_specs=[AWAY if spec is LOAD else spec for spec in in_specs],
        out_specs=[AWAY if spec is SAVE else spec for spec in out_specs],
        out_shape=out_shape,
        scratch_shapes=scratch,
        cost_estimate=pl.CostEstimate(flops=flops, bytes_accessed=moved, transcendentals=0),
        compiler_params=pltpu.CompilerParams(
            collective_id=number, has_side_effects=True, vmem_limit_bytes=VMEM_BYTES
        ),
    )(*operands)


LOAD, SAVE = "load", "save"
NEAR = pl.BlockSpec(memory_space=pltpu.VMEM)
AWAY = pl.BlockSpec(memory_space=pl.ANY)


def token_phase(value_key, query, gates, low, up, bias, starts, gain, out_t, block, down, early):
    count = lax.axis_size("seq")
    batch, length, _ = low.shape
    chunks, width = length // CHUNK, out_t.shape[0]
    return remote_call(
        functools.partial(token_phase_kernel, ring_order(count), early),
        1,
        [LOAD, LOAD, LOAD, LOAD, NEAR, NEAR, NEAR, NEAR, LOAD, LOAD, LOAD],
        [SAVE, SAVE, NEAR, SAVE, SAVE, SAVE, NEAR] + [AWAY] * 2,
        [
            shape_of(F32, batch, length, DK),
            shape_of(F32, batch, length, DK),
            shape_of(F32, batch, 1, DK),
            shape_of(F32, batch, length, DV),
            shape_of(BF16, batch, length, DV),
            shape_of(BF16, 2 * chunks, batch, DV, DK),
            shape_of(BF16, batch * length, width),
            shape_of(BF16, count, *block.shape),
            shape_of(BF16, count, down.shape[0], early),
        ],
        [pltpu.VMEM((batch, DV, DK), F32)]
        + ring_semaphores(count)
        + ring_semaphores(count)
        + marks_scratch(batch, length)
        + handover_scratch(count, batch),
        (value_key, query, gates, low, up, bias, starts, gain, out_t, block, down),
        2 * batch * length * DV * (2 * DK + width),
    )


def row_phase_kernel(
    order, heads, ready, part_ref, input_ref, gain_ref, block_ref,
    resid_ref, normed_ref, whole_ref,
    own, own_sems, ring_send, ring_receive, ring_local, *scratch,
):
    ring = BlockRing(order, block_ref, whole_ref, ring_send, ring_receive, ring_local)
    rows = Rows(part_ref, normed_ref, scratch)
    first = pl.multiple_of(rows.own * rows.share, rows.share)
    copies = near_copies(order, input_ref, own, pl.ds(first, rows.share), own_sems)
    for copy in copies:
        copy.start()
    greet_all(len(order), heads)
    ready(3)
    ring.start()
    ready()
    for p in range(PIECES):
        rows.start(p)

    def middle(here, total):
        resid = wide(own[here]) + total
        resid_ref[here] = resid
        return narrow(resid * root_scale(resid) * gain_ref[1:2])

    for p in range(PIECES):
        rows.cross(p)
    for copy in copies:
        copy.wait()
    ring.advance()
    for p in range(PIECES):
        rows.turn(p, middle)
        if p % 2 == 0:
            ring.advance()
    ring.advance()
    for p in range(PIECES):
        rows.relay(p)
        if p % 2 == 0:
            ring.advance()
    rows.finish()
    ring.finish()


def row_phase(part, inputs, gains, block):
    count, heads = lax.axis_size("seq"), lax.axis_size("head")
    rows, width = part.shape
    return remote_call(
        functools.partial(row_phase_kernel, ring_order(count), heads),
        2,
        [LOAD, AWAY, NEAR, LOAD],
        [NEAR] * 2 + [AWAY],
        [
            shape_of(F32, rows // heads, width),
            shape_of(BF16, rows, width),
            shape_of(BF16, count, *block.shape),
        ],
        [pltpu.VMEM((rows // heads, width), BF16), pltpu.SemaphoreType.DMA((count,))]
        + ring_semaphores(count)
        + rows_scratch(rows // heads, width),
        (part, inputs, gains, block),
        16 * rows * width,
    )


def near_copies(order, source, target, rows, semaphores):
    share = source.shape[1] // len(order)
    return [
        pltpu.make_async_copy(
            source.at[rows, pl.ds(pl.multiple_of(block_at(order, r) * share, share), share)],
            target.at[:, pl.ds(r * share, share)],
            semaphores.at[r],
        )
        for r in range(len(order))
    ]


def home_copies(order, source, target, semaphores):
    share = source.shape[1] // len(order)
    return [
        pltpu.make_async_copy(
            source.at[:, pl.ds(r * share, share)],
            target.at[:, pl.ds(pl.multiple_of(block_at(order, r) * share, share), share)],
            semaphores.at[r],
        )
        for r in range(len(order))
    ]


def fill_marks(starts_ref, mark_ref, row_ref):
    batch, length, _ = mark_ref.shape
    chunks = length // CHUNK
    starts = starts_ref[...].astype(F32)
    across = product(starts, triangle(False), NN, HIGH)
    down = product(triangle(True), starts, NT, HIGH)
    for b in range(batch):
        for i in range(chunks):
            n = b * chunks + i
            mark_ref[b, i * CHUNK : (i + 1) * CHUNK] = down[:, n : n + 1]
            row_ref[i, b] = across[n : n + 1]


def marks_scratch(batch, length):
    return [
        pltpu.VMEM((batch, length, 1), F32),
        pltpu.VMEM((length // CHUNK, batch, 1, CHUNK), F32),
    ]


def split_columns(widths):
    pieces, begin = [], 0
    for item, columns in enumerate(widths):
        number = -(-columns // 1024)
        size = -(-columns // (128 * number)) * 128
        for start in range(0, columns, size):
            pieces.append((item, start, min(size, columns - start), begin + start))
        begin += columns
    return pieces


class SumRing:
    def __init__(self, order, items, out_ref, scratch, visit=None):
        self.visit, self.arrived = visit, 0
        lefts = []
        for left, _, _ in items:
            if not any(left is other for other in lefts):
                lefts.append(left)
        buffers, rest = scratch[: len(lefts)], scratch[len(lefts) :]
        self.sent, self.got, load, send, receive = rest
        self.order, self.items, self.out = order, items, out_ref
        self.count = count = len(order)
        self.half = half = out_ref.shape[0] // 2
        self.buffers = {id(left): buffer for left, buffer in zip(lefts, buffers)}
        self.pieces = split_columns([right.shape[1] for _, right, _ in items])
        homes = {id(left): home for left, _, home in items}
        aims = (block_at(order, 1), block_at(order, -1))
        self.loads, self.hops = {}, {}
        for k in range(count):
            for side in range(2):
                slot = (count - 1 - k) if side == 0 else (k + 1) % count
                for n, (left, buffer) in enumerate(zip(lefts, buffers)):
                    block = block_at(order, slot) if homes[id(left)] else slot
                    column = pl.multiple_of(block * 2 * half + side * half, half)
                    self.loads[k, side, n] = pltpu.make_async_copy(
                        left.at[:, pl.ds(column, half)],
                        buffer.at[k % 2, side],
                        load.at[k % 2, side, n],
                    )
                if k == count - 1:
                    continue
                for n, (_, _, size, begin) in enumerate(self.pieces):
                    self.hops[k, side, n] = pltpu.make_async_remote_copy(
                        src_ref=self.sent.at[k % 2, side, :, pl.ds(begin, size)],
                        dst_ref=self.got.at[k, side, :, pl.ds(begin, size)],
                        send_sem=send.at[k, side, n],
                        recv_sem=receive.at[k, side, n],
                        device_id={"seq": aims[side]},
                        device_id_type=MESH,
                    )
        self.number = len(lefts)
        self.k = 0

    def load(self, k):
        if k < self.count:
            for side in range(2):
                for n in range(self.number):
                    self.loads[k, side, n].start()

    def prepare(self):
        self.load(0)
        self.load(1)

    def arrive(self, k):
        if k < self.arrived:
            return
        self.arrived = k + 1
        for side in range(2):
            for n in range(self.number):
                self.loads[k, side, n].wait()
            if self.visit is not None:
                slot = (self.count - 1 - k) if side == 0 else (k + 1) % self.count
                self.visit(slot, side, self.buffers[id(self.items[0][0])][k % 2, side])

    def advance(self):
        k, last = self.k, self.count - 1
        if k > last:
            return
        self.arrive(k)
        for n, (item, start, size, begin) in enumerate(self.pieces):
            left, right, _ = self.items[item]
            columns = slice(begin, begin + size)
            for side in range(2):
                buffer = self.buffers[id(left)]
                value = product(buffer[k % 2, side], right[:, start : start + size], TN)
                if k > 0:
                    self.hops[k - 1, side, n].wait_recv()
                    value = value + wide(self.got[k - 1, side, :, columns])
                if k < last:
                    if k >= 2:
                        self.hops[k - 2, side, n].wait_send()
                    self.sent[k % 2, side, :, columns] = narrow(value)
                    self.hops[k, side, n].start()
                else:
                    self.out[side * self.half : (side + 1) * self.half, columns] = value
        self.load(k + 2)
        self.k += 1

    def finish(self):
        while self.k < self.count:
            self.advance()
        for k in (self.count - 3, self.count - 2):
            for n in range(len(self.pieces)):
                for side in range(2):
                    self.hops[k, side, n].wait_send()


def sum_scratch(count, rows, lefts, half, widths):
    columns, pieces = sum(widths), len(split_columns(widths))
    return [pltpu.VMEM((2, 2, rows, half), BF16)] * lefts + [
        pltpu.VMEM((2, 2, half, columns), BF16),
        pltpu.VMEM((count - 1, 2, half, columns), BF16),
        pltpu.SemaphoreType.DMA((2, 2, lefts)),
        pltpu.SemaphoreType.DMA((count - 1, 2, pieces)),
        pltpu.SemaphoreType.DMA((count - 1, 2, pieces)),
    ]


def unit_phase_kernel(
    order, ready, normed_ref, gate_ref, up_ref, grad_ref, block_ref, early_ref,
    act_ref, gate_grad_ref, up_grad_ref, ffn_ref, part_ref,
    whole_ref, pre_gate, pre_up, act_grad, tiles, tile_sems, early_sem, ring_send, ring_receive, ring_local,
):
    count = len(order)
    early = early_ref.shape[2]
    late = block_ref.shape[1] - early
    ring = BlockRing(
        order, block_ref.at[:, pl.ds(early, late)], whole_ref.at[:, :, pl.ds(early, late)],
        ring_send, ring_receive, ring_local,
    )
    placed = pltpu.make_async_copy(early_ref, whole_ref.at[:, :, pl.ds(0, early)], early_sem)
    greet("seq", count)
    ring.start()
    rows, width = normed_ref.shape
    tile = 256
    share = block_ref.shape[0]

    def written(kind, target, i):
        return pltpu.make_async_copy(
            tiles.at[kind], target.at[pl.ds(i * tile, tile)], tile_sems.at[kind]
        )

    ready(0, 1, 2)
    placed.start()
    steps = rows // tile
    for i in range(steps):
        here = pl.ds(i * tile, tile)
        field = normed_ref[here]
        gate = product(field, gate_ref[...], NN)
        pre_gate[here] = gate
        up = product(field, up_ref[...], NN)
        pre_up[here] = up
        act_ref[here] = narrow(gate * jax.nn.sigmoid(gate) * up)
        ring.advance()
    ready.save(0)
    ready()
    placed.wait()

    def against(here, columns):
        parts = [
            grad_ref[here, pl.ds(pl.multiple_of(block_at(order, r) * share, share), share)]
            for r in range(count)
        ]
        right = whole_ref[:, :, columns].reshape(width, -1)
        return product(jnp.concatenate(parts, axis=1), right, NN)

    for i in range(steps):
        act_grad[i * tile : (i + 1) * tile] = against(pl.ds(i * tile, tile), slice(0, early))
        if i % 2:
            ring.advance()
    ring.finish()
    for i in range(steps):
        here = pl.ds(i * tile, tile)
        ends = against(here, slice(early, early + late))
        for kind, target in ((0, gate_grad_ref), (1, up_grad_ref)):
            if i > 0:
                written(kind, target, i - 1).wait()
        for columns, grad in ((slice(0, early), act_grad[here]), (slice(early, early + late), ends)):
            gate, up = pre_gate[here, columns], pre_up[here, columns]
            sigma = jax.nn.sigmoid(gate)
            tiles[0, :, columns] = narrow(grad * up * sigma * (1.0 + gate * (1.0 - sigma)))
            tiles[1, :, columns] = narrow(grad * gate * sigma)
        for kind, target in ((0, gate_grad_ref), (1, up_grad_ref)):
            written(kind, target, i).start()
        part = product(tiles[0], gate_ref[...], NT) + product(tiles[1], up_ref[...], NT)
        part_ref[here] = narrow(part)
        ffn_ref[here] = narrow(product(act_ref[here], whole_ref[...].reshape(width, -1), NT))
    for kind, target in ((0, gate_grad_ref), (1, up_grad_ref)):
        written(kind, target, steps - 1).wait()


def unit_phase(normed_two, fgate, fup, grad_rows, block, early):
    count = lax.axis_size("seq")
    rows, width = normed_two.shape
    hidden = block.shape[1]
    flat = shape_of(BF16, rows, hidden)
    return remote_call(
        functools.partial(unit_phase_kernel, ring_order(count)),
        3,
        [LOAD] * 4 + [AWAY, AWAY],
        [SAVE, AWAY, AWAY, SAVE, SAVE],
        [flat, flat, flat, shape_of(BF16, rows, width), shape_of(BF16, rows, width)],
        [
            pltpu.VMEM((count, *block.shape), BF16),
            pltpu.VMEM((rows, hidden), F32),
            pltpu.VMEM((rows, hidden), F32),
            pltpu.VMEM((rows, early.shape[2]), F32),
            pltpu.VMEM((2, 256, hidden), BF16),
            pltpu.SemaphoreType.DMA((2,)),
            pltpu.SemaphoreType.DMA,
        ]
        + ring_semaphores(count),
        (normed_two, fgate, fup, grad_rows, block, early),
        6 * rows * width * hidden,
    )


def resid_phase_kernel(
    order, heads, ready, part_ref, resid_ref, grad_ref, gain_ref, out_ref, act_ref, normed_ref,
    up_grad_ref, gate_ref, mixed_ref, head_gain_ref, query_ref, run_ref, starts_ref, total_ref, ffn_ref,
    resid_grad_ref, attn_grad_ref, gates_grad_ref, mixed_grad_ref, state_ref, gain_grad_ref,
    head_gain_grad_ref, layer_ref, sums_ref,
    own, own_sems, wholes, whole_sems, ffn_sem, pair, pair_sems, heads_grad, state, mark_ref, row_ref,
    *scratch,
):
    count = len(order)
    rows = Rows(part_ref, wholes, scratch[:5])
    hand = Handover(count, True, state, total_ref, scratch[5:13])
    ring = SumRing(
        order, [(grad_ref, act_ref, True), (normed_ref, up_grad_ref, False)], sums_ref, scratch[13:]
    )
    first = pl.multiple_of(rows.own * rows.share, rows.share)
    copies = near_copies(order, grad_ref, own, pl.ds(first, rows.share), own_sems)
    ring.prepare()
    for copy in copies:
        copy.start()
    batch, length, _ = run_ref.shape
    chunks = length // CHUNK
    pairs = [
        [
            pltpu.make_async_copy(
                field.at[:, pl.ds((chunks - 1 - i) * CHUNK, CHUNK)],
                pair.at[i % 2, kind],
                pair_sems.at[i % 2, kind],
            )
            for kind, field in enumerate((gate_ref, mixed_ref))
        ]
        for i in range(chunks)
    ]
    hand.clear()
    greet_all(count, heads)
    ready(0)
    for p in range(PIECES):
        rows.start(p)
    ready(5, 7)
    ring.advance()
    for copy in pairs[0] + pairs[1]:
        copy.start()
    gain_grad_ref[...] = jnp.zeros_like(gain_grad_ref)
    head_gain_grad_ref[...] = jnp.zeros_like(head_gain_grad_ref)
    state[...] = jnp.zeros_like(state)
    fill_marks(starts_ref, mark_ref, row_ref)

    def middle(here, total):
        resid = resid_ref[here]
        scale = root_scale(resid)
        unit = resid * scale
        gain_grad_ref[...] += jnp.sum(total * unit, axis=0, keepdims=True)
        grad = wide(own[here]) + norm_back(total * gain_ref[1:2], unit, scale)
        resid_grad_ref[here] = grad
        return narrow(grad)

    def layer(here, total):
        return narrow(resid_ref[here] + total)

    for p in range(PIECES):
        rows.cross(p)
    for copy in copies:
        copy.wait()
    ready()
    rows.turn(0, middle)
    ring.advance()
    for p in range(1, PIECES):
        rows.turn(p, middle)
    ring.advance()
    for p in range(PIECES):
        rows.relay(p)
        if p == 2:
            ring.advance()
    rows.finish()
    ready.save(0)
    kept = pltpu.make_async_copy(wholes, attn_grad_ref, whole_sems.at[0])
    kept.start()
    following = pltpu.make_async_copy(ffn_ref, part_ref, ffn_sem)
    following.start()

    for i in range(chunks):
        at = pl.ds((chunks - 1 - i) * CHUNK, CHUNK)
        for copy in pairs[i]:
            copy.wait()
        for b in range(batch):
            here = pl.ds(b * length + (chunks - 1 - i) * CHUNK, CHUNK)
            heads_grad[b] = product(wholes[here], out_ref[...], NN)
        head_back_chunk(
            heads_grad, pair.at[i % 2, 0], pair.at[i % 2, 1], head_gain_ref,
            query_ref.at[:, at], run_ref.at[:, at], mark_ref.at[:, at],
            gates_grad_ref.at[:, at], mixed_grad_ref.at[:, at], head_gain_grad_ref, state,
        )
        if i + 2 < chunks:
            for copy in pairs[i + 2]:
                copy.start()

    hand.begin()
    ready.save(2, 3)
    kept.wait()
    following.wait()
    for p in range(PIECES):
        rows.start(p)
    ring.advance()
    hand.join()
    for p in range(PIECES):
        rows.cross(p)
    for r in range(1, count // 2):
        hand.hop(r)
        if r < PIECES:
            rows.turn(r - 1, layer)
        if r == 2:
            ring.advance()
    for r in range(count // 2 - 1, PIECES):
        rows.turn(r, layer)
    hand.close()
    ring.advance()
    hand.finish()
    state_ref[...] = narrow(state[...])
    for p in range(PIECES):
        rows.relay(p)
        if p == 2:
            ring.advance()
    rows.finish()
    backs = home_copies(order, wholes, layer_ref, whole_sems)
    for copy in backs:
        copy.start()
    ring.finish()
    for copy in backs:
        copy.wait()


def resid_phase(
    part, resid, grad_rows, gains, out_t, act, normed_two, d_up, gates, mixed, head_gain, query, run,
    starts, total, ffn_part,
):
    count, heads = lax.axis_size("seq"), lax.axis_size("head")
    rows, width = part.shape
    batch, length, _ = run.shape
    share, hidden = width // count, act.shape[1]
    quarter = rows // heads
    return remote_call(
        functools.partial(resid_phase_kernel, ring_order(count), heads),
        4,
        [LOAD, LOAD, AWAY, NEAR, LOAD, LOAD, AWAY, LOAD, AWAY, AWAY, NEAR, LOAD, LOAD, NEAR, NEAR, AWAY],
        [SAVE, AWAY, SAVE, SAVE, NEAR, NEAR, NEAR, AWAY, NEAR],
        [
            shape_of(F32, quarter, width),
            shape_of(BF16, rows, width),
            shape_of(BF16, batch, length, DV),
            shape_of(BF16, batch, length, DV),
            shape_of(BF16, batch, DV, DK),
            shape_of(F32, 1, width),
            shape_of(F32, 1, DV),
            shape_of(BF16, rows, width),
            shape_of(F32, share, 2 * hidden),
        ],
        [
            pltpu.VMEM((quarter, width), BF16),
            pltpu.SemaphoreType.DMA((count,)),
            pltpu.VMEM((rows, width), BF16),
            pltpu.SemaphoreType.DMA((count,)),
            pltpu.SemaphoreType.DMA,
            pltpu.VMEM((2, 2, batch, CHUNK, DV), F32),
            pltpu.SemaphoreType.DMA((2, 2)),
            pltpu.VMEM((batch, CHUNK, DV), F32),
            pltpu.VMEM((batch, DV, DK), F32),
        ]
        + marks_scratch(batch, length)
        + rows_scratch(quarter, width)
        + handover_scratch(count, batch)
        + sum_scratch(count, rows, 2, share // 2, [hidden, hidden]),
        (part, resid, grad_rows, gains, out_t, act, normed_two, d_up, gates, mixed, head_gain, query,
         run, starts, total, ffn_part),
        2 * rows * width * (2 * hidden + DV),
    )


def back_phase_kernel(
    order, ready, query_ref, vk_ref, run_ref, slope_ref, states_ref, low_ref, up_ref, starts_ref,
    mixed_grad_ref, later_ref, gates_grad_ref, normed_ref, act_grad_ref, weight_ref, down_ref,
    packed_ref, low_grad_ref, up_grad_ref, bias_grad_ref, part_ref, sums_ref,
    state, mark_ref, row_ref, *scratch,
):
    count = len(order)
    ring = SumRing(order, [(normed_ref, act_grad_ref, False)], sums_ref, scratch)
    ring.prepare()
    greet("seq", count)
    ready(12)
    ring.advance()
    batch, length, _ = run_ref.shape
    chunks = length // CHUNK
    gates_from, low_from = DV + 2 * DK, 2 * DV + 2 * DK
    fill_marks(starts_ref, mark_ref, row_ref)
    for ref in (up_grad_ref, bias_grad_ref):
        ref[...] = jnp.zeros_like(ref)
    ready(0, 1, 2, 3, 4, 5, 8, 9, 10)
    state[...] = wide(later_ref[...])
    packed_ref[:, :, gates_from:low_from] = gates_grad_ref[...]

    def back(begin, end):
        @pl.loop(begin, end)
        def _(i):
            n = chunks - 1 - i
            at = chunk_at(n)
            mixer_back_chunk(
                query_ref.at[:, at], vk_ref.at[:, at, pl.ds(0, DV)],
                vk_ref.at[:, at, pl.ds(DV, DK)], run_ref.at[:, at], slope_ref.at[:, at],
                mark_ref.at[:, at], row_ref.at[pl.ds(n, 1)], mixed_grad_ref.at[:, at],
                states_ref.at[pl.ds(2 * n, 1)], states_ref.at[pl.ds(2 * n + 1, 1)],
                low_ref.at[:, at], up_ref,
                packed_ref.at[:, at, pl.ds(DV + DK, DK)], packed_ref.at[:, at, pl.ds(0, DV)],
                packed_ref.at[:, at, pl.ds(DV, DK)], low_grad_ref.at[:, at],
                up_grad_ref, bias_grad_ref, state,
            )

    back(0, chunks // 2)
    ring.advance()
    back(chunks // 2, chunks)
    ready.save(0)
    ring.advance()
    ready()
    tile = 256
    down = [down_ref[block_at(order, r)] for r in range(count)]
    down = jnp.concatenate(down, axis=1)
    for b in range(batch):
        for t in range(length // tile):
            field = packed_ref[b, t * tile : (t + 1) * tile]
            low = low_grad_ref[b, t * tile : (t + 1) * tile]
            start = b * length + t * tile
            total = product(field, weight_ref[...], NT) + product(low, down, NN)
            part_ref[start : start + tile] = narrow(total)
        ring.advance()
    ring.finish()


def back_phase(
    query, vk, run, slope, states, low, up, starts, d_mixed, later, d_gates, normed_two, d_gate, weights,
    down,
):
    count = lax.axis_size("seq")
    batch, length, rank = low.shape
    width, packed_cols = weights.shape
    share, hidden, rows = width // count, d_gate.shape[1], d_gate.shape[0]
    return remote_call(
        functools.partial(back_phase_kernel, ring_order(count)),
        5,
        [LOAD] * 6 + [NEAR, NEAR, LOAD, LOAD, LOAD, AWAY, LOAD, LOAD, NEAR],
        [SAVE] + [NEAR] * 5,
        [
            shape_of(BF16, batch, length, packed_cols),
            shape_of(BF16, batch, length, rank),
            shape_of(F32, rank, DK),
            shape_of(F32, 1, DK),
            shape_of(BF16, rows, width),
            shape_of(F32, share, hidden),
        ],
        [pltpu.VMEM((batch, DV, DK), F32)]
        + marks_scratch(batch, length)
        + sum_scratch(count, rows, 1, share // 2, [hidden]),
        (query, vk, run, slope, states, low, up, starts, d_mixed, later, d_gates, normed_two, d_gate,
         weights, down),
        2 * rows * width * hidden,
    )


SMALL = 24


def last_phase_kernel(
    order, heads, ready, part_ref, input_ref, resid_grad_ref, gain_ref, normed_ref, packed_ref, attn_ref,
    heads_ref, ffn_gain_ref, head_gain_ref, bias_ref, up_ref, low_ref,
    input_grad_ref, sums_ref, small_ref, tail_ref,
    own, own_sems, grads, grad_sems, gain_grad, stage, stage_got, downs, downs_got, shared, shared_got,
    seq_send, seq_receive, head_send, head_receive, *scratch,
):
    count = len(order)
    rows = Rows(part_ref, grads, scratch[:5])
    rank = low_ref.shape[1]

    def visit(slot, side, columns):
        block = narrow(product(low_ref[...], columns, TN))
        downs[block_at(order, slot), side * rank : (side + 1) * rank] = block

    items = [(normed_ref, packed_ref, False), (attn_ref, heads_ref, False)]
    ring = SumRing(order, items, sums_ref, scratch[5:], visit)
    first = pl.multiple_of(rows.own * rows.share, rows.share)
    copies = near_copies(order, input_ref, own, pl.ds(first, rows.share), own_sems)
    for copy in copies:
        copy.start()
    ring.prepare()
    greet_all(count, heads)
    ready(0)
    for p in range(PIECES):
        rows.start(p)
    ready(5, 7)
    ring.advance()
    ready()
    gain_grad[...] = jnp.zeros_like(gain_grad)

    def middle(here, total):
        field = wide(own[here])
        scale = root_scale(field)
        unit = field * scale
        gain_grad[...] += jnp.sum(total * unit, axis=0, keepdims=True)
        return narrow(resid_grad_ref[here] + norm_back(total * gain_ref[0:1], unit, scale))

    for p in range(PIECES):
        rows.cross(p)
    for copy in copies:
        copy.wait()
    ring.advance()
    for p in range(PIECES):
        rows.turn(p, middle)
        if p == 1:
            ring.advance()

    mine, head = lax.axis_index("seq"), lax.axis_index("head")
    share = sums_ref.shape[0]
    stage[...] = jnp.zeros_like(stage)
    pieces = [ref.shape[1] // count for ref in (head_gain_ref, bias_ref, up_ref)]
    for j in range(count):
        stage[j, 0:1, : pieces[0]] = head_gain_ref[:, j * pieces[0] : (j + 1) * pieces[0]]
        stage[j, 1:2, : pieces[1]] = bias_ref[:, j * pieces[1] : (j + 1) * pieces[1]]
        stage[j, 8:, : pieces[2]] = up_ref[:, j * pieces[2] : (j + 1) * pieces[2]]
        owner = block_at(order, j)
        for n, ref in ((2, gain_grad), (4, ffn_gain_ref)):
            for t in range(share // 128):
                start = j * share + t * 128
                stage[owner, n + t : n + t + 1, :] = ref[:, start : start + 128]

    def spread(kind, source, target):
        hops = []
        for d in range(1, count):
            aim = lax.rem(mine + d, count)
            hops.append(
                pltpu.make_async_remote_copy(
                    src_ref=source.at[aim],
                    dst_ref=target.at[d - 1],
                    send_sem=seq_send.at[kind, d - 1],
                    recv_sem=seq_receive.at[kind, d - 1],
                    device_id={"seq": aim},
                    device_id_type=MESH,
                )
            )
            hops[-1].start()
        return hops

    stage_hops = spread(0, stage, stage_got)

    ring.advance()
    rows.relay(0)
    rows.relay(1)
    ring.advance()
    rows.relay(2)
    rows.relay(3)
    ring.advance()
    rows.finish()
    backs = home_copies(order, grads, input_grad_ref, grad_sems)
    for copy in backs:
        copy.start()
    while ring.k < count - 1:
        ring.advance()
    ring.arrive(count - 1)
    down_hops = spread(1, downs, downs_got)
    for hop in stage_hops + down_hops:
        hop.wait_recv()
    total, down = stage[mine], wide(downs[mine])
    for d in range(count - 1):
        total = total + stage_got[d]
        down = down + wide(downs_got[d])
    small_ref[...] = total
    shared[0:8] = total[:8]
    shared[8:] = down
    shared_hops = [
        pltpu.make_async_remote_copy(
            src_ref=shared,
            dst_ref=shared_got.at[d - 1],
            send_sem=head_send.at[d - 1],
            recv_sem=head_receive.at[d - 1],
            device_id={"head": lax.rem(head + d, heads)},
            device_id_type=MESH,
        )
        for d in range(1, heads)
    ]
    for hop in shared_hops:
        hop.start()
    for hop in shared_hops:
        hop.wait_recv()
    total = shared[...] + (shared_got[0] + shared_got[1] + shared_got[2])
    small_ref[0:1] = total[0:1]
    small_ref[2:8] = total[2:8]
    tail_ref[...] = total[8:]
    ring.finish()
    for hop in stage_hops + down_hops + shared_hops:
        hop.wait_send()
    for copy in backs:
        copy.wait()


def last_phase(
    part, inputs, d_resid, gains, normed, packed, d_attn, heads_out, ffn_gain, head_gain, bias, up,
    low,
):
    count, heads = lax.axis_size("seq"), lax.axis_size("head")
    rows, width = part.shape
    share, quarter = width // count, rows // heads
    columns, rank = packed.shape[1] + heads_out.shape[1], low.shape[1]
    return remote_call(
        functools.partial(last_phase_kernel, ring_order(count), heads),
        6,
        [LOAD, AWAY, LOAD, NEAR, AWAY, LOAD, AWAY, LOAD, NEAR, NEAR, NEAR, NEAR, NEAR],
        [AWAY, NEAR, NEAR, NEAR],
        [
            shape_of(BF16, rows, width),
            shape_of(F32, share, columns),
            shape_of(F32, SMALL, 128),
            shape_of(F32, 2 * rank, 128),
        ],
        [
            pltpu.VMEM((quarter, width), BF16),
            pltpu.SemaphoreType.DMA((count,)),
            pltpu.VMEM((rows, width), BF16),
            pltpu.SemaphoreType.DMA((count,)),
            pltpu.VMEM((1, width), F32),
            pltpu.VMEM((count, SMALL, 128), F32),
            pltpu.VMEM((count - 1, SMALL, 128), F32),
            pltpu.VMEM((count, 2 * rank, 128), BF16),
            pltpu.VMEM((count - 1, 2 * rank, 128), BF16),
            pltpu.VMEM((8 + 2 * rank, 128), F32),
            pltpu.VMEM((heads - 1, 8 + 2 * rank, 128), F32),
            pltpu.SemaphoreType.DMA((2, count - 1)),
            pltpu.SemaphoreType.DMA((2, count - 1)),
            pltpu.SemaphoreType.DMA((heads - 1,)),
            pltpu.SemaphoreType.DMA((heads - 1,)),
        ]
        + rows_scratch(quarter, width)
        + sum_scratch(count, rows, 2, share // 2, [packed.shape[1], DV]),
        (part, inputs, d_resid, gains, normed, packed, d_attn, heads_out, ffn_gain, head_gain, bias, up,
         low),
        2 * rows * width * columns,
    )


def leave_kernel(
    layer_ref, input_ref, first_ref, gate_ref, last_ref,
    layer_out, input_out, query_out, key_out, value_out, gates_out, attn_out, ffn_gate_out,
    ffn_up_out, ffn_down_out,
):
    hidden = gate_ref.shape[1]
    used = last_ref.shape[1] - DV
    layer_out[...] = layer_ref[...]
    input_out[...] = input_ref[...]
    ffn_gate_out[...] = gate_ref[...]
    ffn_up_out[...] = first_ref[:, hidden:]
    ffn_down_out[...] = first_ref[:, :hidden].T
    value_out[...] = last_ref[:, :DV]
    key_out[...] = last_ref[:, DV : DV + DK]
    query_out[...] = last_ref[:, DV + DK : DV + 2 * DK]
    gates_out[...] = last_ref[:, DV + 2 * DK : 2 * DV + 2 * DK]
    attn_out[...] = last_ref[:, used:].T


def leave(layer, input_grad, first, gate, last):
    share, hidden = gate.shape
    steps = share // 128

    def by_rows(field):
        return pl.BlockSpec((field.shape[0] // steps, field.shape[1]), lambda i: (i, 0))

    out_shape = [
        shape_of(BF16, *layer.shape),
        shape_of(BF16, *layer.shape),
        shape_of(F32, share, DK),
        shape_of(F32, share, DK),
        shape_of(F32, share, DV),
        shape_of(F32, share, DV),
        shape_of(F32, DV, share),
        shape_of(F32, share, hidden),
        shape_of(F32, share, hidden),
        shape_of(F32, hidden, share),
    ]
    specs = [by_rows(shape) for shape in out_shape]
    for n in (6, 9):
        specs[n] = pl.BlockSpec((out_shape[n].shape[0], 128), lambda i: (0, i))
    operands = (layer, input_grad, first, gate, last)
    return pl.pallas_call(
        leave_kernel,
        grid=(steps,),
        in_specs=[by_rows(field) for field in operands],
        out_specs=specs,
        out_shape=out_shape,
        compiler_params=pltpu.CompilerParams(
            dimension_semantics=("arbitrary",), vmem_limit_bytes=VMEM_BYTES
        ),
    )(*operands)


EARLY = 384


def matmul(left, right):
    return product(left, right, NN)


def matmul_nt(left, right):
    return product(left, right, NT)


def matmul_tn(left, right):
    return product(left, right, TN)


def ring_order(count):
    return list(range(0, count, 2)) + list(range(count - 1 - count % 2, 0, -2))


class Ring:
    def __init__(self, axis):
        self.axis = axis
        self.count = count = lax.axis_size(axis)
        order = ring_order(count)
        place = [order.index(i) for i in range(count)]
        self.right = [(order[i], order[(i + 1) % count]) for i in range(count)]
        self.left = [(order[i], order[(i - 1) % count]) for i in range(count)]
        owners = [[order[(place[i] + r) % count] for r in range(count)] for i in range(count)]
        slots = [[(place[i] - place[me]) % count for i in range(count)] for me in range(count)]
        mine = lax.axis_index(axis)
        self.owners = jnp.asarray(owners, jnp.int32)[mine]
        self.slots = jnp.asarray(slots, jnp.int32)[mine]

    def arrange(self, field, dim, table):
        width = field.shape[dim] // self.count
        return jnp.concatenate(
            [
                lax.dynamic_slice_in_dim(field, table[r] * width, width, dim)
                for r in range(self.count)
            ],
            axis=dim,
        )

    def near(self, field, dim):
        return self.arrange(field, dim, self.owners)

    def home(self, field, dim):
        return self.arrange(field, dim, self.slots)

    def gather(self, block, after=None):
        count, half = self.count, block.shape[0] // 2
        up, down = block[:half], block[half:]
        if after is not None:
            up, down, _ = lax.optimization_barrier((up, down, after))
        pieces = [None] * (2 * count)
        pieces[0], pieces[1] = up, down
        for step in range(1, count):
            up = lax.ppermute(up, self.axis, self.right)
            down = lax.ppermute(down, self.axis, self.left)
            pieces[2 * (count - step)] = up
            pieces[2 * step + 1] = down
            if step == count - 2:
                late = up[:8, :128]
        return jnp.concatenate(pieces, axis=0), late

    def scatter(self, total):
        count = self.count
        rows = total.shape[0] // count
        half = rows // 2

        def piece(slot, part):
            start = slot * rows + part * half
            return total[start : start + half]

        up, down = piece(count - 1, 0), piece(1, 1)
        for step in range(count - 1):
            up = lax.ppermute(up, self.axis, self.right)
            down = lax.ppermute(down, self.axis, self.left)
            up = wide(up) + wide(piece(count - 2 - step, 0))
            down = wide(down) + wide(piece((step + 2) % count, 1))
            if step < count - 2:
                up, down = narrow(up), narrow(down)
        return jnp.concatenate([up, down], axis=0)


def swap(axis, distance):
    return [(i, i ^ distance) for i in range(lax.axis_size(axis))]


def head_scatter(part):
    count, mine = lax.axis_size("head"), lax.axis_index("head")
    rows = part.shape[0] // count
    held = part.reshape((count, rows) + part.shape[1:])
    distance = 1
    while distance < count:
        bit = (mine // distance) % 2
        split = held.reshape((held.shape[0] // 2, 2) + held.shape[1:])
        sent = lax.dynamic_index_in_dim(split, 1 - bit, 1, False)
        kept = lax.dynamic_index_in_dim(split, bit, 1, False)
        got = lax.ppermute(narrow(sent), "head", swap("head", distance))
        held = wide(kept) + wide(got)
        distance *= 2
    return held[0]


def head_gather(share):
    count, mine = lax.axis_size("head"), lax.axis_index("head")
    held = share[None]
    distance = count // 2
    while distance:
        bit = (mine // distance) % 2
        got = lax.ppermute(held, "head", swap("head", distance))
        lower = jnp.where(bit == 0, held, got)
        upper = jnp.where(bit == 0, got, held)
        held = jnp.stack([lower, upper], axis=1).reshape((-1,) + share.shape)
        distance //= 2
    return held.reshape((-1,) + share.shape[1:])


def with_decay(state, decay):
    high = narrow(decay)
    low = narrow(decay - wide(high))
    return jnp.concatenate([narrow(state), high, low], axis=1)


def split_decay(message):
    rows = message.shape[1] - 2
    decay = wide(message[:, rows : rows + 1]) + wide(message[:, rows + 1 :])
    return wide(message[:, :rows]), decay


def entering(state, decay, later):
    count, mine = lax.axis_size("seq"), lax.axis_index("seq")
    inner = mine % 2
    ahead = (inner == 0) != later
    half = state.shape[1] // 2
    kept = wide(lax.dynamic_slice_in_dim(state, inner * half, half, 1))
    sent = lax.dynamic_slice_in_dim(state, (1 - inner) * half, half, 1)
    pair = swap("seq", 1)
    other, other_decay = split_decay(lax.ppermute(with_decay(sent, decay), "seq", pair))
    earliest = jnp.where(ahead, kept, other)
    joined = jnp.where(ahead, other_decay, decay) * earliest + jnp.where(ahead, other, kept)
    message = with_decay(joined, decay * other_decay)
    if later:
        chain = [(i, i - 2) for i in range(2, count)]
    else:
        chain = [(i, i + 2) for i in range(count - 2)]
    before, reach = jnp.zeros_like(kept), jnp.ones_like(decay)
    for _ in range(count // 2 - 1):
        message = lax.ppermute(message, "seq", chain)
        far, far_decay = split_decay(message)
        before = before + reach * far
        reach = reach * far_decay
    second = jnp.where(ahead, decay, other_decay) * before + earliest
    got = lax.ppermute(narrow(jnp.where(ahead, second, before)), "seq", pair)
    own = narrow(jnp.where(ahead, before, second))
    return jnp.concatenate(
        [jnp.where(inner == 0, own, got), jnp.where(inner == 0, got, own)], axis=1
    )


def columns_of(vector, rows):
    width = -(-vector.shape[-1] // rows)
    pad = [(0, 0)] * (vector.ndim - 1) + [(0, width * rows - vector.shape[-1])]
    shaped = jnp.pad(vector, pad).reshape(vector.shape[:-1] + (width, rows))
    return jnp.swapaxes(shaped, -1, -2)


def plain_layer(
    layer_in,
    seg_starts,
    attn_gain,
    query_weight,
    key_weight,
    value_weight,
    gate_weight,
    decay_down,
    decay_up,
    decay_bias,
    head_gain,
    out_weight,
    ffn_gain,
    ffn_gate,
    ffn_up,
    ffn_down,
    out_grad,
):
    ring = Ring("seq")
    count = ring.count
    batch, block, width = layer_in.shape
    rows = batch * block
    chunks = block // CHUNK
    rank, share = decay_down.shape[1], attn_gain.shape[0]
    hidden = ffn_gate.shape[1]

    smalls = [attn_gain, ffn_gain, head_gain, decay_bias, decay_up.reshape(-1)]
    ends = [sum(part.size for part in smalls[: i + 1]) for i in range(len(smalls))]
    small = jnp.pad(jnp.concatenate(smalls), (0, -ends[-1] % 128))[None]
    shard = jnp.concatenate(
        [value_weight, key_weight, query_weight, gate_weight, out_weight.T, decay_down], axis=1
    )
    inputs = layer_in.reshape(rows, width)
    weights, mark = ring.gather(shard)
    small = lax.all_gather(small, "seq")
    gain = wide(small[:, 0, :share]).reshape(width)
    normed = ring.near(narrow(wide(inputs) * root_scale(wide(inputs)) * gain), 1)
    projected = matmul(normed, weights)
    value_key, query = narrow(projected[:, : DV + DK]), narrow(projected[:, DV + DK : DV + 2 * DK])
    gates, low = projected[:, DV + 2 * DK : 2 * DV + 2 * DK], projected[:, -rank:]
    third, mark = ring.gather(jnp.concatenate([ffn_gate, ffn_up], axis=1), mark)
    fdown_t, mark = ring.gather(ffn_down.T, mark)
    projections = weights[:, : 2 * DV + 2 * DK]
    out_t, down_all = weights[:, 2 * DV + 2 * DK : -rank], weights[:, -rank:]
    small = small[:, 0]
    gain_one = wide(ring.near(small[:, : ends[0]], 0)).reshape(width)
    gain_two = wide(ring.near(small[:, ends[0] : ends[1]], 0)).reshape(width)
    gain_head = wide(small[:, ends[1] : ends[2]]).reshape(1, DV)
    bias_all = wide(small[:, ends[2] : ends[3]]).reshape(1, DK)
    up_all = small[:, ends[3] : ends[4]].reshape(count, rank, -1)
    up_all = wide(jnp.swapaxes(up_all, 0, 1).reshape(rank, DK))

    starts = seg_starts.reshape(batch, chunks, CHUNK).astype(jnp.float32)
    places = jnp.arange(CHUNK)
    lower = (places[:, None] >= places[None, :]).astype(jnp.float32)
    marks = jnp.einsum("bcs,ts->bct", starts, lower, precision=HIGH)
    column, row = marks.reshape(batch, block, 1), jnp.swapaxes(marks, 0, 1)[:, :, None, :]

    grad_rows = ring.near(out_grad.reshape(rows, width), 1)
    head = lax.axis_index("head")
    quarter = rows // lax.axis_size("head")
    inputs_own = lax.dynamic_slice_in_dim(inputs, head * quarter, quarter, 0)
    inputs_own = wide(ring.near(inputs_own, 1))
    grad_own = wide(lax.dynamic_slice_in_dim(grad_rows, head * quarter, quarter, 0))

    def tokens(field):
        return field.reshape(batch, block, field.shape[-1])

    value_key, query, gates, low = map(tokens, (value_key, query, gates, low))
    run, slope, state, total = local_states(value_key, low, up_all, bias_all, column)
    state_in = entering(state, total, False)
    heads, mixed, states = mix(query, value_key, run, column, row, state_in, gates, gain_head)
    heads = heads.reshape(rows, DV)
    resid = inputs_own + head_scatter(narrow(matmul_nt(heads, out_t)))
    scale_two = root_scale(resid)
    unit_two = resid * scale_two
    normed_two = head_gather(narrow(unit_two * gain_two))
    pre_gate = matmul(normed_two, third[:, :hidden])
    pre_up = matmul(normed_two, third[:, hidden:])
    sigma = jax.nn.sigmoid(pre_gate)
    act = narrow(pre_gate * sigma * pre_up)
    layer_out = narrow(resid + head_scatter(narrow(matmul_nt(act, fdown_t))))
    layer_out = ring.home(head_gather(layer_out), 1)

    d_act = matmul(grad_rows, fdown_t)
    grad_fdown = ring.scatter(narrow(matmul_tn(grad_rows, act)))
    d_gate = narrow(d_act * pre_up * sigma * (1.0 + pre_gate * (1.0 - sigma)))
    d_up = narrow(d_act * pre_gate * sigma)
    d_third = jnp.concatenate([d_gate, d_up], axis=1)
    grad_third = ring.scatter(narrow(matmul_tn(normed_two, d_third)))
    d_normed_two = head_scatter(narrow(matmul_nt(d_third, third)))
    grad_gain_two = jnp.sum(d_normed_two * unit_two, axis=0)
    d_resid = grad_own + norm_back(d_normed_two * gain_two, unit_two, scale_two)
    d_attn = head_gather(narrow(d_resid))
    d_heads = tokens(matmul(d_attn, out_t))
    d_gates, d_mixed, grad_gain_head, state_grad = head_back(
        d_heads, gates, mixed, gain_head, query, run, column
    )
    state_back = entering(state_grad, total, True)
    d_query, d_value, d_key, d_low, grad_up, grad_bias = mix_back(
        query, value_key, run, slope, column, row, d_mixed, states, state_back, low, up_all
    )
    d_gates = d_gates.reshape(rows, DV)
    grad_out = matmul_tn(d_attn, heads)
    grad_gate = matmul_tn(normed, d_gates)
    grad_fourth = ring.scatter(narrow(jnp.concatenate([grad_gate, grad_out], axis=1)))
    d_low = narrow(d_low.reshape(rows, rank))
    d_last = jnp.concatenate(
        [d_value.reshape(rows, DV), d_key.reshape(rows, DK), d_query.reshape(rows, DK)], axis=1
    )
    d_normed_part = (
        matmul_nt(jnp.concatenate([d_last, d_gates], axis=1), projections)
        + matmul_nt(d_low, down_all)
    )
    d_normed = head_scatter(narrow(d_normed_part))
    scale_own = root_scale(inputs_own)
    unit_own = inputs_own * scale_own
    d_unit = norm_back(d_normed * gain_one, unit_own, scale_own)
    input_grad = ring.home(head_gather(narrow(d_resid + d_unit)), 1)
    unit_all = ring.near(wide(inputs) * root_scale(wide(inputs)), 1)
    grad_gain_one = jnp.sum(d_normed_part * unit_all, axis=0)

    small = jnp.concatenate(
        [
            grad_gain_head.reshape(count, -1),
            grad_bias.reshape(count, -1),
            jnp.swapaxes(grad_up.reshape(rank, count, -1), 0, 1).reshape(count, -1),
        ],
        axis=1,
    )
    small = columns_of(ring.near(small, 0), share).reshape(width, -1)
    small = jnp.concatenate([grad_gain_one[:, None], grad_gain_two[:, None], small], axis=1)
    used = d_last.shape[1] + rank
    spare = -(used + small.shape[1]) % 128
    d_last = jnp.concatenate(
        [d_last, d_low, jnp.zeros((rows, small.shape[1] + spare), BF16)], axis=1
    )
    grad_last = matmul_tn(normed, d_last) + jnp.pad(small, ((0, 0), (used, spare)))
    grad_last = ring.scatter(narrow(grad_last))
    shared = grad_last[:, used - rank :]
    distance = 1
    while distance < lax.axis_size("head"):
        shared = shared + lax.ppermute(shared, "head", swap("head", distance))
        distance *= 2

    def lone(field):
        return jnp.swapaxes(field[:, rank + 2 : rank + small.shape[1]], 0, 1).reshape(-1)

    own = lone(grad_last[:, used - rank :])
    bounds = [0, head_gain.size, head_gain.size + decay_bias.size]
    bounds.append(bounds[2] + decay_up.size)
    return (
        layer_out.reshape(batch, block, width),
        input_grad.reshape(batch, block, width),
        shared[:, rank],
        grad_last[:, DV + DK : DV + 2 * DK],
        grad_last[:, DV : DV + DK],
        grad_last[:, :DV],
        grad_fourth[:, :DV],
        shared[:, :rank],
        own[bounds[2] : bounds[3]].reshape(rank, -1),
        own[bounds[1] : bounds[2]],
        lone(shared)[: bounds[1]],
        grad_fourth[:, DV:].T,
        shared[:, rank + 1],
        grad_third[:, :hidden],
        grad_third[:, hidden:],
        grad_fdown.T,
    )


def fused_layer(
    layer_in,
    seg_starts,
    attn_gain,
    query_weight,
    key_weight,
    value_weight,
    gate_weight,
    decay_down,
    decay_up,
    decay_bias,
    head_gain,
    out_weight,
    ffn_gain,
    ffn_gate,
    ffn_up,
    ffn_down,
    out_grad,
):
    count = lax.axis_size("seq")
    batch, block, width = layer_in.shape
    rows = batch * block
    rank, share = decay_down.shape[1], attn_gain.shape[0]
    hidden = ffn_gate.shape[1]
    used = 2 * DV + 2 * DK
    inputs, grad_rows = layer_in.reshape(rows, width), out_grad.reshape(rows, width)
    starts = seg_starts.reshape(-1, CHUNK)
    small = jnp.concatenate([attn_gain, ffn_gain, head_gain, decay_bias])
    small = jnp.pad(small, (0, -small.size % 128))[None]

    def tokens(field):
        return field.reshape(batch, block, field.shape[-1])

    (
        normed, weights, out_t, down_block, down, value_key, query, gates, low, gains, gain_head, bias, up
    ) = enter(
        inputs, value_weight, key_weight, query_weight, gate_weight, decay_down, out_weight, ffn_down,
        small, decay_up,
    )
    value_key, query, gates, low = map(tokens, (value_key, query, gates, low))
    weights, out_t = weights.reshape(width, -1), out_t.reshape(width, DV)
    run, slope, total, mixed, heads, states, part, fgate, fdown = token_phase(
        value_key, query, gates, low, up, bias, starts, gain_head, out_t, ffn_gate, down_block, EARLY
    )
    resid, normed_two, fup = row_phase(part, inputs, gains, ffn_up)
    fgate, fup = fgate.reshape(width, hidden), fup.reshape(width, hidden)
    act, d_gate, d_up, ffn_part, part = unit_phase(normed_two, fgate, fup, grad_rows, down_block, fdown)
    (
        d_resid, d_attn, d_gates, d_mixed, state_back, grad_gain_two, grad_gain_head, layer_out, grad_first
    ) = resid_phase(
        part, resid, grad_rows, gains, out_t, act, normed_two, d_up, gates, mixed, gain_head, query,
        run, starts, total, ffn_part,
    )
    packed, d_low, grad_up, grad_bias, part, grad_fgate = back_phase(
        query, value_key, run, slope, states, low, up, starts, d_mixed, state_back, d_gates,
        normed_two, d_gate, weights, down,
    )
    packed = packed.reshape(rows, -1)
    input_grad, grad_last, small, tail = last_phase(
        part, inputs, d_resid, gains, normed, packed, d_attn, heads.reshape(rows, DV),
        grad_gain_two, grad_gain_head, grad_bias, grad_up, d_low.reshape(rows, rank),
    )
    lines = share // 128
    results = leave(layer_out, input_grad, grad_first, grad_fgate, grad_last)
    layer_out, input_grad, grad_query, grad_key, grad_value, grad_gate, grad_out = results[:7]
    return (
        layer_out.reshape(batch, block, width),
        input_grad.reshape(batch, block, width),
        small[2 : 2 + lines].reshape(share),
        grad_query,
        grad_key,
        grad_value,
        grad_gate,
        jnp.swapaxes(tail.reshape(2, rank, share // 2), 1, 2).reshape(share, rank),
        small[8:, : decay_up.shape[1]],
        small[1, : decay_bias.size],
        small[0, : head_gain.size],
        grad_out,
        small[4 : 4 + lines].reshape(share),
        *results[7:],
    )


def shards(layer_in, seg_starts, attn_gain, *rest):
    fits = attn_gain.shape[0] == 256 and lax.axis_size("head") == 4
    layer = fused_layer if fits and rest[4].shape[1] == 16 else plain_layer
    return layer(layer_in, seg_starts, attn_gain, *rest)


def solution(mesh):
    return jax.shard_map(
        shards,
        mesh=mesh,
        in_specs=(
            P(None, "seq", None),
            P(None, "seq"),
            P("seq"),
            P("seq", "head"),
            P("seq", "head"),
            P("seq", "head"),
            P("seq", "head"),
            P("seq", None),
            P(None, ("head", "seq")),
            P(("head", "seq")),
            P("seq"),
            P("head", "seq"),
            P("seq"),
            P("seq", "head"),
            P("seq", "head"),
            P("head", "seq"),
            P(None, "seq", None),
        ),
        out_specs=(
            P(None, "seq", None),
            P(None, "seq", None),
            P("seq"),
            P("seq", "head"),
            P("seq", "head"),
            P("seq", "head"),
            P("seq", "head"),
            P("seq", None),
            P(None, ("head", "seq")),
            P(("head", "seq")),
            P("seq"),
            P("head", "seq"),
            P("seq"),
            P("seq", "head"),
            P("seq", "head"),
            P("head", "seq"),
        ),
        check_vma=False,
    )
```
